32 devices in a mesh: dp: 32 (over z, y, x, core).
Axes of the slice: x: 2, y: 2, z: 4, core: 2. Of those that a mesh axis runs over, the one named last changes fastest.
Arguments:
- hidden_in: bfloat16 [4096, 640], P('dp'), may hold values from -6 to 6
- cotangent: bfloat16 [4096, 640], P('dp'), may hold values from -6 to 6
- params: float32 [5573632], P('dp'), may hold values from -4 to 4
- moment_one: float32 [5573632], P('dp'), may hold values from -6 to 6
- moment_two: float32 [5573632], P('dp'), may hold values from 0.02 to 0.5
- seq_lengths: int32 [64], replicated, may hold values from 0 to 128, as said below
- seq_owner: int32 [64], replicated, may hold values from 0 to 31, as said below
Outputs:
- block_out: bfloat16 [4096, 640], P('dp')
- grad_in: float32 [4096, 640], P('dp')
- grad_flat: float32 [5573632], P('dp')
- params_new: float32 [5573632], P('dp')
- moment_one_new: float32 [5573632], P('dp')
- moment_two_new: float32 [5573632], P('dp')
The draws below stay inside these ranges and needn't reach their ends.
Inputs may be any that keep to these rules, and one draw needn't show every extreme that they name: `seq_lengths`: sequences 2j and 2j + 1 go to the same device; on each device their lengths sum to 1 to 128, and sequence 2j has a token or more; one sequence has exactly 128 tokens and its partner has none; other sequences 2j + 1 may have none too. `seq_owner`: each device holds exactly the two sequences 2j and 2j + 1 for one j.
All inputs are finite; a program needn't handle non-finite values.
Results may differ from the reference program's by a relative error of at most 0.012.
The reference program's roundings to bfloat16 on the way count: a program that leaves them out, or rounds other values in their place, can miss the bound.
Values may be sent and summed in bfloat16 or wider, within the bound.
No kernel may reach another device: no remote copies, remote signals or barrier semaphores. Data moves between devices by JAX's collectives and lax.ppermute only.
A program may use at most 128 MiB of HBM per device.

```python
import math
import jax
import jax.numpy as jnp
from jax import lax

D = 640
FF = 2048
HD = 256
HQ = 1024
CAP = 128
WINDOW = 64
STEP = 3
TOKENS = 4096
G1LEN = 1638400
G2LEN = 3932160
G3LEN = 3072
FLAT = 5573632
N_DP = 32


def normal_block(key, entries, fan_in):
    return jax.random.truncated_normal(key, -3.0, 3.0, (entries,), jnp.float32) * fan_in ** (-0.5)


def draw_params(key, part):
    subkeys = jax.random.split(jax.random.fold_in(key, 11), 9)
    attn_group = jnp.concatenate([normal_block(subkeys[0], D * HQ, D), normal_block(subkeys[1], D * HD, D), normal_block(subkeys[2], D * HD, D), normal_block(subkeys[3], HQ * D, HQ) * 2.0])
    ffn_group = jnp.concatenate([normal_block(subkeys[4], D * FF, D), normal_block(subkeys[5], D * FF, D), normal_block(subkeys[6], FF * D, FF)])
    outer_gains = jax.random.uniform(subkeys[7], (4 * D,), jnp.float32, -0.3, 0.3)
    inner_gains = jax.random.uniform(subkeys[8], (2 * HD,), jnp.float32, -0.3, 0.3)
    gain_group = jnp.concatenate([outer_gains[:D], inner_gains, outer_gains[D:]])
    table = jnp.concatenate([attn_group.reshape(N_DP, -1), ffn_group.reshape(N_DP, -1), gain_group.reshape(N_DP, -1)], axis=1)
    return table.reshape(-1)


def pair_draw(key):
    subkeys = jax.random.split(jax.random.fold_in(key, 29), 5)
    pair_index = jnp.arange(N_DP, dtype=jnp.int32)
    radius = jax.random.randint(subkeys[0], (N_DP,), 7, 17)
    summed = jnp.maximum(CAP * radius * radius // 256, 1)
    chosen = jax.random.randint(subkeys[1], (), 0, N_DP)
    summed = jnp.where(pair_index == chosen, CAP, summed)
    divided = jax.random.randint(subkeys[2], (N_DP,), 0, 2)
    divided = jnp.where(pair_index == chosen, 0, divided)
    leading = 1 + jax.random.randint(subkeys[3], (N_DP,), 0, jnp.maximum(summed - 1, 1))
    leading = jnp.where(divided == 1, leading, summed)
    trailing = summed - leading
    lengths = jnp.stack([leading, trailing], axis=1).reshape(-1).astype(jnp.int32)
    owners = jnp.repeat(jax.random.permutation(subkeys[4], N_DP).astype(jnp.int32), 2)
    return (lengths, owners)


def draw_seq_lengths(key, part):
    return pair_draw(key)[0]


def draw_seq_owner(key, part):
    return pair_draw(key)[1]


def levels(stream_key, shape, pieces, low, top_value):
    factor_of = 1.0
    for dim, parts in pieces:
        draws = jax.random.uniform(jax.random.fold_in(jax.random.fold_in(stream_key, 6), dim), (parts,), jnp.float32, low / len(pieces), top_value / len(pieces))
        factor_of = factor_of * jnp.repeat(jnp.exp(draws), shape[dim] // parts).reshape((-1,) + (1,) * (len(shape) - 1 - dim))
    return factor_of


def noise(own_key, extent, spread, reach, shards=(), held_as=jnp.bfloat16):
    drawn = spread * jax.random.normal(own_key, extent, jnp.float32)
    if shards:
        drawn = drawn * levels(own_key, extent, shards, -0.22, 0.18)
    return jnp.clip(drawn, -reach, reach).astype(held_as)


def setup_inputs(seed: int = 0) -> dict:
    key_list = jax.random.split(jax.random.key(seed), 8)
    hidden_in = noise(key_list[0], (TOKENS, D), 1.0, 6.0, ((0, 32),))
    cotangent = noise(key_list[1], (TOKENS, D), 1.0, 6.0, ((0, 32),))
    params = draw_params(jax.random.fold_in(key_list[7], 71), 0)
    moment_one = noise(key_list[3], (FLAT,), 1.5, 6.0, ((0, 32),), jnp.float32)
    moment_two = jnp.clip(jnp.exp(math.log(0.5) - 3.218876 * jax.random.uniform(key_list[4], (FLAT,), jnp.float32) ** levels(key_list[4], (FLAT,), ((0, 32),), -0.2, 0.2)), 0.02, 0.5)
    seq_lengths = draw_seq_lengths(jax.random.fold_in(key_list[7], 71), 0)
    seq_owner = draw_seq_owner(jax.random.fold_in(key_list[7], 71), 0)
    return dict(hidden_in=hidden_in, cotangent=cotangent, params=params, moment_one=moment_one, moment_two=moment_two, seq_lengths=seq_lengths, seq_owner=seq_owner)


def rms_scale(values, gain_vec):
    return values * lax.rsqrt(lax.optimization_barrier(jnp.mean(values * values, axis=-1, keepdims=True)) + 1e-06) * (1.0 + gain_vec)

def rotate(values, cos_tab, sin_tab):
    half_dim = values.shape[-1] // 2
    lower_half = values[..., :half_dim]
    upper_half = values[..., half_dim:]
    return jnp.concatenate([lower_half * cos_tab - upper_half * sin_tab, upper_half * cos_tab + lower_half * sin_tab], axis=-1)

def query_key(query_raw, key_raw, gain_query, gain_key, cos_tab, sin_tab):
    per_head = query_raw.reshape(query_raw.shape[0], -1, HD).transpose(1, 0, 2)
    rot_query = rotate(rms_scale(per_head, gain_query), cos_tab, sin_tab) * HD ** (-0.5)
    rot_key = rotate(rms_scale(key_raw, gain_key), cos_tab, sin_tab)
    return (rot_query, rot_key)

def gated_gelu(gate_proj, up_proj):
    return jax.nn.gelu(gate_proj, approximate=True) * up_proj

def outer_sum(left_side, right_side):
    return lax.dot_general(left_side, right_side, (((0,), (0,)), ((), ())), preferred_element_type=jnp.float32)

def times_transposed(rows_in, matrix):
    return lax.dot_general(rows_in, matrix, (((1,), (1,)), ((), ())), preferred_element_type=jnp.float32)

def slot_setup(seq_lengths, seq_owner, device):
    mine_mask = seq_owner == device
    own_lengths = jnp.where(mine_mask, seq_lengths, 0).astype(jnp.int32)
    seq_ends = jnp.cumsum(own_lengths, dtype=jnp.int32)
    seq_begins = seq_ends - own_lengths
    slot_index = jnp.arange(CAP, dtype=jnp.int32)
    column = slot_index[:, None]
    inside_mask = mine_mask[None, :] & (seq_begins[None, :] <= column) & (column < seq_ends[None, :])
    live_mask = jnp.any(inside_mask, axis=1)
    seq_label = lax.optimization_barrier(jnp.sum((mine_mask[None, :] & (seq_ends[None, :] <= column)).astype(jnp.int32), axis=1, dtype=jnp.int32))
    position = lax.optimization_barrier(jnp.sum(jnp.where(inside_mask, column - seq_begins[None, :], 0), axis=1, dtype=jnp.int32))
    row_slot = slot_index[:, None]
    col_slot = slot_index[None, :]
    allowed = live_mask[:, None] & live_mask[None, :] & (seq_label[:, None] == seq_label[None, :]) & (col_slot <= row_slot) & (row_slot - col_slot < WINDOW) | (row_slot == col_slot)
    half_dim = HD // 2
    frequency = 10000.0 ** (-2.0 * jnp.arange(half_dim, dtype=jnp.float32) / HD)
    angles = position.astype(jnp.float32)[:, None] * frequency[None, :]
    return (live_mask.astype(jnp.float32), allowed, jnp.cos(angles), jnp.sin(angles))

def attend(rot_query, rot_key, value_vec, allowed):
    num_heads = rot_query.shape[0]
    num_slots = rot_key.shape[0]
    flat_query = rot_query.reshape(num_heads * num_slots, HD)
    scores = lax.dot_general(flat_query, rot_key, (((1,), (1,)), ((), ())), preferred_element_type=jnp.float32)
    scores = jnp.where(allowed[None], scores.reshape(num_heads, num_slots, num_slots), -1e+30)
    row_max = lax.optimization_barrier(jnp.max(scores, axis=-1, keepdims=True))
    raised = jnp.exp(scores - row_max)
    summed = lax.optimization_barrier(jnp.sum(raised, axis=-1, keepdims=True))
    log_total = row_max + jnp.log(summed)
    attn_prob = (raised / summed).astype(jnp.bfloat16)
    context = jnp.dot(attn_prob.reshape(num_heads * num_slots, num_slots), value_vec, preferred_element_type=jnp.float32)
    context = context.reshape(num_heads, num_slots, HD).transpose(1, 0, 2).reshape(num_slots, num_heads * HD)
    return (context.astype(jnp.bfloat16), log_total)

def attend_back(rot_query, rot_key, value_vec, allowed, log_total, context, delta_context):
    num_heads = rot_query.shape[0]
    num_slots = rot_key.shape[0]
    head_delta = delta_context.reshape(num_slots, num_heads, HD).transpose(1, 0, 2).reshape(-1, HD)
    head_context = context.reshape(num_slots, num_heads, HD).transpose(1, 0, 2).reshape(-1, HD)
    row_dot = lax.optimization_barrier(jnp.sum(head_delta.astype(jnp.float32) * head_context.astype(jnp.float32), axis=-1, keepdims=True))
    flat_query = rot_query.reshape(-1, HD)
    scores = lax.dot_general(flat_query, rot_key, (((1,), (1,)), ((), ())), preferred_element_type=jnp.float32)
    scores = jnp.where(allowed[None], scores.reshape(num_heads, num_slots, num_slots), -1e+30)
    prob_exact = jnp.exp(scores - log_total).reshape(-1, num_slots)
    delta_value = lax.dot_general(prob_exact.astype(jnp.bfloat16), head_delta, (((0,), (0,)), ((), ())), preferred_element_type=jnp.float32)
    delta_prob = lax.dot_general(head_delta, value_vec, (((1,), (1,)), ((), ())), preferred_element_type=jnp.float32)
    delta_score = (prob_exact * (delta_prob - row_dot)).astype(jnp.bfloat16)
    delta_query = jnp.dot(delta_score, rot_key, preferred_element_type=jnp.float32).reshape(num_heads, num_slots, HD)
    delta_key = lax.dot_general(delta_score, flat_query, (((0,), (0,)), ((), ())), preferred_element_type=jnp.float32)
    return (delta_query, delta_key, delta_value.astype(jnp.bfloat16))

def split_groups(flat_vec, devices):
    table = flat_vec.reshape(devices, -1)
    attn_len = G1LEN // devices
    ffn_len = G2LEN // devices
    return (table[:, :attn_len].reshape(-1), table[:, attn_len:attn_len + ffn_len].reshape(-1), table[:, attn_len + ffn_len:].reshape(-1))

def join_groups(groups, devices):
    return jnp.concatenate([member.reshape(devices, -1) for member in groups], axis=1).reshape(-1)

def flat_join(arrays):
    return jnp.concatenate([member.reshape(-1) for member in arrays])

def unpack_weights(attn_flat, ffn_flat, gain_flat):
    cut_query = D * HQ
    cut_key = cut_query + D * HD
    cut_value = cut_key + D * HD
    query_weight = attn_flat[:cut_query].reshape(D, HQ)
    key_weight = attn_flat[cut_query:cut_key].reshape(D, HD)
    value_weight = attn_flat[cut_key:cut_value].reshape(D, HD)
    out_weight = attn_flat[cut_value:].reshape(HQ, D)
    cut_gate = D * FF
    gate_weight = ffn_flat[:cut_gate].reshape(D, FF)
    up_weight = ffn_flat[cut_gate:2 * cut_gate].reshape(D, FF)
    down_weight = ffn_flat[2 * cut_gate:].reshape(FF, D)
    gains = gain_flat.astype(jnp.float32)
    gain_set = (gains[:D], gains[D:D + HD], gains[D + HD:D + 2 * HD], gains[D + 2 * HD:2 * D + 2 * HD], gains[2 * D + 2 * HD:3 * D + 2 * HD], gains[3 * D + 2 * HD:])
    return (query_weight, key_weight, value_weight, out_weight, gate_weight, up_weight, down_weight, gain_set)

def forward_pass(input_rows, weights, allowed, cos_tab, sin_tab):
    query_weight, key_weight, value_weight, out_weight, gate_weight, up_weight, down_weight, gain_set = weights
    gain_in, gain_query, gain_key, gain_post, gain_mid, gain_last = gain_set
    resid_in = input_rows.astype(jnp.float32)
    normed_in = rms_scale(resid_in, gain_in).astype(jnp.bfloat16)
    query_raw = jnp.dot(normed_in, query_weight, preferred_element_type=jnp.float32)
    key_raw = jnp.dot(normed_in, key_weight, preferred_element_type=jnp.float32)
    value_vec = jnp.dot(normed_in, value_weight, preferred_element_type=jnp.float32).astype(jnp.bfloat16)
    rot_query, rot_key = query_key(query_raw, key_raw, gain_query, gain_key, cos_tab, sin_tab)
    rot_query = rot_query.astype(jnp.bfloat16)
    rot_key = rot_key.astype(jnp.bfloat16)
    context, log_total = attend(rot_query, rot_key, value_vec, allowed)
    attn_out = jnp.dot(context, out_weight, preferred_element_type=jnp.float32)
    mid_stream = resid_in + rms_scale(attn_out, gain_post)
    normed_mid = rms_scale(mid_stream, gain_mid).astype(jnp.bfloat16)
    gate_proj = jnp.dot(normed_mid, gate_weight, preferred_element_type=jnp.float32)
    up_proj = jnp.dot(normed_mid, up_weight, preferred_element_type=jnp.float32)
    hidden = gated_gelu(gate_proj, up_proj).astype(jnp.bfloat16)
    ffn_out = jnp.dot(hidden, down_weight, preferred_element_type=jnp.float32)
    block_out = (mid_stream + rms_scale(ffn_out, gain_last)).astype(jnp.bfloat16)
    saved = (resid_in, normed_in, query_raw, key_raw, value_vec, rot_query, rot_key, context, log_total, attn_out, mid_stream, normed_mid, gate_proj, up_proj, hidden, ffn_out)
    return (block_out, saved)

def ffn_backward(cot_rows, live_mask, weights, saved):
    gate_weight, up_weight, down_weight, gain_set = (weights[4], weights[5], weights[6], weights[7])
    gain_mid, gain_last = (gain_set[4], gain_set[5])
    mid_stream, normed_mid, gate_proj, up_proj, hidden, ffn_out = saved[10:]
    delta_out = cot_rows.astype(jnp.float32) * live_mask[:, None]
    unused, pullback = jax.vjp(rms_scale, ffn_out, gain_last)
    delta_ffn, gain_last_grad = pullback(delta_out)
    delta_ffn = delta_ffn.astype(jnp.bfloat16)
    down_grad = outer_sum(hidden, delta_ffn)
    delta_hidden = times_transposed(delta_ffn, down_weight)
    unused, pullback = jax.vjp(gated_gelu, gate_proj, up_proj)
    delta_gate, delta_up = pullback(delta_hidden)
    delta_gate = delta_gate.astype(jnp.bfloat16)
    delta_up = delta_up.astype(jnp.bfloat16)
    gate_grad = outer_sum(normed_mid, delta_gate)
    up_grad = outer_sum(normed_mid, delta_up)
    delta_normed = times_transposed(delta_gate, gate_weight) + times_transposed(delta_up, up_weight)
    unused, pullback = jax.vjp(rms_scale, mid_stream, gain_mid)
    delta_part, gain_mid_grad = pullback(delta_normed)
    delta_mid = delta_out + delta_part
    return (delta_mid, (gate_grad, up_grad, down_grad), (gain_mid_grad, gain_last_grad))

def attn_backward(delta_mid, weights, saved, allowed, cos_tab, sin_tab):
    query_weight, key_weight, value_weight, out_weight = weights[:4]
    gain_in, gain_query, gain_key, gain_post = weights[7][:4]
    resid_in, normed_in, query_raw, key_raw, value_vec, rot_query, rot_key, context, log_total, attn_out = saved[:10]
    unused, pullback = jax.vjp(rms_scale, attn_out, gain_post)
    delta_attn, gain_post_grad = pullback(delta_mid)
    delta_attn = delta_attn.astype(jnp.bfloat16)
    out_grad = outer_sum(context, delta_attn)
    delta_context = times_transposed(delta_attn, out_weight).astype(jnp.bfloat16)
    delta_query, delta_key, delta_value = attend_back(rot_query, rot_key, value_vec, allowed, log_total, context, delta_context)

    def rope_map(raw_query, raw_key, query_gain, key_gain):
        return query_key(raw_query, raw_key, query_gain, key_gain, cos_tab, sin_tab)
    unused, pullback = jax.vjp(rope_map, query_raw, key_raw, gain_query, gain_key)
    delta_qraw, delta_kraw, gain_query_grad, gain_key_grad = pullback((delta_query, delta_key))
    delta_qraw = delta_qraw.astype(jnp.bfloat16)
    delta_kraw = delta_kraw.astype(jnp.bfloat16)
    query_grad = outer_sum(normed_in, delta_qraw)
    key_grad = outer_sum(normed_in, delta_kraw)
    value_grad = outer_sum(normed_in, delta_value)
    delta_in = times_transposed(delta_qraw, query_weight) + times_transposed(delta_kraw, key_weight) + times_transposed(delta_value, value_weight)
    unused, pullback = jax.vjp(rms_scale, resid_in, gain_in)
    delta_part, gain_in_grad = pullback(delta_in)
    grad_in = delta_mid + delta_part
    return (grad_in, (query_grad, key_grad, value_grad, out_grad), (gain_in_grad, gain_query_grad, gain_key_grad, gain_post_grad))

def adam_update(weight_shard, gradient, moment_one, moment_two):
    moment_one = 0.9 * moment_one + 0.1 * gradient
    moment_two = 0.999 * moment_two + 0.001 * gradient * gradient
    fix_one = 1.0 - 0.9 ** STEP
    fix_two = 1.0 - 0.999 ** STEP
    weight_shard = weight_shard - 0.02 * (moment_one / fix_one / (jnp.sqrt(moment_two / fix_two) + 1e-08) + 0.1 * weight_shard)
    return (weight_shard, moment_one, moment_two)

def reference(hidden_in, cotangent, params, moment_one, moment_two, seq_lengths, seq_owner):
    weights = unpack_weights(*split_groups(params.astype(jnp.bfloat16), N_DP))

    def one_block(running, block_item):
        input_rows, cot_rows, device = block_item
        live_mask, allowed, cos_tab, sin_tab = slot_setup(seq_lengths, seq_owner, device)
        block_out, saved = forward_pass(input_rows, weights, allowed, cos_tab, sin_tab)
        delta_mid, ffn_grads, late_gains = ffn_backward(cot_rows, live_mask, weights, saved)
        grad_in, attn_grads, early_gains = attn_backward(delta_mid, weights, saved, allowed, cos_tab, sin_tab)
        groups = (flat_join(attn_grads), flat_join(ffn_grads), flat_join(early_gains + late_gains))
        return (tuple((total + term for total, term in zip(running, groups))), (block_out, grad_in))
    zeros = (jnp.zeros((G1LEN,), jnp.float32), jnp.zeros((G2LEN,), jnp.float32), jnp.zeros((G3LEN,), jnp.float32))
    items = (hidden_in.reshape(N_DP, CAP, D), cotangent.reshape(N_DP, CAP, D), jnp.arange(N_DP, dtype=jnp.int32))
    groups, (outputs, input_grads) = lax.scan(one_block, zeros, items)
    grad_flat = join_groups(groups, N_DP)
    params_new, moment_one_new, moment_two_new = adam_update(params, grad_flat, moment_one, moment_two)
    return (outputs.reshape(TOKENS, D), input_grads.reshape(TOKENS, D), grad_flat, params_new, moment_one_new, moment_two_new)
```

```python
import jax
import jax.numpy as jnp
from jax import lax
from jax.sharding import PartitionSpec as P

D = 640
FF = 2048
HD = 256
HQ = 1024
CAP = 128
WINDOW = 64
STEP = 3
G1LEN = 1638400
G2LEN = 3932160
LANES = 128
ROWS = 16


def rms_scale(values, gain_vec):
    return (
        values
        * lax.rsqrt(jnp.mean(values * values, axis=-1, keepdims=True) + 1e-06)
        * (1.0 + gain_vec)
    )


def rotate(values, cos_tab, sin_tab):
    half_dim = values.shape[-1] // 2
    lower_half = values[..., :half_dim]
    upper_half = values[..., half_dim:]
    return jnp.concatenate(
        [lower_half * cos_tab - upper_half * sin_tab, upper_half * cos_tab + lower_half * sin_tab],
        axis=-1,
    )


def query_key(query_raw, key_raw, gain_query, gain_key, cos_tab, sin_tab):
    per_head = query_raw.reshape(query_raw.shape[0], -1, HD).transpose(1, 0, 2)
    rot_query = rotate(rms_scale(per_head, gain_query), cos_tab, sin_tab) * HD ** (-0.5)
    rot_key = rotate(rms_scale(key_raw, gain_key), cos_tab, sin_tab)
    return (rot_query, rot_key)


def gated_gelu(gate_proj, up_proj):
    return jax.nn.gelu(gate_proj, approximate=True) * up_proj


def outer_sum(left_side, right_side):
    return lax.dot_general(
        left_side, right_side, (((0,), (0,)), ((), ())), preferred_element_type=jnp.float32
    )


def times_transposed(rows_in, matrix):
    return lax.dot_general(
        rows_in, matrix, (((1,), (1,)), ((), ())), preferred_element_type=jnp.float32
    )


def slot_setup(seq_lengths, seq_owner, device):
    mine_mask = seq_owner == device
    own_lengths = jnp.where(mine_mask, seq_lengths, 0)
    seq_ends = jnp.cumsum(own_lengths, dtype=jnp.int32)
    seq_begins = seq_ends - own_lengths
    slot_index = jnp.arange(CAP, dtype=jnp.int32)
    column = slot_index[:, None]
    inside_mask = (
        mine_mask[None, :] & (seq_begins[None, :] <= column) & (column < seq_ends[None, :])
    )
    live_mask = jnp.any(inside_mask, axis=1)
    seq_label = jnp.sum(
        (mine_mask[None, :] & (seq_ends[None, :] <= column)).astype(jnp.int32),
        axis=1,
        dtype=jnp.int32,
    )
    position = jnp.sum(
        jnp.where(inside_mask, column - seq_begins[None, :], 0), axis=1, dtype=jnp.int32
    )
    row_slot = slot_index[:, None]
    col_slot = slot_index[None, :]
    allowed = live_mask[:, None] & live_mask[None, :] & (
        seq_label[:, None] == seq_label[None, :]
    ) & (col_slot <= row_slot) & (row_slot - col_slot < WINDOW) | (row_slot == col_slot)
    half_dim = HD // 2
    frequency = 10000.0 ** (-2.0 * jnp.arange(half_dim, dtype=jnp.float32) / HD)
    angles = position.astype(jnp.float32)[:, None] * frequency[None, :]
    return (live_mask.astype(jnp.float32), allowed, jnp.cos(angles), jnp.sin(angles))


def attend(rot_query, rot_key, value_vec, allowed):
    num_heads = rot_query.shape[0]
    num_slots = rot_key.shape[0]
    flat_query = rot_query.reshape(num_heads * num_slots, HD)
    scores = lax.dot_general(
        flat_query, rot_key, (((1,), (1,)), ((), ())), preferred_element_type=jnp.float32
    )
    scores = jnp.where(allowed[None], scores.reshape(num_heads, num_slots, num_slots), -1e30)
    row_max = jnp.max(scores, axis=-1, keepdims=True)
    raised = jnp.exp(scores - row_max)
    summed = jnp.sum(raised, axis=-1, keepdims=True)
    log_total = row_max + jnp.log(summed)
    attn_prob = (raised / summed).astype(jnp.bfloat16)
    context = jnp.dot(
        attn_prob.reshape(num_heads * num_slots, num_slots),
        value_vec,
        preferred_element_type=jnp.float32,
    )
    context = (
        context.reshape(num_heads, num_slots, HD)
        .transpose(1, 0, 2)
        .reshape(num_slots, num_heads * HD)
    )
    return (context.astype(jnp.bfloat16), log_total)


def attend_back(rot_query, rot_key, value_vec, allowed, log_total, context, delta_context):
    num_heads = rot_query.shape[0]
    num_slots = rot_key.shape[0]
    head_delta = delta_context.reshape(num_slots, num_heads, HD).transpose(1, 0, 2).reshape(-1, HD)
    head_context = context.reshape(num_slots, num_heads, HD).transpose(1, 0, 2).reshape(-1, HD)
    row_dot = jnp.sum(
        head_delta.astype(jnp.float32) * head_context.astype(jnp.float32), axis=-1, keepdims=True
    )
    flat_query = rot_query.reshape(-1, HD)
    scores = lax.dot_general(
        flat_query, rot_key, (((1,), (1,)), ((), ())), preferred_element_type=jnp.float32
    )
    scores = jnp.where(allowed[None], scores.reshape(num_heads, num_slots, num_slots), -1e30)
    prob_exact = jnp.exp(scores - log_total).reshape(-1, num_slots)
    delta_value = lax.dot_general(
        prob_exact.astype(jnp.bfloat16),
        head_delta,
        (((0,), (0,)), ((), ())),
        preferred_element_type=jnp.float32,
    )
    delta_prob = lax.dot_general(
        head_delta, value_vec, (((1,), (1,)), ((), ())), preferred_element_type=jnp.float32
    )
    delta_score = (prob_exact * (delta_prob - row_dot)).astype(jnp.bfloat16)
    delta_query = jnp.dot(delta_score, rot_key, preferred_element_type=jnp.float32).reshape(
        num_heads, num_slots, HD
    )
    delta_key = lax.dot_general(
        delta_score, flat_query, (((0,), (0,)), ((), ())), preferred_element_type=jnp.float32
    )
    return (delta_query, delta_key, delta_value.astype(jnp.bfloat16))


def flat_table(arrays, devices, rows):
    flat = jnp.concatenate([member.astype(jnp.bfloat16).reshape(-1) for member in arrays])
    table = flat.reshape(devices, -1)
    short = rows * LANES - table.shape[1]
    if short:
        table = jnp.concatenate([table, jnp.zeros((devices, short), jnp.bfloat16)], axis=1)
    return table.reshape(devices, rows, LANES)


def bit_orders(devices, tuned):
    bits = devices.bit_length() - 1
    if bits == 5:
        return [["cxyab".index(letter) for letter in order] for order in tuned]
    return [[1 + (shift + step) % (bits - 1) for step in range(bits - 1)] for shift in range(3)]


def across(block, bit, devices):
    return lax.ppermute(block, "dp", [(i, i ^ (1 << bit)) for i in range(devices)])


def gather_chunk(piece, order, devices, device):
    order = list(order) + [0]
    held = piece[None]
    for bit in order:
        high = (device >> bit) & 1
        other = across(held, bit, devices)
        grown = jnp.zeros((2,) + held.shape, held.dtype)
        grown = lax.dynamic_update_index_in_dim(grown, held, high, 0)
        grown = lax.dynamic_update_index_in_dim(grown, other, 1 - high, 0)
        held = grown.reshape((-1,) + piece.shape)
    held = held.reshape((2,) * len(order) + piece.shape)
    slowest = order[::-1]
    axes = [slowest.index(bit) for bit in range(len(order) - 1, -1, -1)]
    held = held.transpose(axes + [len(order), len(order) + 1])
    return held.reshape((devices,) + piece.shape)


def scatter_chunk(table, order, devices, device):
    left = list(range(devices.bit_length() - 2, -1, -1))
    table = table.reshape((2,) * len(left) + table.shape[1:])
    for bit in [0] + list(order):
        axis = left.index(bit)
        high = (device >> bit) & 1
        away = lax.dynamic_index_in_dim(table, 1 - high, axis, keepdims=False)
        home = lax.dynamic_index_in_dim(table, high, axis, keepdims=False)
        came = across(away, bit, devices)
        table = home.astype(jnp.float32) + came.astype(jnp.float32)
        left.remove(bit)
        if left:
            table = table.astype(jnp.bfloat16)
    return table


def cut_rows(rows, parts):
    each = -(-rows // (parts * ROWS)) * ROWS
    return [(low, min(low + each, rows)) for low in range(0, rows, each)]


def unpack_weights(attn_flat, ffn_flat, gain_flat):
    cut_query = D * HQ
    cut_key = cut_query + D * HD
    cut_value = cut_key + D * HD
    query_weight = attn_flat[:cut_query].reshape(D, HQ)
    key_weight = attn_flat[cut_query:cut_key].reshape(D, HD)
    value_weight = attn_flat[cut_key:cut_value].reshape(D, HD)
    out_weight = attn_flat[cut_value:].reshape(HQ, D)
    cut_gate = D * FF
    gate_weight = ffn_flat[:cut_gate].reshape(D, FF)
    up_weight = ffn_flat[cut_gate : 2 * cut_gate].reshape(D, FF)
    down_weight = ffn_flat[2 * cut_gate :].reshape(FF, D)
    gains = gain_flat.astype(jnp.float32)
    gain_set = (
        gains[:D],
        gains[D : D + HD],
        gains[D + HD : D + 2 * HD],
        gains[D + 2 * HD : 2 * D + 2 * HD],
        gains[2 * D + 2 * HD : 3 * D + 2 * HD],
        gains[3 * D + 2 * HD :],
    )
    return (
        query_weight,
        key_weight,
        value_weight,
        out_weight,
        gate_weight,
        up_weight,
        down_weight,
        gain_set,
    )


def forward_pass(input_rows, weights, allowed, cos_tab, sin_tab):
    (
        query_weight,
        key_weight,
        value_weight,
        out_weight,
        gate_weight,
        up_weight,
        down_weight,
        gain_set,
    ) = weights
    gain_in, gain_query, gain_key, gain_post, gain_mid, gain_last = gain_set
    resid_in = input_rows.astype(jnp.float32)
    normed_in = rms_scale(resid_in, gain_in).astype(jnp.bfloat16)
    query_raw = jnp.dot(normed_in, query_weight, preferred_element_type=jnp.float32)
    key_raw = jnp.dot(normed_in, key_weight, preferred_element_type=jnp.float32)
    value_vec = jnp.dot(normed_in, value_weight, preferred_element_type=jnp.float32).astype(
        jnp.bfloat16
    )
    rot_query, rot_key = query_key(query_raw, key_raw, gain_query, gain_key, cos_tab, sin_tab)
    rot_query = rot_query.astype(jnp.bfloat16)
    rot_key = rot_key.astype(jnp.bfloat16)
    context, log_total = attend(rot_query, rot_key, value_vec, allowed)
    attn_out = jnp.dot(context, out_weight, preferred_element_type=jnp.float32)
    mid_stream = resid_in + rms_scale(attn_out, gain_post)
    normed_mid = rms_scale(mid_stream, gain_mid).astype(jnp.bfloat16)
    gate_proj = jnp.dot(normed_mid, gate_weight, preferred_element_type=jnp.float32)
    up_proj = jnp.dot(normed_mid, up_weight, preferred_element_type=jnp.float32)
    hidden = gated_gelu(gate_proj, up_proj).astype(jnp.bfloat16)
    ffn_out = jnp.dot(hidden, down_weight, preferred_element_type=jnp.float32)
    block_out = (mid_stream + rms_scale(ffn_out, gain_last)).astype(jnp.bfloat16)
    saved = (
        resid_in,
        normed_in,
        query_raw,
        key_raw,
        value_vec,
        rot_query,
        rot_key,
        context,
        log_total,
        attn_out,
        mid_stream,
        normed_mid,
        gate_proj,
        up_proj,
        hidden,
        ffn_out,
    )
    return (block_out, saved)


def ffn_backward(cot_rows, live_mask, weights, saved):
    gate_weight, up_weight, down_weight, gain_set = (weights[4], weights[5], weights[6], weights[7])
    gain_mid, gain_last = (gain_set[4], gain_set[5])
    mid_stream, normed_mid, gate_proj, up_proj, hidden, ffn_out = saved[10:]
    delta_out = cot_rows.astype(jnp.float32) * live_mask[:, None]
    unused, pullback = jax.vjp(rms_scale, ffn_out, gain_last)
    delta_ffn, gain_last_grad = pullback(delta_out)
    delta_ffn = delta_ffn.astype(jnp.bfloat16)
    down_grad = outer_sum(hidden, delta_ffn)
    delta_hidden = times_transposed(delta_ffn, down_weight)
    unused, pullback = jax.vjp(gated_gelu, gate_proj, up_proj)
    delta_gate, delta_up = pullback(delta_hidden)
    delta_gate = delta_gate.astype(jnp.bfloat16)
    delta_up = delta_up.astype(jnp.bfloat16)
    gate_grad = outer_sum(normed_mid, delta_gate)
    up_grad = outer_sum(normed_mid, delta_up)
    delta_normed = times_transposed(delta_gate, gate_weight) + times_transposed(delta_up, up_weight)
    unused, pullback = jax.vjp(rms_scale, mid_stream, gain_mid)
    delta_part, gain_mid_grad = pullback(delta_normed)
    delta_mid = delta_out + delta_part
    return (delta_mid, (gate_grad, up_grad, down_grad), (gain_mid_grad, gain_last_grad))


def attn_backward(delta_mid, weights, saved, allowed, cos_tab, sin_tab):
    query_weight, key_weight, value_weight, out_weight = weights[:4]
    gain_in, gain_query, gain_key, gain_post = weights[7][:4]
    (
        resid_in,
        normed_in,
        query_raw,
        key_raw,
        value_vec,
        rot_query,
        rot_key,
        context,
        log_total,
        attn_out,
    ) = saved[:10]
    unused, pullback = jax.vjp(rms_scale, attn_out, gain_post)
    delta_attn, gain_post_grad = pullback(delta_mid)
    delta_attn = delta_attn.astype(jnp.bfloat16)
    out_grad = outer_sum(context, delta_attn)
    delta_context = times_transposed(delta_attn, out_weight).astype(jnp.bfloat16)
    delta_query, delta_key, delta_value = attend_back(
        rot_query, rot_key, value_vec, allowed, log_total, context, delta_context
    )

    def rope_map(raw_query, raw_key, query_gain, key_gain):
        return query_key(raw_query, raw_key, query_gain, key_gain, cos_tab, sin_tab)

    unused, pullback = jax.vjp(rope_map, query_raw, key_raw, gain_query, gain_key)
    delta_qraw, delta_kraw, gain_query_grad, gain_key_grad = pullback((delta_query, delta_key))
    delta_qraw = delta_qraw.astype(jnp.bfloat16)
    delta_kraw = delta_kraw.astype(jnp.bfloat16)
    query_grad = outer_sum(normed_in, delta_qraw)
    key_grad = outer_sum(normed_in, delta_kraw)
    value_grad = outer_sum(normed_in, delta_value)
    delta_in = (
        times_transposed(delta_qraw, query_weight)
        + times_transposed(delta_kraw, key_weight)
        + times_transposed(delta_value, value_weight)
    )
    unused, pullback = jax.vjp(rms_scale, resid_in, gain_in)
    delta_part, gain_in_grad = pullback(delta_in)
    grad_in = delta_mid + delta_part
    return (
        grad_in,
        (query_grad, key_grad, value_grad, out_grad),
        (gain_in_grad, gain_query_grad, gain_key_grad, gain_post_grad),
    )


def adam_update(weight_shard, gradient, moment_one, moment_two):
    moment_one = 0.9 * moment_one + 0.1 * gradient
    moment_two = 0.999 * moment_two + 0.001 * gradient * gradient
    fix_one = 1.0 - 0.9**STEP
    fix_two = 1.0 - 0.999**STEP
    weight_shard = weight_shard - 0.02 * (
        moment_one / fix_one / (jnp.sqrt(moment_two / fix_two) + 1e-08) + 0.1 * weight_shard
    )
    return (weight_shard, moment_one, moment_two)


def per_device(hidden_in, cotangent, params, moment_one, moment_two, seq_lengths, seq_owner):
    devices = lax.axis_size("dp")
    device = lax.axis_index("dp")
    attn_len = G1LEN // devices
    ffn_len = G2LEN // devices
    gain_len = params.shape[0] - attn_len - ffn_len
    first_rows = -(-(attn_len + gain_len) // (ROWS * LANES)) * ROWS
    second_rows = ffn_len // LANES
    pad = first_rows * LANES - attn_len - gain_len
    rounded = params.astype(jnp.bfloat16)
    first_piece = jnp.concatenate(
        [rounded[:attn_len], rounded[attn_len + ffn_len :], jnp.zeros((pad,), jnp.bfloat16)]
    ).reshape(-1, LANES)
    second_piece = rounded[attn_len : attn_len + ffn_len].reshape(-1, LANES)
    orders = bit_orders(devices, ("abxy", "bxya", "byax"))
    pieces = [first_piece] + [second_piece[low:high] for low, high in cut_rows(second_rows, 2)]
    first_all, *second_all = [
        gather_chunk(piece, order, devices, device) for piece, order in zip(pieces, orders)
    ]
    first_all = first_all.reshape(devices, -1)
    attn_flat = first_all[:, :attn_len].reshape(-1)
    gain_flat = first_all[:, attn_len : attn_len + gain_len].reshape(-1)
    ffn_flat = jnp.concatenate(second_all, axis=1).reshape(-1)
    weights = unpack_weights(attn_flat, ffn_flat, gain_flat)
    live_mask, allowed, cos_tab, sin_tab = slot_setup(seq_lengths, seq_owner, device)
    block_out, saved = forward_pass(hidden_in, weights, allowed, cos_tab, sin_tab)
    delta_mid, ffn_grads, late_gains = ffn_backward(cotangent, live_mask, weights, saved)
    ffn_table = flat_table(ffn_grads, devices, second_rows)
    orders = bit_orders(devices, ("yxba", "ayxb", "xayb"))
    ffn_shard = [
        scatter_chunk(ffn_table[:, low:high], order, devices, device)
        for (low, high), order in zip(cut_rows(second_rows, 3), orders)
    ]
    grad_in, attn_grads, early_gains = attn_backward(
        delta_mid, weights, saved, allowed, cos_tab, sin_tab
    )
    attn_group = flat_table(attn_grads, devices, attn_len // LANES)
    gain_group = flat_table(early_gains + late_gains, devices, first_rows - attn_len // LANES)
    attn_table = jnp.concatenate([attn_group, gain_group], axis=1)
    orders = bit_orders(devices, ("yabx", "axyb", "xyab"))
    attn_shard = [
        scatter_chunk(attn_table[:, low:high], order, devices, device)
        for (low, high), order in zip(cut_rows(first_rows, 3), orders)
    ]
    attn_shard = jnp.concatenate(attn_shard).reshape(-1)
    grad_shard = jnp.concatenate(
        [attn_shard[:attn_len]]
        + [member.reshape(-1) for member in ffn_shard]
        + [attn_shard[attn_len : attn_len + gain_len]]
    )
    params_new, moment_one_new, moment_two_new = adam_update(
        params, grad_shard, moment_one, moment_two
    )
    return (block_out, grad_in, grad_shard, params_new, moment_one_new, moment_two_new)


def solution(mesh):
    in_specs = (P("dp", None), P("dp", None), P("dp"), P("dp"), P("dp"), P(), P())
    out_specs = (P("dp", None), P("dp", None), P("dp"), P("dp"), P("dp"), P("dp"))
    return jax.shard_map(
        per_device, mesh=mesh, in_specs=in_specs, out_specs=out_specs, check_vma=False
    )
```

```python
import functools

import jax
import jax.numpy as jnp
from jax import lax
from jax.experimental import pallas as pl
from jax.experimental.pallas import tpu as pltpu
from jax.sharding import PartitionSpec as P

D = 640
FF = 2048
HD = 256
HQ = 1024
CAP = 128
WINDOW = 64
STEP = 3
G1LEN = 1638400
G2LEN = 3932160
LANES = 128
ROWS = 16
ATTN_SIZES = ((D, HQ), (D, HD), (D, HD), (HQ, D))
FFN_SIZES = ((D, FF), (D, FF), (FF, D))


def rms_scale(values, gain_vec):
    return (
        values
        * lax.rsqrt(jnp.mean(values * values, axis=-1, keepdims=True) + 1e-06)
        * (1.0 + gain_vec)
    )


def rotate(values, cos_tab, sin_tab):
    half_dim = values.shape[-1] // 2
    lower_half = values[..., :half_dim]
    upper_half = values[..., half_dim:]
    return jnp.concatenate(
        [lower_half * cos_tab - upper_half * sin_tab, upper_half * cos_tab + lower_half * sin_tab],
        axis=-1,
    )


def query_key(query_raw, key_raw, gain_query, gain_key, cos_tab, sin_tab):
    per_head = query_raw.reshape(query_raw.shape[0], -1, HD).transpose(1, 0, 2)
    rot_query = rotate(rms_scale(per_head, gain_query), cos_tab, sin_tab) * HD ** (-0.5)
    rot_key = rotate(rms_scale(key_raw, gain_key), cos_tab, sin_tab)
    return (rot_query, rot_key)


def gated_gelu(gate_proj, up_proj):
    return jax.nn.gelu(gate_proj, approximate=True) * up_proj


def times_transposed(rows_in, matrix):
    return lax.dot_general(
        rows_in, matrix, (((1,), (1,)), ((), ())), preferred_element_type=jnp.float32
    )


def slot_setup(seq_lengths, seq_owner, device):
    mine_mask = seq_owner == device
    own_lengths = jnp.where(mine_mask, seq_lengths, 0)
    seq_ends = jnp.cumsum(own_lengths, dtype=jnp.int32)
    seq_begins = seq_ends - own_lengths
    slot_index = jnp.arange(CAP, dtype=jnp.int32)
    column = slot_index[:, None]
    inside_mask = (
        mine_mask[None, :] & (seq_begins[None, :] <= column) & (column < seq_ends[None, :])
    )
    live_mask = jnp.any(inside_mask, axis=1)
    seq_label = jnp.sum(
        (mine_mask[None, :] & (seq_ends[None, :] <= column)).astype(jnp.int32),
        axis=1,
        dtype=jnp.int32,
    )
    position = jnp.sum(
        jnp.where(inside_mask, column - seq_begins[None, :], 0), axis=1, dtype=jnp.int32
    )
    row_slot = slot_index[:, None]
    col_slot = slot_index[None, :]
    allowed = live_mask[:, None] & live_mask[None, :] & (
        seq_label[:, None] == seq_label[None, :]
    ) & (col_slot <= row_slot) & (row_slot - col_slot < WINDOW) | (row_slot == col_slot)
    half_dim = HD // 2
    frequency = 10000.0 ** (-2.0 * jnp.arange(half_dim, dtype=jnp.float32) / HD)
    angles = position.astype(jnp.float32)[:, None] * frequency[None, :]
    return (live_mask.astype(jnp.float32), allowed, jnp.cos(angles), jnp.sin(angles))


def attend(rot_query, rot_key, value_vec, allowed):
    num_heads = rot_query.shape[0]
    num_slots = rot_key.shape[0]
    flat_query = rot_query.reshape(num_heads * num_slots, HD)
    scores = lax.dot_general(
        flat_query, rot_key, (((1,), (1,)), ((), ())), preferred_element_type=jnp.float32
    )
    scores = jnp.where(allowed[None], scores.reshape(num_heads, num_slots, num_slots), -1e30)
    row_max = jnp.max(scores, axis=-1, keepdims=True)
    raised = jnp.exp(scores - row_max)
    summed = jnp.sum(raised, axis=-1, keepdims=True)
    log_total = row_max + jnp.log(summed)
    attn_prob = (raised / summed).astype(jnp.bfloat16)
    context = jnp.dot(
        attn_prob.reshape(num_heads * num_slots, num_slots),
        value_vec,
        preferred_element_type=jnp.float32,
    )
    context = (
        context.reshape(num_heads, num_slots, HD)
        .transpose(1, 0, 2)
        .reshape(num_slots, num_heads * HD)
    )
    return (context.astype(jnp.bfloat16), log_total)


def attend_back(rot_query, rot_key, value_vec, allowed, log_total, context, delta_context):
    num_heads = rot_query.shape[0]
    num_slots = rot_key.shape[0]
    head_delta = delta_context.reshape(num_slots, num_heads, HD).transpose(1, 0, 2).reshape(-1, HD)
    head_context = context.reshape(num_slots, num_heads, HD).transpose(1, 0, 2).reshape(-1, HD)
    row_dot = jnp.sum(
        head_delta.astype(jnp.float32) * head_context.astype(jnp.float32), axis=-1, keepdims=True
    )
    flat_query = rot_query.reshape(-1, HD)
    scores = lax.dot_general(
        flat_query, rot_key, (((1,), (1,)), ((), ())), preferred_element_type=jnp.float32
    )
    scores = jnp.where(allowed[None], scores.reshape(num_heads, num_slots, num_slots), -1e30)
    prob_exact = jnp.exp(scores - log_total).reshape(-1, num_slots)
    delta_value = lax.dot_general(
        prob_exact.astype(jnp.bfloat16),
        head_delta,
        (((0,), (0,)), ((), ())),
        preferred_element_type=jnp.float32,
    )
    delta_prob = lax.dot_general(
        head_delta, value_vec, (((1,), (1,)), ((), ())), preferred_element_type=jnp.float32
    )
    delta_score = (prob_exact * (delta_prob - row_dot)).astype(jnp.bfloat16)
    delta_query = jnp.dot(delta_score, rot_key, preferred_element_type=jnp.float32).reshape(
        num_heads, num_slots, HD
    )
    delta_key = lax.dot_general(
        delta_score, flat_query, (((0,), (0,)), ((), ())), preferred_element_type=jnp.float32
    )
    return (delta_query, delta_key, delta_value.astype(jnp.bfloat16))


def bit_orders(devices, tuned):
    bits = devices.bit_length() - 1
    if bits == 5:
        return [["cxyab".index(letter) for letter in order] for order in tuned]
    return [[1 + (shift + step) % (bits - 1) for step in range(bits - 1)] for shift in range(3)]


def across(block, bit, devices):
    return lax.ppermute(block, "dp", [(i, i ^ (1 << bit)) for i in range(devices)])


def offset_of(place, order):
    return sum(((place >> k) & 1) << bit for k, bit in enumerate(order))


def gather_chunk(piece, order, devices):
    held = piece[None]
    for bit in order[:-1]:
        held = jnp.concatenate([held, across(held, bit, devices)])
    last = across(held, order[-1], devices)
    return (held, last, across(held, 0, devices), across(last, 0, devices))


def scatter_chunk(home, away, order, devices):
    for bit in [0] + list(order):
        came = across(away, bit, devices)
        half = home.shape[0] // 2

        def added(low, high):
            total = home[low:high].astype(jnp.float32) + came[low:high].astype(jnp.float32)
            return total.astype(jnp.bfloat16) if half else total

        if half:
            home, away = (added(0, half), added(half, 2 * half))
        else:
            home = added(0, 1)
    return home[0]


def cut_rows(rows, parts):
    each = -(-rows // (parts * ROWS)) * ROWS
    return [(low, min(low + each, rows)) for low in range(0, rows, each)]


def whole_specs(count):
    return [pl.BlockSpec(memory_space=pltpu.VMEM)] * count


def place_specs(count):
    return [pl.BlockSpec(memory_space=pl.ANY)] * count


def unpack_kernel(plan, sizes, tail_rows, sources, device_ref, *refs):
    source_refs = refs[:sources]
    matrices = refs[sources : sources + len(sizes)]
    refs = refs[sources + len(sizes) :]
    tails = None
    if tail_rows:
        tails, refs = refs[0], refs[1:]
    flat, spread, sems = refs
    device = device_ref[0]
    copies = []
    for source, index, offset, low, take, start, each in plan:
        owner = device ^ offset
        if start is None:
            target = tails.at[owner]
        else:
            target = flat.at[pl.ds(pl.multiple_of(owner * each + start, ROWS), take), :]
        copies.append(
            pltpu.make_async_copy(
                source_refs[source].at[index, pl.ds(low, take), :], target, sems.at[len(copies)]
            )
        )
    for copy in copies:
        copy.start()
    for copy in copies:
        copy.wait()
    first = 0
    for matrix, (rows, columns) in zip(matrices, sizes):
        blocks = columns // LANES

        @pl.loop(0, rows // LANES)
        def _(step, matrix=matrix, blocks=blocks, first=first):
            base = pl.multiple_of(first + step * (LANES * blocks), ROWS)
            spread[: LANES * blocks] = flat[pl.ds(base, LANES * blocks), :].astype(jnp.float32)
            at = pl.ds(pl.multiple_of(step * LANES, LANES), LANES)
            for block in range(blocks):
                matrix[at, block * LANES : (block + 1) * LANES] = spread[
                    pl.ds(block, LANES, stride=blocks), :
                ].astype(jnp.bfloat16)

        first += rows * blocks


def unpack_matrices(plan, sizes, tail_rows, device, arrays, devices):
    flat_rows = sum(rows * columns for rows, columns in sizes) // LANES
    widest = max(columns for _, columns in sizes)
    shapes = [jax.ShapeDtypeStruct(size, jnp.bfloat16) for size in sizes]
    if tail_rows:
        shapes.append(jax.ShapeDtypeStruct((devices, tail_rows, LANES), jnp.bfloat16))
    return pl.pallas_call(
        functools.partial(unpack_kernel, plan, sizes, tail_rows, len(arrays)),
        out_shape=shapes,
        in_specs=[pl.BlockSpec(memory_space=pltpu.SMEM)] + place_specs(len(arrays)),
        out_specs=whole_specs(len(shapes)),
        scratch_shapes=[
            pltpu.VMEM((flat_rows, LANES), jnp.bfloat16),
            pltpu.VMEM((widest, LANES), jnp.float32),
            pltpu.SemaphoreType.DMA((len(plan),)),
        ],
        compiler_params=pltpu.CompilerParams(vmem_limit_bytes=40 << 20),
        cost_estimate=pl.CostEstimate(
            flops=0, bytes_accessed=flat_rows * LANES * 4, transcendentals=0
        ),
    )(device, *arrays)


def grads_kernel(plan, sizes, has_tails, device_ref, *refs):
    pairs = refs[: 2 * len(sizes)]
    refs = refs[2 * len(sizes) :]
    tails = None
    if has_tails:
        tails, refs = refs[0], refs[1:]
    targets = refs[:-3]
    spread, flat, sems = refs[-3:]
    device = device_ref[0]
    first = 0
    for number, (rows, columns) in enumerate(sizes):
        left, right = pairs[2 * number : 2 * number + 2]
        blocks = columns // LANES
        wide = 2 - blocks % 2
        turned = left[...].T
        for block in range(0, blocks, wide):
            product = jnp.dot(
                turned,
                right[:, block * LANES : (block + wide) * LANES],
                preferred_element_type=jnp.float32,
            )
            for part in range(wide):
                spread[pl.ds(block + part, rows, stride=blocks), :] = product[
                    :, part * LANES : (part + 1) * LANES
                ]

        step_rows = 1280 if rows * blocks % 1280 == 0 else 1024

        @pl.loop(0, rows * blocks // step_rows)
        def _(step, first=first, step_rows=step_rows):
            low = pl.multiple_of(step * step_rows, step_rows)
            flat[pl.ds(pl.multiple_of(first + low, ROWS), step_rows), :] = spread[
                pl.ds(low, step_rows), :
            ].astype(jnp.bfloat16)

        first += rows * blocks
    copies = []
    for target, index, offset, low, take, start, each in plan:
        owner = device ^ offset
        if start is None:
            source = tails.at[owner]
        else:
            source = flat.at[pl.ds(pl.multiple_of(owner * each + start, ROWS), take), :]
        copies.append(
            pltpu.make_async_copy(
                source, targets[target].at[index, pl.ds(low, take), :], sems.at[len(copies)]
            )
        )
    for copy in copies:
        copy.start()
    for copy in copies:
        copy.wait()


def grad_blocks(plan, sizes, pairs, tails, device, shapes):
    flat_rows = sum(rows * columns for rows, columns in sizes) // LANES
    longest = max(rows * columns for rows, columns in sizes) // LANES
    inputs = [member for pair in pairs for member in pair] + ([] if tails is None else [tails])
    return pl.pallas_call(
        functools.partial(grads_kernel, plan, sizes, tails is not None),
        out_shape=[jax.ShapeDtypeStruct(shape, jnp.bfloat16) for shape in shapes],
        in_specs=[pl.BlockSpec(memory_space=pltpu.SMEM)] + whole_specs(len(inputs)),
        out_specs=place_specs(len(shapes)),
        scratch_shapes=[
            pltpu.VMEM((longest, LANES), jnp.float32),
            pltpu.VMEM((flat_rows, LANES), jnp.bfloat16),
            pltpu.SemaphoreType.DMA((len(plan),)),
        ],
        compiler_params=pltpu.CompilerParams(vmem_limit_bytes=40 << 20),
        cost_estimate=pl.CostEstimate(
            flops=2 * CAP * flat_rows * LANES,
            bytes_accessed=flat_rows * LANES * 4,
            transcendentals=0,
        ),
    )(device, *inputs)


def gathered_matrices(pieces, orders, sizes, tail_rows, devices, device):
    each = sum(rows * columns for rows, columns in sizes) // LANES // devices
    arrays, plan, start = [], [], 0
    for piece, order in zip(pieces, orders):
        blocks = gather_chunk(piece, order, devices)
        take = min(piece.shape[0], each - start)
        if each % ROWS:
            table = jnp.concatenate(blocks)
            places = [offset_of(place, list(order) + [0]) for place in range(devices)]
            back = sorted(range(devices), key=places.__getitem__)
            mixed = offset_bits(device[0], list(order) + [0])
            arrays.append(jnp.take(table, jnp.array(back, jnp.int32) ^ mixed, axis=0))
            continue
        for part, block in enumerate(blocks):
            for index in range(block.shape[0]):
                offset = offset_of(part * block.shape[0] + index, list(order) + [0])
                plan.append((len(arrays), index, offset, 0, take, start, each))
                if take < piece.shape[0]:
                    plan.append((len(arrays), index, offset, take, tail_rows, None, each))
            arrays.append(block)
        start += take
    if each % ROWS == 0:
        return unpack_matrices(plan, sizes, tail_rows, device, arrays, devices)
    table = jnp.concatenate(arrays, axis=1)
    flat = table[:, :each].reshape(1, devices * each, LANES)
    plan = [(0, 0, 0, 0, devices * each, 0, 0)]
    found = list(unpack_matrices(plan, sizes, 0, device, [flat], devices))
    return found + ([table[:, each : each + tail_rows]] if tail_rows else [])


def offset_bits(device, order):
    return sum(((device >> bit) & 1) << k for k, bit in enumerate(order))


def scattered_rows(pairs, tails, orders, sizes, devices, device):
    each = sum(rows * columns for rows, columns in sizes) // LANES // devices
    tail_rows = 0 if tails is None else tails.shape[1]
    parts = cut_rows(each + tail_rows, 3)
    half = devices // 2
    plan, shapes = [], []
    for (low, high), order in zip(parts, orders):
        order = list(order)[::-1]
        for with_core in (0, 1):
            for index in range(half):
                offset = offset_of(index, order) ^ with_core
                take = min(high, each) - low
                plan.append((len(shapes), index, offset, 0, take, low, each))
                if high > each:
                    plan.append((len(shapes), index, offset, take, tail_rows, None, each))
            shapes.append((half, high - low, LANES))
    if each % ROWS == 0 and parts[-1][0] < each:
        blocks = grad_blocks(plan, sizes, pairs, tails, device, shapes)
    else:
        flat = grad_blocks(
            [(0, 0, 0, 0, devices * each, 0, 0)],
            sizes,
            pairs,
            None,
            device,
            [(1, devices * each, LANES)],
        )[0]
        table = flat.reshape(devices, each, LANES)
        table = table if tails is None else jnp.concatenate([table, tails], axis=1)
        blocks = []
        for (low, high), order in zip(parts, orders):
            order = list(order)[::-1]
            for with_core in (0, 1):
                offsets = [offset_of(index, order) ^ with_core for index in range(half)]
                owners = jnp.array(offsets, jnp.int32) ^ device[0]
                blocks.append(jnp.take(table[:, low:high], owners, axis=0))
    return jnp.concatenate(
        [
            scatter_chunk(blocks[2 * k], blocks[2 * k + 1], order, devices)
            for k, order in enumerate(orders[: len(parts)])
        ]
    )


def cut_gains(gain_flat):
    gains = gain_flat.astype(jnp.float32)
    return (
        gains[:D],
        gains[D : D + HD],
        gains[D + HD : D + 2 * HD],
        gains[D + 2 * HD : 2 * D + 2 * HD],
        gains[2 * D + 2 * HD : 3 * D + 2 * HD],
        gains[3 * D + 2 * HD :],
    )


def forward_pass(input_rows, weights, allowed, cos_tab, sin_tab):
    (
        query_weight,
        key_weight,
        value_weight,
        out_weight,
        gate_weight,
        up_weight,
        down_weight,
        gain_set,
    ) = weights
    gain_in, gain_query, gain_key, gain_post, gain_mid, gain_last = gain_set
    resid_in = input_rows.astype(jnp.float32)
    normed_in = rms_scale(resid_in, gain_in).astype(jnp.bfloat16)
    query_raw = jnp.dot(normed_in, query_weight, preferred_element_type=jnp.float32)
    key_raw = jnp.dot(normed_in, key_weight, preferred_element_type=jnp.float32)
    value_vec = jnp.dot(normed_in, value_weight, preferred_element_type=jnp.float32).astype(
        jnp.bfloat16
    )
    rot_query, rot_key = query_key(query_raw, key_raw, gain_query, gain_key, cos_tab, sin_tab)
    rot_query = rot_query.astype(jnp.bfloat16)
    rot_key = rot_key.astype(jnp.bfloat16)
    context, log_total = attend(rot_query, rot_key, value_vec, allowed)
    attn_out = jnp.dot(context, out_weight, preferred_element_type=jnp.float32)
    mid_stream = resid_in + rms_scale(attn_out, gain_post)
    normed_mid = rms_scale(mid_stream, gain_mid).astype(jnp.bfloat16)
    gate_proj = jnp.dot(normed_mid, gate_weight, preferred_element_type=jnp.float32)
    up_proj = jnp.dot(normed_mid, up_weight, preferred_element_type=jnp.float32)
    hidden = gated_gelu(gate_proj, up_proj).astype(jnp.bfloat16)
    ffn_out = jnp.dot(hidden, down_weight, preferred_element_type=jnp.float32)
    block_out = (mid_stream + rms_scale(ffn_out, gain_last)).astype(jnp.bfloat16)
    saved = (
        resid_in,
        normed_in,
        query_raw,
        key_raw,
        value_vec,
        rot_query,
        rot_key,
        context,
        log_total,
        attn_out,
        mid_stream,
        normed_mid,
        gate_proj,
        up_proj,
        hidden,
        ffn_out,
    )
    return (block_out, saved)


def ffn_backward(cot_rows, live_mask, weights, saved):
    gate_weight, up_weight, down_weight, gain_set = (weights[4], weights[5], weights[6], weights[7])
    gain_mid, gain_last = (gain_set[4], gain_set[5])
    mid_stream, normed_mid, gate_proj, up_proj, hidden, ffn_out = saved[10:]
    delta_out = cot_rows.astype(jnp.float32) * live_mask[:, None]
    unused, pullback = jax.vjp(rms_scale, ffn_out, gain_last)
    delta_ffn, gain_last_grad = pullback(delta_out)
    delta_ffn = delta_ffn.astype(jnp.bfloat16)
    delta_hidden = times_transposed(delta_ffn, down_weight)
    unused, pullback = jax.vjp(gated_gelu, gate_proj, up_proj)
    delta_gate, delta_up = pullback(delta_hidden)
    delta_gate = delta_gate.astype(jnp.bfloat16)
    delta_up = delta_up.astype(jnp.bfloat16)
    delta_normed = times_transposed(delta_gate, gate_weight) + times_transposed(delta_up, up_weight)
    unused, pullback = jax.vjp(rms_scale, mid_stream, gain_mid)
    delta_part, gain_mid_grad = pullback(delta_normed)
    delta_mid = delta_out + delta_part
    pairs = ((normed_mid, delta_gate), (normed_mid, delta_up), (hidden, delta_ffn))
    return (delta_mid, pairs, (gain_mid_grad, gain_last_grad))


def attn_backward(delta_mid, weights, saved, allowed, cos_tab, sin_tab):
    query_weight, key_weight, value_weight, out_weight = weights[:4]
    gain_in, gain_query, gain_key, gain_post = weights[7][:4]
    (
        resid_in,
        normed_in,
        query_raw,
        key_raw,
        value_vec,
        rot_query,
        rot_key,
        context,
        log_total,
        attn_out,
    ) = saved[:10]
    unused, pullback = jax.vjp(rms_scale, attn_out, gain_post)
    delta_attn, gain_post_grad = pullback(delta_mid)
    delta_attn = delta_attn.astype(jnp.bfloat16)
    delta_context = times_transposed(delta_attn, out_weight).astype(jnp.bfloat16)
    delta_query, delta_key, delta_value = attend_back(
        rot_query, rot_key, value_vec, allowed, log_total, context, delta_context
    )

    def rope_map(raw_query, raw_key, query_gain, key_gain):
        return query_key(raw_query, raw_key, query_gain, key_gain, cos_tab, sin_tab)

    unused, pullback = jax.vjp(rope_map, query_raw, key_raw, gain_query, gain_key)
    delta_qraw, delta_kraw, gain_query_grad, gain_key_grad = pullback((delta_query, delta_key))
    delta_qraw = delta_qraw.astype(jnp.bfloat16)
    delta_kraw = delta_kraw.astype(jnp.bfloat16)
    pairs = (
        (normed_in, delta_qraw),
        (normed_in, delta_kraw),
        (normed_in, delta_value),
        (context, delta_attn),
    )
    delta_in = (
        times_transposed(delta_qraw, query_weight)
        + times_transposed(delta_kraw, key_weight)
        + times_transposed(delta_value, value_weight)
    )
    unused, pullback = jax.vjp(rms_scale, resid_in, gain_in)
    delta_part, gain_in_grad = pullback(delta_in)
    grad_in = delta_mid + delta_part
    return (
        grad_in,
        pairs,
        (gain_in_grad, gain_query_grad, gain_key_grad, gain_post_grad),
    )


def adam_update(weight_shard, gradient, moment_one, moment_two):
    moment_one = 0.9 * moment_one + 0.1 * gradient
    moment_two = 0.999 * moment_two + 0.001 * gradient * gradient
    fix_one = 1.0 - 0.9**STEP
    fix_two = 1.0 - 0.999**STEP
    weight_shard = weight_shard - 0.02 * (
        moment_one / fix_one / (jnp.sqrt(moment_two / fix_two) + 1e-08) + 0.1 * weight_shard
    )
    return (weight_shard, moment_one, moment_two)


def per_device(hidden_in, cotangent, params, moment_one, moment_two, seq_lengths, seq_owner):
    devices = lax.axis_size("dp")
    device = lax.axis_index("dp").astype(jnp.int32)
    here = device.reshape(1)
    attn_len = G1LEN // devices
    ffn_len = G2LEN // devices
    gain_len = params.shape[0] - attn_len - ffn_len
    attn_rows = attn_len // LANES
    tail_rows = -(-(attn_rows + 1) // ROWS) * ROWS - attn_rows
    pad = tail_rows * LANES - gain_len
    rounded = params.astype(jnp.bfloat16)
    first_piece = jnp.concatenate(
        [rounded[:attn_len], rounded[attn_len + ffn_len :], jnp.zeros((pad,), jnp.bfloat16)]
    ).reshape(-1, LANES)
    second_piece = rounded[attn_len : attn_len + ffn_len].reshape(-1, LANES)
    second_pieces = [second_piece[low:high] for low, high in cut_rows(ffn_len // LANES, 2)]
    orders = bit_orders(devices, ("abxy", "bxya", "byax"))
    *attn_weights, tails = gathered_matrices(
        [first_piece], orders[:1], ATTN_SIZES, tail_rows, devices, here
    )
    ffn_weights = gathered_matrices(second_pieces, orders[1:], FFN_SIZES, 0, devices, here)
    gain_flat = tails.reshape(devices, -1)[:, :gain_len].reshape(-1)
    weights = (*attn_weights, *ffn_weights, cut_gains(gain_flat))
    live_mask, allowed, cos_tab, sin_tab = slot_setup(seq_lengths, seq_owner, device)
    block_out, saved = forward_pass(hidden_in, weights, allowed, cos_tab, sin_tab)
    delta_mid, ffn_pairs, late_gains = ffn_backward(cotangent, live_mask, weights, saved)
    orders = bit_orders(devices, ("yxba", "ayxb", "xayb"))
    ffn_shard = scattered_rows(ffn_pairs, None, orders, FFN_SIZES, devices, here)
    grad_in, attn_pairs, early_gains = attn_backward(
        delta_mid, weights, saved, allowed, cos_tab, sin_tab
    )
    gain_table = jnp.concatenate(early_gains + late_gains).reshape(devices, gain_len)
    gain_table = jnp.pad(gain_table.astype(jnp.bfloat16), ((0, 0), (0, pad)))
    gain_table = gain_table.reshape(devices, tail_rows, LANES)
    orders = bit_orders(devices, ("yabx", "axyb", "xyab"))
    attn_shard = scattered_rows(
        attn_pairs, gain_table, orders, ATTN_SIZES, devices, here
    ).reshape(-1)
    grad_shard = jnp.concatenate(
        [attn_shard[:attn_len], ffn_shard.reshape(-1), attn_shard[attn_len : attn_len + gain_len]]
    )
    params_new, moment_one_new, moment_two_new = adam_update(
        params, grad_shard, moment_one, moment_two
    )
    return (block_out, grad_in, grad_shard, params_new, moment_one_new, moment_two_new)


def solution(mesh):
    in_specs = (P("dp", None), P("dp", None), P("dp"), P("dp"), P("dp"), P(), P())
    out_specs = (P("dp", None), P("dp", None), P("dp"), P("dp"), P("dp"), P("dp"))
    return jax.shard_map(
        per_device, mesh=mesh, in_specs=in_specs, out_specs=out_specs, check_vma=False
    )
```

```python
import functools

import jax
import jax.numpy as jnp
from jax import lax
from jax.experimental import pallas as pl
from jax.experimental.pallas import tpu as pltpu
from jax.sharding import PartitionSpec as P

D = 640
FF = 2048
HD = 256
HQ = 1024
CAP = 128
WINDOW = 64
STEP = 3
G1LEN = 1638400
G2LEN = 3932160
LANES = 128
ROWS = 16
ATTN_SIZES = ((D, HQ), (D, HD), (D, HD), (HQ, D))
FFN_SIZES = ((D, FF), (D, FF), (FF, D))


def rms_scale(values, gain_vec):
    return (
        values
        * lax.rsqrt(jnp.mean(values * values, axis=-1, keepdims=True) + 1e-06)
        * (1.0 + gain_vec)
    )


def rotate(values, cos_tab, sin_tab):
    half_dim = values.shape[-1] // 2
    lower_half = values[..., :half_dim]
    upper_half = values[..., half_dim:]
    return jnp.concatenate(
        [lower_half * cos_tab - upper_half * sin_tab, upper_half * cos_tab + lower_half * sin_tab],
        axis=-1,
    )


def query_key(query_raw, key_raw, gain_query, gain_key, cos_tab, sin_tab):
    per_head = query_raw.reshape(query_raw.shape[0], -1, HD).transpose(1, 0, 2)
    rot_query = rotate(rms_scale(per_head, gain_query), cos_tab, sin_tab) * HD ** (-0.5)
    rot_key = rotate(rms_scale(key_raw, gain_key), cos_tab, sin_tab)
    return (rot_query, rot_key)


def gated_gelu(gate_proj, up_proj):
    return jax.nn.gelu(gate_proj, approximate=True) * up_proj


def times_transposed(rows_in, matrix):
    return lax.dot_general(
        rows_in, matrix, (((1,), (1,)), ((), ())), preferred_element_type=jnp.float32
    )


def slot_setup(seq_lengths, seq_owner, device):
    mine_mask = seq_owner == device
    own_lengths = jnp.where(mine_mask, seq_lengths, 0)
    seq_ends = jnp.cumsum(own_lengths, dtype=jnp.int32)
    seq_begins = seq_ends - own_lengths
    slot_index = jnp.arange(CAP, dtype=jnp.int32)
    column = slot_index[:, None]
    inside_mask = (
        mine_mask[None, :] & (seq_begins[None, :] <= column) & (column < seq_ends[None, :])
    )
    live_mask = jnp.any(inside_mask, axis=1)
    seq_label = jnp.sum(
        (mine_mask[None, :] & (seq_ends[None, :] <= column)).astype(jnp.int32),
        axis=1,
        dtype=jnp.int32,
    )
    position = jnp.sum(
        jnp.where(inside_mask, column - seq_begins[None, :], 0), axis=1, dtype=jnp.int32
    )
    row_slot = slot_index[:, None]
    col_slot = slot_index[None, :]
    allowed = live_mask[:, None] & live_mask[None, :] & (
        seq_label[:, None] == seq_label[None, :]
    ) & (col_slot <= row_slot) & (row_slot - col_slot < WINDOW) | (row_slot == col_slot)
    half_dim = HD // 2
    frequency = 10000.0 ** (-2.0 * jnp.arange(half_dim, dtype=jnp.float32) / HD)
    angles = position.astype(jnp.float32)[:, None] * frequency[None, :]
    return (live_mask.astype(jnp.float32), allowed, jnp.cos(angles), jnp.sin(angles))


def attend(rot_query, rot_key, value_vec, allowed):
    num_heads = rot_query.shape[0]
    num_slots = rot_key.shape[0]
    flat_query = rot_query.reshape(num_heads * num_slots, HD)
    scores = lax.dot_general(
        flat_query, rot_key, (((1,), (1,)), ((), ())), preferred_element_type=jnp.float32
    )
    scores = jnp.where(allowed[None], scores.reshape(num_heads, num_slots, num_slots), -1e30)
    row_max = jnp.max(scores, axis=-1, keepdims=True)
    raised = jnp.exp(scores - row_max)
    summed = jnp.sum(raised, axis=-1, keepdims=True)
    log_total = row_max + jnp.log(summed)
    attn_prob = (raised / summed).astype(jnp.bfloat16)
    context = jnp.dot(
        attn_prob.reshape(num_heads * num_slots, num_slots),
        value_vec,
        preferred_element_type=jnp.float32,
    )
    context = (
        context.reshape(num_heads, num_slots, HD)
        .transpose(1, 0, 2)
        .reshape(num_slots, num_heads * HD)
    )
    return (context.astype(jnp.bfloat16), log_total)


def attend_back(rot_query, rot_key, value_vec, allowed, log_total, context, delta_context):
    num_heads = rot_query.shape[0]
    num_slots = rot_key.shape[0]
    head_delta = delta_context.reshape(num_slots, num_heads, HD).transpose(1, 0, 2).reshape(-1, HD)
    head_context = context.reshape(num_slots, num_heads, HD).transpose(1, 0, 2).reshape(-1, HD)
    row_dot = jnp.sum(
        head_delta.astype(jnp.float32) * head_context.astype(jnp.float32), axis=-1, keepdims=True
    )
    flat_query = rot_query.reshape(-1, HD)
    scores = lax.dot_general(
        flat_query, rot_key, (((1,), (1,)), ((), ())), preferred_element_type=jnp.float32
    )
    scores = jnp.where(allowed[None], scores.reshape(num_heads, num_slots, num_slots), -1e30)
    prob_exact = jnp.exp(scores - log_total).reshape(-1, num_slots)
    delta_value = lax.dot_general(
        prob_exact.astype(jnp.bfloat16),
        head_delta,
        (((0,), (0,)), ((), ())),
        preferred_element_type=jnp.float32,
    )
    delta_prob = lax.dot_general(
        head_delta, value_vec, (((1,), (1,)), ((), ())), preferred_element_type=jnp.float32
    )
    delta_score = (prob_exact * (delta_prob - row_dot)).astype(jnp.bfloat16)
    delta_query = jnp.dot(delta_score, rot_key, preferred_element_type=jnp.float32).reshape(
        num_heads, num_slots, HD
    )
    delta_key = lax.dot_general(
        delta_score, flat_query, (((0,), (0,)), ((), ())), preferred_element_type=jnp.float32
    )
    return (delta_query, delta_key, delta_value.astype(jnp.bfloat16))


def bit_orders(devices, tuned):
    bits = devices.bit_length() - 1
    if bits == 5:
        return [["cxyab".index(letter) for letter in order] for order in tuned]
    return [[1 + (shift + step) % (bits - 1) for step in range(bits - 1)] for shift in range(3)]


def across(block, bit, devices):
    return lax.ppermute(block, "dp", [(i, i ^ (1 << bit)) for i in range(devices)])


def offset_of(place, order):
    return sum(((place >> k) & 1) << bit for k, bit in enumerate(order))


def gather_chunk(piece, order, devices):
    held = piece[None]
    for bit in order[:-1]:
        held = jnp.concatenate([held, across(held, bit, devices)])
    last = across(held, order[-1], devices)
    return (held, last, across(held, 0, devices), across(last, 0, devices))


def sent_blocks(chunks, orders, stage, devices):
    return [
        across(away, order[stage], devices)
        for (_, away), order in zip(chunks, orders)
    ]


def merged_blocks(chunks, came):
    merged = []
    for (home, _), arrived in zip(chunks, came):
        half = home.shape[0] // 2

        def added(low, high):
            return home[low:high].astype(jnp.float32) + arrived[low:high].astype(jnp.float32)

        if half:
            merged.append(
                (
                    added(0, half).astype(jnp.bfloat16),
                    added(half, 2 * half).astype(jnp.bfloat16),
                )
            )
        else:
            merged.append((added(0, 1)[0], None))
    return merged


def cut_rows(rows, parts):
    each = -(-rows // (parts * ROWS)) * ROWS
    return [(low, min(low + each, rows)) for low in range(0, rows, each)]


def whole_specs(count):
    return [pl.BlockSpec(memory_space=pltpu.VMEM)] * count


def place_specs(count):
    return [pl.BlockSpec(memory_space=pl.ANY)] * count


def unpack_kernel(plan, sizes, tail_rows, sources, device_ref, *refs):
    source_refs = refs[:sources]
    matrices = refs[sources : sources + len(sizes)]
    refs = refs[sources + len(sizes) :]
    tails = None
    if tail_rows:
        tails, refs = refs[0], refs[1:]
    flat, spread, sems = refs
    device = device_ref[0]
    copies = []
    for source, index, offset, low, take, start, each in plan:
        owner = device ^ offset
        if start is None:
            target = tails.at[owner]
        else:
            target = flat.at[pl.ds(pl.multiple_of(owner * each + start, ROWS), take), :]
        copies.append(
            pltpu.make_async_copy(
                source_refs[source].at[index, pl.ds(low, take), :], target, sems.at[len(copies)]
            )
        )
    for copy in copies:
        copy.start()
    for copy in copies:
        copy.wait()
    first = 0
    for matrix, (rows, columns) in zip(matrices, sizes):
        blocks = columns // LANES

        @pl.loop(0, rows // LANES)
        def _(step, matrix=matrix, blocks=blocks, first=first):
            base = pl.multiple_of(first + step * (LANES * blocks), ROWS)
            spread[: LANES * blocks] = flat[pl.ds(base, LANES * blocks), :].astype(jnp.float32)
            at = pl.ds(pl.multiple_of(step * LANES, LANES), LANES)
            for block in range(blocks):
                matrix[at, block * LANES : (block + 1) * LANES] = spread[
                    pl.ds(block, LANES, stride=blocks), :
                ].astype(jnp.bfloat16)

        first += rows * blocks


def unpack_matrices(plan, sizes, tail_rows, device, arrays, devices):
    flat_rows = sum(rows * columns for rows, columns in sizes) // LANES
    widest = max(columns for _, columns in sizes)
    shapes = [jax.ShapeDtypeStruct(size, jnp.bfloat16) for size in sizes]
    if tail_rows:
        shapes.append(jax.ShapeDtypeStruct((devices, tail_rows, LANES), jnp.bfloat16))
    return pl.pallas_call(
        functools.partial(unpack_kernel, plan, sizes, tail_rows, len(arrays)),
        out_shape=shapes,
        in_specs=[pl.BlockSpec(memory_space=pltpu.SMEM)] + place_specs(len(arrays)),
        out_specs=whole_specs(len(shapes)),
        scratch_shapes=[
            pltpu.VMEM((flat_rows, LANES), jnp.bfloat16),
            pltpu.VMEM((widest, LANES), jnp.float32),
            pltpu.SemaphoreType.DMA((len(plan),)),
        ],
        compiler_params=pltpu.CompilerParams(vmem_limit_bytes=40 << 20),
        cost_estimate=pl.CostEstimate(flops=0, bytes_accessed=0, transcendentals=0),
    )(device, *arrays)


def grads_kernel(plan, sizes, has_tails, device_ref, *refs):
    pairs = refs[: 2 * len(sizes)]
    refs = refs[2 * len(sizes) :]
    tails = None
    if has_tails:
        tails, refs = refs[0], refs[1:]
    targets = refs[:-3]
    spread, flat, sems = refs[-3:]
    device = device_ref[0]
    first = 0
    for number, (rows, columns) in enumerate(sizes):
        left, right = pairs[2 * number : 2 * number + 2]
        blocks = columns // LANES
        wide = 2 - blocks % 2
        turned = left[...].T
        for block in range(0, blocks, wide):
            product = jnp.dot(
                turned,
                right[:, block * LANES : (block + wide) * LANES],
                preferred_element_type=jnp.float32,
            )
            for part in range(wide):
                spread[pl.ds(block + part, rows, stride=blocks), :] = product[
                    :, part * LANES : (part + 1) * LANES
                ]

        step_rows = 1280 if rows * blocks % 1280 == 0 else 1024

        @pl.loop(0, rows * blocks // step_rows)
        def _(step, first=first, step_rows=step_rows):
            low = pl.multiple_of(step * step_rows, step_rows)
            flat[pl.ds(pl.multiple_of(first + low, ROWS), step_rows), :] = spread[
                pl.ds(low, step_rows), :
            ].astype(jnp.bfloat16)

        first += rows * blocks
    copies = []
    for target, index, offset, low, take, start, each in plan:
        owner = device ^ offset
        if start is None:
            source = tails.at[owner]
        else:
            source = flat.at[pl.ds(pl.multiple_of(owner * each + start, ROWS), take), :]
        copies.append(
            pltpu.make_async_copy(
                source, targets[target].at[index, pl.ds(low, take), :], sems.at[len(copies)]
            )
        )
    for copy in copies:
        copy.start()
    for copy in copies:
        copy.wait()


def grad_blocks(plan, sizes, pairs, tails, device, shapes):
    flat_rows = sum(rows * columns for rows, columns in sizes) // LANES
    longest = max(rows * columns for rows, columns in sizes) // LANES
    inputs = [member for pair in pairs for member in pair] + ([] if tails is None else [tails])
    return pl.pallas_call(
        functools.partial(grads_kernel, plan, sizes, tails is not None),
        out_shape=[jax.ShapeDtypeStruct(shape, jnp.bfloat16) for shape in shapes],
        in_specs=[pl.BlockSpec(memory_space=pltpu.SMEM)] + whole_specs(len(inputs)),
        out_specs=place_specs(len(shapes)),
        scratch_shapes=[
            pltpu.VMEM((longest, LANES), jnp.float32),
            pltpu.VMEM((flat_rows, LANES), jnp.bfloat16),
            pltpu.SemaphoreType.DMA((len(plan),)),
        ],
        compiler_params=pltpu.CompilerParams(vmem_limit_bytes=40 << 20),
        cost_estimate=pl.CostEstimate(flops=0, bytes_accessed=0, transcendentals=0),
    )(device, *inputs)


def gathered_matrices(pieces, orders, sizes, tail_rows, devices, device):
    each = sum(rows * columns for rows, columns in sizes) // LANES // devices
    arrays, plan, start = [], [], 0
    for piece, order in zip(pieces, orders):
        blocks = gather_chunk(piece, order, devices)
        take = min(piece.shape[0], each - start)
        if each % ROWS:
            table = jnp.concatenate(blocks)
            places = [offset_of(place, list(order) + [0]) for place in range(devices)]
            back = sorted(range(devices), key=places.__getitem__)
            mixed = offset_bits(device[0], list(order) + [0])
            arrays.append(jnp.take(table, jnp.array(back, jnp.int32) ^ mixed, axis=0))
            continue
        for part, block in enumerate(blocks):
            for index in range(block.shape[0]):
                offset = offset_of(part * block.shape[0] + index, list(order) + [0])
                plan.append((len(arrays), index, offset, 0, take, start, each))
                if take < piece.shape[0]:
                    plan.append((len(arrays), index, offset, take, tail_rows, None, each))
            arrays.append(block)
        start += take
    if each % ROWS == 0:
        return unpack_matrices(plan, sizes, tail_rows, device, arrays, devices)
    table = jnp.concatenate(arrays, axis=1)
    flat = table[:, :each].reshape(1, devices * each, LANES)
    plan = [(0, 0, 0, 0, devices * each, 0, 0)]
    found = list(unpack_matrices(plan, sizes, 0, device, [flat], devices))
    return found + ([table[:, each : each + tail_rows]] if tail_rows else [])


def offset_bits(device, order):
    return sum(((device >> bit) & 1) << k for k, bit in enumerate(order))


def scatter_blocks(pairs, tails, orders, sizes, devices, device):
    each = sum(rows * columns for rows, columns in sizes) // LANES // devices
    tail_rows = 0 if tails is None else tails.shape[1]
    parts = cut_rows(each + tail_rows, len(orders))
    half = devices // 2
    plan = []
    for (low, high), order in zip(parts, orders):
        for with_core in (0, 1):
            for index in range(half):
                offset = offset_of(index, order[::-1]) ^ with_core
                plan.append((with_core, index, offset, low, min(high, each) - low, low, each))
    if tail_rows:
        for with_core in (0, 1):
            for index in range(half):
                offset = offset_of(index, orders[len(parts) - 1][::-1]) ^ with_core
                plan.append((with_core, index, offset, each, tail_rows, None, each))
    shape = (half, each + tail_rows, LANES)
    if each % ROWS == 0 and parts[-1][0] < each:
        blocks = grad_blocks(plan, sizes, pairs, tails, device, [shape, shape])
    else:
        flat = grad_blocks(
            [(0, 0, 0, 0, devices * each, 0, 0)],
            sizes,
            pairs,
            None,
            device,
            [(1, devices * each, LANES)],
        )[0]
        table = flat.reshape(devices, each, LANES)
        table = table if tails is None else jnp.concatenate([table, tails], axis=1)
        blocks = []
        for with_core in (0, 1):
            chunks = []
            for (low, high), order in zip(parts, orders):
                offsets = [offset_of(index, order[::-1]) ^ with_core for index in range(half)]
                owners = jnp.array(offsets, jnp.int32) ^ device[0]
                chunks.append(jnp.take(table[:, low:high], owners, axis=0))
            blocks.append(jnp.concatenate(chunks, axis=1))
    return blocks, parts


def cores_merged(home, came, parts):
    half = home.shape[0] // 2

    def added(first, low, high):
        at = (slice(first, first + half), slice(low, high))
        return (home[at].astype(jnp.float32) + came[at].astype(jnp.float32)).astype(jnp.bfloat16)

    return [(added(0, low, high), added(half, low, high)) for low, high in parts]


def cut_gains(gain_flat):
    gains = gain_flat.astype(jnp.float32)
    return (
        gains[:D],
        gains[D : D + HD],
        gains[D + HD : D + 2 * HD],
        gains[D + 2 * HD : 2 * D + 2 * HD],
        gains[2 * D + 2 * HD : 3 * D + 2 * HD],
        gains[3 * D + 2 * HD :],
    )


def forward_pass(input_rows, weights, allowed, cos_tab, sin_tab):
    (
        query_weight,
        key_weight,
        value_weight,
        out_weight,
        gate_weight,
        up_weight,
        down_weight,
        gain_set,
    ) = weights
    gain_in, gain_query, gain_key, gain_post, gain_mid, gain_last = gain_set
    resid_in = input_rows.astype(jnp.float32)
    normed_in = rms_scale(resid_in, gain_in).astype(jnp.bfloat16)
    query_raw = jnp.dot(normed_in, query_weight, preferred_element_type=jnp.float32)
    key_raw = jnp.dot(normed_in, key_weight, preferred_element_type=jnp.float32)
    value_vec = jnp.dot(normed_in, value_weight, preferred_element_type=jnp.float32).astype(
        jnp.bfloat16
    )
    rot_query, rot_key = query_key(query_raw, key_raw, gain_query, gain_key, cos_tab, sin_tab)
    rot_query = rot_query.astype(jnp.bfloat16)
    rot_key = rot_key.astype(jnp.bfloat16)
    context, log_total = attend(rot_query, rot_key, value_vec, allowed)
    attn_out = jnp.dot(context, out_weight, preferred_element_type=jnp.float32)
    mid_stream = resid_in + rms_scale(attn_out, gain_post)
    normed_mid = rms_scale(mid_stream, gain_mid).astype(jnp.bfloat16)
    gate_proj = jnp.dot(normed_mid, gate_weight, preferred_element_type=jnp.float32)
    up_proj = jnp.dot(normed_mid, up_weight, preferred_element_type=jnp.float32)
    hidden = gated_gelu(gate_proj, up_proj).astype(jnp.bfloat16)
    ffn_out = jnp.dot(hidden, down_weight, preferred_element_type=jnp.float32)
    block_out = (mid_stream + rms_scale(ffn_out, gain_last)).astype(jnp.bfloat16)
    saved = (
        resid_in,
        normed_in,
        query_raw,
        key_raw,
        value_vec,
        rot_query,
        rot_key,
        context,
        log_total,
        attn_out,
        mid_stream,
        normed_mid,
        gate_proj,
        up_proj,
        hidden,
        ffn_out,
    )
    return (block_out, saved)


def ffn_backward(cot_rows, live_mask, weights, saved):
    gate_weight, up_weight, down_weight, gain_set = (weights[4], weights[5], weights[6], weights[7])
    gain_mid, gain_last = (gain_set[4], gain_set[5])
    mid_stream, normed_mid, gate_proj, up_proj, hidden, ffn_out = saved[10:]
    delta_out = cot_rows.astype(jnp.float32) * live_mask[:, None]
    unused, pullback = jax.vjp(rms_scale, ffn_out, gain_last)
    delta_ffn, gain_last_grad = pullback(delta_out)
    delta_ffn = delta_ffn.astype(jnp.bfloat16)
    delta_hidden = times_transposed(delta_ffn, down_weight)
    unused, pullback = jax.vjp(gated_gelu, gate_proj, up_proj)
    delta_gate, delta_up = pullback(delta_hidden)
    delta_gate = delta_gate.astype(jnp.bfloat16)
    delta_up = delta_up.astype(jnp.bfloat16)
    delta_normed = times_transposed(delta_gate, gate_weight) + times_transposed(delta_up, up_weight)
    unused, pullback = jax.vjp(rms_scale, mid_stream, gain_mid)
    delta_part, gain_mid_grad = pullback(delta_normed)
    delta_mid = delta_out + delta_part
    pairs = ((normed_mid, delta_gate), (normed_mid, delta_up), (hidden, delta_ffn))
    return (delta_mid, pairs, (gain_mid_grad, gain_last_grad))


def attn_backward(delta_mid, weights, saved, allowed, cos_tab, sin_tab, pause):
    query_weight, key_weight, value_weight, out_weight = weights[:4]
    gain_in, gain_query, gain_key, gain_post = weights[7][:4]
    (
        resid_in,
        normed_in,
        query_raw,
        key_raw,
        value_vec,
        rot_query,
        rot_key,
        context,
        log_total,
        attn_out,
    ) = saved[:10]
    unused, pullback = jax.vjp(rms_scale, attn_out, gain_post)
    delta_attn, gain_post_grad = pullback(delta_mid)
    delta_attn = delta_attn.astype(jnp.bfloat16)
    delta_context = times_transposed(delta_attn, out_weight).astype(jnp.bfloat16)
    delta_context, delta_attn = pause((delta_context, delta_attn))
    delta_query, delta_key, delta_value = attend_back(
        rot_query, rot_key, value_vec, allowed, log_total, context, delta_context
    )

    def rope_map(raw_query, raw_key, query_gain, key_gain):
        return query_key(raw_query, raw_key, query_gain, key_gain, cos_tab, sin_tab)

    unused, pullback = jax.vjp(rope_map, query_raw, key_raw, gain_query, gain_key)
    delta_qraw, delta_kraw, gain_query_grad, gain_key_grad = pullback((delta_query, delta_key))
    delta_qraw = delta_qraw.astype(jnp.bfloat16)
    delta_kraw = delta_kraw.astype(jnp.bfloat16)
    pairs = (
        (normed_in, delta_qraw),
        (normed_in, delta_kraw),
        (normed_in, delta_value),
        (context, delta_attn),
    )
    delta_in = (
        times_transposed(delta_qraw, query_weight)
        + times_transposed(delta_kraw, key_weight)
        + times_transposed(delta_value, value_weight)
    )
    unused, pullback = jax.vjp(rms_scale, resid_in, gain_in)
    delta_part, gain_in_grad = pullback(delta_in)
    grad_in = delta_mid + delta_part
    return (
        grad_in,
        pairs,
        (gain_in_grad, gain_query_grad, gain_key_grad, gain_post_grad),
    )


def adam_update(weight_shard, gradient, moment_one, moment_two):
    moment_one = 0.9 * moment_one + 0.1 * gradient
    moment_two = 0.999 * moment_two + 0.001 * gradient * gradient
    fix_one = 1.0 - 0.9**STEP
    fix_two = 1.0 - 0.999**STEP
    weight_shard = weight_shard - 0.02 * (
        moment_one / fix_one / (jnp.sqrt(moment_two / fix_two) + 1e-08) + 0.1 * weight_shard
    )
    return (weight_shard, moment_one, moment_two)


def per_device(hidden_in, cotangent, params, moment_one, moment_two, seq_lengths, seq_owner):
    devices = lax.axis_size("dp")
    device = lax.axis_index("dp").astype(jnp.int32)
    here = device.reshape(1)
    attn_len = G1LEN // devices
    ffn_len = G2LEN // devices
    gain_len = params.shape[0] - attn_len - ffn_len
    attn_rows = attn_len // LANES
    tail_rows = -(-(attn_rows + 1) // ROWS) * ROWS - attn_rows
    pad = tail_rows * LANES - gain_len
    rounded = params.astype(jnp.bfloat16)
    first_piece = jnp.concatenate(
        [rounded[:attn_len], rounded[attn_len + ffn_len :], jnp.zeros((pad,), jnp.bfloat16)]
    ).reshape(-1, LANES)
    second_piece = rounded[attn_len : attn_len + ffn_len].reshape(-1, LANES)
    second_pieces = [second_piece[low:high] for low, high in cut_rows(ffn_len // LANES, 2)]
    orders = bit_orders(devices, ("abxy", "bxya", "byax"))
    *attn_weights, tails = gathered_matrices(
        [first_piece], orders[:1], ATTN_SIZES, tail_rows, devices, here
    )
    ffn_weights = gathered_matrices(second_pieces, orders[1:], FFN_SIZES, 0, devices, here)
    gain_flat = tails.reshape(devices, -1)[:, :gain_len].reshape(-1)
    weights = (*attn_weights, *ffn_weights, cut_gains(gain_flat))
    live_mask, allowed, cos_tab, sin_tab = slot_setup(seq_lengths, seq_owner, device)
    block_out, saved = forward_pass(hidden_in, weights, allowed, cos_tab, sin_tab)
    delta_mid, ffn_pairs, late_gains = ffn_backward(cotangent, live_mask, weights, saved)
    ffn_orders = bit_orders(devices, ("xaby", "yxab", "ayxb"))
    attn_orders = bit_orders(devices, ("xyab", "yxba"))[:2]
    (ffn_home, ffn_away), ffn_parts = scatter_blocks(
        ffn_pairs, None, ffn_orders, FFN_SIZES, devices, here
    )
    delta_mid, ffn_home, ffn_away = lax.optimization_barrier((delta_mid, ffn_home, ffn_away))
    ffn_came = across(ffn_away, 0, devices)
    ffn_chunks = []

    def pause(values):
        nonlocal ffn_chunks, ffn_came
        values, ffn_came = lax.optimization_barrier((values, ffn_came))
        ffn_chunks = cores_merged(ffn_home, ffn_came, ffn_parts)
        values, ffn_chunks = lax.optimization_barrier((values, ffn_chunks))
        ffn_came = sent_blocks(ffn_chunks, ffn_orders, 0, devices)
        return values

    grad_in, attn_pairs, early_gains = attn_backward(
        delta_mid, weights, saved, allowed, cos_tab, sin_tab, pause
    )
    gain_table = jnp.concatenate(early_gains + late_gains).reshape(devices, gain_len)
    gain_table = jnp.pad(gain_table.astype(jnp.bfloat16), ((0, 0), (0, pad)))
    gain_table = gain_table.reshape(devices, tail_rows, LANES)
    (attn_home, attn_away), attn_parts = scatter_blocks(
        attn_pairs, gain_table, attn_orders, ATTN_SIZES, devices, here
    )
    attn_home, attn_away, ffn_came = lax.optimization_barrier((attn_home, attn_away, ffn_came))
    stages = len(ffn_orders[0])
    ffn_chunks = merged_blocks(ffn_chunks, ffn_came)
    ffn_came = sent_blocks(ffn_chunks, ffn_orders, 1, devices)
    attn_came = across(attn_away, 0, devices)
    attn_came, ffn_came = lax.optimization_barrier((attn_came, ffn_came))
    attn_chunks = cores_merged(attn_home, attn_came, attn_parts)
    for stage in range(stages):
        attn_came = sent_blocks(attn_chunks, attn_orders, stage, devices)
        if stage < stages - 1:
            ffn_chunks = merged_blocks(ffn_chunks, ffn_came)
        ffn_came = sent_blocks(ffn_chunks, ffn_orders, stage + 2, devices) if stage + 2 < stages else []
        ffn_came, attn_came = lax.optimization_barrier((ffn_came, attn_came))
        attn_chunks = merged_blocks(attn_chunks, attn_came)
    attn_shard = jnp.concatenate([rows for rows, _ in attn_chunks]).reshape(-1)
    ffn_shard = jnp.concatenate([rows for rows, _ in ffn_chunks])
    grad_shard = jnp.concatenate(
        [attn_shard[:attn_len], ffn_shard.reshape(-1), attn_shard[attn_len : attn_len + gain_len]]
    )
    params_new, moment_one_new, moment_two_new = adam_update(
        params, grad_shard, moment_one, moment_two
    )
    return (block_out, grad_in, grad_shard, params_new, moment_one_new, moment_two_new)


def solution(mesh):
    in_specs = (P("dp", None), P("dp", None), P("dp"), P("dp"), P("dp"), P(), P())
    out_specs = (P("dp", None), P("dp", None), P("dp"), P("dp"), P("dp"), P("dp"))
    return jax.shard_map(
        per_device, mesh=mesh, in_specs=in_specs, out_specs=out_specs, check_vma=False
    )
```

```python
import functools

import jax
import jax.numpy as jnp
from jax import lax
from jax.experimental import pallas as pl
from jax.experimental.pallas import tpu as pltpu
from jax.sharding import PartitionSpec as P

D = 640
FF = 2048
HD = 256
HQ = 1024
CAP = 128
WINDOW = 64
STEP = 3
G1LEN = 1638400
G2LEN = 3932160
LANES = 128
ROWS = 16
ATTN_SIZES = ((D, HQ), (D, HD), (D, HD), (HQ, D))
FFN_SIZES = ((D, FF), (D, FF), (FF, D))


def rms_scale(values, gain_vec):
    return (
        values
        * lax.rsqrt(jnp.mean(values * values, axis=-1, keepdims=True) + 1e-06)
        * (1.0 + gain_vec)
    )


def rotate(values, cos_tab, sin_tab):
    half_dim = values.shape[-1] // 2
    lower_half = values[..., :half_dim]
    upper_half = values[..., half_dim:]
    return jnp.concatenate(
        [lower_half * cos_tab - upper_half * sin_tab, upper_half * cos_tab + lower_half * sin_tab],
        axis=-1,
    )


def query_key(query_raw, key_raw, gain_query, gain_key, cos_tab, sin_tab):
    per_head = query_raw.reshape(query_raw.shape[0], -1, HD).transpose(1, 0, 2)
    rot_query = rotate(rms_scale(per_head, gain_query), cos_tab, sin_tab) * HD ** (-0.5)
    rot_key = rotate(rms_scale(key_raw, gain_key), cos_tab, sin_tab)
    return (rot_query, rot_key)


def gated_gelu(gate_proj, up_proj):
    return jax.nn.gelu(gate_proj, approximate=True) * up_proj


def times_transposed(rows_in, matrix):
    return lax.dot_general(
        rows_in, matrix, (((1,), (1,)), ((), ())), preferred_element_type=jnp.float32
    )


def slot_setup(seq_lengths, seq_owner, device):
    mine_mask = seq_owner == device
    own_lengths = jnp.where(mine_mask, seq_lengths, 0)
    seq_ends = jnp.cumsum(own_lengths, dtype=jnp.int32)
    seq_begins = seq_ends - own_lengths
    slot_index = jnp.arange(CAP, dtype=jnp.int32)
    column = slot_index[:, None]
    inside_mask = (
        mine_mask[None, :] & (seq_begins[None, :] <= column) & (column < seq_ends[None, :])
    )
    live_mask = jnp.any(inside_mask, axis=1)
    seq_label = jnp.sum(
        (mine_mask[None, :] & (seq_ends[None, :] <= column)).astype(jnp.int32),
        axis=1,
        dtype=jnp.int32,
    )
    position = jnp.sum(
        jnp.where(inside_mask, column - seq_begins[None, :], 0), axis=1, dtype=jnp.int32
    )
    row_slot = slot_index[:, None]
    col_slot = slot_index[None, :]
    allowed = live_mask[:, None] & live_mask[None, :] & (
        seq_label[:, None] == seq_label[None, :]
    ) & (col_slot <= row_slot) & (row_slot - col_slot < WINDOW) | (row_slot == col_slot)
    half_dim = HD // 2
    frequency = 10000.0 ** (-2.0 * jnp.arange(half_dim, dtype=jnp.float32) / HD)
    angles = position.astype(jnp.float32)[:, None] * frequency[None, :]
    return (live_mask.astype(jnp.float32), allowed, jnp.cos(angles), jnp.sin(angles))


def attend(rot_query, rot_key, value_vec, allowed):
    num_heads = rot_query.shape[0]
    num_slots = rot_key.shape[0]
    flat_query = rot_query.reshape(num_heads * num_slots, HD)
    scores = lax.dot_general(
        flat_query, rot_key, (((1,), (1,)), ((), ())), preferred_element_type=jnp.float32
    )
    scores = jnp.where(allowed[None], scores.reshape(num_heads, num_slots, num_slots), -1e30)
    row_max = jnp.max(scores, axis=-1, keepdims=True)
    raised = jnp.exp(scores - row_max)
    summed = jnp.sum(raised, axis=-1, keepdims=True)
    log_total = row_max + jnp.log(summed)
    attn_prob = (raised / summed).astype(jnp.bfloat16)
    context = jnp.dot(
        attn_prob.reshape(num_heads * num_slots, num_slots),
        value_vec,
        preferred_element_type=jnp.float32,
    )
    context = (
        context.reshape(num_heads, num_slots, HD)
        .transpose(1, 0, 2)
        .reshape(num_slots, num_heads * HD)
    )
    return (context.astype(jnp.bfloat16), log_total)


def rms_pull(raw, gain_vec, delta):
    scale = lax.rsqrt(jnp.mean(raw * raw, axis=-1, keepdims=True) + 1e-06)
    weighed = delta * (1.0 + gain_vec)
    shared = jnp.mean(raw * weighed, axis=-1, keepdims=True)
    return scale * weighed - raw * (scale * scale * scale * shared), delta * raw * scale


def rotate_pull(delta, cos_tab, sin_tab):
    half_dim = delta.shape[-1] // 2
    lower_half = delta[:, :half_dim]
    upper_half = delta[:, half_dim:]
    return jnp.concatenate(
        [lower_half * cos_tab + upper_half * sin_tab, upper_half * cos_tab - lower_half * sin_tab],
        axis=-1,
    )


def attn_back_kernel(
    delta_attn,
    delta_mid,
    resid_in,
    query_raw,
    key_raw,
    value_vec,
    rot_query,
    rot_key,
    context,
    log_total,
    allowed,
    cos_ref,
    sin_ref,
    gain_in,
    gain_query,
    gain_key,
    query_weight,
    key_weight,
    value_weight,
    out_weight,
    grad_in,
    delta_qraw,
    delta_kraw,
    delta_value,
    gain_in_grad,
    gain_query_grad,
    gain_key_grad,
):
    cos_tab = cos_ref[...]
    sin_tab = sin_ref[...]
    keys = rot_key[...]
    values = value_vec[...]
    open_pairs = allowed[...] > 0.0
    delta_context = times_transposed(delta_attn[...], out_weight[...]).astype(jnp.bfloat16)
    delta_key = jnp.zeros((CAP, HD), jnp.float32)
    delta_values = jnp.zeros((CAP, HD), jnp.float32)
    query_gain_rows = jnp.zeros((CAP, HD), jnp.float32)
    for head in range(HQ // HD):
        at = slice(head * HD, (head + 1) * HD)
        head_delta = delta_context[:, at]
        row_dot = jnp.sum(
            head_delta.astype(jnp.float32) * context[:, at].astype(jnp.float32),
            axis=-1,
            keepdims=True,
        )
        queries = rot_query[head]
        scores = jnp.where(open_pairs, times_transposed(queries, keys), -1e30)
        prob_exact = jnp.exp(scores - log_total[:, head : head + 1])
        delta_prob = times_transposed(head_delta, values)
        delta_score = prob_exact * (delta_prob - row_dot)
        turned = delta_score.T.astype(jnp.bfloat16)
        delta_score = delta_score.astype(jnp.bfloat16)
        delta_query = jnp.dot(delta_score, keys, preferred_element_type=jnp.float32)
        delta_key += jnp.dot(turned, queries, preferred_element_type=jnp.float32)
        delta_values += jnp.dot(
            prob_exact.T.astype(jnp.bfloat16), head_delta, preferred_element_type=jnp.float32
        )
        delta_rot = rotate_pull(delta_query * HD ** (-0.5), cos_tab, sin_tab)
        delta_raw, gain_rows = rms_pull(query_raw[:, at], gain_query[...], delta_rot)
        query_gain_rows += gain_rows
        delta_qraw[:, at] = delta_raw.astype(jnp.bfloat16)
    delta_raw, gain_rows = rms_pull(
        key_raw[...], gain_key[...], rotate_pull(delta_key, cos_tab, sin_tab)
    )
    delta_kraw[...] = delta_raw.astype(jnp.bfloat16)
    delta_value[...] = delta_values.astype(jnp.bfloat16)
    gain_query_grad[...] = jnp.sum(query_gain_rows, axis=0, keepdims=True)
    gain_key_grad[...] = jnp.sum(gain_rows, axis=0, keepdims=True)
    delta_in = (
        times_transposed(delta_qraw[...], query_weight[...])
        + times_transposed(delta_kraw[...], key_weight[...])
        + times_transposed(delta_value[...], value_weight[...])
    )
    delta_part, gain_rows = rms_pull(resid_in[...].astype(jnp.float32), gain_in[...], delta_in)
    grad_in[...] = delta_mid[...] + delta_part
    gain_in_grad[...] = jnp.sum(gain_rows, axis=0, keepdims=True)


def bit_orders(devices, tuned):
    bits = devices.bit_length() - 1
    if bits == 5:
        return [["cxyab".index(letter) for letter in order] for order in tuned]
    return [[1 + (shift + step) % (bits - 1) for step in range(bits - 1)] for shift in range(3)]


def across(block, bit, devices):
    return lax.ppermute(block, "dp", [(i, i ^ (1 << bit)) for i in range(devices)])


def offset_of(place, order):
    return sum(((place >> k) & 1) << bit for k, bit in enumerate(order))


def gather_chunk(piece, order, devices):
    held = piece[None]
    for bit in order[:-1]:
        held = jnp.concatenate([held, across(held, bit, devices)])
    last = across(held, order[-1], devices)
    return (held, last, across(held, 0, devices), across(last, 0, devices))


def sent_blocks(chunks, orders, stage, devices):
    return [
        across(away, order[stage], devices)
        for (_, away), order in zip(chunks, orders)
    ]


def merged_blocks(chunks, came):
    merged = []
    for (home, _), arrived in zip(chunks, came):
        half = home.shape[0] // 2

        def added(low, high):
            return home[low:high].astype(jnp.float32) + arrived[low:high].astype(jnp.float32)

        if half:
            merged.append(
                (
                    added(0, half).astype(jnp.bfloat16),
                    added(half, 2 * half).astype(jnp.bfloat16),
                )
            )
        else:
            merged.append((added(0, 1)[0], None))
    return merged


def cut_rows(rows, parts):
    each = -(-rows // (parts * ROWS)) * ROWS
    return [(low, min(low + each, rows)) for low in range(0, rows, each)]


def whole_specs(count):
    return [pl.BlockSpec(memory_space=pltpu.VMEM)] * count


def copy_step(rows):
    return max(step for step in range(ROWS, 513, ROWS) if rows % step == 0)


def owner_rows(device, index, order, extra, start, each):
    owner = device ^ extra
    for k, bit in enumerate(order):
        owner = owner ^ (((index >> k) & 1) << bit)
    return owner, pl.multiple_of(owner * each + start, ROWS)


def unpack_kernel(plan, sizes, tail_rows, sources, device_ref, *refs):
    source_refs = refs[:sources]
    matrices = refs[sources : sources + len(sizes)]
    refs = refs[sources + len(sizes) :]
    tails = refs[0] if tail_rows else None
    spread = refs[-1]
    device = device_ref[0]
    for source, order, extra, take, start, each in plan:
        block_ref = source_refs[source]
        step = copy_step(take)

        @pl.loop(0, block_ref.shape[0])
        def _(index, block_ref=block_ref, order=order, extra=extra, take=take, start=start, each=each, step=step):
            owner, first = owner_rows(device, index, order, extra, start, each)
            for low in range(0, take, step):
                spread[pl.ds(pl.multiple_of(first + low, ROWS), step), :] = block_ref[
                    index, low : low + step, :
                ].astype(jnp.float32)
            if take < block_ref.shape[1]:
                tails[owner] = block_ref[index, take : take + tail_rows, :]

    first = 0
    for matrix, (rows, columns) in zip(matrices, sizes):
        blocks = columns // LANES

        @pl.loop(0, rows // LANES)
        def _(step, matrix=matrix, blocks=blocks, first=first):
            base = pl.multiple_of(first + step * (LANES * blocks), ROWS)
            at = pl.ds(pl.multiple_of(step * LANES, LANES), LANES)
            for block in range(blocks):
                matrix[at, block * LANES : (block + 1) * LANES] = spread[
                    pl.ds(base + block, LANES, stride=blocks), :
                ].astype(jnp.bfloat16)

        first += rows * blocks


def unpack_matrices(plan, sizes, tail_rows, device, arrays, devices):
    flat_rows = sum(rows * columns for rows, columns in sizes) // LANES
    shapes = [jax.ShapeDtypeStruct(size, jnp.bfloat16) for size in sizes]
    if tail_rows:
        shapes.append(jax.ShapeDtypeStruct((devices, tail_rows, LANES), jnp.bfloat16))
    return pl.pallas_call(
        functools.partial(unpack_kernel, plan, sizes, tail_rows, len(arrays)),
        out_shape=shapes,
        in_specs=[pl.BlockSpec(memory_space=pltpu.SMEM)] + whole_specs(len(arrays)),
        out_specs=whole_specs(len(shapes)),
        scratch_shapes=[pltpu.VMEM((flat_rows, LANES), jnp.float32)],
        compiler_params=pltpu.CompilerParams(vmem_limit_bytes=48 << 20),
        cost_estimate=pl.CostEstimate(flops=0, bytes_accessed=0, transcendentals=0),
    )(device, *arrays)


def grads_kernel(plan, sizes, has_tails, device_ref, *refs):
    pairs = refs[: 2 * len(sizes)]
    refs = refs[2 * len(sizes) :]
    tails = refs[0] if has_tails else None
    targets = refs[1 if has_tails else 0 : -1]
    spread = refs[-1]
    device = device_ref[0]
    first = 0
    for number, (rows, columns) in enumerate(sizes):
        left, right = pairs[2 * number : 2 * number + 2]
        blocks = columns // LANES
        wide = 2 - blocks % 2
        turned = left[...].T
        for block in range(0, blocks, wide):
            product = jnp.dot(
                turned,
                right[:, block * LANES : (block + wide) * LANES],
                preferred_element_type=jnp.float32,
            )
            for part in range(wide):
                spread[pl.ds(first + block + part, rows, stride=blocks), :] = product[
                    :, part * LANES : (part + 1) * LANES
                ]
        first += rows * blocks
    for target, order, extra, low, take, start, each in plan:
        target_ref = targets[target]
        step = copy_step(take)

        @pl.loop(0, target_ref.shape[0])
        def _(index, target_ref=target_ref, order=order, extra=extra, low=low, take=take, start=start, each=each, step=step):
            owner, first = owner_rows(device, index, order, extra, start or 0, each)
            if start is None:
                target_ref[index, low : low + take, :] = tails[owner]
                return

            @pl.loop(0, take // step)
            def _(part):
                at = pl.multiple_of(part * step, ROWS)
                target_ref[index, pl.ds(pl.multiple_of(low + at, ROWS), step), :] = spread[
                    pl.ds(pl.multiple_of(first + at, ROWS), step), :
                ].astype(jnp.bfloat16)


def grad_blocks(plan, sizes, pairs, tails, device, shapes):
    flat_rows = sum(rows * columns for rows, columns in sizes) // LANES
    inputs = [member for pair in pairs for member in pair] + ([] if tails is None else [tails])
    return pl.pallas_call(
        functools.partial(grads_kernel, plan, sizes, tails is not None),
        out_shape=[jax.ShapeDtypeStruct(shape, jnp.bfloat16) for shape in shapes],
        in_specs=[pl.BlockSpec(memory_space=pltpu.SMEM)] + whole_specs(len(inputs)),
        out_specs=whole_specs(len(shapes)),
        scratch_shapes=[pltpu.VMEM((flat_rows, LANES), jnp.float32)],
        compiler_params=pltpu.CompilerParams(vmem_limit_bytes=48 << 20),
        cost_estimate=pl.CostEstimate(flops=0, bytes_accessed=0, transcendentals=0),
    )(device, *inputs)


def gathered_matrices(pieces, orders, sizes, tail_rows, devices, device):
    each = sum(rows * columns for rows, columns in sizes) // LANES // devices
    arrays, plan, start = [], [], 0
    for piece, order in zip(pieces, orders):
        blocks = gather_chunk(piece, order, devices)
        take = min(piece.shape[0], each - start)
        if each % ROWS:
            table = jnp.concatenate(blocks)
            places = [offset_of(place, list(order) + [0]) for place in range(devices)]
            back = sorted(range(devices), key=places.__getitem__)
            mixed = offset_bits(device[0], list(order) + [0])
            arrays.append(jnp.take(table, jnp.array(back, jnp.int32) ^ mixed, axis=0))
            continue
        for part, block in enumerate(blocks):
            extra = offset_of(part, [order[-1], 0])
            plan.append((len(arrays), order[:-1], extra, take, start, each))
            arrays.append(block)
        start += take
    if each % ROWS == 0:
        return unpack_matrices(plan, sizes, tail_rows, device, arrays, devices)
    table = jnp.concatenate(arrays, axis=1)
    flat = table[:, :each].reshape(1, devices * each, LANES)
    plan = [(0, [], 0, devices * each, 0, 0)]
    found = list(unpack_matrices(plan, sizes, 0, device, [flat], devices))
    return found + ([table[:, each : each + tail_rows]] if tail_rows else [])


def offset_bits(device, order):
    return sum(((device >> bit) & 1) << k for k, bit in enumerate(order))


def scatter_blocks(pairs, tails, orders, sizes, devices, device):
    each = sum(rows * columns for rows, columns in sizes) // LANES // devices
    tail_rows = 0 if tails is None else tails.shape[1]
    parts = cut_rows(each + tail_rows, len(orders))
    half = devices // 2
    plan = []
    for with_core in (1, 0):
        for (low, high), order in zip(parts, orders):
            order = order[::-1]
            plan.append((with_core, order, with_core, low, min(high, each) - low, low, each))
            if high > each:
                plan.append((with_core, order, with_core, each, tail_rows, None, each))
    shape = (half, each + tail_rows, LANES)
    if each % ROWS == 0 and parts[-1][0] < each:
        blocks = grad_blocks(plan, sizes, pairs, tails, device, [shape, shape])
    else:
        flat = grad_blocks(
            [(0, [], 0, 0, devices * each, 0, 0)],
            sizes,
            pairs,
            None,
            device,
            [(1, devices * each, LANES)],
        )[0]
        table = flat.reshape(devices, each, LANES)
        table = table if tails is None else jnp.concatenate([table, tails], axis=1)
        blocks = []
        for with_core in (0, 1):
            chunks = []
            for (low, high), order in zip(parts, orders):
                offsets = [offset_of(index, order[::-1]) ^ with_core for index in range(half)]
                owners = jnp.array(offsets, jnp.int32) ^ device[0]
                chunks.append(jnp.take(table[:, low:high], owners, axis=0))
            blocks.append(jnp.concatenate(chunks, axis=1))
    return blocks, parts


def cores_merged(home, came, parts):
    half = home.shape[0] // 2

    def added(first, low, high):
        at = (slice(first, first + half), slice(low, high))
        return (home[at].astype(jnp.float32) + came[at].astype(jnp.float32)).astype(jnp.bfloat16)

    return [(added(0, low, high), added(half, low, high)) for low, high in parts]


def cut_gains(gain_flat):
    gains = gain_flat.astype(jnp.float32)
    return (
        gains[:D],
        gains[D : D + HD],
        gains[D + HD : D + 2 * HD],
        gains[D + 2 * HD : 2 * D + 2 * HD],
        gains[2 * D + 2 * HD : 3 * D + 2 * HD],
        gains[3 * D + 2 * HD :],
    )


def forward_pass(input_rows, weights, allowed, cos_tab, sin_tab):
    (
        query_weight,
        key_weight,
        value_weight,
        out_weight,
        gate_weight,
        up_weight,
        down_weight,
        gain_set,
    ) = weights
    gain_in, gain_query, gain_key, gain_post, gain_mid, gain_last = gain_set
    resid_in = input_rows.astype(jnp.float32)
    normed_in = rms_scale(resid_in, gain_in).astype(jnp.bfloat16)
    query_raw = jnp.dot(normed_in, query_weight, preferred_element_type=jnp.float32)
    key_raw = jnp.dot(normed_in, key_weight, preferred_element_type=jnp.float32)
    value_vec = jnp.dot(normed_in, value_weight, preferred_element_type=jnp.float32).astype(
        jnp.bfloat16
    )
    rot_query, rot_key = query_key(query_raw, key_raw, gain_query, gain_key, cos_tab, sin_tab)
    rot_query = rot_query.astype(jnp.bfloat16)
    rot_key = rot_key.astype(jnp.bfloat16)
    context, log_total = attend(rot_query, rot_key, value_vec, allowed)
    attn_out = jnp.dot(context, out_weight, preferred_element_type=jnp.float32)
    mid_stream = resid_in + rms_scale(attn_out, gain_post)
    normed_mid = rms_scale(mid_stream, gain_mid).astype(jnp.bfloat16)
    gate_proj = jnp.dot(normed_mid, gate_weight, preferred_element_type=jnp.float32)
    up_proj = jnp.dot(normed_mid, up_weight, preferred_element_type=jnp.float32)
    hidden = gated_gelu(gate_proj, up_proj).astype(jnp.bfloat16)
    ffn_out = jnp.dot(hidden, down_weight, preferred_element_type=jnp.float32)
    block_out = (mid_stream + rms_scale(ffn_out, gain_last)).astype(jnp.bfloat16)
    saved = (
        resid_in,
        normed_in,
        query_raw,
        key_raw,
        value_vec,
        rot_query,
        rot_key,
        context,
        log_total,
        attn_out,
        mid_stream,
        normed_mid,
        gate_proj,
        up_proj,
        hidden,
        ffn_out,
    )
    return (block_out, saved)


def ffn_backward(cot_rows, live_mask, weights, saved):
    gate_weight, up_weight, down_weight, gain_set = (weights[4], weights[5], weights[6], weights[7])
    gain_mid, gain_last = (gain_set[4], gain_set[5])
    mid_stream, normed_mid, gate_proj, up_proj, hidden, ffn_out = saved[10:]
    delta_out = cot_rows.astype(jnp.float32) * live_mask[:, None]
    unused, pullback = jax.vjp(rms_scale, ffn_out, gain_last)
    delta_ffn, gain_last_grad = pullback(delta_out)
    delta_ffn = delta_ffn.astype(jnp.bfloat16)
    delta_hidden = times_transposed(delta_ffn, down_weight)
    unused, pullback = jax.vjp(gated_gelu, gate_proj, up_proj)
    delta_gate, delta_up = pullback(delta_hidden)
    delta_gate = delta_gate.astype(jnp.bfloat16)
    delta_up = delta_up.astype(jnp.bfloat16)
    delta_normed = times_transposed(delta_gate, gate_weight) + times_transposed(delta_up, up_weight)
    unused, pullback = jax.vjp(rms_scale, mid_stream, gain_mid)
    delta_part, gain_mid_grad = pullback(delta_normed)
    delta_mid = delta_out + delta_part
    pairs = ((normed_mid, delta_gate), (normed_mid, delta_up), (hidden, delta_ffn))
    return (delta_mid, pairs, (gain_mid_grad, gain_last_grad))


def attn_backward(delta_mid, delta_attn, input_rows, weights, saved, allowed, cos_tab, sin_tab):
    query_weight, key_weight, value_weight, out_weight = weights[:4]
    gain_in, gain_query, gain_key = weights[7][:3]
    (
        resid_in,
        normed_in,
        query_raw,
        key_raw,
        value_vec,
        rot_query,
        rot_key,
        context,
        log_total,
        attn_out,
    ) = saved[:10]
    shapes = [
        jax.ShapeDtypeStruct((CAP, D), jnp.float32),
        jax.ShapeDtypeStruct((CAP, HQ), jnp.bfloat16),
        jax.ShapeDtypeStruct((CAP, HD), jnp.bfloat16),
        jax.ShapeDtypeStruct((CAP, HD), jnp.bfloat16),
        jax.ShapeDtypeStruct((1, D), jnp.float32),
        jax.ShapeDtypeStruct((1, HD), jnp.float32),
        jax.ShapeDtypeStruct((1, HD), jnp.float32),
    ]
    grad_in, delta_qraw, delta_kraw, delta_value, *gain_grads = pl.pallas_call(
        attn_back_kernel,
        out_shape=shapes,
        in_specs=whole_specs(20),
        out_specs=whole_specs(len(shapes)),
        compiler_params=pltpu.CompilerParams(vmem_limit_bytes=32 << 20),
        cost_estimate=pl.CostEstimate(flops=0, bytes_accessed=0, transcendentals=0),
    )(
        delta_attn,
        delta_mid,
        input_rows,
        query_raw,
        key_raw,
        value_vec,
        rot_query,
        rot_key,
        context,
        log_total.reshape(HQ // HD, CAP).T,
        allowed.astype(jnp.float32),
        cos_tab,
        sin_tab,
        gain_in[None],
        gain_query[None],
        gain_key[None],
        query_weight,
        key_weight,
        value_weight,
        out_weight,
    )
    pairs = (
        (normed_in, delta_qraw),
        (normed_in, delta_kraw),
        (normed_in, delta_value),
        (context, delta_attn),
    )
    return (grad_in, pairs, [member.reshape(-1) for member in gain_grads])


def adam_update(weight_shard, gradient, moment_one, moment_two):
    moment_one = 0.9 * moment_one + 0.1 * gradient
    moment_two = 0.999 * moment_two + 0.001 * gradient * gradient
    fix_one = 1.0 - 0.9**STEP
    fix_two = 1.0 - 0.999**STEP
    weight_shard = weight_shard - 0.02 * (
        moment_one / fix_one / (jnp.sqrt(moment_two / fix_two) + 1e-08) + 0.1 * weight_shard
    )
    return (weight_shard, moment_one, moment_two)


def per_device(hidden_in, cotangent, params, moment_one, moment_two, seq_lengths, seq_owner):
    devices = lax.axis_size("dp")
    device = lax.axis_index("dp").astype(jnp.int32)
    here = device.reshape(1)
    attn_len = G1LEN // devices
    ffn_len = G2LEN // devices
    gain_len = params.shape[0] - attn_len - ffn_len
    attn_rows = attn_len // LANES
    tail_rows = -(-(attn_rows + 1) // ROWS) * ROWS - attn_rows
    pad = tail_rows * LANES - gain_len
    rounded = params.astype(jnp.bfloat16)
    first_piece = jnp.concatenate(
        [rounded[:attn_len], rounded[attn_len + ffn_len :], jnp.zeros((pad,), jnp.bfloat16)]
    ).reshape(-1, LANES)
    second_piece = rounded[attn_len : attn_len + ffn_len].reshape(-1, LANES)
    second_pieces = [second_piece[low:high] for low, high in cut_rows(ffn_len // LANES, 2)]
    orders = bit_orders(devices, ("abxy", "bxya", "byax"))
    *attn_weights, tails = gathered_matrices(
        [first_piece], orders[:1], ATTN_SIZES, tail_rows, devices, here
    )
    ffn_weights = gathered_matrices(second_pieces, orders[1:], FFN_SIZES, 0, devices, here)
    gain_flat = tails.reshape(devices, -1)[:, :gain_len].reshape(-1)
    weights = (*attn_weights, *ffn_weights, cut_gains(gain_flat))
    live_mask, allowed, cos_tab, sin_tab = slot_setup(seq_lengths, seq_owner, device)
    block_out, saved = forward_pass(hidden_in, weights, allowed, cos_tab, sin_tab)
    delta_mid, ffn_pairs, late_gains = ffn_backward(cotangent, live_mask, weights, saved)
    ffn_orders = bit_orders(devices, ("xaby", "yxab", "ayxb"))
    attn_orders = bit_orders(devices, ("xyab", "yxba"))[:2]
    (ffn_home, ffn_away), ffn_parts = scatter_blocks(
        ffn_pairs, None, ffn_orders, FFN_SIZES, devices, here
    )
    delta_mid, ffn_home, ffn_away = lax.optimization_barrier((delta_mid, ffn_home, ffn_away))
    ffn_came = across(ffn_away, 0, devices)
    unused, pullback = jax.vjp(rms_scale, saved[9], weights[7][3])
    delta_attn, gain_post_grad = pullback(delta_mid)
    delta_attn = delta_attn.astype(jnp.bfloat16)
    delta_attn, ffn_came = lax.optimization_barrier((delta_attn, ffn_came))
    ffn_chunks = cores_merged(ffn_home, ffn_came, ffn_parts)
    delta_attn, ffn_chunks = lax.optimization_barrier((delta_attn, ffn_chunks))
    ffn_came = sent_blocks(ffn_chunks, ffn_orders, 0, devices)
    grad_in, attn_pairs, early_gains = attn_backward(
        delta_mid, delta_attn, hidden_in, weights, saved, allowed, cos_tab, sin_tab
    )
    early_gains = (*early_gains, gain_post_grad)
    gain_table = jnp.concatenate(early_gains + late_gains).reshape(devices, gain_len)
    gain_table = jnp.pad(gain_table.astype(jnp.bfloat16), ((0, 0), (0, pad)))
    gain_table = gain_table.reshape(devices, tail_rows, LANES)
    (attn_home, attn_away), attn_parts = scatter_blocks(
        attn_pairs, gain_table, attn_orders, ATTN_SIZES, devices, here
    )
    attn_home, attn_away, ffn_came = lax.optimization_barrier((attn_home, attn_away, ffn_came))
    stages = len(ffn_orders[0])
    ffn_chunks = merged_blocks(ffn_chunks, ffn_came)
    ffn_came = sent_blocks(ffn_chunks, ffn_orders, 1, devices)
    attn_came = across(attn_away, 0, devices)
    ffn_came[0], attn_came = lax.optimization_barrier((ffn_came[0], attn_came))
    attn_chunks = cores_merged(attn_home, attn_came, attn_parts)
    for stage in range(1, stages + 1):
        attn_came = sent_blocks(attn_chunks, attn_orders, stage - 1, devices)
        if stage < stages:
            ffn_chunks = merged_blocks(ffn_chunks, ffn_came)
        if stage + 1 < stages:
            ffn_came = sent_blocks(ffn_chunks, ffn_orders, stage + 1, devices)
            for chunk, arrived in enumerate(attn_came):
                ffn_came[chunk], attn_came[chunk] = lax.optimization_barrier(
                    (ffn_came[chunk], arrived)
                )
        attn_chunks = merged_blocks(attn_chunks, attn_came)
    attn_shard = jnp.concatenate([rows for rows, _ in attn_chunks]).reshape(-1)
    ffn_shard = jnp.concatenate([rows for rows, _ in ffn_chunks])
    grad_shard = jnp.concatenate(
        [attn_shard[:attn_len], ffn_shard.reshape(-1), attn_shard[attn_len : attn_len + gain_len]]
    )
    params_new, moment_one_new, moment_two_new = adam_update(
        params, grad_shard, moment_one, moment_two
    )
    return (block_out, grad_in, grad_shard, params_new, moment_one_new, moment_two_new)


def solution(mesh):
    in_specs = (P("dp", None), P("dp", None), P("dp"), P("dp"), P("dp"), P(), P())
    out_specs = (P("dp", None), P("dp", None), P("dp"), P("dp"), P("dp"), P("dp"))
    return jax.shard_map(
        per_device, mesh=mesh, in_specs=in_specs, out_specs=out_specs, check_vma=False
    )
```

```python
import functools
import math

import jax
import jax.numpy as jnp
from jax import lax
from jax.experimental import pallas as pl
from jax.experimental.pallas import tpu as pltpu
from jax.sharding import PartitionSpec as P

D = 640
FF = 2048
HD = 256
HQ = 1024
CAP = 128
WINDOW = 64
STEP = 3
G1LEN = 1638400
G2LEN = 3932160
LANES = 128
ROWS = 16
GELU_SCALE = math.sqrt(2 / math.pi)


def rms_scale(values, gain_vec):
    return (
        values
        * lax.rsqrt(jnp.mean(values * values, axis=-1, keepdims=True) + 1e-06)
        * (1.0 + gain_vec)
    )


def rotate(values, cos_tab, sin_tab):
    half_dim = values.shape[-1] // 2
    lower_half = values[..., :half_dim]
    upper_half = values[..., half_dim:]
    return jnp.concatenate(
        [lower_half * cos_tab - upper_half * sin_tab, upper_half * cos_tab + lower_half * sin_tab],
        axis=-1,
    )


def gated_gelu(gate_proj, up_proj):
    return jax.nn.gelu(gate_proj, approximate=True) * up_proj


def times_transposed(rows_in, matrix):
    return lax.dot_general(
        rows_in, matrix, (((1,), (1,)), ((), ())), preferred_element_type=jnp.float32
    )


def slot_setup(seq_lengths, seq_owner, device):
    mine_mask = seq_owner == device
    own_lengths = jnp.where(mine_mask, seq_lengths, 0)
    seq_ends = jnp.cumsum(own_lengths, dtype=jnp.int32)
    seq_begins = seq_ends - own_lengths
    slot_index = jnp.arange(CAP, dtype=jnp.int32)
    column = slot_index[:, None]
    inside_mask = (
        mine_mask[None, :] & (seq_begins[None, :] <= column) & (column < seq_ends[None, :])
    )
    live_mask = jnp.any(inside_mask, axis=1)
    seq_label = jnp.sum(
        (mine_mask[None, :] & (seq_ends[None, :] <= column)).astype(jnp.int32),
        axis=1,
        dtype=jnp.int32,
    )
    position = jnp.sum(
        jnp.where(inside_mask, column - seq_begins[None, :], 0), axis=1, dtype=jnp.int32
    )
    row_slot = slot_index[:, None]
    col_slot = slot_index[None, :]
    allowed = live_mask[:, None] & live_mask[None, :] & (
        seq_label[:, None] == seq_label[None, :]
    ) & (col_slot <= row_slot) & (row_slot - col_slot < WINDOW) | (row_slot == col_slot)
    half_dim = HD // 2
    frequency = 10000.0 ** (-2.0 * jnp.arange(half_dim, dtype=jnp.float32) / HD)
    angles = position.astype(jnp.float32)[:, None] * frequency[None, :]
    live_wide = jnp.broadcast_to(live_mask[:, None], (CAP, LANES)).astype(jnp.float32)
    return jnp.concatenate(
        [jnp.cos(angles), jnp.sin(angles), allowed.astype(jnp.float32), live_wide], axis=1
    )


def rms_pull(raw, gain_vec, delta):
    scale = lax.rsqrt(jnp.mean(raw * raw, axis=-1, keepdims=True) + 1e-06)
    weighed = delta * (1.0 + gain_vec)
    shared = jnp.mean(raw * weighed, axis=-1, keepdims=True)
    return scale * weighed - raw * (scale * scale * scale * shared), delta * raw * scale


def rotate_pull(delta, cos_tab, sin_tab):
    half_dim = delta.shape[-1] // 2
    lower_half = delta[:, :half_dim]
    upper_half = delta[:, half_dim:]
    return jnp.concatenate(
        [lower_half * cos_tab + upper_half * sin_tab, upper_half * cos_tab - lower_half * sin_tab],
        axis=-1,
    )


def bit_orders(devices, tuned):
    bits = devices.bit_length() - 1
    if bits == 5:
        return [["cxyab".index(letter) for letter in order] for order in tuned]
    return [[1 + (shift + step) % (bits - 1) for step in range(bits - 1)] for shift in range(3)]


def across(block, bit, devices):
    return lax.ppermute(block, "dp", [(i, i ^ (1 << bit)) for i in range(devices)])


def offset_of(place, order):
    return sum(((place >> k) & 1) << bit for k, bit in enumerate(order))


def gather_chunk(piece, order, devices):
    held = piece[None]
    for bit in order[:-1]:
        held = jnp.concatenate([held, across(held, bit, devices)])
    last = across(held, order[-1], devices)
    return (held, last, across(held, 0, devices), across(last, 0, devices))


def sent_blocks(chunks, orders, stage, devices):
    return [
        across(away, order[stage], devices)
        for (_, away), order in zip(chunks, orders)
    ]


def merged_blocks(chunks, came):
    merged = []
    for (home, _), arrived in zip(chunks, came):
        half = home.shape[0] // 2

        def added(low, high):
            return home[low:high].astype(jnp.float32) + arrived[low:high].astype(jnp.float32)

        if half:
            merged.append(
                (
                    added(0, half).astype(jnp.bfloat16),
                    added(half, 2 * half).astype(jnp.bfloat16),
                )
            )
        else:
            merged.append((added(0, 1)[0], None))
    return merged


def cut_rows(rows, parts):
    each = -(-rows // (parts * ROWS)) * ROWS
    return [(low, min(low + each, rows)) for low in range(0, rows, each)]


def whole_specs(count):
    return [pl.BlockSpec(memory_space=pltpu.VMEM)] * count


def copy_step(rows):
    return max(step for step in range(ROWS, 513, ROWS) if rows % step == 0)


def owner_rows(device, index, order, extra, start, each):
    owner = device ^ extra
    for k, bit in enumerate(order):
        owner = owner ^ (((index >> k) & 1) << bit)
    return owner, pl.multiple_of(owner * each + start, ROWS)


def spread_blocks(plan, views, device, spread, tails):
    for (order, extra, take, start, each), (block_ref, first_index, count, first_row) in zip(
        plan, views
    ):
        step = copy_step(take)

        @pl.loop(0, count)
        def _(
            index,
            order=order,
            extra=extra,
            take=take,
            start=start,
            each=each,
            block_ref=block_ref,
            first_index=first_index,
            first_row=first_row,
            step=step,
        ):
            owner, first = owner_rows(device, index, order, extra, start, each)
            for low in range(0, take, step):
                spread[pl.ds(pl.multiple_of(first + low, ROWS), step), :] = block_ref[
                    first_index + index, first_row + low : first_row + low + step, :
                ].astype(jnp.float32)
            if tails is not None:
                tails[owner] = block_ref[index, take : take + tails.shape[1], :]


def fold_matrices(spread, targets):
    first = 0
    for matrix, offset, rows, columns in targets:
        blocks = columns // LANES

        @pl.loop(0, rows // LANES)
        def _(step, matrix=matrix, offset=offset, blocks=blocks, first=first):
            base = pl.multiple_of(first + step * (LANES * blocks), ROWS)
            at = pl.ds(pl.multiple_of(step * LANES, LANES), LANES)
            for block in range(blocks):
                low = offset + block * LANES
                matrix[at, low : low + LANES] = spread[
                    pl.ds(base + block, LANES, stride=blocks), :
                ].astype(jnp.bfloat16)

        first += rows * blocks


def attn_unpack_kernel(plan, has_tails, device_ref, *refs):
    sources = refs[: len(plan)]
    qkv_weight, out_weight = refs[len(plan) : len(plan) + 2]
    tails = refs[len(plan) + 2] if has_tails else None
    spread = refs[-1]
    views = [(source, 0, source.shape[0], 0) for source in sources]
    spread_blocks(plan, views, device_ref[0], spread, tails)
    fold_matrices(
        spread,
        (
            (qkv_weight, 0, D, HQ),
            (qkv_weight, HQ, D, HD),
            (qkv_weight, HQ + HD, D, HD),
            (out_weight, 0, HQ, D),
        ),
    )


def unpack_attn(plan, tail_rows, device, arrays, devices):
    flat_rows = G1LEN // LANES
    shapes = [
        jax.ShapeDtypeStruct((D, HQ + 2 * HD), jnp.bfloat16),
        jax.ShapeDtypeStruct((HQ, D), jnp.bfloat16),
    ]
    if tail_rows:
        shapes.append(jax.ShapeDtypeStruct((devices, tail_rows, LANES), jnp.bfloat16))
    return pl.pallas_call(
        functools.partial(attn_unpack_kernel, plan, bool(tail_rows)),
        out_shape=shapes,
        in_specs=[pl.BlockSpec(memory_space=pltpu.SMEM)] + whole_specs(len(arrays)),
        out_specs=whole_specs(len(shapes)),
        scratch_shapes=[pltpu.VMEM((flat_rows, LANES), jnp.float32)],
        compiler_params=pltpu.CompilerParams(vmem_limit_bytes=16 << 20),
        cost_estimate=pl.CostEstimate(flops=0, bytes_accessed=0, transcendentals=0),
    )(device, *arrays)


def spread_grads(spread, products):
    first = 0
    for turned, right, columns in products:
        rows = turned.shape[0]
        blocks = columns // LANES
        wide = 2 - blocks % 2
        for block in range(0, blocks, wide):
            product = jnp.dot(
                turned,
                right(block * LANES, (block + wide) * LANES),
                preferred_element_type=jnp.float32,
            )
            for part in range(wide):
                spread[pl.ds(first + block + part, rows, stride=blocks), :] = product[
                    :, part * LANES : (part + 1) * LANES
                ]
        first += rows * blocks


def place_blocks(plan, device, spread, tails, targets):
    for target, order, extra, low, take, start, each in plan:
        target_ref = targets[target]
        step = copy_step(take)

        @pl.loop(0, target_ref.shape[0])
        def _(
            index,
            target_ref=target_ref,
            order=order,
            extra=extra,
            low=low,
            take=take,
            start=start,
            each=each,
            step=step,
        ):
            owner, first = owner_rows(device, index, order, extra, start or 0, each)
            if start is None:
                target_ref[index, low : low + take, :] = tails[owner].astype(jnp.bfloat16)
                return

            @pl.loop(0, take // step)
            def _(part):
                at = pl.multiple_of(part * step, ROWS)
                target_ref[index, pl.ds(pl.multiple_of(low + at, ROWS), step), :] = spread[
                    pl.ds(pl.multiple_of(first + at, ROWS), step), :
                ].astype(jnp.bfloat16)


def attn_forward(hidden_in, qkv_weight, tables, gains):
    cos_tab = tables[:, :LANES]
    sin_tab = tables[:, LANES : 2 * LANES]
    open_pairs = tables[:, 2 * LANES : 3 * LANES] > 0.0
    gain_query = gains[:, D : D + HD]
    gain_key = gains[:, D + HD : D + 2 * HD]
    normed_in = rms_scale(hidden_in[...].astype(jnp.float32), gains[:, :D]).astype(jnp.bfloat16)
    raw = jnp.dot(normed_in, qkv_weight[...], preferred_element_type=jnp.float32)
    key_raw = raw[:, HQ : HQ + HD]
    values = raw[:, HQ + HD :].astype(jnp.bfloat16)
    keys = rotate(rms_scale(key_raw, gain_key), cos_tab, sin_tab).astype(jnp.bfloat16)
    heads = []
    for head in range(HQ // HD):
        query_raw = raw[:, head * HD : (head + 1) * HD]
        rot_query = rotate(rms_scale(query_raw, gain_query), cos_tab, sin_tab) * HD ** (-0.5)
        rot_query = rot_query.astype(jnp.bfloat16)
        scores = jnp.where(open_pairs, times_transposed(rot_query, keys), -1e30)
        row_max = jnp.max(scores, axis=-1, keepdims=True)
        raised = jnp.exp(scores - row_max)
        summed = jnp.sum(raised, axis=-1, keepdims=True)
        context = jnp.dot(
            (raised / summed).astype(jnp.bfloat16), values, preferred_element_type=jnp.float32
        ).astype(jnp.bfloat16)
        heads.append((query_raw, rot_query, scores, row_max + jnp.log(summed), context))
    return normed_in, key_raw, values, keys, heads, cos_tab, sin_tab


def attn_forward_kernel(
    hidden_in, qkv_weight, out_weight, tables, gains, attn_out, mid_stream, context
):
    heads = attn_forward(hidden_in, qkv_weight, tables, gains)[4]
    for head, parts in enumerate(heads):
        context[:, head * HD : (head + 1) * HD] = parts[-1]
    out = jnp.dot(context[...], out_weight[...], preferred_element_type=jnp.float32)
    attn_out[...] = out
    gain_post = gains[:, D + 2 * HD : 2 * D + 2 * HD]
    mid_stream[...] = hidden_in[...].astype(jnp.float32) + rms_scale(out, gain_post)


def forward_attn(hidden_in, qkv_weight, out_weight, tables, gains):
    shapes = [jax.ShapeDtypeStruct((CAP, D), jnp.float32)] * 2
    return pl.pallas_call(
        attn_forward_kernel,
        out_shape=shapes,
        in_specs=whole_specs(5),
        out_specs=whole_specs(2),
        scratch_shapes=[pltpu.VMEM((CAP, HQ), jnp.bfloat16)],
        compiler_params=pltpu.CompilerParams(vmem_limit_bytes=12 << 20),
        cost_estimate=pl.CostEstimate(flops=0, bytes_accessed=0, transcendentals=0),
    )(hidden_in, qkv_weight, out_weight, tables, gains)


def ffn_kernel(
    plan_in,
    staged,
    plan_out,
    device_ref,
    mid_ref,
    attn_out,
    cotangent,
    tables,
    gains,
    *refs,
):
    sources = refs[: len(plan_in)]
    refs = refs[len(plan_in) :]
    block_out, delta_mid_ref, delta_attn_ref, late_gains = refs[:4]
    targets = refs[4:-10]
    spread, gate_weight, up_weight, down_weight = refs[-10:-6]
    gates, ups, hidden, delta_gate, delta_up, sems = refs[-6:]
    device = device_ref[0]
    copies, views = [], []
    for source, (target, first_index, first_row) in zip(sources, staged):
        count, rows = source.shape[:2]
        held = targets[target]
        copies.append(
            pltpu.make_async_copy(
                source,
                held.at[pl.ds(first_index, count), pl.ds(first_row, rows), :],
                sems.at[len(copies)],
            )
        )
        views.append((held, first_index, count, first_row))
    for copy in copies:
        copy.start()
    mid_stream = mid_ref[...]
    gain_post = gains[:, D + 2 * HD : 2 * D + 2 * HD]
    gain_mid = gains[:, 2 * D + 2 * HD : 3 * D + 2 * HD]
    gain_last = gains[:, 3 * D + 2 * HD :]
    normed_mid = rms_scale(mid_stream, gain_mid).astype(jnp.bfloat16)
    for copy, plan, view in zip(copies, plan_in, views):
        copy.wait()
        spread_blocks([plan], [view], device, spread, None)
    fold_matrices(
        spread, ((gate_weight, 0, D, FF), (up_weight, 0, D, FF), (down_weight, 0, FF, D))
    )
    parts = [slice(low, low + 512) for low in range(0, FF, 512)]
    for at in parts:
        gate = jnp.dot(normed_mid, gate_weight[:, at], preferred_element_type=jnp.float32)
        up = jnp.dot(normed_mid, up_weight[:, at], preferred_element_type=jnp.float32)
        gates[:, at] = gate
        ups[:, at] = up
        hidden[:, at] = gated_gelu(gate, up).astype(jnp.bfloat16)
    ffn_out = jnp.dot(hidden[...], down_weight[...], preferred_element_type=jnp.float32)
    block_out[...] = (mid_stream + rms_scale(ffn_out, gain_last)).astype(jnp.bfloat16)
    delta_out = cotangent[...].astype(jnp.float32) * tables[:, 3 * LANES : 3 * LANES + 1]
    delta_ffn, gain_rows = rms_pull(ffn_out, gain_last, delta_out)
    late_gains[2:3, :] = jnp.sum(gain_rows, axis=0, keepdims=True)
    delta_ffn = delta_ffn.astype(jnp.bfloat16)
    delta_normed = jnp.zeros((CAP, D), jnp.float32)
    for at in parts:
        delta_hidden = times_transposed(delta_ffn, down_weight[at, :])
        gate = gates[:, at]
        raised = jnp.tanh(GELU_SCALE * (gate + 0.044715 * (gate * gate * gate)))
        share = 0.5 * (1.0 + raised)
        slope = share + (0.5 * GELU_SCALE) * gate * (1.0 - raised * raised) * (
            1.0 + (3 * 0.044715) * (gate * gate)
        )
        delta_gate[:, at] = (delta_hidden * ups[:, at] * slope).astype(jnp.bfloat16)
        delta_up[:, at] = (delta_hidden * (gate * share)).astype(jnp.bfloat16)
        delta_normed += times_transposed(delta_gate[:, at], gate_weight[:, at])
        delta_normed += times_transposed(delta_up[:, at], up_weight[:, at])
    delta_part, gain_rows = rms_pull(mid_stream, gain_mid, delta_normed)
    late_gains[1:2, :] = jnp.sum(gain_rows, axis=0, keepdims=True)
    delta_mid = delta_out + delta_part
    delta_mid_ref[...] = delta_mid
    delta_attn, gain_rows = rms_pull(attn_out[...], gain_post, delta_mid)
    late_gains[0:1, :] = jnp.sum(gain_rows, axis=0, keepdims=True)
    delta_attn_ref[...] = delta_attn.astype(jnp.bfloat16)
    turned = normed_mid.T
    spread_grads(
        spread,
        (
            (turned, lambda low, high: delta_gate[:, low:high], FF),
            (turned, lambda low, high: delta_up[:, low:high], FF),
            (hidden[...].T, lambda low, high: delta_ffn[:, low:high], D),
        ),
    )
    place_blocks(plan_out, device, spread, None, targets)


def run_ffn(
    plan_in, staged, plan_out, block_shapes, device, mid, attn_out, cotangent, tables, gains, arrays
):
    flat_rows = G2LEN // LANES
    shapes = [
        jax.ShapeDtypeStruct((CAP, D), jnp.bfloat16),
        jax.ShapeDtypeStruct((CAP, D), jnp.float32),
        jax.ShapeDtypeStruct((CAP, D), jnp.bfloat16),
        jax.ShapeDtypeStruct((3, D), jnp.float32),
    ] + [jax.ShapeDtypeStruct(shape, jnp.bfloat16) for shape in block_shapes]
    wide = pltpu.VMEM((CAP, FF), jnp.float32)
    narrow = pltpu.VMEM((CAP, FF), jnp.bfloat16)
    return pl.pallas_call(
        functools.partial(ffn_kernel, plan_in, staged, plan_out),
        out_shape=shapes,
        in_specs=[pl.BlockSpec(memory_space=pltpu.SMEM)]
        + whole_specs(5)
        + [pl.BlockSpec(memory_space=pl.ANY)] * len(arrays),
        out_specs=whole_specs(len(shapes)),
        scratch_shapes=[
            pltpu.VMEM((flat_rows, LANES), jnp.float32),
            pltpu.VMEM((D, FF), jnp.bfloat16),
            pltpu.VMEM((D, FF), jnp.bfloat16),
            pltpu.VMEM((FF, D), jnp.bfloat16),
            wide,
            wide,
            narrow,
            narrow,
            narrow,
            pltpu.SemaphoreType.DMA((len(arrays),)),
        ],
        compiler_params=pltpu.CompilerParams(vmem_limit_bytes=44 << 20),
        cost_estimate=pl.CostEstimate(flops=0, bytes_accessed=0, transcendentals=0),
    )(device, mid, attn_out, cotangent, tables, gains, *arrays)


def attn_back_kernel(
    plan,
    gain_len,
    device_ref,
    delta_attn,
    delta_mid,
    hidden_in,
    tables,
    gains,
    late_gains,
    qkv_weight,
    out_weight,
    grad_in,
    gain_grads,
    *refs,
):
    targets = refs[:-4]
    spread, tails, delta_raws, contexts = refs[-4:]
    device = device_ref[0]
    normed_in, key_raw, values, keys, heads, cos_tab, sin_tab = attn_forward(
        hidden_in, qkv_weight, tables, gains
    )
    gain_query = gains[:, D : D + HD]
    gain_key = gains[:, D + HD : D + 2 * HD]
    delta_context = times_transposed(delta_attn[...], out_weight[...]).astype(jnp.bfloat16)
    delta_key = jnp.zeros((CAP, HD), jnp.float32)
    delta_value = jnp.zeros((CAP, HD), jnp.float32)
    query_gain_rows = jnp.zeros((CAP, HD), jnp.float32)
    for head, (query_raw, queries, scores, log_total, context) in enumerate(heads):
        at = slice(head * HD, (head + 1) * HD)
        contexts[:, at] = context
        head_delta = delta_context[:, at]
        row_dot = jnp.sum(
            head_delta.astype(jnp.float32) * context.astype(jnp.float32), axis=-1, keepdims=True
        )
        prob_exact = jnp.exp(scores - log_total)
        delta_prob = times_transposed(head_delta, values)
        delta_score = prob_exact * (delta_prob - row_dot)
        turned = delta_score.T.astype(jnp.bfloat16)
        delta_score = delta_score.astype(jnp.bfloat16)
        delta_query = jnp.dot(delta_score, keys, preferred_element_type=jnp.float32)
        delta_key += jnp.dot(turned, queries, preferred_element_type=jnp.float32)
        delta_value += jnp.dot(
            prob_exact.T.astype(jnp.bfloat16), head_delta, preferred_element_type=jnp.float32
        )
        delta_rot = rotate_pull(delta_query * HD ** (-0.5), cos_tab, sin_tab)
        delta_raw, gain_rows = rms_pull(query_raw, gain_query, delta_rot)
        query_gain_rows += gain_rows
        delta_raws[:, at] = delta_raw.astype(jnp.bfloat16)
    delta_raw, gain_rows = rms_pull(key_raw, gain_key, rotate_pull(delta_key, cos_tab, sin_tab))
    delta_raws[:, HQ : HQ + HD] = delta_raw.astype(jnp.bfloat16)
    delta_raws[:, HQ + HD :] = delta_value.astype(jnp.bfloat16)
    gain_grads[:, D : D + HD] = jnp.sum(query_gain_rows, axis=0, keepdims=True)
    gain_grads[:, D + HD : D + 2 * HD] = jnp.sum(gain_rows, axis=0, keepdims=True)
    delta_in = times_transposed(delta_raws[...], qkv_weight[...])
    delta_part, gain_rows = rms_pull(
        hidden_in[...].astype(jnp.float32), gains[:, :D], delta_in
    )
    grad_in[...] = delta_mid[...] + delta_part
    gain_grads[:, :D] = jnp.sum(gain_rows, axis=0, keepdims=True)
    for late in range(3):
        at = slice((late + 1) * D + 2 * HD, (late + 2) * D + 2 * HD)
        gain_grads[:, at] = late_gains[late : late + 1, :]
    if gain_len:
        tails[...] = jnp.zeros_like(tails)
        lane = lax.broadcasted_iota(jnp.int32, (1, LANES), 1)
        for owner in range(tails.shape[0]):
            row, shift = divmod(owner * gain_len, LANES)
            piece = gain_grads[:, row * LANES : (row + 1) * LANES]
            if shift:
                piece = pltpu.roll(piece, LANES - shift, 1)
            if shift + gain_len > LANES:
                after = gain_grads[:, (row + 1) * LANES : (row + 2) * LANES]
                after = pltpu.roll(after, LANES - shift, 1)
                piece = jnp.where(lane < LANES - shift, piece, after)
            tails[owner, 0:1, :] = jnp.where(lane < gain_len, piece, 0.0)
    turned = normed_in.T
    delta_attn_value = delta_attn[...]
    spread_grads(
        spread,
        (
            (turned, lambda low, high: delta_raws[:, low:high], HQ),
            (turned, lambda low, high: delta_raws[:, HQ + low : HQ + high], HD),
            (turned, lambda low, high: delta_raws[:, HQ + HD + low : HQ + HD + high], HD),
            (contexts[...].T, lambda low, high: delta_attn_value[:, low:high], D),
        ),
    )
    place_blocks(plan, device, spread, tails, targets)


def back_attn(plan, gain_len, tail_rows, devices, block_shapes, device, *inputs):
    flat_rows = G1LEN // LANES
    shapes = [
        jax.ShapeDtypeStruct((CAP, D), jnp.float32),
        jax.ShapeDtypeStruct((1, 4 * D + 2 * HD), jnp.float32),
    ] + [jax.ShapeDtypeStruct(shape, jnp.bfloat16) for shape in block_shapes]
    tail_shape = (devices, tail_rows, LANES) if gain_len else (1, ROWS, LANES)
    return pl.pallas_call(
        functools.partial(attn_back_kernel, plan, gain_len),
        out_shape=shapes,
        in_specs=[pl.BlockSpec(memory_space=pltpu.SMEM)] + whole_specs(len(inputs)),
        out_specs=whole_specs(len(shapes)),
        scratch_shapes=[
            pltpu.VMEM((flat_rows, LANES), jnp.float32),
            pltpu.VMEM(tail_shape, jnp.float32),
            pltpu.VMEM((CAP, HQ + 2 * HD), jnp.bfloat16),
            pltpu.VMEM((CAP, HQ), jnp.bfloat16),
        ],
        compiler_params=pltpu.CompilerParams(vmem_limit_bytes=22 << 20),
        cost_estimate=pl.CostEstimate(flops=0, bytes_accessed=0, transcendentals=0),
    )(device, *inputs)


def gathered_blocks(pieces, orders, each, devices, device):
    arrays, plan, start = [], [], 0
    for piece, order in zip(pieces, orders):
        blocks = gather_chunk(piece, order, devices)
        take = min(piece.shape[0], each - start)
        if each % ROWS:
            places = [offset_of(place, list(order) + [0]) for place in range(devices)]
            back = sorted(range(devices), key=places.__getitem__)
            mixed = offset_bits(device[0], list(order) + [0])
            arrays.append(
                jnp.take(jnp.concatenate(blocks), jnp.array(back, jnp.int32) ^ mixed, axis=0)
            )
            continue
        for part, block in enumerate(blocks):
            plan.append((order[:-1], offset_of(part, [order[-1], 0]), take, start, each))
            arrays.append(block)
        start += take
    if each % ROWS == 0:
        return arrays, plan, None
    table = jnp.concatenate(arrays, axis=1)
    flat = table[:, :each].reshape(1, devices * each, LANES)
    return [flat], [([], 0, devices * each, 0, 0)], table[:, each:]


def offset_bits(device, order):
    return sum(((device >> bit) & 1) << k for k, bit in enumerate(order))


def scatter_plan(each, tail_rows, orders, devices):
    parts = cut_rows(each + tail_rows, len(orders))
    half = devices // 2
    if each % ROWS:
        return [(0, [], 0, 0, devices * each, 0, 0)], [(1, devices * each, LANES)], parts
    plan = []
    for with_core in (1, 0):
        for (low, high), order in zip(parts, orders):
            order = order[::-1]
            plan.append((with_core, order, with_core, low, min(high, each) - low, low, each))
            if high > each:
                plan.append((with_core, order, with_core, each, tail_rows, None, each))
    return plan, [(half, each + tail_rows, LANES)] * 2, parts


def blocks_of(found, tails, parts, orders, devices, device):
    if len(found) == 2:
        return found
    table = found[0].reshape(devices, -1, LANES)
    table = table if tails is None else jnp.concatenate([table, tails], axis=1)
    blocks = []
    for with_core in (0, 1):
        chunks = []
        for (low, high), order in zip(parts, orders):
            places = range(devices // 2)
            offsets = [offset_of(place, order[::-1]) ^ with_core for place in places]
            owners = jnp.array(offsets, jnp.int32) ^ device[0]
            chunks.append(jnp.take(table[:, low:high], owners, axis=0))
        blocks.append(jnp.concatenate(chunks, axis=1))
    return blocks


def cores_merged(home, came, parts):
    half = home.shape[0] // 2

    def added(first, low, high):
        at = (slice(first, first + half), slice(low, high))
        return (home[at].astype(jnp.float32) + came[at].astype(jnp.float32)).astype(jnp.bfloat16)

    return [(added(0, low, high), added(half, low, high)) for low, high in parts]


def adam_update(weight_shard, gradient, moment_one, moment_two):
    moment_one = 0.9 * moment_one + 0.1 * gradient
    moment_two = 0.999 * moment_two + 0.001 * gradient * gradient
    fix_one = 1.0 - 0.9**STEP
    fix_two = 1.0 - 0.999**STEP
    weight_shard = weight_shard - 0.02 * (
        moment_one / fix_one / (jnp.sqrt(moment_two / fix_two) + 1e-08) + 0.1 * weight_shard
    )
    return (weight_shard, moment_one, moment_two)


def per_device(hidden_in, cotangent, params, moment_one, moment_two, seq_lengths, seq_owner):
    devices = lax.axis_size("dp")
    device = lax.axis_index("dp").astype(jnp.int32)
    here = device.reshape(1)
    attn_len = G1LEN // devices
    ffn_len = G2LEN // devices
    gain_len = params.shape[0] - attn_len - ffn_len
    attn_rows = attn_len // LANES
    tail_rows = -(-(attn_rows + 1) // ROWS) * ROWS - attn_rows
    pad = tail_rows * LANES - gain_len
    rounded = params.astype(jnp.bfloat16)
    first_piece = jnp.concatenate(
        [rounded[:attn_len], rounded[attn_len + ffn_len :], jnp.zeros((pad,), jnp.bfloat16)]
    ).reshape(-1, LANES)
    second_piece = rounded[attn_len : attn_len + ffn_len].reshape(-1, LANES)
    ffn_rows = ffn_len // LANES
    second_pieces = [second_piece[low:high] for low, high in cut_rows(ffn_rows, 2)]
    orders = bit_orders(devices, ("abxy", "bxya", "byax"))
    arrays, plan, tails = gathered_blocks([first_piece], orders[:1], attn_rows, devices, here)
    ffn_arrays, ffn_plan, unused = gathered_blocks(
        second_pieces, orders[1:], ffn_rows, devices, here
    )
    aligned = attn_rows % ROWS == 0
    qkv_weight, out_weight, *found = unpack_attn(
        plan, tail_rows if aligned else 0, here, arrays, devices
    )
    tails = found[0] if aligned else tails
    gains = tails.reshape(devices, -1)[:, :gain_len].astype(jnp.float32).reshape(1, -1)
    tables = slot_setup(seq_lengths, seq_owner, device)
    attn_out, mid_stream = forward_attn(hidden_in, qkv_weight, out_weight, tables, gains)
    ffn_orders = bit_orders(devices, ("xaby", "yxab", "ayxb"))
    attn_orders = bit_orders(devices, ("xyab", "yxba"))[:2]
    out_plan, block_shapes, ffn_parts = scatter_plan(ffn_rows, 0, ffn_orders, devices)
    staged = [(0, 0, 0)]
    if len(block_shapes) == 2:
        staged = [
            (part // 2, part % 2 * (devices // 4), low)
            for low, _ in cut_rows(ffn_rows, 2)
            for part in range(4)
        ]
    block_out, delta_mid, delta_attn, late_gains, *found = run_ffn(
        ffn_plan,
        staged,
        out_plan,
        block_shapes,
        here,
        mid_stream,
        attn_out,
        cotangent,
        tables,
        gains,
        ffn_arrays,
    )
    ffn_home, ffn_away = blocks_of(found, None, ffn_parts, ffn_orders, devices, here)
    ffn_came = across(ffn_away, 0, devices)
    delta_attn, ffn_came = lax.optimization_barrier((delta_attn, ffn_came))
    ffn_chunks = cores_merged(ffn_home, ffn_came, ffn_parts)
    delta_attn, ffn_chunks = lax.optimization_barrier((delta_attn, ffn_chunks))
    ffn_came = sent_blocks(ffn_chunks, ffn_orders, 0, devices)
    attn_plan, block_shapes, attn_parts = scatter_plan(attn_rows, tail_rows, attn_orders, devices)
    grad_in, gain_grads, *found = back_attn(
        attn_plan,
        gain_len if aligned else 0,
        tail_rows,
        devices,
        block_shapes,
        here,
        delta_attn,
        delta_mid,
        hidden_in,
        tables,
        gains,
        late_gains,
        qkv_weight,
        out_weight,
    )
    gain_table = None
    if not aligned:
        gain_table = gain_grads.reshape(devices, gain_len).astype(jnp.bfloat16)
        gain_table = jnp.pad(gain_table, ((0, 0), (0, pad))).reshape(devices, tail_rows, LANES)
    attn_home, attn_away = blocks_of(found, gain_table, attn_parts, attn_orders, devices, here)
    attn_home, attn_away, ffn_came = lax.optimization_barrier((attn_home, attn_away, ffn_came))
    stages = len(ffn_orders[0])
    ffn_chunks = merged_blocks(ffn_chunks, ffn_came)
    ffn_came = sent_blocks(ffn_chunks, ffn_orders, 1, devices)
    attn_came = across(attn_away, 0, devices)
    ffn_came[0], attn_came = lax.optimization_barrier((ffn_came[0], attn_came))
    attn_chunks = cores_merged(attn_home, attn_came, attn_parts)
    for stage in range(1, stages + 1):
        attn_came = sent_blocks(attn_chunks, attn_orders, stage - 1, devices)
        if stage < stages:
            ffn_chunks = merged_blocks(ffn_chunks, ffn_came)
        if stage + 1 < stages:
            ffn_came = sent_blocks(ffn_chunks, ffn_orders, stage + 1, devices)
            for chunk, arrived in enumerate(attn_came):
                ffn_came[chunk], attn_came[chunk] = lax.optimization_barrier(
                    (ffn_came[chunk], arrived)
                )
        attn_chunks = merged_blocks(attn_chunks, attn_came)
    attn_shard = jnp.concatenate([rows for rows, _ in attn_chunks]).reshape(-1)
    ffn_shard = jnp.concatenate([rows for rows, _ in ffn_chunks])
    grad_shard = jnp.concatenate(
        [attn_shard[:attn_len], ffn_shard.reshape(-1), attn_shard[attn_len : attn_len + gain_len]]
    )
    params_new, moment_one_new, moment_two_new = adam_update(
        params, grad_shard, moment_one, moment_two
    )
    return (block_out, grad_in, grad_shard, params_new, moment_one_new, moment_two_new)


def solution(mesh):
    in_specs = (P("dp", None), P("dp", None), P("dp"), P("dp"), P("dp"), P(), P())
    out_specs = (P("dp", None), P("dp", None), P("dp"), P("dp"), P("dp"), P("dp"))
    return jax.shard_map(
        per_device, mesh=mesh, in_specs=in_specs, out_specs=out_specs, check_vma=False
    )
```

```python
import functools
import math

import jax
import jax.numpy as jnp
from jax import lax
from jax.experimental import pallas as pl
from jax.experimental.pallas import tpu as pltpu
from jax.sharding import PartitionSpec as P

D = 640
FF = 2048
HD = 256
HQ = 1024
CAP = 128
WINDOW = 64
STEP = 3
G1LEN = 1638400
G2LEN = 3932160
LANES = 128
ROWS = 16
GELU_SCALE = math.sqrt(2 / math.pi)


def rms_scale(values, gain_vec):
    return (
        values
        * lax.rsqrt(jnp.mean(values * values, axis=-1, keepdims=True) + 1e-06)
        * (1.0 + gain_vec)
    )


def rotate(values, cos_tab, sin_tab):
    half_dim = values.shape[-1] // 2
    lower_half = values[..., :half_dim]
    upper_half = values[..., half_dim:]
    return jnp.concatenate(
        [lower_half * cos_tab - upper_half * sin_tab, upper_half * cos_tab + lower_half * sin_tab],
        axis=-1,
    )


def gated_gelu(gate_proj, up_proj):
    return jax.nn.gelu(gate_proj, approximate=True) * up_proj


def times_transposed(rows_in, matrix):
    return lax.dot_general(
        rows_in, matrix, (((1,), (1,)), ((), ())), preferred_element_type=jnp.float32
    )


def slot_setup(seq_lengths, seq_owner, device):
    mine_mask = seq_owner == device
    own_lengths = jnp.where(mine_mask, seq_lengths, 0)
    seq_ends = jnp.cumsum(own_lengths, dtype=jnp.int32)
    seq_begins = seq_ends - own_lengths
    slot_index = jnp.arange(CAP, dtype=jnp.int32)
    column = slot_index[:, None]
    inside_mask = (
        mine_mask[None, :] & (seq_begins[None, :] <= column) & (column < seq_ends[None, :])
    )
    live_mask = jnp.any(inside_mask, axis=1)
    seq_label = jnp.sum(
        (mine_mask[None, :] & (seq_ends[None, :] <= column)).astype(jnp.int32),
        axis=1,
        dtype=jnp.int32,
    )
    position = jnp.sum(
        jnp.where(inside_mask, column - seq_begins[None, :], 0), axis=1, dtype=jnp.int32
    )
    row_slot = slot_index[:, None]
    col_slot = slot_index[None, :]
    allowed = live_mask[:, None] & live_mask[None, :] & (
        seq_label[:, None] == seq_label[None, :]
    ) & (col_slot <= row_slot) & (row_slot - col_slot < WINDOW) | (row_slot == col_slot)
    half_dim = HD // 2
    frequency = 10000.0 ** (-2.0 * jnp.arange(half_dim, dtype=jnp.float32) / HD)
    angles = position.astype(jnp.float32)[:, None] * frequency[None, :]
    live_wide = jnp.broadcast_to(live_mask[:, None], (CAP, LANES)).astype(jnp.float32)
    return jnp.concatenate(
        [jnp.cos(angles), jnp.sin(angles), allowed.astype(jnp.float32), live_wide], axis=1
    )


def rms_pull(raw, gain_vec, delta):
    scale = lax.rsqrt(jnp.mean(raw * raw, axis=-1, keepdims=True) + 1e-06)
    weighed = delta * (1.0 + gain_vec)
    shared = jnp.mean(raw * weighed, axis=-1, keepdims=True)
    return scale * weighed - raw * (scale * scale * scale * shared), delta * raw * scale


def rotate_pull(delta, cos_tab, sin_tab):
    half_dim = delta.shape[-1] // 2
    lower_half = delta[:, :half_dim]
    upper_half = delta[:, half_dim:]
    return jnp.concatenate(
        [lower_half * cos_tab + upper_half * sin_tab, upper_half * cos_tab - lower_half * sin_tab],
        axis=-1,
    )


def bit_orders(devices, tuned):
    bits = devices.bit_length() - 1
    if bits == 5:
        return [["cxyab".index(letter) for letter in order] for order in tuned]
    return [[1 + (shift + step) % (bits - 1) for step in range(bits - 1)] for shift in range(3)]


def across(block, bit, devices):
    return lax.ppermute(block, "dp", [(i, i ^ (1 << bit)) for i in range(devices)])


def offset_of(place, order):
    return sum(((place >> k) & 1) << bit for k, bit in enumerate(order))


def gather_chunk(piece, order, devices):
    held = piece[None]
    for bit in order[:-1]:
        held = jnp.concatenate([held, across(held, bit, devices)])
    last = across(held, order[-1], devices)
    return (held, last, across(held, 0, devices), across(last, 0, devices))


def sent_blocks(chunks, orders, stage, devices):
    return [
        across(away, order[stage], devices)
        for (_, away), order in zip(chunks, orders)
    ]


def merged_blocks(chunks, came):
    merged = []
    for (home, _), arrived in zip(chunks, came):
        half = home.shape[0] // 2

        def added(low, high):
            return home[low:high].astype(jnp.float32) + arrived[low:high].astype(jnp.float32)

        if half:
            merged.append(
                (
                    added(0, half).astype(jnp.bfloat16),
                    added(half, 2 * half).astype(jnp.bfloat16),
                )
            )
        else:
            merged.append((added(0, 1)[0], None))
    return merged


def cut_rows(rows, parts):
    each = -(-rows // (parts * ROWS)) * ROWS
    return [(low, min(low + each, rows)) for low in range(0, rows, each)]


def whole_specs(count):
    return [pl.BlockSpec(memory_space=pltpu.VMEM)] * count


def copy_step(rows):
    return max(step for step in range(ROWS, 513, ROWS) if rows % step == 0)


def owner_rows(device, index, order, extra, start, each):
    owner = device ^ extra
    for k, bit in enumerate(order):
        owner = owner ^ (((index >> k) & 1) << bit)
    return owner, pl.multiple_of(owner * each + start, ROWS)


def spread_blocks(plan, views, device, spread, tails):
    for (order, extra, take, start, each), (block_ref, first_index, count, first_row) in zip(
        plan, views
    ):
        step = copy_step(take)

        @pl.loop(0, count)
        def _(
            index,
            order=order,
            extra=extra,
            take=take,
            start=start,
            each=each,
            block_ref=block_ref,
            first_index=first_index,
            first_row=first_row,
            step=step,
        ):
            owner, first = owner_rows(device, index, order, extra, start, each)
            for low in range(0, take, step):
                spread[pl.ds(pl.multiple_of(first + low, ROWS), step), :] = block_ref[
                    first_index + index, first_row + low : first_row + low + step, :
                ].astype(jnp.float32)
            if tails is not None:
                tails[owner] = block_ref[index, take : take + tails.shape[1], :]


def fold_matrices(spread, targets):
    first = 0
    for matrix, offset, rows, columns in targets:
        blocks = columns // LANES

        @pl.loop(0, rows // LANES)
        def _(step, matrix=matrix, offset=offset, blocks=blocks, first=first):
            base = pl.multiple_of(first + step * (LANES * blocks), ROWS)
            at = pl.ds(pl.multiple_of(step * LANES, LANES), LANES)
            for block in range(blocks):
                low = offset + block * LANES
                matrix[at, low : low + LANES] = spread[
                    pl.ds(base + block, LANES, stride=blocks), :
                ].astype(jnp.bfloat16)

        first += rows * blocks


def spread_grads(spread, products):
    first = 0
    for turned, right, columns in products:
        rows = turned.shape[0]
        blocks = columns // LANES
        wide = 2 - blocks % 2
        for block in range(0, blocks, wide):
            product = jnp.dot(
                turned,
                right(block * LANES, (block + wide) * LANES),
                preferred_element_type=jnp.float32,
            )
            for part in range(wide):
                spread[pl.ds(first + block + part, rows, stride=blocks), :] = product[
                    :, part * LANES : (part + 1) * LANES
                ]
        first += rows * blocks


def place_blocks(plan, device, spread, tails, targets):
    for target, order, extra, low, take, start, each in plan:
        target_ref = targets[target]
        step = copy_step(take)

        @pl.loop(0, target_ref.shape[0])
        def _(
            index,
            target_ref=target_ref,
            order=order,
            extra=extra,
            low=low,
            take=take,
            start=start,
            each=each,
            step=step,
        ):
            owner, first = owner_rows(device, index, order, extra, start or 0, each)
            if start is None:
                target_ref[index, low : low + take, :] = tails[owner].astype(jnp.bfloat16)
                return

            @pl.loop(0, take // step)
            def _(part):
                at = pl.multiple_of(part * step, ROWS)
                target_ref[index, pl.ds(pl.multiple_of(low + at, ROWS), step), :] = spread[
                    pl.ds(pl.multiple_of(first + at, ROWS), step), :
                ].astype(jnp.bfloat16)


def attn_forward(hidden_in, qkv_weight, tables, gains):
    cos_tab = tables[:, :LANES]
    sin_tab = tables[:, LANES : 2 * LANES]
    open_pairs = tables[:, 2 * LANES : 3 * LANES] > 0.0
    gain_query = gains[:, D : D + HD]
    gain_key = gains[:, D + HD : D + 2 * HD]
    normed_in = rms_scale(hidden_in[...].astype(jnp.float32), gains[:, :D]).astype(jnp.bfloat16)
    raw = jnp.dot(normed_in, qkv_weight[...], preferred_element_type=jnp.float32)
    key_raw = raw[:, HQ : HQ + HD]
    values = raw[:, HQ + HD :].astype(jnp.bfloat16)
    keys = rotate(rms_scale(key_raw, gain_key), cos_tab, sin_tab).astype(jnp.bfloat16)
    heads = []
    for head in range(HQ // HD):
        query_raw = raw[:, head * HD : (head + 1) * HD]
        rot_query = rotate(rms_scale(query_raw, gain_query), cos_tab, sin_tab) * HD ** (-0.5)
        rot_query = rot_query.astype(jnp.bfloat16)
        scores = jnp.where(open_pairs, times_transposed(rot_query, keys), -1e30)
        row_max = jnp.max(scores, axis=-1, keepdims=True)
        raised = jnp.exp(scores - row_max)
        summed = jnp.sum(raised, axis=-1, keepdims=True)
        context = jnp.dot(
            (raised / summed).astype(jnp.bfloat16), values, preferred_element_type=jnp.float32
        ).astype(jnp.bfloat16)
        heads.append((query_raw, rot_query, scores, row_max + jnp.log(summed), context))
    return normed_in, key_raw, values, keys, heads, cos_tab, sin_tab


def join_gains(tails, gain_len, gains):
    lane = lax.broadcasted_iota(jnp.int32, (1, LANES), 1)
    tiles = [jnp.zeros((1, LANES), jnp.float32) for _ in range(gains.shape[1] // LANES)]
    for owner in range(tails.shape[0]):
        tile, shift = divmod(owner * gain_len, LANES)
        run = jnp.where(lane < gain_len, tails[owner].astype(jnp.float32)[0:1, :], 0.0)
        if shift:
            run = pltpu.roll(run, shift, 1)
        tiles[tile] += jnp.where(lane >= shift, run, 0.0)
        if shift + gain_len > LANES:
            tiles[tile + 1] += jnp.where(lane < shift, run, 0.0)
    for number, tile in enumerate(tiles):
        gains[:, number * LANES : (number + 1) * LANES] = tile


def attn_forward_kernel(plan, gain_len, device_ref, hidden_in, tables, *refs):
    if not gain_len:
        given, refs = refs[0], refs[1:]
    sources = refs[: len(plan)]
    refs = refs[len(plan) :]
    qkv_weight, out_weight, gains, attn_out, mid_stream = refs[:5]
    staging, spread, tails, context, sems = refs[5:]
    copies, views = [], []
    for number, source in enumerate(sources):
        count = source.shape[0]
        held = staging.at[pl.ds(number * count, count)]
        copies.append(pltpu.make_async_copy(source, held, sems.at[number]))
        views.append((held, 0, count, 0))
    for copy in copies:
        copy.start()
    for copy, step, view in zip(copies, plan, views):
        copy.wait()
        spread_blocks([step], [view], device_ref[0], spread, tails if gain_len else None)
    if gain_len:
        join_gains(tails, gain_len, gains)
    else:
        gains[...] = given[...]
    fold_matrices(
        spread,
        (
            (qkv_weight, 0, D, HQ),
            (qkv_weight, HQ, D, HD),
            (qkv_weight, HQ + HD, D, HD),
            (out_weight, 0, HQ, D),
        ),
    )
    heads = attn_forward(hidden_in, qkv_weight, tables, gains)[4]
    for head, parts in enumerate(heads):
        context[:, head * HD : (head + 1) * HD] = parts[-1]
    out = jnp.dot(context[...], out_weight[...], preferred_element_type=jnp.float32)
    attn_out[...] = out
    gain_post = gains[:, D + 2 * HD : 2 * D + 2 * HD]
    mid_stream[...] = hidden_in[...].astype(jnp.float32) + rms_scale(out, gain_post)


def forward_attn(plan, gain_len, tail_rows, devices, device, hidden_in, tables, given, arrays):
    shapes = [
        jax.ShapeDtypeStruct((D, HQ + 2 * HD), jnp.bfloat16),
        jax.ShapeDtypeStruct((HQ, D), jnp.bfloat16),
        jax.ShapeDtypeStruct((1, 4 * D + 2 * HD), jnp.float32),
        jax.ShapeDtypeStruct((CAP, D), jnp.float32),
        jax.ShapeDtypeStruct((CAP, D), jnp.float32),
    ]
    given = [] if gain_len else [given]
    held = (sum(array.shape[0] for array in arrays),) + arrays[0].shape[1:]
    return pl.pallas_call(
        functools.partial(attn_forward_kernel, plan, gain_len),
        out_shape=shapes,
        in_specs=[pl.BlockSpec(memory_space=pltpu.SMEM)]
        + whole_specs(2 + len(given))
        + [pl.BlockSpec(memory_space=pltpu.HBM)] * len(arrays),
        out_specs=whole_specs(len(shapes)),
        scratch_shapes=[
            pltpu.VMEM(held, jnp.bfloat16),
            pltpu.VMEM((G1LEN // LANES, LANES), jnp.float32),
            pltpu.VMEM((devices, tail_rows, LANES) if gain_len else (1, ROWS, LANES), jnp.bfloat16),
            pltpu.VMEM((CAP, HQ), jnp.bfloat16),
            pltpu.SemaphoreType.DMA((len(arrays),)),
        ],
        compiler_params=pltpu.CompilerParams(vmem_limit_bytes=24 << 20),
        cost_estimate=pl.CostEstimate(flops=0, bytes_accessed=0, transcendentals=0),
    )(device, hidden_in, tables, *given, *arrays)


def ffn_kernel(
    plan_in,
    staged,
    plan_out,
    device_ref,
    mid_ref,
    attn_out,
    cotangent,
    tables,
    gains,
    *refs,
):
    sources = refs[: len(plan_in)]
    refs = refs[len(plan_in) :]
    block_out, delta_mid_ref, delta_attn_ref, late_gains = refs[:4]
    targets = refs[4:-10]
    spread, gate_weight, up_weight, down_weight = refs[-10:-6]
    gates, ups, hidden, delta_gate, delta_up, sems = refs[-6:]
    device = device_ref[0]
    copies, views = [], []
    for source, (target, first_index, first_row) in zip(sources, staged):
        count, rows = source.shape[:2]
        held = targets[target]
        copies.append(
            pltpu.make_async_copy(
                source,
                held.at[pl.ds(first_index, count), pl.ds(first_row, rows), :],
                sems.at[len(copies)],
            )
        )
        views.append((held, first_index, count, first_row))
    for copy in copies:
        copy.start()
    mid_stream = mid_ref[...]
    gain_post = gains[:, D + 2 * HD : 2 * D + 2 * HD]
    gain_mid = gains[:, 2 * D + 2 * HD : 3 * D + 2 * HD]
    gain_last = gains[:, 3 * D + 2 * HD :]
    normed_mid = rms_scale(mid_stream, gain_mid).astype(jnp.bfloat16)
    for copy, plan, view in zip(copies, plan_in, views):
        copy.wait()
        spread_blocks([plan], [view], device, spread, None)
    fold_matrices(
        spread, ((gate_weight, 0, D, FF), (up_weight, 0, D, FF), (down_weight, 0, FF, D))
    )
    parts = [slice(low, low + 512) for low in range(0, FF, 512)]
    for at in parts:
        gate = jnp.dot(normed_mid, gate_weight[:, at], preferred_element_type=jnp.float32)
        up = jnp.dot(normed_mid, up_weight[:, at], preferred_element_type=jnp.float32)
        gates[:, at] = gate
        ups[:, at] = up
        hidden[:, at] = gated_gelu(gate, up).astype(jnp.bfloat16)
    ffn_out = jnp.dot(hidden[...], down_weight[...], preferred_element_type=jnp.float32)
    block_out[...] = (mid_stream + rms_scale(ffn_out, gain_last)).astype(jnp.bfloat16)
    delta_out = cotangent[...].astype(jnp.float32) * tables[:, 3 * LANES : 3 * LANES + 1]
    delta_ffn, gain_rows = rms_pull(ffn_out, gain_last, delta_out)
    late_gains[2:3, :] = jnp.sum(gain_rows, axis=0, keepdims=True)
    delta_ffn = delta_ffn.astype(jnp.bfloat16)
    delta_normed = jnp.zeros((CAP, D), jnp.float32)
    for at in parts:
        delta_hidden = times_transposed(delta_ffn, down_weight[at, :])
        gate = gates[:, at]
        raised = jnp.tanh(GELU_SCALE * (gate + 0.044715 * (gate * gate * gate)))
        share = 0.5 * (1.0 + raised)
        slope = share + (0.5 * GELU_SCALE) * gate * (1.0 - raised * raised) * (
            1.0 + (3 * 0.044715) * (gate * gate)
        )
        delta_gate[:, at] = (delta_hidden * ups[:, at] * slope).astype(jnp.bfloat16)
        delta_up[:, at] = (delta_hidden * (gate * share)).astype(jnp.bfloat16)
        delta_normed += times_transposed(delta_gate[:, at], gate_weight[:, at])
        delta_normed += times_transposed(delta_up[:, at], up_weight[:, at])
    delta_part, gain_rows = rms_pull(mid_stream, gain_mid, delta_normed)
    late_gains[1:2, :] = jnp.sum(gain_rows, axis=0, keepdims=True)
    delta_mid = delta_out + delta_part
    delta_mid_ref[...] = delta_mid
    delta_attn, gain_rows = rms_pull(attn_out[...], gain_post, delta_mid)
    late_gains[0:1, :] = jnp.sum(gain_rows, axis=0, keepdims=True)
    delta_attn_ref[...] = delta_attn.astype(jnp.bfloat16)
    turned = normed_mid.T
    spread_grads(
        spread,
        (
            (turned, lambda low, high: delta_gate[:, low:high], FF),
            (turned, lambda low, high: delta_up[:, low:high], FF),
            (hidden[...].T, lambda low, high: delta_ffn[:, low:high], D),
        ),
    )
    place_blocks(plan_out, device, spread, None, targets)


def run_ffn(
    plan_in, staged, plan_out, block_shapes, device, mid, attn_out, cotangent, tables, gains, arrays
):
    flat_rows = G2LEN // LANES
    shapes = [
        jax.ShapeDtypeStruct((CAP, D), jnp.bfloat16),
        jax.ShapeDtypeStruct((CAP, D), jnp.float32),
        jax.ShapeDtypeStruct((CAP, D), jnp.bfloat16),
        jax.ShapeDtypeStruct((3, D), jnp.float32),
    ] + [jax.ShapeDtypeStruct(shape, jnp.bfloat16) for shape in block_shapes]
    wide = pltpu.VMEM((CAP, FF), jnp.float32)
    narrow = pltpu.VMEM((CAP, FF), jnp.bfloat16)
    return pl.pallas_call(
        functools.partial(ffn_kernel, plan_in, staged, plan_out),
        out_shape=shapes,
        in_specs=[pl.BlockSpec(memory_space=pltpu.SMEM)]
        + whole_specs(5)
        + [pl.BlockSpec(memory_space=pltpu.HBM)] * len(arrays),
        out_specs=whole_specs(len(shapes)),
        scratch_shapes=[
            pltpu.VMEM((flat_rows, LANES), jnp.float32),
            pltpu.VMEM((D, FF), jnp.bfloat16),
            pltpu.VMEM((D, FF), jnp.bfloat16),
            pltpu.VMEM((FF, D), jnp.bfloat16),
            wide,
            wide,
            narrow,
            narrow,
            narrow,
            pltpu.SemaphoreType.DMA((len(arrays),)),
        ],
        compiler_params=pltpu.CompilerParams(vmem_limit_bytes=44 << 20),
        cost_estimate=pl.CostEstimate(flops=0, bytes_accessed=0, transcendentals=0),
    )(device, mid, attn_out, cotangent, tables, gains, *arrays)


def attn_back_kernel(
    plan,
    gain_len,
    device_ref,
    delta_attn,
    delta_mid,
    hidden_in,
    tables,
    gains,
    late_gains,
    qkv_weight,
    out_weight,
    grad_in,
    gain_grads,
    *refs,
):
    targets = refs[:-4]
    spread, tails, delta_raws, contexts = refs[-4:]
    device = device_ref[0]
    normed_in, key_raw, values, keys, heads, cos_tab, sin_tab = attn_forward(
        hidden_in, qkv_weight, tables, gains
    )
    gain_query = gains[:, D : D + HD]
    gain_key = gains[:, D + HD : D + 2 * HD]
    delta_context = times_transposed(delta_attn[...], out_weight[...]).astype(jnp.bfloat16)
    delta_key = jnp.zeros((CAP, HD), jnp.float32)
    delta_value = jnp.zeros((CAP, HD), jnp.float32)
    query_gain_rows = jnp.zeros((CAP, HD), jnp.float32)
    for head, (query_raw, queries, scores, log_total, context) in enumerate(heads):
        at = slice(head * HD, (head + 1) * HD)
        contexts[:, at] = context
        head_delta = delta_context[:, at]
        row_dot = jnp.sum(
            head_delta.astype(jnp.float32) * context.astype(jnp.float32), axis=-1, keepdims=True
        )
        prob_exact = jnp.exp(scores - log_total)
        delta_prob = times_transposed(head_delta, values)
        delta_score = prob_exact * (delta_prob - row_dot)
        turned = delta_score.T.astype(jnp.bfloat16)
        delta_score = delta_score.astype(jnp.bfloat16)
        delta_query = jnp.dot(delta_score, keys, preferred_element_type=jnp.float32)
        delta_key += jnp.dot(turned, queries, preferred_element_type=jnp.float32)
        delta_value += jnp.dot(
            prob_exact.T.astype(jnp.bfloat16), head_delta, preferred_element_type=jnp.float32
        )
        delta_rot = rotate_pull(delta_query * HD ** (-0.5), cos_tab, sin_tab)
        delta_raw, gain_rows = rms_pull(query_raw, gain_query, delta_rot)
        query_gain_rows += gain_rows
        delta_raws[:, at] = delta_raw.astype(jnp.bfloat16)
    delta_raw, gain_rows = rms_pull(key_raw, gain_key, rotate_pull(delta_key, cos_tab, sin_tab))
    delta_raws[:, HQ : HQ + HD] = delta_raw.astype(jnp.bfloat16)
    delta_raws[:, HQ + HD :] = delta_value.astype(jnp.bfloat16)
    gain_grads[:, D : D + HD] = jnp.sum(query_gain_rows, axis=0, keepdims=True)
    gain_grads[:, D + HD : D + 2 * HD] = jnp.sum(gain_rows, axis=0, keepdims=True)
    delta_in = times_transposed(delta_raws[...], qkv_weight[...])
    delta_part, gain_rows = rms_pull(
        hidden_in[...].astype(jnp.float32), gains[:, :D], delta_in
    )
    grad_in[...] = delta_mid[...] + delta_part
    gain_grads[:, :D] = jnp.sum(gain_rows, axis=0, keepdims=True)
    for late in range(3):
        at = slice((late + 1) * D + 2 * HD, (late + 2) * D + 2 * HD)
        gain_grads[:, at] = late_gains[late : late + 1, :]
    if gain_len:
        tails[...] = jnp.zeros_like(tails)
        lane = lax.broadcasted_iota(jnp.int32, (1, LANES), 1)
        for owner in range(tails.shape[0]):
            row, shift = divmod(owner * gain_len, LANES)
            piece = gain_grads[:, row * LANES : (row + 1) * LANES]
            if shift:
                piece = pltpu.roll(piece, LANES - shift, 1)
            if shift + gain_len > LANES:
                after = gain_grads[:, (row + 1) * LANES : (row + 2) * LANES]
                after = pltpu.roll(after, LANES - shift, 1)
                piece = jnp.where(lane < LANES - shift, piece, after)
            tails[owner, 0:1, :] = jnp.where(lane < gain_len, piece, 0.0)
    turned = normed_in.T
    delta_attn_value = delta_attn[...]
    spread_grads(
        spread,
        (
            (turned, lambda low, high: delta_raws[:, low:high], HQ),
            (turned, lambda low, high: delta_raws[:, HQ + low : HQ + high], HD),
            (turned, lambda low, high: delta_raws[:, HQ + HD + low : HQ + HD + high], HD),
            (contexts[...].T, lambda low, high: delta_attn_value[:, low:high], D),
        ),
    )
    place_blocks(plan, device, spread, tails, targets)


def back_attn(plan, gain_len, tail_rows, devices, block_shapes, device, *inputs):
    flat_rows = G1LEN // LANES
    shapes = [
        jax.ShapeDtypeStruct((CAP, D), jnp.float32),
        jax.ShapeDtypeStruct((1, 4 * D + 2 * HD), jnp.float32),
    ] + [jax.ShapeDtypeStruct(shape, jnp.bfloat16) for shape in block_shapes]
    tail_shape = (devices, tail_rows, LANES) if gain_len else (1, ROWS, LANES)
    return pl.pallas_call(
        functools.partial(attn_back_kernel, plan, gain_len),
        out_shape=shapes,
        in_specs=[pl.BlockSpec(memory_space=pltpu.SMEM)] + whole_specs(len(inputs)),
        out_specs=whole_specs(len(shapes)),
        scratch_shapes=[
            pltpu.VMEM((flat_rows, LANES), jnp.float32),
            pltpu.VMEM(tail_shape, jnp.float32),
            pltpu.VMEM((CAP, HQ + 2 * HD), jnp.bfloat16),
            pltpu.VMEM((CAP, HQ), jnp.bfloat16),
        ],
        compiler_params=pltpu.CompilerParams(vmem_limit_bytes=22 << 20),
        cost_estimate=pl.CostEstimate(flops=0, bytes_accessed=0, transcendentals=0),
    )(device, *inputs)


def gathered_blocks(pieces, orders, each, devices, device):
    arrays, plan, start = [], [], 0
    for piece, order in zip(pieces, orders):
        blocks = gather_chunk(piece, order, devices)
        take = min(piece.shape[0], each - start)
        if each % ROWS:
            places = [offset_of(place, list(order) + [0]) for place in range(devices)]
            back = sorted(range(devices), key=places.__getitem__)
            mixed = offset_bits(device[0], list(order) + [0])
            arrays.append(
                jnp.take(jnp.concatenate(blocks), jnp.array(back, jnp.int32) ^ mixed, axis=0)
            )
            continue
        for part, block in enumerate(blocks):
            plan.append((order[:-1], offset_of(part, [order[-1], 0]), take, start, each))
            arrays.append(block)
        start += take
    if each % ROWS == 0:
        return arrays, plan, None
    table = jnp.concatenate(arrays, axis=1)
    flat = table[:, :each].reshape(1, devices * each, LANES)
    return [flat], [([], 0, devices * each, 0, 0)], table[:, each:]


def offset_bits(device, order):
    return sum(((device >> bit) & 1) << k for k, bit in enumerate(order))


def scatter_plan(each, tail_rows, orders, devices):
    parts = cut_rows(each + tail_rows, len(orders))
    half = devices // 2
    if each % ROWS:
        return [(0, [], 0, 0, devices * each, 0, 0)], [(1, devices * each, LANES)], parts
    plan = []
    for with_core in (1, 0):
        for (low, high), order in zip(parts, orders):
            order = order[::-1]
            plan.append((with_core, order, with_core, low, min(high, each) - low, low, each))
            if high > each:
                plan.append((with_core, order, with_core, each, tail_rows, None, each))
    return plan, [(half, each + tail_rows, LANES)] * 2, parts


def blocks_of(found, tails, parts, orders, devices, device):
    if len(found) == 2:
        return found
    table = found[0].reshape(devices, -1, LANES)
    table = table if tails is None else jnp.concatenate([table, tails], axis=1)
    blocks = []
    for with_core in (0, 1):
        chunks = []
        for (low, high), order in zip(parts, orders):
            places = range(devices // 2)
            offsets = [offset_of(place, order[::-1]) ^ with_core for place in places]
            owners = jnp.array(offsets, jnp.int32) ^ device[0]
            chunks.append(jnp.take(table[:, low:high], owners, axis=0))
        blocks.append(jnp.concatenate(chunks, axis=1))
    return blocks


def merge_kernel(parts, *refs):
    pairs = ((refs[0], refs[1]), (refs[2], refs[3]))
    targets = refs[4:]
    half = refs[0].shape[0] // 2
    for number, target in enumerate(targets):
        chunk, second = divmod(number, 2)

        @pl.loop(0, half)
        def _(index, target=target, chunk=chunk, first=second * half):
            at = 0
            for (home, came), (low, high) in zip(pairs, parts[chunk]):
                total = home[first + index, low:high, :].astype(jnp.float32)
                total += came[first + index, low:high, :].astype(jnp.float32)
                target[index, at : at + high - low, :] = total.astype(jnp.bfloat16)
                at += high - low


def cores_merged(parts, *blocks):
    half = blocks[0].shape[0] // 2
    if any((high - low) % ROWS for chunk in parts for low, high in chunk):
        pairs = (blocks[:2], blocks[2:])
        joined = []
        for chunk in parts:
            sums = [
                home[:, low:high].astype(jnp.float32) + came[:, low:high].astype(jnp.float32)
                for (home, came), (low, high) in zip(pairs, chunk)
            ]
            total = jnp.concatenate(sums, axis=1).astype(jnp.bfloat16)
            joined.append((total[:half], total[half:]))
        return joined
    shapes = [
        jax.ShapeDtypeStruct((half, sum(high - low for low, high in chunk), LANES), jnp.bfloat16)
        for chunk in parts
        for _ in range(2)
    ]
    found = pl.pallas_call(
        functools.partial(merge_kernel, parts),
        out_shape=shapes,
        in_specs=whole_specs(4),
        out_specs=whole_specs(len(shapes)),
        compiler_params=pltpu.CompilerParams(vmem_limit_bytes=20 << 20),
        cost_estimate=pl.CostEstimate(flops=0, bytes_accessed=0, transcendentals=0),
    )(*blocks)
    return list(zip(found[::2], found[1::2]))


def adam_update(weight_shard, gradient, moment_one, moment_two):
    moment_one = 0.9 * moment_one + 0.1 * gradient
    moment_two = 0.999 * moment_two + 0.001 * gradient * gradient
    fix_one = 1.0 - 0.9**STEP
    fix_two = 1.0 - 0.999**STEP
    weight_shard = weight_shard - 0.02 * (
        moment_one / fix_one / (jnp.sqrt(moment_two / fix_two) + 1e-08) + 0.1 * weight_shard
    )
    return (weight_shard, moment_one, moment_two)


def per_device(hidden_in, cotangent, params, moment_one, moment_two, seq_lengths, seq_owner):
    devices = lax.axis_size("dp")
    device = lax.axis_index("dp").astype(jnp.int32)
    here = device.reshape(1)
    attn_len = G1LEN // devices
    ffn_len = G2LEN // devices
    gain_len = params.shape[0] - attn_len - ffn_len
    attn_rows = attn_len // LANES
    tail_rows = -(-(attn_rows + 1) // ROWS) * ROWS - attn_rows
    pad = tail_rows * LANES - gain_len
    rounded = params.astype(jnp.bfloat16)
    first_piece = jnp.concatenate(
        [rounded[:attn_len], rounded[attn_len + ffn_len :], jnp.zeros((pad,), jnp.bfloat16)]
    ).reshape(-1, LANES)
    second_piece = rounded[attn_len : attn_len + ffn_len].reshape(-1, LANES)
    ffn_rows = ffn_len // LANES
    second_pieces = [second_piece[low:high] for low, high in cut_rows(ffn_rows, 2)]
    orders = bit_orders(devices, ("abxy", "bxya", "byax"))
    arrays, plan, tails = gathered_blocks([first_piece], orders[:1], attn_rows, devices, here)
    ffn_arrays, ffn_plan, unused = gathered_blocks(
        second_pieces, orders[1:], ffn_rows, devices, here
    )
    aligned = attn_rows % ROWS == 0
    tables = slot_setup(seq_lengths, seq_owner, device)
    given = None
    if not aligned:
        given = tails.reshape(devices, -1)[:, :gain_len].astype(jnp.float32).reshape(1, -1)
    qkv_weight, out_weight, gains, attn_out, mid_stream = forward_attn(
        plan,
        gain_len if aligned else 0,
        tail_rows,
        devices,
        here,
        hidden_in,
        tables,
        given,
        arrays,
    )
    orders = bit_orders(devices, ("yxba", "ayxb", "xayb"))
    out_plan, block_shapes, ffn_parts = scatter_plan(ffn_rows, 0, orders, devices)
    staged = [(0, 0, 0)]
    if len(block_shapes) == 2:
        staged = [
            (part // 2, part % 2 * (devices // 4), low)
            for low, _ in cut_rows(ffn_rows, 2)
            for part in range(4)
        ]
    block_out, delta_mid, delta_attn, late_gains, *found = run_ffn(
        ffn_plan,
        staged,
        out_plan,
        block_shapes,
        here,
        mid_stream,
        attn_out,
        cotangent,
        tables,
        gains,
        ffn_arrays,
    )
    ffn_home, ffn_away = blocks_of(found, None, ffn_parts, orders, devices, here)
    ffn_came = across(ffn_away, 0, devices)
    attn_plan, block_shapes, attn_parts = scatter_plan(attn_rows, tail_rows, orders, devices)
    grad_in, gain_grads, *found = back_attn(
        attn_plan,
        gain_len if aligned else 0,
        tail_rows,
        devices,
        block_shapes,
        here,
        delta_attn,
        delta_mid,
        hidden_in,
        tables,
        gains,
        late_gains,
        qkv_weight,
        out_weight,
    )
    gain_table = None
    if not aligned:
        gain_table = gain_grads.reshape(devices, gain_len).astype(jnp.bfloat16)
        gain_table = jnp.pad(gain_table, ((0, 0), (0, pad))).reshape(devices, tail_rows, LANES)
    attn_home, attn_away = blocks_of(found, gain_table, attn_parts, orders, devices, here)
    attn_came = across(attn_away, 0, devices)
    parts = [
        [cut[chunk] for cut in (ffn_parts, attn_parts) if chunk < len(cut)]
        for chunk in range(len(ffn_parts))
    ]
    chunks = cores_merged(parts, ffn_home, ffn_came, attn_home, attn_came)
    for stage in range(len(orders[0])):
        chunks = merged_blocks(chunks, sent_blocks(chunks, orders, stage, devices))
    rows = [chunk for chunk, _ in chunks]
    ffn_take = [high - low for low, high in ffn_parts]
    ffn_shard = [chunk[:take].reshape(-1) for chunk, take in zip(rows, ffn_take)]
    attn_shard = jnp.concatenate([chunk[take:].reshape(-1) for chunk, take in zip(rows, ffn_take)])
    grad_shard = jnp.concatenate(
        [attn_shard[:attn_len], *ffn_shard, attn_shard[attn_len : attn_len + gain_len]]
    )
    params_new, moment_one_new, moment_two_new = adam_update(
        params, grad_shard, moment_one, moment_two
    )
    return (block_out, grad_in, grad_shard, params_new, moment_one_new, moment_two_new)


def solution(mesh):
    in_specs = (P("dp", None), P("dp", None), P("dp"), P("dp"), P("dp"), P(), P())
    out_specs = (P("dp", None), P("dp", None), P("dp"), P("dp"), P("dp"), P("dp"))
    return jax.shard_map(
        per_device, mesh=mesh, in_specs=in_specs, out_specs=out_specs, check_vma=False
    )
```

```python
import functools
import math

import jax
import jax.numpy as jnp
from jax import lax
from jax.experimental import pallas as pl
from jax.experimental.pallas import tpu as pltpu
from jax.sharding import PartitionSpec as P

D = 640
FF = 2048
HD = 256
HQ = 1024
CAP = 128
WINDOW = 64
STEP = 3
G1LEN = 1638400
G2LEN = 3932160
LANES = 128
ROWS = 16
GELU_SCALE = math.sqrt(2 / math.pi)
ATTN_PADDED, FFN_PADDED = 0, 2 * D


def rms_scale(values, gain_vec):
    return (
        values
        * lax.rsqrt(jnp.mean(values * values, axis=-1, keepdims=True) + 1e-06)
        * (1.0 + gain_vec)
    )


def rotate(values, cos_tab, sin_tab):
    half_dim = values.shape[-1] // 2
    lower_half = values[..., :half_dim]
    upper_half = values[..., half_dim:]
    return jnp.concatenate(
        [lower_half * cos_tab - upper_half * sin_tab, upper_half * cos_tab + lower_half * sin_tab],
        axis=-1,
    )


def gated_gelu(gate_proj, up_proj):
    return jax.nn.gelu(gate_proj, approximate=True) * up_proj


def times_transposed(rows_in, matrix):
    return lax.dot_general(
        rows_in, matrix, (((1,), (1,)), ((), ())), preferred_element_type=jnp.float32
    )


def slot_setup(seq_lengths, seq_owner, device):
    mine_mask = seq_owner == device
    own_lengths = jnp.where(mine_mask, seq_lengths, 0)
    seq_ends = jnp.cumsum(own_lengths, dtype=jnp.int32)
    seq_begins = seq_ends - own_lengths
    slot_index = jnp.arange(CAP, dtype=jnp.int32)
    column = slot_index[:, None]
    inside_mask = (
        mine_mask[None, :] & (seq_begins[None, :] <= column) & (column < seq_ends[None, :])
    )
    live_mask = jnp.any(inside_mask, axis=1)
    seq_label = jnp.sum(
        (mine_mask[None, :] & (seq_ends[None, :] <= column)).astype(jnp.int32),
        axis=1,
        dtype=jnp.int32,
    )
    position = jnp.sum(
        jnp.where(inside_mask, column - seq_begins[None, :], 0), axis=1, dtype=jnp.int32
    )
    row_slot = slot_index[:, None]
    col_slot = slot_index[None, :]
    allowed = live_mask[:, None] & live_mask[None, :] & (
        seq_label[:, None] == seq_label[None, :]
    ) & (col_slot <= row_slot) & (row_slot - col_slot < WINDOW) | (row_slot == col_slot)
    half_dim = HD // 2
    frequency = 10000.0 ** (-2.0 * jnp.arange(half_dim, dtype=jnp.float32) / HD)
    angles = position.astype(jnp.float32)[:, None] * frequency[None, :]
    live_wide = jnp.broadcast_to(live_mask[:, None], (CAP, LANES)).astype(jnp.float32)
    return jnp.concatenate(
        [jnp.cos(angles), jnp.sin(angles), allowed.astype(jnp.float32), live_wide], axis=1
    )


def rms_pull(raw, gain_vec, delta):
    scale = lax.rsqrt(jnp.mean(raw * raw, axis=-1, keepdims=True) + 1e-06)
    weighed = delta * (1.0 + gain_vec)
    shared = jnp.mean(raw * weighed, axis=-1, keepdims=True)
    return scale * weighed - raw * (scale * scale * scale * shared), delta * raw * scale


def rotate_pull(delta, cos_tab, sin_tab):
    half_dim = delta.shape[-1] // 2
    lower_half = delta[:, :half_dim]
    upper_half = delta[:, half_dim:]
    return jnp.concatenate(
        [lower_half * cos_tab + upper_half * sin_tab, upper_half * cos_tab - lower_half * sin_tab],
        axis=-1,
    )


def bit_orders(devices, tuned):
    bits = devices.bit_length() - 1
    if bits == 5:
        return [["cxyab".index(letter) for letter in order] for order in tuned]
    return [[1 + (shift + step) % (bits - 1) for step in range(bits - 1)] for shift in range(3)]


def across(block, bit, devices):
    return lax.ppermute(block, "dp", [(i, i ^ (1 << bit)) for i in range(devices)])


def offset_of(place, order):
    return sum(((place >> k) & 1) << bit for k, bit in enumerate(order))


def gather_chunks(pieces, orders, devices):
    held = [piece[None] for piece in pieces]
    for stage in range(len(orders[0]) - 1):
        came = [across(block, order[stage], devices) for block, order in zip(held, orders)]
        for chunk in range(1, len(came)):
            came[chunk] = lax.optimization_barrier((came[chunk], came[0]))[0]
        held = [jnp.concatenate(pair) for pair in zip(held, came)]
    last = [across(block, order[-1], devices) for block, order in zip(held, orders)]
    chunks = []
    for block, final in zip(held, last):
        if chunks:
            final = lax.optimization_barrier((final, chunks[0][-1]))[0]
        beside = across(block, 0, devices)
        final = lax.optimization_barrier((final, beside))[0]
        chunks.append((block, final, beside, across(final, 0, devices)))
    return chunks


def sent_blocks(chunks, orders, stage, devices):
    return [
        across(away, order[stage], devices)
        for (_, away), order in zip(chunks, orders)
    ]


def merged_blocks(chunks, came):
    merged = []
    for (home, _), arrived in zip(chunks, came):
        half = home.shape[0] // 2

        def added(low, high):
            return home[low:high].astype(jnp.float32) + arrived[low:high].astype(jnp.float32)

        if half:
            merged.append(
                (
                    added(0, half).astype(jnp.bfloat16),
                    added(half, 2 * half).astype(jnp.bfloat16),
                )
            )
        else:
            merged.append((added(0, 1)[0], None))
    return merged


def cut_rows(rows, parts):
    each = -(-rows // (parts * ROWS)) * ROWS
    return [(low, min(low + each, rows)) for low in range(0, rows, each)]


def whole_specs(count):
    return [pl.BlockSpec(memory_space=pltpu.VMEM)] * count


def owner_rows(device, index, order, extra, start, each):
    owner = device ^ extra
    for k, bit in enumerate(order):
        owner = owner ^ (((index >> k) & 1) << bit)
    return owner, owner * each + start


def copy_step(rows):
    return max(step for step in range(ROWS, 513, ROWS) if rows % step == 0)


def each_piece(padded, first, take, visit):
    def visit_plain(shift):
        step = copy_step(take)

        def visit_step(part):
            at = part * step
            visit(at, step, pl.multiple_of(first + shift + at, ROWS))

        if take == step:
            visit_step(0)
        else:
            pl.loop(0, take // step)(visit_step)

    if not padded:
        visit_plain(0)
        return
    units = take // ROWS
    inner = max(count for count in range(1, 41) if units % count == 0)
    number = first // ROWS

    def visit_units(row_of):
        def visit_some(step):
            for part in range(inner):
                at = (step * inner + part) * ROWS
                visit(at, ROWS, row_of(step * inner + part))

        if units == inner:
            visit_some(0)
        else:
            pl.loop(0, units // inner)(visit_some)

    longer = (ROWS + 1) * number
    pl.when(number + units <= padded)(lambda: visit_units(lambda k: longer + (ROWS + 1) * k))
    pl.when(number >= padded)(lambda: visit_plain(padded))
    pl.when((number < padded) & (number + units > padded))(
        lambda: visit_units(lambda k: ROWS * (number + k) + jnp.minimum(number + k, padded))
    )


def spread_blocks(padded, plan, views, device, spread, tails):
    for (order, extra, take, start, each), (block_ref, first_index, count, first_row) in zip(
        plan, views
    ):

        @pl.loop(0, count)
        def _(
            index,
            order=order,
            extra=extra,
            take=take,
            start=start,
            each=each,
            block_ref=block_ref,
            first_index=first_index,
            first_row=first_row,
        ):
            owner, first = owner_rows(device, index, order, extra, start, each)

            def spread_unit(at, unit, row):
                low = first_row + at
                if not isinstance(low, int):
                    low = pl.multiple_of(low, ROWS)
                spread[pl.ds(row, unit), :] = block_ref[
                    first_index + index, pl.ds(low, unit), :
                ].astype(jnp.float32)

            each_piece(padded, first, take, spread_unit)
            if tails is not None:
                tails[owner] = block_ref[index, take : take + tails.shape[1], :]


def pitch_of(columns):
    blocks = columns // LANES
    return blocks + (blocks == ROWS)


def fold_matrices(spread, targets):
    first = 0
    for matrix, offset, rows, columns in targets:
        blocks = columns // LANES
        pitch = pitch_of(columns)

        @pl.loop(0, rows // LANES)
        def _(step, matrix=matrix, offset=offset, blocks=blocks, pitch=pitch, first=first):
            base = first + step * (LANES * pitch)
            at = pl.ds(pl.multiple_of(step * LANES, LANES), LANES)
            for block in range(blocks):
                low = offset + block * LANES
                matrix[at, low : low + LANES] = spread[
                    pl.ds(base + block, LANES, stride=pitch), :
                ].astype(jnp.bfloat16)

        first += rows * pitch


def spread_grads(spread, products):
    first = 0
    for turned, right, columns in products:
        rows = turned.shape[0]
        blocks = columns // LANES
        pitch = pitch_of(columns)
        wide = 2 - blocks % 2
        for block in range(0, blocks, wide):
            product = jnp.dot(
                turned,
                right(block * LANES, (block + wide) * LANES),
                preferred_element_type=jnp.float32,
            )
            for part in range(wide):
                spread[pl.ds(first + block + part, rows, stride=pitch), :] = product[
                    :, part * LANES : (part + 1) * LANES
                ]
        first += rows * pitch


def place_blocks(padded, plan, device, spread, tails, targets):
    for target, order, extra, low, take, start, each in plan:
        target_ref = targets[target]

        @pl.loop(0, target_ref.shape[0])
        def _(
            index,
            target_ref=target_ref,
            order=order,
            extra=extra,
            low=low,
            take=take,
            start=start,
            each=each,
        ):
            owner, first = owner_rows(device, index, order, extra, start or 0, each)
            if start is None:
                target_ref[index, low : low + take, :] = tails[owner].astype(jnp.bfloat16)
                return

            def place_unit(at, unit, row):
                at = low + at
                if not isinstance(at, int):
                    at = pl.multiple_of(at, ROWS)
                target_ref[index, pl.ds(at, unit), :] = spread[pl.ds(row, unit), :].astype(
                    jnp.bfloat16
                )

            each_piece(padded, first, take, place_unit)


def attn_forward(hidden_in, qkv_weight, tables, gains):
    cos_tab = tables[:, :LANES]
    sin_tab = tables[:, LANES : 2 * LANES]
    open_pairs = tables[:, 2 * LANES : 3 * LANES] > 0.0
    gain_query = gains[:, D : D + HD]
    gain_key = gains[:, D + HD : D + 2 * HD]
    normed_in = rms_scale(hidden_in[...].astype(jnp.float32), gains[:, :D]).astype(jnp.bfloat16)
    raw = jnp.dot(normed_in, qkv_weight[...], preferred_element_type=jnp.float32)
    key_raw = raw[:, HQ : HQ + HD]
    values = raw[:, HQ + HD :].astype(jnp.bfloat16)
    keys = rotate(rms_scale(key_raw, gain_key), cos_tab, sin_tab).astype(jnp.bfloat16)
    heads = []
    for head in range(HQ // HD):
        query_raw = raw[:, head * HD : (head + 1) * HD]
        rot_query = rotate(rms_scale(query_raw, gain_query), cos_tab, sin_tab) * HD ** (-0.5)
        rot_query = rot_query.astype(jnp.bfloat16)
        scores = jnp.where(open_pairs, times_transposed(rot_query, keys), -1e30)
        row_max = jnp.max(scores, axis=-1, keepdims=True)
        raised = jnp.exp(scores - row_max)
        summed = jnp.sum(raised, axis=-1, keepdims=True)
        context = jnp.dot(
            (raised / summed).astype(jnp.bfloat16), values, preferred_element_type=jnp.float32
        ).astype(jnp.bfloat16)
        heads.append((query_raw, rot_query, scores, row_max + jnp.log(summed), context))
    return normed_in, key_raw, values, keys, heads, cos_tab, sin_tab


def join_gains(tails, gain_len, gains):
    lane = lax.broadcasted_iota(jnp.int32, (1, LANES), 1)
    tiles = [jnp.zeros((1, LANES), jnp.float32) for _ in range(gains.shape[1] // LANES)]
    for owner in range(tails.shape[0]):
        tile, shift = divmod(owner * gain_len, LANES)
        run = jnp.where(lane < gain_len, tails[owner].astype(jnp.float32)[0:1, :], 0.0)
        if shift:
            run = pltpu.roll(run, shift, 1)
        tiles[tile] += jnp.where(lane >= shift, run, 0.0)
        if shift + gain_len > LANES:
            tiles[tile + 1] += jnp.where(lane < shift, run, 0.0)
    for number, tile in enumerate(tiles):
        gains[:, number * LANES : (number + 1) * LANES] = tile


def attn_forward_kernel(plan, gain_len, device_ref, hidden_in, tables, *refs):
    if not gain_len:
        given, refs = refs[0], refs[1:]
    sources = refs[: len(plan)]
    refs = refs[len(plan) :]
    qkv_weight, out_weight, gains, attn_out, mid_stream = refs[:5]
    staging, spread, tails, context, sems = refs[5:]
    copies, views = [], []
    for number, source in enumerate(sources):
        count = source.shape[0]
        held = staging.at[pl.ds(number * count, count)]
        copies.append(pltpu.make_async_copy(source, held, sems.at[number]))
        views.append((held, 0, count, 0))
    for copy in copies:
        copy.start()
    for copy, step, view in zip(copies, plan, views):
        copy.wait()
        spread_blocks(
            ATTN_PADDED,
            [step],
            [view],
            device_ref[0],
            spread,
            tails if gain_len else None,
        )
    if gain_len:
        join_gains(tails, gain_len, gains)
    else:
        gains[...] = given[...]
    fold_matrices(
        spread,
        (
            (qkv_weight, 0, D, HQ),
            (qkv_weight, HQ, D, HD),
            (qkv_weight, HQ + HD, D, HD),
            (out_weight, 0, HQ, D),
        ),
    )
    heads = attn_forward(hidden_in, qkv_weight, tables, gains)[4]
    for head, parts in enumerate(heads):
        context[:, head * HD : (head + 1) * HD] = parts[-1]
    out = jnp.dot(context[...], out_weight[...], preferred_element_type=jnp.float32)
    attn_out[...] = out
    gain_post = gains[:, D + 2 * HD : 2 * D + 2 * HD]
    mid_stream[...] = hidden_in[...].astype(jnp.float32) + rms_scale(out, gain_post)


def forward_attn(plan, gain_len, tail_rows, devices, device, hidden_in, tables, given, arrays):
    shapes = [
        jax.ShapeDtypeStruct((D, HQ + 2 * HD), jnp.bfloat16),
        jax.ShapeDtypeStruct((HQ, D), jnp.bfloat16),
        jax.ShapeDtypeStruct((1, 4 * D + 2 * HD), jnp.float32),
        jax.ShapeDtypeStruct((CAP, D), jnp.float32),
        jax.ShapeDtypeStruct((CAP, D), jnp.float32),
    ]
    given = [] if gain_len else [given]
    held = (sum(array.shape[0] for array in arrays),) + arrays[0].shape[1:]
    return pl.pallas_call(
        functools.partial(attn_forward_kernel, plan, gain_len),
        out_shape=shapes,
        in_specs=[pl.BlockSpec(memory_space=pltpu.SMEM)]
        + whole_specs(2 + len(given))
        + [pl.BlockSpec(memory_space=pltpu.HBM)] * len(arrays),
        out_specs=whole_specs(len(shapes)),
        scratch_shapes=[
            pltpu.VMEM(held, jnp.bfloat16),
            pltpu.VMEM((G1LEN // LANES + ATTN_PADDED, LANES), jnp.float32),
            pltpu.VMEM((devices, tail_rows, LANES) if gain_len else (1, ROWS, LANES), jnp.bfloat16),
            pltpu.VMEM((CAP, HQ), jnp.bfloat16),
            pltpu.SemaphoreType.DMA((len(arrays),)),
        ],
        compiler_params=pltpu.CompilerParams(vmem_limit_bytes=24 << 20),
        cost_estimate=pl.CostEstimate(flops=0, bytes_accessed=64 << 20, transcendentals=0),
    )(device, hidden_in, tables, *given, *arrays)


def ffn_kernel(
    plan_in,
    staged,
    plan_out,
    device_ref,
    mid_ref,
    attn_out,
    cotangent,
    tables,
    gains,
    *refs,
):
    sources = refs[: len(plan_in)]
    refs = refs[len(plan_in) :]
    block_out, delta_mid_ref, delta_attn_ref, late_gains = refs[:4]
    targets = refs[4:-10]
    spread, gate_weight, up_weight, down_weight = refs[-10:-6]
    gates, ups, hidden, delta_gate, delta_up, sems = refs[-6:]
    device = device_ref[0]
    copies, views = [], []
    for source, (target, first_index, first_row) in zip(sources, staged):
        count, rows = source.shape[:2]
        held = targets[target]
        copies.append(
            pltpu.make_async_copy(
                source,
                held.at[pl.ds(first_index, count), pl.ds(first_row, rows), :],
                sems.at[len(copies)],
            )
        )
        views.append((held, first_index, count, first_row))
    for copy in copies:
        copy.start()
    mid_stream = mid_ref[...]
    gain_post = gains[:, D + 2 * HD : 2 * D + 2 * HD]
    gain_mid = gains[:, 2 * D + 2 * HD : 3 * D + 2 * HD]
    gain_last = gains[:, 3 * D + 2 * HD :]
    normed_mid = rms_scale(mid_stream, gain_mid).astype(jnp.bfloat16)
    for copy, plan, view in zip(copies, plan_in, views):
        copy.wait()
        spread_blocks(FFN_PADDED, [plan], [view], device, spread, None)
    fold_matrices(
        spread, ((gate_weight, 0, D, FF), (up_weight, 0, D, FF), (down_weight, 0, FF, D))
    )
    parts = [slice(low, low + 512) for low in range(0, FF, 512)]
    for at in parts:
        gate = jnp.dot(normed_mid, gate_weight[:, at], preferred_element_type=jnp.float32)
        up = jnp.dot(normed_mid, up_weight[:, at], preferred_element_type=jnp.float32)
        gates[:, at] = gate
        ups[:, at] = up
        hidden[:, at] = gated_gelu(gate, up).astype(jnp.bfloat16)
    ffn_out = jnp.dot(hidden[...], down_weight[...], preferred_element_type=jnp.float32)
    block_out[...] = (mid_stream + rms_scale(ffn_out, gain_last)).astype(jnp.bfloat16)
    delta_out = cotangent[...].astype(jnp.float32) * tables[:, 3 * LANES : 3 * LANES + 1]
    delta_ffn, gain_rows = rms_pull(ffn_out, gain_last, delta_out)
    late_gains[2:3, :] = jnp.sum(gain_rows, axis=0, keepdims=True)
    delta_ffn = delta_ffn.astype(jnp.bfloat16)
    delta_normed = jnp.zeros((CAP, D), jnp.float32)
    for at in parts:
        delta_hidden = times_transposed(delta_ffn, down_weight[at, :])
        gate = gates[:, at]
        raised = jnp.tanh(GELU_SCALE * (gate + 0.044715 * (gate * gate * gate)))
        share = 0.5 * (1.0 + raised)
        slope = share + (0.5 * GELU_SCALE) * gate * (1.0 - raised * raised) * (
            1.0 + (3 * 0.044715) * (gate * gate)
        )
        delta_gate[:, at] = (delta_hidden * ups[:, at] * slope).astype(jnp.bfloat16)
        delta_up[:, at] = (delta_hidden * (gate * share)).astype(jnp.bfloat16)
        delta_normed += times_transposed(delta_gate[:, at], gate_weight[:, at])
        delta_normed += times_transposed(delta_up[:, at], up_weight[:, at])
    delta_part, gain_rows = rms_pull(mid_stream, gain_mid, delta_normed)
    late_gains[1:2, :] = jnp.sum(gain_rows, axis=0, keepdims=True)
    delta_mid = delta_out + delta_part
    delta_mid_ref[...] = delta_mid
    delta_attn, gain_rows = rms_pull(attn_out[...], gain_post, delta_mid)
    late_gains[0:1, :] = jnp.sum(gain_rows, axis=0, keepdims=True)
    delta_attn_ref[...] = delta_attn.astype(jnp.bfloat16)
    turned = normed_mid.T
    spread_grads(
        spread,
        (
            (turned, lambda low, high: delta_gate[:, low:high], FF),
            (turned, lambda low, high: delta_up[:, low:high], FF),
            (hidden[...].T, lambda low, high: delta_ffn[:, low:high], D),
        ),
    )
    place_blocks(FFN_PADDED, plan_out, device, spread, None, targets)


def run_ffn(
    plan_in, staged, plan_out, block_shapes, device, mid, attn_out, cotangent, tables, gains, arrays
):
    flat_rows = G2LEN // LANES + FFN_PADDED
    shapes = [
        jax.ShapeDtypeStruct((CAP, D), jnp.bfloat16),
        jax.ShapeDtypeStruct((CAP, D), jnp.float32),
        jax.ShapeDtypeStruct((CAP, D), jnp.bfloat16),
        jax.ShapeDtypeStruct((3, D), jnp.float32),
    ] + [jax.ShapeDtypeStruct(shape, jnp.bfloat16) for shape in block_shapes]
    wide = pltpu.VMEM((CAP, FF), jnp.float32)
    narrow = pltpu.VMEM((CAP, FF), jnp.bfloat16)
    return pl.pallas_call(
        functools.partial(ffn_kernel, plan_in, staged, plan_out),
        out_shape=shapes,
        in_specs=[pl.BlockSpec(memory_space=pltpu.SMEM)]
        + whole_specs(5)
        + [pl.BlockSpec(memory_space=pltpu.HBM)] * len(arrays),
        out_specs=whole_specs(len(shapes)),
        scratch_shapes=[
            pltpu.VMEM((flat_rows, LANES), jnp.float32),
            pltpu.VMEM((D, FF), jnp.bfloat16),
            pltpu.VMEM((D, FF), jnp.bfloat16),
            pltpu.VMEM((FF, D), jnp.bfloat16),
            wide,
            wide,
            narrow,
            narrow,
            narrow,
            pltpu.SemaphoreType.DMA((len(arrays),)),
        ],
        compiler_params=pltpu.CompilerParams(vmem_limit_bytes=44 << 20),
        cost_estimate=pl.CostEstimate(flops=0, bytes_accessed=0, transcendentals=0),
    )(device, mid, attn_out, cotangent, tables, gains, *arrays)


def attn_back_kernel(
    plan,
    gain_len,
    device_ref,
    delta_attn,
    delta_mid,
    hidden_in,
    tables,
    gains,
    late_gains,
    qkv_weight,
    out_weight,
    grad_in,
    gain_grads,
    *refs,
):
    targets = refs[:-4]
    spread, tails, delta_raws, contexts = refs[-4:]
    device = device_ref[0]
    normed_in, key_raw, values, keys, heads, cos_tab, sin_tab = attn_forward(
        hidden_in, qkv_weight, tables, gains
    )
    gain_query = gains[:, D : D + HD]
    gain_key = gains[:, D + HD : D + 2 * HD]
    delta_context = times_transposed(delta_attn[...], out_weight[...]).astype(jnp.bfloat16)
    delta_key = jnp.zeros((CAP, HD), jnp.float32)
    delta_value = jnp.zeros((CAP, HD), jnp.float32)
    query_gain_rows = jnp.zeros((CAP, HD), jnp.float32)
    for head, (query_raw, queries, scores, log_total, context) in enumerate(heads):
        at = slice(head * HD, (head + 1) * HD)
        contexts[:, at] = context
        head_delta = delta_context[:, at]
        row_dot = jnp.sum(
            head_delta.astype(jnp.float32) * context.astype(jnp.float32), axis=-1, keepdims=True
        )
        prob_exact = jnp.exp(scores - log_total)
        delta_prob = times_transposed(head_delta, values)
        delta_score = prob_exact * (delta_prob - row_dot)
        turned = delta_score.T.astype(jnp.bfloat16)
        delta_score = delta_score.astype(jnp.bfloat16)
        delta_query = jnp.dot(delta_score, keys, preferred_element_type=jnp.float32)
        delta_key += jnp.dot(turned, queries, preferred_element_type=jnp.float32)
        delta_value += jnp.dot(
            prob_exact.T.astype(jnp.bfloat16), head_delta, preferred_element_type=jnp.float32
        )
        delta_rot = rotate_pull(delta_query * HD ** (-0.5), cos_tab, sin_tab)
        delta_raw, gain_rows = rms_pull(query_raw, gain_query, delta_rot)
        query_gain_rows += gain_rows
        delta_raws[:, at] = delta_raw.astype(jnp.bfloat16)
    delta_raw, gain_rows = rms_pull(key_raw, gain_key, rotate_pull(delta_key, cos_tab, sin_tab))
    delta_raws[:, HQ : HQ + HD] = delta_raw.astype(jnp.bfloat16)
    delta_raws[:, HQ + HD :] = delta_value.astype(jnp.bfloat16)
    gain_grads[:, D : D + HD] = jnp.sum(query_gain_rows, axis=0, keepdims=True)
    gain_grads[:, D + HD : D + 2 * HD] = jnp.sum(gain_rows, axis=0, keepdims=True)
    delta_in = times_transposed(delta_raws[...], qkv_weight[...])
    delta_part, gain_rows = rms_pull(
        hidden_in[...].astype(jnp.float32), gains[:, :D], delta_in
    )
    grad_in[...] = delta_mid[...] + delta_part
    gain_grads[:, :D] = jnp.sum(gain_rows, axis=0, keepdims=True)
    for late in range(3):
        at = slice((late + 1) * D + 2 * HD, (late + 2) * D + 2 * HD)
        gain_grads[:, at] = late_gains[late : late + 1, :]
    if gain_len:
        tails[...] = jnp.zeros_like(tails)
        lane = lax.broadcasted_iota(jnp.int32, (1, LANES), 1)
        for owner in range(tails.shape[0]):
            row, shift = divmod(owner * gain_len, LANES)
            piece = gain_grads[:, row * LANES : (row + 1) * LANES]
            if shift:
                piece = pltpu.roll(piece, LANES - shift, 1)
            if shift + gain_len > LANES:
                after = gain_grads[:, (row + 1) * LANES : (row + 2) * LANES]
                after = pltpu.roll(after, LANES - shift, 1)
                piece = jnp.where(lane < LANES - shift, piece, after)
            tails[owner, 0:1, :] = jnp.where(lane < gain_len, piece, 0.0)
    turned = normed_in.T
    delta_attn_value = delta_attn[...]
    spread_grads(
        spread,
        (
            (turned, lambda low, high: delta_raws[:, low:high], HQ),
            (turned, lambda low, high: delta_raws[:, HQ + low : HQ + high], HD),
            (turned, lambda low, high: delta_raws[:, HQ + HD + low : HQ + HD + high], HD),
            (contexts[...].T, lambda low, high: delta_attn_value[:, low:high], D),
        ),
    )
    place_blocks(ATTN_PADDED, plan, device, spread, tails, targets)


def back_attn(plan, gain_len, tail_rows, devices, block_shapes, device, *inputs):
    flat_rows = G1LEN // LANES + ATTN_PADDED
    shapes = [
        jax.ShapeDtypeStruct((CAP, D), jnp.float32),
        jax.ShapeDtypeStruct((1, 4 * D + 2 * HD), jnp.float32),
    ] + [jax.ShapeDtypeStruct(shape, jnp.bfloat16) for shape in block_shapes]
    tail_shape = (devices, tail_rows, LANES) if gain_len else (1, ROWS, LANES)
    return pl.pallas_call(
        functools.partial(attn_back_kernel, plan, gain_len),
        out_shape=shapes,
        in_specs=[pl.BlockSpec(memory_space=pltpu.SMEM)] + whole_specs(len(inputs)),
        out_specs=whole_specs(len(shapes)),
        scratch_shapes=[
            pltpu.VMEM((flat_rows, LANES), jnp.float32),
            pltpu.VMEM(tail_shape, jnp.float32),
            pltpu.VMEM((CAP, HQ + 2 * HD), jnp.bfloat16),
            pltpu.VMEM((CAP, HQ), jnp.bfloat16),
        ],
        compiler_params=pltpu.CompilerParams(vmem_limit_bytes=22 << 20),
        cost_estimate=pl.CostEstimate(flops=0, bytes_accessed=0, transcendentals=0),
    )(device, *inputs)


def gathered_blocks(pieces, chunks, orders, each, devices, device):
    arrays, plan, start = [], [], 0
    for piece, blocks, order in zip(pieces, chunks, orders):
        take = min(piece.shape[0], each - start)
        if each % ROWS:
            places = [offset_of(place, list(order) + [0]) for place in range(devices)]
            back = sorted(range(devices), key=places.__getitem__)
            mixed = offset_bits(device[0], list(order) + [0])
            arrays.append(
                jnp.take(jnp.concatenate(blocks), jnp.array(back, jnp.int32) ^ mixed, axis=0)
            )
            continue
        for part, block in enumerate(blocks):
            plan.append((order[:-1], offset_of(part, [order[-1], 0]), take, start, each))
            arrays.append(block)
        start += take
    if each % ROWS == 0:
        return arrays, plan, None
    table = jnp.concatenate(arrays, axis=1)
    flat = table[:, :each].reshape(1, devices * each, LANES)
    return [flat], [([], 0, devices * each, 0, 0)], table[:, each:]


def offset_bits(device, order):
    return sum(((device >> bit) & 1) << k for k, bit in enumerate(order))


def scatter_plan(each, tail_rows, orders, devices):
    parts = cut_rows(each + tail_rows, len(orders))
    half = devices // 2
    if each % ROWS:
        return [(0, [], 0, 0, devices * each, 0, 0)], [(1, devices * each, LANES)], parts
    plan = []
    for with_core in (1, 0):
        for (low, high), order in zip(parts, orders):
            order = order[::-1]
            plan.append((with_core, order, with_core, low, min(high, each) - low, low, each))
            if high > each:
                plan.append((with_core, order, with_core, each, tail_rows, None, each))
    return plan, [(half, each + tail_rows, LANES)] * 2, parts


def blocks_of(found, tails, parts, orders, devices, device):
    if len(found) == 2:
        return found
    table = found[0].reshape(devices, -1, LANES)
    table = table if tails is None else jnp.concatenate([table, tails], axis=1)
    blocks = []
    for with_core in (0, 1):
        chunks = []
        for (low, high), order in zip(parts, orders):
            places = range(devices // 2)
            offsets = [offset_of(place, order[::-1]) ^ with_core for place in places]
            owners = jnp.array(offsets, jnp.int32) ^ device[0]
            chunks.append(jnp.take(table[:, low:high], owners, axis=0))
        blocks.append(jnp.concatenate(chunks, axis=1))
    return blocks


def merge_kernel(parts, *refs):
    pairs = ((refs[0], refs[1]), (refs[2], refs[3]))
    targets = refs[4:]
    half = refs[0].shape[0] // 2
    for number, target in enumerate(targets):
        chunk, second = divmod(number, 2)

        @pl.loop(0, half)
        def _(index, target=target, chunk=chunk, first=second * half):
            at = 0
            for (home, came), (low, high) in zip(pairs, parts[chunk]):
                total = home[first + index, low:high, :].astype(jnp.float32)
                total += came[first + index, low:high, :].astype(jnp.float32)
                target[index, at : at + high - low, :] = total.astype(jnp.bfloat16)
                at += high - low


def cores_merged(parts, *blocks):
    half = blocks[0].shape[0] // 2
    if any((high - low) % ROWS for chunk in parts for low, high in chunk):
        pairs = (blocks[:2], blocks[2:])
        joined = []
        for chunk in parts:
            sums = [
                home[:, low:high].astype(jnp.float32) + came[:, low:high].astype(jnp.float32)
                for (home, came), (low, high) in zip(pairs, chunk)
            ]
            total = jnp.concatenate(sums, axis=1).astype(jnp.bfloat16)
            joined.append((total[:half], total[half:]))
        return joined
    shapes = [
        jax.ShapeDtypeStruct((half, sum(high - low for low, high in chunk), LANES), jnp.bfloat16)
        for chunk in parts
        for _ in range(2)
    ]
    found = pl.pallas_call(
        functools.partial(merge_kernel, parts),
        out_shape=shapes,
        in_specs=whole_specs(4),
        out_specs=whole_specs(len(shapes)),
        compiler_params=pltpu.CompilerParams(vmem_limit_bytes=20 << 20),
        cost_estimate=pl.CostEstimate(flops=0, bytes_accessed=0, transcendentals=0),
    )(*blocks)
    return list(zip(found[::2], found[1::2]))


def adam_update(weight_shard, gradient, moment_one, moment_two):
    moment_one = 0.9 * moment_one + 0.1 * gradient
    moment_two = 0.999 * moment_two + 0.001 * gradient * gradient
    fix_one = 1.0 - 0.9**STEP
    fix_two = 1.0 - 0.999**STEP
    weight_shard = weight_shard - 0.02 * (
        moment_one / fix_one / (jnp.sqrt(moment_two / fix_two) + 1e-08) + 0.1 * weight_shard
    )
    return (weight_shard, moment_one, moment_two)


def per_device(hidden_in, cotangent, params, moment_one, moment_two, seq_lengths, seq_owner):
    devices = lax.axis_size("dp")
    device = lax.axis_index("dp").astype(jnp.int32)
    here = device.reshape(1)
    attn_len = G1LEN // devices
    ffn_len = G2LEN // devices
    gain_len = params.shape[0] - attn_len - ffn_len
    attn_rows = attn_len // LANES
    tail_rows = -(-(attn_rows + 1) // ROWS) * ROWS - attn_rows
    pad = tail_rows * LANES - gain_len
    rounded = params.astype(jnp.bfloat16)
    first_piece = jnp.concatenate(
        [rounded[:attn_len], rounded[attn_len + ffn_len :], jnp.zeros((pad,), jnp.bfloat16)]
    ).reshape(-1, LANES)
    second_piece = rounded[attn_len : attn_len + ffn_len].reshape(-1, LANES)
    ffn_rows = ffn_len // LANES
    second_pieces = [second_piece[low:high] for low, high in cut_rows(ffn_rows, 2)]
    orders = bit_orders(devices, ("abxy", "bxya", "byax"))
    pieces = [first_piece, *second_pieces]
    chunks = gather_chunks(pieces, orders, devices)
    arrays, plan, tails = gathered_blocks(
        pieces[:1], chunks[:1], orders[:1], attn_rows, devices, here
    )
    ffn_arrays, ffn_plan, unused = gathered_blocks(
        pieces[1:], chunks[1:], orders[1:], ffn_rows, devices, here
    )
    aligned = attn_rows % ROWS == 0
    tables = slot_setup(seq_lengths, seq_owner, device)
    given = None
    if not aligned:
        given = tails.reshape(devices, -1)[:, :gain_len].astype(jnp.float32).reshape(1, -1)
    qkv_weight, out_weight, gains, attn_out, mid_stream = forward_attn(
        plan,
        gain_len if aligned else 0,
        tail_rows,
        devices,
        here,
        hidden_in,
        tables,
        given,
        arrays,
    )
    orders = bit_orders(devices, ("yxba", "ayxb", "xayb"))
    out_plan, block_shapes, ffn_parts = scatter_plan(ffn_rows, 0, orders, devices)
    staged = [(0, 0, 0)]
    if len(block_shapes) == 2:
        staged = [
            (part // 2, part % 2 * (devices // 4), low)
            for low, _ in cut_rows(ffn_rows, 2)
            for part in range(4)
        ]
    block_out, delta_mid, delta_attn, late_gains, *found = run_ffn(
        ffn_plan,
        staged,
        out_plan,
        block_shapes,
        here,
        mid_stream,
        attn_out,
        cotangent,
        tables,
        gains,
        ffn_arrays,
    )
    ffn_home, ffn_away = blocks_of(found, None, ffn_parts, orders, devices, here)
    ffn_came = across(ffn_away, 0, devices)
    attn_plan, block_shapes, attn_parts = scatter_plan(attn_rows, tail_rows, orders, devices)
    grad_in, gain_grads, *found = back_attn(
        attn_plan,
        gain_len if aligned else 0,
        tail_rows,
        devices,
        block_shapes,
        here,
        delta_attn,
        delta_mid,
        hidden_in,
        tables,
        gains,
        late_gains,
        qkv_weight,
        out_weight,
    )
    gain_table = None
    if not aligned:
        gain_table = gain_grads.reshape(devices, gain_len).astype(jnp.bfloat16)
        gain_table = jnp.pad(gain_table, ((0, 0), (0, pad))).reshape(devices, tail_rows, LANES)
    attn_home, attn_away = blocks_of(found, gain_table, attn_parts, orders, devices, here)
    attn_came = across(attn_away, 0, devices)
    parts = [
        [cut[chunk] for cut in (ffn_parts, attn_parts) if chunk < len(cut)]
        for chunk in range(len(ffn_parts))
    ]
    chunks = cores_merged(parts, ffn_home, ffn_came, attn_home, attn_came)
    for stage in range(len(orders[0])):
        chunks = merged_blocks(chunks, sent_blocks(chunks, orders, stage, devices))
    rows = [chunk for chunk, _ in chunks]
    ffn_take = [high - low for low, high in ffn_parts]
    ffn_shard = [chunk[:take].reshape(-1) for chunk, take in zip(rows, ffn_take)]
    attn_shard = jnp.concatenate([chunk[take:].reshape(-1) for chunk, take in zip(rows, ffn_take)])
    grad_shard = jnp.concatenate(
        [attn_shard[:attn_len], *ffn_shard, attn_shard[attn_len : attn_len + gain_len]]
    )
    params_new, moment_one_new, moment_two_new = adam_update(
        params, grad_shard, moment_one, moment_two
    )
    return (block_out, grad_in, grad_shard, params_new, moment_one_new, moment_two_new)


def solution(mesh):
    in_specs = (P("dp", None), P("dp", None), P("dp"), P("dp"), P("dp"), P(), P())
    out_specs = (P("dp", None), P("dp", None), P("dp"), P("dp"), P("dp"), P("dp"))
    return jax.shard_map(
        per_device, mesh=mesh, in_specs=in_specs, out_specs=out_specs, check_vma=False
    )
```

```python
import functools
import math

import jax
import jax.numpy as jnp
from jax import lax
from jax.experimental import pallas as pl
from jax.experimental.pallas import tpu as pltpu
from jax.sharding import PartitionSpec as P

D = 640
FF = 2048
HD = 256
HQ = 1024
CAP = 128
WINDOW = 64
STEP = 3
G1LEN = 1638400
G2LEN = 3932160
LANES = 128
ROWS = 16
GELU_SCALE = math.sqrt(2 / math.pi)
ATTN_PADDED, FFN_PADDED = 0, 2 * D


def rms_scale(values, gain_vec):
    return (
        values
        * lax.rsqrt(jnp.mean(values * values, axis=-1, keepdims=True) + 1e-06)
        * (1.0 + gain_vec)
    )


def rotate(values, cos_tab, sin_tab):
    half_dim = values.shape[-1] // 2
    lower_half = values[..., :half_dim]
    upper_half = values[..., half_dim:]
    return jnp.concatenate(
        [lower_half * cos_tab - upper_half * sin_tab, upper_half * cos_tab + lower_half * sin_tab],
        axis=-1,
    )


def gated_gelu(gate_proj, up_proj):
    return jax.nn.gelu(gate_proj, approximate=True) * up_proj


def times_transposed(rows_in, matrix):
    return lax.dot_general(
        rows_in, matrix, (((1,), (1,)), ((), ())), preferred_element_type=jnp.float32
    )


def slot_setup(seq_lengths, seq_owner, device):
    mine_mask = seq_owner == device
    own_lengths = jnp.where(mine_mask, seq_lengths, 0)
    seq_ends = jnp.cumsum(own_lengths, dtype=jnp.int32)
    seq_begins = seq_ends - own_lengths
    slot_index = jnp.arange(CAP, dtype=jnp.int32)
    column = slot_index[:, None]
    inside_mask = (
        mine_mask[None, :] & (seq_begins[None, :] <= column) & (column < seq_ends[None, :])
    )
    live_mask = jnp.any(inside_mask, axis=1)
    seq_label = jnp.sum(
        (mine_mask[None, :] & (seq_ends[None, :] <= column)).astype(jnp.int32),
        axis=1,
        dtype=jnp.int32,
    )
    position = jnp.sum(
        jnp.where(inside_mask, column - seq_begins[None, :], 0), axis=1, dtype=jnp.int32
    )
    row_slot = slot_index[:, None]
    col_slot = slot_index[None, :]
    allowed = live_mask[:, None] & live_mask[None, :] & (
        seq_label[:, None] == seq_label[None, :]
    ) & (col_slot <= row_slot) & (row_slot - col_slot < WINDOW) | (row_slot == col_slot)
    half_dim = HD // 2
    frequency = 10000.0 ** (-2.0 * jnp.arange(half_dim, dtype=jnp.float32) / HD)
    angles = position.astype(jnp.float32)[:, None] * frequency[None, :]
    live_wide = jnp.broadcast_to(live_mask[:, None], (CAP, LANES)).astype(jnp.float32)
    return jnp.concatenate(
        [jnp.cos(angles), jnp.sin(angles), allowed.astype(jnp.float32), live_wide], axis=1
    )


def rms_pull(raw, gain_vec, delta):
    scale = lax.rsqrt(jnp.mean(raw * raw, axis=-1, keepdims=True) + 1e-06)
    weighed = delta * (1.0 + gain_vec)
    shared = jnp.mean(raw * weighed, axis=-1, keepdims=True)
    return scale * weighed - raw * (scale * scale * scale * shared), delta * raw * scale


def rotate_pull(delta, cos_tab, sin_tab):
    half_dim = delta.shape[-1] // 2
    lower_half = delta[:, :half_dim]
    upper_half = delta[:, half_dim:]
    return jnp.concatenate(
        [lower_half * cos_tab + upper_half * sin_tab, upper_half * cos_tab - lower_half * sin_tab],
        axis=-1,
    )


def bit_orders(devices, tuned):
    bits = devices.bit_length() - 1
    if bits == 5:
        return [["cxyab".index(letter) for letter in order] for order in tuned]
    return [[1 + (shift + step) % (bits - 1) for step in range(bits - 1)] for shift in range(3)]


def across(block, bit, devices):
    return lax.ppermute(block, "dp", [(i, i ^ (1 << bit)) for i in range(devices)])


def offset_of(place, order):
    return sum(((place >> k) & 1) << bit for k, bit in enumerate(order))


def gather_chunk(piece, order, devices):
    held = piece[None]
    for bit in order[:-1]:
        held = jnp.concatenate([held, across(held, bit, devices)])
    last = across(held, order[-1], devices)
    return (held, last, across(held, 0, devices), across(last, 0, devices))


def sent_blocks(chunks, orders, stage, devices):
    return [
        across(away, order[stage], devices)
        for (_, away), order in zip(chunks, orders)
    ]


def merged_blocks(chunks, came):
    merged = []
    for (home, _), arrived in zip(chunks, came):
        half = home.shape[0] // 2

        def added(low, high):
            return home[low:high].astype(jnp.float32) + arrived[low:high].astype(jnp.float32)

        if half:
            merged.append(
                (
                    added(0, half).astype(jnp.bfloat16),
                    added(half, 2 * half).astype(jnp.bfloat16),
                )
            )
        else:
            merged.append((added(0, 1)[0], None))
    return merged


def cut_rows(rows, parts):
    each = -(-rows // (parts * ROWS)) * ROWS
    return [(low, min(low + each, rows)) for low in range(0, rows, each)]


def whole_specs(count):
    return [pl.BlockSpec(memory_space=pltpu.VMEM)] * count


def owner_rows(device, index, order, extra, start, each):
    owner = device ^ extra
    for k, bit in enumerate(order):
        owner = owner ^ (((index >> k) & 1) << bit)
    return owner, owner * each + start


def copy_step(rows):
    return max(step for step in range(ROWS, 513, ROWS) if rows % step == 0)


def each_piece(padded, first, take, visit):
    def visit_plain(shift):
        step = copy_step(take)

        def visit_step(part):
            at = part * step
            visit(at, step, pl.multiple_of(first + shift + at, ROWS))

        if take == step:
            visit_step(0)
        else:
            pl.loop(0, take // step)(visit_step)

    if not padded:
        visit_plain(0)
        return
    units = take // ROWS
    inner = max(count for count in range(1, 41) if units % count == 0)
    number = first // ROWS

    def visit_units(row_of):
        def visit_some(step):
            for part in range(inner):
                at = (step * inner + part) * ROWS
                visit(at, ROWS, row_of(step * inner + part))

        if units == inner:
            visit_some(0)
        else:
            pl.loop(0, units // inner)(visit_some)

    longer = (ROWS + 1) * number
    pl.when(number + units <= padded)(lambda: visit_units(lambda k: longer + (ROWS + 1) * k))
    pl.when(number >= padded)(lambda: visit_plain(padded))
    pl.when((number < padded) & (number + units > padded))(
        lambda: visit_units(lambda k: ROWS * (number + k) + jnp.minimum(number + k, padded))
    )


def spread_blocks(padded, plan, views, device, spread, tails):
    for (order, extra, take, start, each), (block_ref, first_index, count, first_row) in zip(
        plan, views
    ):

        @pl.loop(0, count)
        def _(
            index,
            order=order,
            extra=extra,
            take=take,
            start=start,
            each=each,
            block_ref=block_ref,
            first_index=first_index,
            first_row=first_row,
        ):
            owner, first = owner_rows(device, index, order, extra, start, each)

            def spread_unit(at, unit, row):
                low = first_row + at
                if not isinstance(low, int):
                    low = pl.multiple_of(low, ROWS)
                spread[pl.ds(row, unit), :] = block_ref[
                    first_index + index, pl.ds(low, unit), :
                ].astype(jnp.float32)

            each_piece(padded, first, take, spread_unit)
            if tails is not None and start + take == each:
                tails[owner] = block_ref[
                    first_index + index, first_row + take : first_row + take + tails.shape[1], :
                ]


def pitch_of(columns):
    blocks = columns // LANES
    return blocks + (blocks == ROWS)


def fold_matrices(spread, targets):
    first = 0
    for matrix, offset, rows, columns in targets:
        blocks = columns // LANES
        pitch = pitch_of(columns)

        @pl.loop(0, rows // LANES)
        def _(step, matrix=matrix, offset=offset, blocks=blocks, pitch=pitch, first=first):
            base = first + step * (LANES * pitch)
            at = pl.ds(pl.multiple_of(step * LANES, LANES), LANES)
            for block in range(blocks):
                low = offset + block * LANES
                matrix[at, low : low + LANES] = spread[
                    pl.ds(base + block, LANES, stride=pitch), :
                ].astype(jnp.bfloat16)

        first += rows * pitch


def spread_grads(spread, products):
    first = 0
    for turned, right, columns in products:
        rows = turned.shape[0]
        blocks = columns // LANES
        pitch = pitch_of(columns)
        wide = 2 - blocks % 2
        for block in range(0, blocks, wide):
            product = jnp.dot(
                turned,
                right(block * LANES, (block + wide) * LANES),
                preferred_element_type=jnp.float32,
            )
            for part in range(wide):
                spread[pl.ds(first + block + part, rows, stride=pitch), :] = product[
                    :, part * LANES : (part + 1) * LANES
                ]
        first += rows * pitch


def place_blocks(padded, plan, device, spread, tails, targets):
    for target, order, extra, low, take, start, each in plan:
        target_ref = targets[target]

        @pl.loop(0, target_ref.shape[0])
        def _(
            index,
            target_ref=target_ref,
            order=order,
            extra=extra,
            low=low,
            take=take,
            start=start,
            each=each,
        ):
            owner, first = owner_rows(device, index, order, extra, start or 0, each)
            if start is None:
                target_ref[index, low : low + take, :] = tails[owner].astype(jnp.bfloat16)
                return

            def place_unit(at, unit, row):
                at = low + at
                if not isinstance(at, int):
                    at = pl.multiple_of(at, ROWS)
                target_ref[index, pl.ds(at, unit), :] = spread[pl.ds(row, unit), :].astype(
                    jnp.bfloat16
                )

            each_piece(padded, first, take, place_unit)


def attn_forward(hidden_in, qkv_weight, tables, gains):
    cos_tab = tables[:, :LANES]
    sin_tab = tables[:, LANES : 2 * LANES]
    open_pairs = tables[:, 2 * LANES : 3 * LANES] > 0.0
    gain_query = gains[:, D : D + HD]
    gain_key = gains[:, D + HD : D + 2 * HD]
    normed_in = rms_scale(hidden_in[...].astype(jnp.float32), gains[:, :D]).astype(jnp.bfloat16)
    raw = jnp.dot(normed_in, qkv_weight[...], preferred_element_type=jnp.float32)
    key_raw = raw[:, HQ : HQ + HD]
    values = raw[:, HQ + HD :].astype(jnp.bfloat16)
    keys = rotate(rms_scale(key_raw, gain_key), cos_tab, sin_tab).astype(jnp.bfloat16)
    heads = []
    for head in range(HQ // HD):
        query_raw = raw[:, head * HD : (head + 1) * HD]
        rot_query = rotate(rms_scale(query_raw, gain_query), cos_tab, sin_tab) * HD ** (-0.5)
        rot_query = rot_query.astype(jnp.bfloat16)
        scores = jnp.where(open_pairs, times_transposed(rot_query, keys), -1e30)
        row_max = jnp.max(scores, axis=-1, keepdims=True)
        raised = jnp.exp(scores - row_max)
        summed = jnp.sum(raised, axis=-1, keepdims=True)
        context = jnp.dot(
            (raised / summed).astype(jnp.bfloat16), values, preferred_element_type=jnp.float32
        ).astype(jnp.bfloat16)
        heads.append((query_raw, rot_query, scores, row_max + jnp.log(summed), context))
    return normed_in, key_raw, values, keys, heads, cos_tab, sin_tab


def join_gains(tails, gain_len, gains):
    lane = lax.broadcasted_iota(jnp.int32, (1, LANES), 1)
    tiles = [jnp.zeros((1, LANES), jnp.float32) for _ in range(gains.shape[1] // LANES)]
    for owner in range(tails.shape[0]):
        tile, shift = divmod(owner * gain_len, LANES)
        run = jnp.where(lane < gain_len, tails[owner].astype(jnp.float32)[0:1, :], 0.0)
        if shift:
            run = pltpu.roll(run, shift, 1)
        tiles[tile] += jnp.where(lane >= shift, run, 0.0)
        if shift + gain_len > LANES:
            tiles[tile + 1] += jnp.where(lane < shift, run, 0.0)
    for number, tile in enumerate(tiles):
        gains[:, number * LANES : (number + 1) * LANES] = tile


def attn_forward_kernel(plan, windows, gain_len, device_ref, hidden_in, tables, *refs):
    if not gain_len:
        given, refs = refs[0], refs[1:]
    sources = refs[: len(plan)]
    refs = refs[len(plan) :]
    qkv_weight, out_weight, gains, attn_out, mid_stream = refs[:5]
    staging, spread, tails, context, sems = refs[5:]
    copies, views = [], []
    for number, (source, (low, rows)) in enumerate(zip(sources, windows)):
        count = source.shape[0]
        copies.append(
            pltpu.make_async_copy(
                source.at[:, pl.ds(low, rows), :],
                staging.at[pl.ds(number * count, count), pl.ds(0, rows), :],
                sems.at[number],
            )
        )
        views.append((staging, number * count, count, 0))
    for copy in copies:
        copy.start()
    for copy, step, view in zip(copies, plan, views):
        copy.wait()
        spread_blocks(
            ATTN_PADDED,
            [step],
            [view],
            device_ref[0],
            spread,
            tails if gain_len else None,
        )
    if gain_len:
        join_gains(tails, gain_len, gains)
    else:
        gains[...] = given[...]
    fold_matrices(
        spread,
        (
            (qkv_weight, 0, D, HQ),
            (qkv_weight, HQ, D, HD),
            (qkv_weight, HQ + HD, D, HD),
            (out_weight, 0, HQ, D),
        ),
    )
    heads = attn_forward(hidden_in, qkv_weight, tables, gains)[4]
    for head, parts in enumerate(heads):
        context[:, head * HD : (head + 1) * HD] = parts[-1]
    out = jnp.dot(context[...], out_weight[...], preferred_element_type=jnp.float32)
    attn_out[...] = out
    gain_post = gains[:, D + 2 * HD : 2 * D + 2 * HD]
    mid_stream[...] = hidden_in[...].astype(jnp.float32) + rms_scale(out, gain_post)


def forward_attn(
    plan, windows, gain_len, tail_rows, devices, device, hidden_in, tables, given, arrays
):
    shapes = [
        jax.ShapeDtypeStruct((D, HQ + 2 * HD), jnp.bfloat16),
        jax.ShapeDtypeStruct((HQ, D), jnp.bfloat16),
        jax.ShapeDtypeStruct((1, 4 * D + 2 * HD), jnp.float32),
        jax.ShapeDtypeStruct((CAP, D), jnp.float32),
        jax.ShapeDtypeStruct((CAP, D), jnp.float32),
    ]
    given = [] if gain_len else [given]
    most = max(rows for _, rows in windows)
    held = (sum(array.shape[0] for array in arrays), most, LANES)
    return pl.pallas_call(
        functools.partial(attn_forward_kernel, plan, windows, gain_len),
        out_shape=shapes,
        in_specs=[pl.BlockSpec(memory_space=pltpu.SMEM)]
        + whole_specs(2 + len(given))
        + [pl.BlockSpec(memory_space=pltpu.HBM)] * len(arrays),
        out_specs=whole_specs(len(shapes)),
        scratch_shapes=[
            pltpu.VMEM(held, jnp.bfloat16),
            pltpu.VMEM((G1LEN // LANES + ATTN_PADDED, LANES), jnp.float32),
            pltpu.VMEM((devices, tail_rows, LANES) if gain_len else (1, ROWS, LANES), jnp.bfloat16),
            pltpu.VMEM((CAP, HQ), jnp.bfloat16),
            pltpu.SemaphoreType.DMA((len(arrays),)),
        ],
        compiler_params=pltpu.CompilerParams(vmem_limit_bytes=24 << 20),
        cost_estimate=pl.CostEstimate(flops=0, bytes_accessed=64 << 20, transcendentals=0),
    )(device, hidden_in, tables, *given, *arrays)


def ffn_kernel(
    plan_in,
    staged,
    plan_out,
    device_ref,
    mid_ref,
    attn_out,
    cotangent,
    tables,
    gains,
    *refs,
):
    sources = refs[: len(plan_in)]
    refs = refs[len(plan_in) :]
    block_out, delta_mid_ref, delta_attn_ref, late_gains = refs[:4]
    targets = refs[4:-10]
    spread, gate_weight, up_weight, down_weight = refs[-10:-6]
    gates, ups, hidden, delta_gate, delta_up, sems = refs[-6:]
    device = device_ref[0]
    copies, views = [], []
    for source, (target, first_index, first_row, low, rows) in zip(sources, staged):
        count = source.shape[0]
        held = targets[target]
        copies.append(
            pltpu.make_async_copy(
                source.at[:, pl.ds(low, rows), :],
                held.at[pl.ds(first_index, count), pl.ds(first_row, rows), :],
                sems.at[len(copies)],
            )
        )
        views.append((held, first_index, count, first_row))
    for copy in copies:
        copy.start()
    mid_stream = mid_ref[...]
    gain_post = gains[:, D + 2 * HD : 2 * D + 2 * HD]
    gain_mid = gains[:, 2 * D + 2 * HD : 3 * D + 2 * HD]
    gain_last = gains[:, 3 * D + 2 * HD :]
    normed_mid = rms_scale(mid_stream, gain_mid).astype(jnp.bfloat16)
    for copy, plan, view in zip(copies, plan_in, views):
        copy.wait()
        spread_blocks(FFN_PADDED, [plan], [view], device, spread, None)
    fold_matrices(
        spread, ((gate_weight, 0, D, FF), (up_weight, 0, D, FF), (down_weight, 0, FF, D))
    )
    parts = [slice(low, low + 512) for low in range(0, FF, 512)]
    for at in parts:
        gate = jnp.dot(normed_mid, gate_weight[:, at], preferred_element_type=jnp.float32)
        up = jnp.dot(normed_mid, up_weight[:, at], preferred_element_type=jnp.float32)
        gates[:, at] = gate
        ups[:, at] = up
        hidden[:, at] = gated_gelu(gate, up).astype(jnp.bfloat16)
    ffn_out = jnp.dot(hidden[...], down_weight[...], preferred_element_type=jnp.float32)
    block_out[...] = (mid_stream + rms_scale(ffn_out, gain_last)).astype(jnp.bfloat16)
    delta_out = cotangent[...].astype(jnp.float32) * tables[:, 3 * LANES : 3 * LANES + 1]
    delta_ffn, gain_rows = rms_pull(ffn_out, gain_last, delta_out)
    late_gains[2:3, :] = jnp.sum(gain_rows, axis=0, keepdims=True)
    delta_ffn = delta_ffn.astype(jnp.bfloat16)
    delta_normed = jnp.zeros((CAP, D), jnp.float32)
    for at in parts:
        delta_hidden = times_transposed(delta_ffn, down_weight[at, :])
        gate = gates[:, at]
        raised = jnp.tanh(GELU_SCALE * (gate + 0.044715 * (gate * gate * gate)))
        share = 0.5 * (1.0 + raised)
        slope = share + (0.5 * GELU_SCALE) * gate * (1.0 - raised * raised) * (
            1.0 + (3 * 0.044715) * (gate * gate)
        )
        delta_gate[:, at] = (delta_hidden * ups[:, at] * slope).astype(jnp.bfloat16)
        delta_up[:, at] = (delta_hidden * (gate * share)).astype(jnp.bfloat16)
        delta_normed += times_transposed(delta_gate[:, at], gate_weight[:, at])
        delta_normed += times_transposed(delta_up[:, at], up_weight[:, at])
    delta_part, gain_rows = rms_pull(mid_stream, gain_mid, delta_normed)
    late_gains[1:2, :] = jnp.sum(gain_rows, axis=0, keepdims=True)
    delta_mid = delta_out + delta_part
    delta_mid_ref[...] = delta_mid
    delta_attn, gain_rows = rms_pull(attn_out[...], gain_post, delta_mid)
    late_gains[0:1, :] = jnp.sum(gain_rows, axis=0, keepdims=True)
    delta_attn_ref[...] = delta_attn.astype(jnp.bfloat16)
    turned = normed_mid.T
    spread_grads(
        spread,
        (
            (turned, lambda low, high: delta_gate[:, low:high], FF),
            (turned, lambda low, high: delta_up[:, low:high], FF),
            (hidden[...].T, lambda low, high: delta_ffn[:, low:high], D),
        ),
    )
    place_blocks(FFN_PADDED, plan_out, device, spread, None, targets)


def run_ffn(
    plan_in, staged, plan_out, block_shapes, device, mid, attn_out, cotangent, tables, gains, arrays
):
    flat_rows = G2LEN // LANES + FFN_PADDED
    shapes = [
        jax.ShapeDtypeStruct((CAP, D), jnp.bfloat16),
        jax.ShapeDtypeStruct((CAP, D), jnp.float32),
        jax.ShapeDtypeStruct((CAP, D), jnp.bfloat16),
        jax.ShapeDtypeStruct((3, D), jnp.float32),
    ] + [jax.ShapeDtypeStruct(shape, jnp.bfloat16) for shape in block_shapes]
    wide = pltpu.VMEM((CAP, FF), jnp.float32)
    narrow = pltpu.VMEM((CAP, FF), jnp.bfloat16)
    return pl.pallas_call(
        functools.partial(ffn_kernel, plan_in, staged, plan_out),
        out_shape=shapes,
        in_specs=[pl.BlockSpec(memory_space=pltpu.SMEM)]
        + whole_specs(5)
        + [pl.BlockSpec(memory_space=pltpu.HBM)] * len(arrays),
        out_specs=whole_specs(len(shapes)),
        scratch_shapes=[
            pltpu.VMEM((flat_rows, LANES), jnp.float32),
            pltpu.VMEM((D, FF), jnp.bfloat16),
            pltpu.VMEM((D, FF), jnp.bfloat16),
            pltpu.VMEM((FF, D), jnp.bfloat16),
            wide,
            wide,
            narrow,
            narrow,
            narrow,
            pltpu.SemaphoreType.DMA((len(arrays),)),
        ],
        compiler_params=pltpu.CompilerParams(vmem_limit_bytes=44 << 20),
        cost_estimate=pl.CostEstimate(flops=0, bytes_accessed=0, transcendentals=0),
    )(device, mid, attn_out, cotangent, tables, gains, *arrays)


def attn_back_kernel(
    plan,
    gain_len,
    device_ref,
    delta_attn,
    delta_mid,
    hidden_in,
    tables,
    gains,
    late_gains,
    qkv_weight,
    out_weight,
    grad_in,
    gain_grads,
    *refs,
):
    targets = refs[:-4]
    spread, tails, delta_raws, contexts = refs[-4:]
    device = device_ref[0]
    normed_in, key_raw, values, keys, heads, cos_tab, sin_tab = attn_forward(
        hidden_in, qkv_weight, tables, gains
    )
    gain_query = gains[:, D : D + HD]
    gain_key = gains[:, D + HD : D + 2 * HD]
    delta_context = times_transposed(delta_attn[...], out_weight[...]).astype(jnp.bfloat16)
    delta_key = jnp.zeros((CAP, HD), jnp.float32)
    delta_value = jnp.zeros((CAP, HD), jnp.float32)
    query_gain_rows = jnp.zeros((CAP, HD), jnp.float32)
    for head, (query_raw, queries, scores, log_total, context) in enumerate(heads):
        at = slice(head * HD, (head + 1) * HD)
        contexts[:, at] = context
        head_delta = delta_context[:, at]
        row_dot = jnp.sum(
            head_delta.astype(jnp.float32) * context.astype(jnp.float32), axis=-1, keepdims=True
        )
        prob_exact = jnp.exp(scores - log_total)
        delta_prob = times_transposed(head_delta, values)
        delta_score = prob_exact * (delta_prob - row_dot)
        turned = delta_score.T.astype(jnp.bfloat16)
        delta_score = delta_score.astype(jnp.bfloat16)
        delta_query = jnp.dot(delta_score, keys, preferred_element_type=jnp.float32)
        delta_key += jnp.dot(turned, queries, preferred_element_type=jnp.float32)
        delta_value += jnp.dot(
            prob_exact.T.astype(jnp.bfloat16), head_delta, preferred_element_type=jnp.float32
        )
        delta_rot = rotate_pull(delta_query * HD ** (-0.5), cos_tab, sin_tab)
        delta_raw, gain_rows = rms_pull(query_raw, gain_query, delta_rot)
        query_gain_rows += gain_rows
        delta_raws[:, at] = delta_raw.astype(jnp.bfloat16)
    delta_raw, gain_rows = rms_pull(key_raw, gain_key, rotate_pull(delta_key, cos_tab, sin_tab))
    delta_raws[:, HQ : HQ + HD] = delta_raw.astype(jnp.bfloat16)
    delta_raws[:, HQ + HD :] = delta_value.astype(jnp.bfloat16)
    gain_grads[:, D : D + HD] = jnp.sum(query_gain_rows, axis=0, keepdims=True)
    gain_grads[:, D + HD : D + 2 * HD] = jnp.sum(gain_rows, axis=0, keepdims=True)
    delta_in = times_transposed(delta_raws[...], qkv_weight[...])
    delta_part, gain_rows = rms_pull(
        hidden_in[...].astype(jnp.float32), gains[:, :D], delta_in
    )
    grad_in[...] = delta_mid[...] + delta_part
    gain_grads[:, :D] = jnp.sum(gain_rows, axis=0, keepdims=True)
    for late in range(3):
        at = slice((late + 1) * D + 2 * HD, (late + 2) * D + 2 * HD)
        gain_grads[:, at] = late_gains[late : late + 1, :]
    if gain_len:
        tails[...] = jnp.zeros_like(tails)
        lane = lax.broadcasted_iota(jnp.int32, (1, LANES), 1)
        for owner in range(tails.shape[0]):
            row, shift = divmod(owner * gain_len, LANES)
            piece = gain_grads[:, row * LANES : (row + 1) * LANES]
            if shift:
                piece = pltpu.roll(piece, LANES - shift, 1)
            if shift + gain_len > LANES:
                after = gain_grads[:, (row + 1) * LANES : (row + 2) * LANES]
                after = pltpu.roll(after, LANES - shift, 1)
                piece = jnp.where(lane < LANES - shift, piece, after)
            tails[owner, 0:1, :] = jnp.where(lane < gain_len, piece, 0.0)
    turned = normed_in.T
    delta_attn_value = delta_attn[...]
    spread_grads(
        spread,
        (
            (turned, lambda low, high: delta_raws[:, low:high], HQ),
            (turned, lambda low, high: delta_raws[:, HQ + low : HQ + high], HD),
            (turned, lambda low, high: delta_raws[:, HQ + HD + low : HQ + HD + high], HD),
            (contexts[...].T, lambda low, high: delta_attn_value[:, low:high], D),
        ),
    )
    place_blocks(ATTN_PADDED, plan, device, spread, tails, targets)


def back_attn(plan, gain_len, tail_rows, devices, block_shapes, device, *inputs):
    flat_rows = G1LEN // LANES + ATTN_PADDED
    shapes = [
        jax.ShapeDtypeStruct((CAP, D), jnp.float32),
        jax.ShapeDtypeStruct((1, 4 * D + 2 * HD), jnp.float32),
    ] + [jax.ShapeDtypeStruct(shape, jnp.bfloat16) for shape in block_shapes]
    tail_shape = (devices, tail_rows, LANES) if gain_len else (1, ROWS, LANES)
    return pl.pallas_call(
        functools.partial(attn_back_kernel, plan, gain_len),
        out_shape=shapes,
        in_specs=[pl.BlockSpec(memory_space=pltpu.SMEM)] + whole_specs(len(inputs)),
        out_specs=whole_specs(len(shapes)),
        scratch_shapes=[
            pltpu.VMEM((flat_rows, LANES), jnp.float32),
            pltpu.VMEM(tail_shape, jnp.float32),
            pltpu.VMEM((CAP, HQ + 2 * HD), jnp.bfloat16),
            pltpu.VMEM((CAP, HQ), jnp.bfloat16),
        ],
        compiler_params=pltpu.CompilerParams(vmem_limit_bytes=22 << 20),
        cost_estimate=pl.CostEstimate(flops=0, bytes_accessed=0, transcendentals=0),
    )(device, *inputs)


def gathered_blocks(chunks, cuts, orders, each, devices, device):
    arrays, windows, plan, start = [], [], [], 0
    for blocks, (low, high), order in zip(chunks, cuts, orders):
        take = min(high - low, each - start)
        if each % ROWS:
            places = [offset_of(place, list(order) + [0]) for place in range(devices)]
            back = sorted(range(devices), key=places.__getitem__)
            mixed = offset_bits(device[0], list(order) + [0])
            table = jnp.take(jnp.concatenate(blocks), jnp.array(back, jnp.int32) ^ mixed, axis=0)
            arrays.append(table[:, low:high])
            continue
        for part, block in enumerate(blocks):
            plan.append((order[:-1], offset_of(part, [order[-1], 0]), take, start, each))
            windows.append((low, high - low))
            arrays.append(block)
        start += take
    if each % ROWS == 0:
        return arrays, windows, plan, None
    table = jnp.concatenate(arrays, axis=1)
    flat = table[:, :each].reshape(1, devices * each, LANES)
    return [flat], [(0, devices * each)], [([], 0, devices * each, 0, 0)], table[:, each:]


def offset_bits(device, order):
    return sum(((device >> bit) & 1) << k for k, bit in enumerate(order))


def scatter_plan(each, tail_rows, orders, devices):
    parts = cut_rows(each + tail_rows, len(orders))
    half = devices // 2
    if each % ROWS:
        return [(0, [], 0, 0, devices * each, 0, 0)], [(1, devices * each, LANES)], parts
    plan = []
    for with_core in (1, 0):
        for (low, high), order in zip(parts, orders):
            order = order[::-1]
            plan.append((with_core, order, with_core, low, min(high, each) - low, low, each))
            if high > each:
                plan.append((with_core, order, with_core, each, tail_rows, None, each))
    return plan, [(half, each + tail_rows, LANES)] * 2, parts


def blocks_of(found, tails, parts, orders, devices, device):
    if len(found) == 2:
        return found
    table = found[0].reshape(devices, -1, LANES)
    table = table if tails is None else jnp.concatenate([table, tails], axis=1)
    blocks = []
    for with_core in (0, 1):
        chunks = []
        for (low, high), order in zip(parts, orders):
            places = range(devices // 2)
            offsets = [offset_of(place, order[::-1]) ^ with_core for place in places]
            owners = jnp.array(offsets, jnp.int32) ^ device[0]
            chunks.append(jnp.take(table[:, low:high], owners, axis=0))
        blocks.append(jnp.concatenate(chunks, axis=1))
    return blocks


def merge_kernel(parts, *refs):
    pairs = ((refs[0], refs[1]), (refs[2], refs[3]))
    targets = refs[4:]
    half = refs[0].shape[0] // 2
    for number, target in enumerate(targets):
        chunk, second = divmod(number, 2)

        @pl.loop(0, half)
        def _(index, target=target, chunk=chunk, first=second * half):
            at = 0
            for (home, came), (low, high) in zip(pairs, parts[chunk]):
                total = home[first + index, low:high, :].astype(jnp.float32)
                total += came[first + index, low:high, :].astype(jnp.float32)
                target[index, at : at + high - low, :] = total.astype(jnp.bfloat16)
                at += high - low


def cores_merged(parts, *blocks):
    half = blocks[0].shape[0] // 2
    if any((high - low) % ROWS for chunk in parts for low, high in chunk):
        pairs = (blocks[:2], blocks[2:])
        joined = []
        for chunk in parts:
            sums = [
                home[:, low:high].astype(jnp.float32) + came[:, low:high].astype(jnp.float32)
                for (home, came), (low, high) in zip(pairs, chunk)
            ]
            total = jnp.concatenate(sums, axis=1).astype(jnp.bfloat16)
            joined.append((total[:half], total[half:]))
        return joined
    shapes = [
        jax.ShapeDtypeStruct((half, sum(high - low for low, high in chunk), LANES), jnp.bfloat16)
        for chunk in parts
        for _ in range(2)
    ]
    found = pl.pallas_call(
        functools.partial(merge_kernel, parts),
        out_shape=shapes,
        in_specs=whole_specs(4),
        out_specs=whole_specs(len(shapes)),
        compiler_params=pltpu.CompilerParams(vmem_limit_bytes=20 << 20),
        cost_estimate=pl.CostEstimate(flops=0, bytes_accessed=0, transcendentals=0),
    )(*blocks)
    return list(zip(found[::2], found[1::2]))


def adam_update(weight_shard, gradient, moment_one, moment_two):
    moment_one = 0.9 * moment_one + 0.1 * gradient
    moment_two = 0.999 * moment_two + 0.001 * gradient * gradient
    fix_one = 1.0 - 0.9**STEP
    fix_two = 1.0 - 0.999**STEP
    weight_shard = weight_shard - 0.02 * (
        moment_one / fix_one / (jnp.sqrt(moment_two / fix_two) + 1e-08) + 0.1 * weight_shard
    )
    return (weight_shard, moment_one, moment_two)


def per_device(hidden_in, cotangent, params, moment_one, moment_two, seq_lengths, seq_owner):
    devices = lax.axis_size("dp")
    device = lax.axis_index("dp").astype(jnp.int32)
    here = device.reshape(1)
    attn_len = G1LEN // devices
    ffn_len = G2LEN // devices
    gain_len = params.shape[0] - attn_len - ffn_len
    attn_rows = attn_len // LANES
    tail_rows = -(-(attn_rows + 1) // ROWS) * ROWS - attn_rows
    pad = tail_rows * LANES - gain_len
    rounded = params.astype(jnp.bfloat16)
    first_piece = jnp.concatenate(
        [rounded[:attn_len], rounded[attn_len + ffn_len :], jnp.zeros((pad,), jnp.bfloat16)]
    ).reshape(-1, LANES)
    second_piece = rounded[attn_len : attn_len + ffn_len].reshape(-1, LANES)
    ffn_rows = ffn_len // LANES
    orders = bit_orders(devices, ("abxy", "bxya", "byax"))
    ffn_parts = cut_rows(ffn_rows, 3)
    attn_parts = cut_rows(attn_rows + tail_rows, 3)
    pieces, attn_cuts = [], []
    for chunk, (low, high) in enumerate(ffn_parts):
        piece = second_piece[low:high]
        if chunk < len(attn_parts):
            attn_cuts.append((high - low, high - low + attn_parts[chunk][1] - attn_parts[chunk][0]))
            piece = jnp.concatenate([piece, first_piece[slice(*attn_parts[chunk])]])
        pieces.append(piece)
    chunks = [gather_chunk(piece, order, devices) for piece, order in zip(pieces, orders)]
    arrays, attn_windows, plan, tails = gathered_blocks(
        chunks, attn_cuts, orders, attn_rows, devices, here
    )
    ffn_cuts = [(0, high - low) for low, high in ffn_parts]
    ffn_arrays, ffn_windows, ffn_plan, unused = gathered_blocks(
        chunks, ffn_cuts, orders, ffn_rows, devices, here
    )
    aligned = attn_rows % ROWS == 0
    tables = slot_setup(seq_lengths, seq_owner, device)
    given = None
    if not aligned:
        given = tails.reshape(devices, -1)[:, :gain_len].astype(jnp.float32).reshape(1, -1)
    qkv_weight, out_weight, gains, attn_out, mid_stream = forward_attn(
        plan,
        attn_windows,
        gain_len if aligned else 0,
        tail_rows,
        devices,
        here,
        hidden_in,
        tables,
        given,
        arrays,
    )
    orders = bit_orders(devices, ("yxba", "ayxb", "xayb"))
    out_plan, block_shapes, ffn_parts = scatter_plan(ffn_rows, 0, orders, devices)
    staged = [(0, 0, 0, *ffn_windows[0])]
    if len(block_shapes) == 2:
        staged = [
            (part // 2, part % 2 * (devices // 4), low, 0, high - low)
            for low, high in ffn_parts
            for part in range(4)
        ]
    block_out, delta_mid, delta_attn, late_gains, *found = run_ffn(
        ffn_plan,
        staged,
        out_plan,
        block_shapes,
        here,
        mid_stream,
        attn_out,
        cotangent,
        tables,
        gains,
        ffn_arrays,
    )
    ffn_home, ffn_away = blocks_of(found, None, ffn_parts, orders, devices, here)
    ffn_came = across(ffn_away, 0, devices)
    attn_plan, block_shapes, attn_parts = scatter_plan(attn_rows, tail_rows, orders, devices)
    grad_in, gain_grads, *found = back_attn(
        attn_plan,
        gain_len if aligned else 0,
        tail_rows,
        devices,
        block_shapes,
        here,
        delta_attn,
        delta_mid,
        hidden_in,
        tables,
        gains,
        late_gains,
        qkv_weight,
        out_weight,
    )
    gain_table = None
    if not aligned:
        gain_table = gain_grads.reshape(devices, gain_len).astype(jnp.bfloat16)
        gain_table = jnp.pad(gain_table, ((0, 0), (0, pad))).reshape(devices, tail_rows, LANES)
    attn_home, attn_away = blocks_of(found, gain_table, attn_parts, orders, devices, here)
    attn_came = across(attn_away, 0, devices)
    parts = [
        [cut[chunk] for cut in (ffn_parts, attn_parts) if chunk < len(cut)]
        for chunk in range(len(ffn_parts))
    ]
    chunks = cores_merged(parts, ffn_home, ffn_came, attn_home, attn_came)
    for stage in range(len(orders[0])):
        chunks = merged_blocks(chunks, sent_blocks(chunks, orders, stage, devices))
    rows = [chunk for chunk, _ in chunks]
    ffn_take = [high - low for low, high in ffn_parts]
    ffn_shard = [chunk[:take].reshape(-1) for chunk, take in zip(rows, ffn_take)]
    attn_shard = jnp.concatenate([chunk[take:].reshape(-1) for chunk, take in zip(rows, ffn_take)])
    grad_shard = jnp.concatenate(
        [attn_shard[:attn_len], *ffn_shard, attn_shard[attn_len : attn_len + gain_len]]
    )
    params_new, moment_one_new, moment_two_new = adam_update(
        params, grad_shard, moment_one, moment_two
    )
    return (block_out, grad_in, grad_shard, params_new, moment_one_new, moment_two_new)


def solution(mesh):
    in_specs = (P("dp", None), P("dp", None), P("dp"), P("dp"), P("dp"), P(), P())
    out_specs = (P("dp", None), P("dp", None), P("dp"), P("dp"), P("dp"), P("dp"))
    return jax.shard_map(
        per_device, mesh=mesh, in_specs=in_specs, out_specs=out_specs, check_vma=False
    )
```

```python
import functools
import math

import jax
import jax.numpy as jnp
from jax import lax
from jax.experimental import pallas as pl
from jax.experimental.pallas import tpu as pltpu
from jax.sharding import PartitionSpec as P

D = 640
FF = 2048
HD = 256
HQ = 1024
CAP = 128
WINDOW = 64
STEP = 3
G1LEN = 1638400
G2LEN = 3932160
LANES = 128
ROWS = 16
GELU_SCALE = math.sqrt(2 / math.pi)
ATTN_PADDED, FFN_PADDED = 0, 2 * D


def rms_scale(values, gain_vec):
    return (
        values
        * lax.rsqrt(jnp.mean(values * values, axis=-1, keepdims=True) + 1e-06)
        * (1.0 + gain_vec)
    )


def rotate(values, cos_tab, sin_tab):
    half_dim = values.shape[-1] // 2
    lower_half = values[..., :half_dim]
    upper_half = values[..., half_dim:]
    return jnp.concatenate(
        [lower_half * cos_tab - upper_half * sin_tab, upper_half * cos_tab + lower_half * sin_tab],
        axis=-1,
    )


def gated_gelu(gate_proj, up_proj):
    return jax.nn.gelu(gate_proj, approximate=True) * up_proj


def times_transposed(rows_in, matrix):
    return lax.dot_general(
        rows_in, matrix, (((1,), (1,)), ((), ())), preferred_element_type=jnp.float32
    )


def slot_setup(seq_lengths, seq_owner, device):
    mine_mask = seq_owner == device
    own_lengths = jnp.where(mine_mask, seq_lengths, 0)
    seq_ends = jnp.cumsum(own_lengths, dtype=jnp.int32)
    seq_begins = seq_ends - own_lengths
    slot_index = jnp.arange(CAP, dtype=jnp.int32)
    column = slot_index[:, None]
    inside_mask = (
        mine_mask[None, :] & (seq_begins[None, :] <= column) & (column < seq_ends[None, :])
    )
    live_mask = jnp.any(inside_mask, axis=1)
    seq_label = jnp.sum(
        (mine_mask[None, :] & (seq_ends[None, :] <= column)).astype(jnp.int32),
        axis=1,
        dtype=jnp.int32,
    )
    position = jnp.sum(
        jnp.where(inside_mask, column - seq_begins[None, :], 0), axis=1, dtype=jnp.int32
    )
    row_slot = slot_index[:, None]
    col_slot = slot_index[None, :]
    allowed = live_mask[:, None] & live_mask[None, :] & (
        seq_label[:, None] == seq_label[None, :]
    ) & (col_slot <= row_slot) & (row_slot - col_slot < WINDOW) | (row_slot == col_slot)
    half_dim = HD // 2
    frequency = 10000.0 ** (-2.0 * jnp.arange(half_dim, dtype=jnp.float32) / HD)
    angles = position.astype(jnp.float32)[:, None] * frequency[None, :]
    live_wide = jnp.broadcast_to(live_mask[:, None], (CAP, LANES)).astype(jnp.float32)
    return jnp.concatenate(
        [jnp.cos(angles), jnp.sin(angles), allowed.astype(jnp.float32), live_wide], axis=1
    )


def rms_pull(raw, gain_vec, delta):
    scale = lax.rsqrt(jnp.mean(raw * raw, axis=-1, keepdims=True) + 1e-06)
    weighed = delta * (1.0 + gain_vec)
    shared = jnp.mean(raw * weighed, axis=-1, keepdims=True)
    return scale * weighed - raw * (scale * scale * scale * shared), delta * raw * scale


def rotate_pull(delta, cos_tab, sin_tab):
    half_dim = delta.shape[-1] // 2
    lower_half = delta[:, :half_dim]
    upper_half = delta[:, half_dim:]
    return jnp.concatenate(
        [lower_half * cos_tab + upper_half * sin_tab, upper_half * cos_tab - lower_half * sin_tab],
        axis=-1,
    )


def bit_orders(devices, tuned):
    bits = devices.bit_length() - 1
    if bits == 5:
        return [["cxyab".index(letter) for letter in order] for order in tuned]
    return [[1 + (shift + step) % (bits - 1) for step in range(bits - 1)] for shift in range(3)]


def across(block, bit, devices):
    return lax.ppermute(block, "dp", [(i, i ^ (1 << bit)) for i in range(devices)])


def offset_of(place, order):
    return sum(((place >> k) & 1) << bit for k, bit in enumerate(order))


def gather_chunks(pieces, orders, devices):
    held = [piece[None] for piece in pieces]
    for stage in range(len(orders[0]) - 1):
        came = [across(block, order[stage], devices) for block, order in zip(held, orders)]
        for chunk in range(1, len(came)):
            came[chunk] = lax.optimization_barrier((came[chunk], came[0]))[0]
        held = [jnp.concatenate(pair) for pair in zip(held, came)]
    last = [across(block, order[-1], devices) for block, order in zip(held, orders)]
    chunks = []
    for block, final in zip(held, last):
        if chunks:
            final = lax.optimization_barrier((final, *chunks[0][2:]))[0]
        chunks.append((block, final, across(block, 0, devices), across(final, 0, devices)))
    return chunks


def sent_blocks(chunks, orders, stage, devices):
    return [
        across(away, order[stage], devices)
        for (_, away), order in zip(chunks, orders)
    ]


def merged_blocks(chunks, came):
    merged = []
    for (home, _), arrived in zip(chunks, came):
        half = home.shape[0] // 2

        def added(low, high):
            return home[low:high].astype(jnp.float32) + arrived[low:high].astype(jnp.float32)

        if half:
            merged.append(
                (
                    added(0, half).astype(jnp.bfloat16),
                    added(half, 2 * half).astype(jnp.bfloat16),
                )
            )
        else:
            merged.append((added(0, 1)[0], None))
    return merged


def cut_rows(rows, parts):
    each = -(-rows // (parts * ROWS)) * ROWS
    return [(low, min(low + each, rows)) for low in range(0, rows, each)]


def whole_specs(count):
    return [pl.BlockSpec(memory_space=pltpu.VMEM)] * count


def owner_rows(device, index, order, extra, start, each):
    owner = device ^ extra
    for k, bit in enumerate(order):
        owner = owner ^ (((index >> k) & 1) << bit)
    return owner, owner * each + start


def copy_step(rows):
    return max(step for step in range(ROWS, 513, ROWS) if rows % step == 0)


def each_piece(padded, first, take, visit):
    def visit_plain(shift):
        step = copy_step(take)

        def visit_step(part):
            at = part * step
            visit(at, step, pl.multiple_of(first + shift + at, ROWS))

        if take == step:
            visit_step(0)
        else:
            pl.loop(0, take // step)(visit_step)

    if not padded:
        visit_plain(0)
        return
    units = take // ROWS
    inner = max(count for count in range(1, 41) if units % count == 0)
    number = first // ROWS

    def visit_units(row_of):
        def visit_some(step):
            for part in range(inner):
                at = (step * inner + part) * ROWS
                visit(at, ROWS, row_of(step * inner + part))

        if units == inner:
            visit_some(0)
        else:
            pl.loop(0, units // inner)(visit_some)

    longer = (ROWS + 1) * number
    pl.when(number + units <= padded)(lambda: visit_units(lambda k: longer + (ROWS + 1) * k))
    pl.when(number >= padded)(lambda: visit_plain(padded))
    pl.when((number < padded) & (number + units > padded))(
        lambda: visit_units(lambda k: ROWS * (number + k) + jnp.minimum(number + k, padded))
    )


def spread_blocks(padded, plan, views, device, spread, tails):
    for (order, extra, take, start, each), (block_ref, first_index, count, first_row) in zip(
        plan, views
    ):

        @pl.loop(0, count)
        def _(
            index,
            order=order,
            extra=extra,
            take=take,
            start=start,
            each=each,
            block_ref=block_ref,
            first_index=first_index,
            first_row=first_row,
        ):
            owner, first = owner_rows(device, index, order, extra, start, each)

            def spread_unit(at, unit, row):
                low = first_row + at
                if not isinstance(low, int):
                    low = pl.multiple_of(low, ROWS)
                spread[pl.ds(row, unit), :] = block_ref[
                    first_index + index, pl.ds(low, unit), :
                ].astype(jnp.float32)

            each_piece(padded, first, take, spread_unit)
            if tails is not None:
                tails[owner] = block_ref[index, take : take + tails.shape[1], :]


def pitch_of(columns):
    blocks = columns // LANES
    return blocks + (blocks == ROWS)


def fold_matrices(spread, targets):
    first = 0
    for matrix, offset, rows, columns in targets:
        blocks = columns // LANES
        pitch = pitch_of(columns)

        @pl.loop(0, rows // LANES)
        def _(step, matrix=matrix, offset=offset, blocks=blocks, pitch=pitch, first=first):
            base = first + step * (LANES * pitch)
            at = pl.ds(pl.multiple_of(step * LANES, LANES), LANES)
            for block in range(blocks):
                low = offset + block * LANES
                matrix[at, low : low + LANES] = spread[
                    pl.ds(base + block, LANES, stride=pitch), :
                ].astype(jnp.bfloat16)

        first += rows * pitch


def spread_grads(spread, products):
    first = 0
    for turned, right, columns in products:
        rows = turned.shape[0]
        blocks = columns // LANES
        pitch = pitch_of(columns)
        wide = 2 - blocks % 2
        for block in range(0, blocks, wide):
            product = jnp.dot(
                turned,
                right(block * LANES, (block + wide) * LANES),
                preferred_element_type=jnp.float32,
            )
            for part in range(wide):
                spread[pl.ds(first + block + part, rows, stride=pitch), :] = product[
                    :, part * LANES : (part + 1) * LANES
                ]
        first += rows * pitch


def place_blocks(padded, plan, device, spread, tails, targets):
    for target, order, extra, low, take, start, each in plan:
        target_ref = targets[target]

        @pl.loop(0, target_ref.shape[0])
        def _(
            index,
            target_ref=target_ref,
            order=order,
            extra=extra,
            low=low,
            take=take,
            start=start,
            each=each,
        ):
            owner, first = owner_rows(device, index, order, extra, start or 0, each)
            if start is None:
                target_ref[index, low : low + take, :] = tails[owner].astype(jnp.bfloat16)
                return

            def place_unit(at, unit, row):
                at = low + at
                if not isinstance(at, int):
                    at = pl.multiple_of(at, ROWS)
                target_ref[index, pl.ds(at, unit), :] = spread[pl.ds(row, unit), :].astype(
                    jnp.bfloat16
                )

            each_piece(padded, first, take, place_unit)


def attn_forward(hidden_in, qkv_weight, tables, gains):
    cos_tab = tables[:, :LANES]
    sin_tab = tables[:, LANES : 2 * LANES]
    open_pairs = tables[:, 2 * LANES : 3 * LANES] > 0.0
    gain_query = gains[:, D : D + HD]
    gain_key = gains[:, D + HD : D + 2 * HD]
    normed_in = rms_scale(hidden_in[...].astype(jnp.float32), gains[:, :D]).astype(jnp.bfloat16)
    raw = jnp.dot(normed_in, qkv_weight[...], preferred_element_type=jnp.float32)
    key_raw = raw[:, HQ : HQ + HD]
    values = raw[:, HQ + HD :].astype(jnp.bfloat16)
    keys = rotate(rms_scale(key_raw, gain_key), cos_tab, sin_tab).astype(jnp.bfloat16)
    heads = []
    for head in range(HQ // HD):
        query_raw = raw[:, head * HD : (head + 1) * HD]
        rot_query = rotate(rms_scale(query_raw, gain_query), cos_tab, sin_tab) * HD ** (-0.5)
        rot_query = rot_query.astype(jnp.bfloat16)
        scores = jnp.where(open_pairs, times_transposed(rot_query, keys), -1e30)
        row_max = jnp.max(scores, axis=-1, keepdims=True)
        raised = jnp.exp(scores - row_max)
        summed = jnp.sum(raised, axis=-1, keepdims=True)
        context = jnp.dot(
            (raised / summed).astype(jnp.bfloat16), values, preferred_element_type=jnp.float32
        ).astype(jnp.bfloat16)
        heads.append((query_raw, rot_query, scores, row_max + jnp.log(summed), context))
    return normed_in, key_raw, values, keys, heads, cos_tab, sin_tab


def join_gains(tails, gain_len, gains):
    lane = lax.broadcasted_iota(jnp.int32, (1, LANES), 1)
    tiles = [jnp.zeros((1, LANES), jnp.float32) for _ in range(gains.shape[1] // LANES)]
    for owner in range(tails.shape[0]):
        tile, shift = divmod(owner * gain_len, LANES)
        run = jnp.where(lane < gain_len, tails[owner].astype(jnp.float32)[0:1, :], 0.0)
        if shift:
            run = pltpu.roll(run, shift, 1)
        tiles[tile] += jnp.where(lane >= shift, run, 0.0)
        if shift + gain_len > LANES:
            tiles[tile + 1] += jnp.where(lane < shift, run, 0.0)
    for number, tile in enumerate(tiles):
        gains[:, number * LANES : (number + 1) * LANES] = tile


def attn_forward_kernel(plan, gain_len, device_ref, hidden_in, tables, *refs):
    if not gain_len:
        given, refs = refs[0], refs[1:]
    sources = refs[: len(plan)]
    refs = refs[len(plan) :]
    qkv_weight, out_weight, gains, attn_out, mid_stream = refs[:5]
    staging, spread, tails, context, sems = refs[5:]
    copies, views = [], []
    for number, source in enumerate(sources):
        count = source.shape[0]
        held = staging.at[pl.ds(number * count, count)]
        copies.append(pltpu.make_async_copy(source, held, sems.at[number]))
        views.append((held, 0, count, 0))
    for copy in copies:
        copy.start()
    for copy, step, view in zip(copies, plan, views):
        copy.wait()
        spread_blocks(
            ATTN_PADDED,
            [step],
            [view],
            device_ref[0],
            spread,
            tails if gain_len else None,
        )
    if gain_len:
        join_gains(tails, gain_len, gains)
    else:
        gains[...] = given[...]
    fold_matrices(
        spread,
        (
            (qkv_weight, 0, D, HQ),
            (qkv_weight, HQ, D, HD),
            (qkv_weight, HQ + HD, D, HD),
            (out_weight, 0, HQ, D),
        ),
    )
    heads = attn_forward(hidden_in, qkv_weight, tables, gains)[4]
    for head, parts in enumerate(heads):
        context[:, head * HD : (head + 1) * HD] = parts[-1]
    out = jnp.dot(context[...], out_weight[...], preferred_element_type=jnp.float32)
    attn_out[...] = out
    gain_post = gains[:, D + 2 * HD : 2 * D + 2 * HD]
    mid_stream[...] = hidden_in[...].astype(jnp.float32) + rms_scale(out, gain_post)


def forward_attn(plan, gain_len, tail_rows, devices, device, hidden_in, tables, given, arrays):
    shapes = [
        jax.ShapeDtypeStruct((D, HQ + 2 * HD), jnp.bfloat16),
        jax.ShapeDtypeStruct((HQ, D), jnp.bfloat16),
        jax.ShapeDtypeStruct((1, 4 * D + 2 * HD), jnp.float32),
        jax.ShapeDtypeStruct((CAP, D), jnp.float32),
        jax.ShapeDtypeStruct((CAP, D), jnp.float32),
    ]
    given = [] if gain_len else [given]
    held = (sum(array.shape[0] for array in arrays),) + arrays[0].shape[1:]
    return pl.pallas_call(
        functools.partial(attn_forward_kernel, plan, gain_len),
        out_shape=shapes,
        in_specs=[pl.BlockSpec(memory_space=pltpu.SMEM)]
        + whole_specs(2 + len(given))
        + [pl.BlockSpec(memory_space=pltpu.HBM)] * len(arrays),
        out_specs=whole_specs(len(shapes)),
        scratch_shapes=[
            pltpu.VMEM(held, jnp.bfloat16),
            pltpu.VMEM((G1LEN // LANES + ATTN_PADDED, LANES), jnp.float32),
            pltpu.VMEM((devices, tail_rows, LANES) if gain_len else (1, ROWS, LANES), jnp.bfloat16),
            pltpu.VMEM((CAP, HQ), jnp.bfloat16),
            pltpu.SemaphoreType.DMA((len(arrays),)),
        ],
        compiler_params=pltpu.CompilerParams(vmem_limit_bytes=24 << 20),
        cost_estimate=pl.CostEstimate(flops=0, bytes_accessed=64 << 20, transcendentals=0),
    )(device, hidden_in, tables, *given, *arrays)


def ffn_kernel(
    plan_in,
    staged,
    plan_out,
    device_ref,
    mid_ref,
    attn_out,
    cotangent,
    tables,
    gains,
    *refs,
):
    sources = refs[: len(plan_in)]
    refs = refs[len(plan_in) :]
    block_out, delta_mid_ref, delta_attn_ref, late_gains = refs[:4]
    targets = refs[4:-10]
    spread, gate_weight, up_weight, down_weight = refs[-10:-6]
    gates, ups, hidden, delta_gate, delta_up, sems = refs[-6:]
    device = device_ref[0]
    copies, views = [], []
    for source, (target, first_index, first_row) in zip(sources, staged):
        count, rows = source.shape[:2]
        held = targets[target]
        copies.append(
            pltpu.make_async_copy(
                source,
                held.at[pl.ds(first_index, count), pl.ds(first_row, rows), :],
                sems.at[len(copies)],
            )
        )
        views.append((held, first_index, count, first_row))
    for copy in copies:
        copy.start()
    mid_stream = mid_ref[...]
    gain_post = gains[:, D + 2 * HD : 2 * D + 2 * HD]
    gain_mid = gains[:, 2 * D + 2 * HD : 3 * D + 2 * HD]
    gain_last = gains[:, 3 * D + 2 * HD :]
    normed_mid = rms_scale(mid_stream, gain_mid).astype(jnp.bfloat16)
    for copy, plan, view in zip(copies, plan_in, views):
        copy.wait()
        spread_blocks(FFN_PADDED, [plan], [view], device, spread, None)
    fold_matrices(
        spread, ((gate_weight, 0, D, FF), (up_weight, 0, D, FF), (down_weight, 0, FF, D))
    )
    parts = [slice(low, low + 512) for low in range(0, FF, 512)]
    for at in parts:
        gate = jnp.dot(normed_mid, gate_weight[:, at], preferred_element_type=jnp.float32)
        up = jnp.dot(normed_mid, up_weight[:, at], preferred_element_type=jnp.float32)
        gates[:, at] = gate
        ups[:, at] = up
        hidden[:, at] = gated_gelu(gate, up).astype(jnp.bfloat16)
    ffn_out = jnp.dot(hidden[...], down_weight[...], preferred_element_type=jnp.float32)
    block_out[...] = (mid_stream + rms_scale(ffn_out, gain_last)).astype(jnp.bfloat16)
    delta_out = cotangent[...].astype(jnp.float32) * tables[:, 3 * LANES : 3 * LANES + 1]
    delta_ffn, gain_rows = rms_pull(ffn_out, gain_last, delta_out)
    late_gains[2:3, :] = jnp.sum(gain_rows, axis=0, keepdims=True)
    delta_ffn = delta_ffn.astype(jnp.bfloat16)
    delta_normed = jnp.zeros((CAP, D), jnp.float32)
    for at in parts:
        delta_hidden = times_transposed(delta_ffn, down_weight[at, :])
        gate = gates[:, at]
        raised = jnp.tanh(GELU_SCALE * (gate + 0.044715 * (gate * gate * gate)))
        share = 0.5 * (1.0 + raised)
        slope = share + (0.5 * GELU_SCALE) * gate * (1.0 - raised * raised) * (
            1.0 + (3 * 0.044715) * (gate * gate)
        )
        delta_gate[:, at] = (delta_hidden * ups[:, at] * slope).astype(jnp.bfloat16)
        delta_up[:, at] = (delta_hidden * (gate * share)).astype(jnp.bfloat16)
        delta_normed += times_transposed(delta_gate[:, at], gate_weight[:, at])
        delta_normed += times_transposed(delta_up[:, at], up_weight[:, at])
    delta_part, gain_rows = rms_pull(mid_stream, gain_mid, delta_normed)
    late_gains[1:2, :] = jnp.sum(gain_rows, axis=0, keepdims=True)
    delta_mid = delta_out + delta_part
    delta_mid_ref[...] = delta_mid
    delta_attn, gain_rows = rms_pull(attn_out[...], gain_post, delta_mid)
    late_gains[0:1, :] = jnp.sum(gain_rows, axis=0, keepdims=True)
    delta_attn_ref[...] = delta_attn.astype(jnp.bfloat16)
    turned = normed_mid.T
    spread_grads(
        spread,
        (
            (turned, lambda low, high: delta_gate[:, low:high], FF),
            (turned, lambda low, high: delta_up[:, low:high], FF),
            (hidden[...].T, lambda low, high: delta_ffn[:, low:high], D),
        ),
    )
    place_blocks(FFN_PADDED, plan_out, device, spread, None, targets)


def run_ffn(
    plan_in, staged, plan_out, block_shapes, device, mid, attn_out, cotangent, tables, gains, arrays
):
    flat_rows = G2LEN // LANES + FFN_PADDED
    shapes = [
        jax.ShapeDtypeStruct((CAP, D), jnp.bfloat16),
        jax.ShapeDtypeStruct((CAP, D), jnp.float32),
        jax.ShapeDtypeStruct((CAP, D), jnp.bfloat16),
        jax.ShapeDtypeStruct((3, D), jnp.float32),
    ] + [jax.ShapeDtypeStruct(shape, jnp.bfloat16) for shape in block_shapes]
    wide = pltpu.VMEM((CAP, FF), jnp.float32)
    narrow = pltpu.VMEM((CAP, FF), jnp.bfloat16)
    return pl.pallas_call(
        functools.partial(ffn_kernel, plan_in, staged, plan_out),
        out_shape=shapes,
        in_specs=[pl.BlockSpec(memory_space=pltpu.SMEM)]
        + whole_specs(5)
        + [pl.BlockSpec(memory_space=pltpu.HBM)] * len(arrays),
        out_specs=whole_specs(len(shapes)),
        scratch_shapes=[
            pltpu.VMEM((flat_rows, LANES), jnp.float32),
            pltpu.VMEM((D, FF), jnp.bfloat16),
            pltpu.VMEM((D, FF), jnp.bfloat16),
            pltpu.VMEM((FF, D), jnp.bfloat16),
            wide,
            wide,
            narrow,
            narrow,
            narrow,
            pltpu.SemaphoreType.DMA((len(arrays),)),
        ],
        compiler_params=pltpu.CompilerParams(vmem_limit_bytes=44 << 20),
        cost_estimate=pl.CostEstimate(flops=0, bytes_accessed=0, transcendentals=0),
    )(device, mid, attn_out, cotangent, tables, gains, *arrays)


def attn_back_kernel(
    plan,
    gain_len,
    device_ref,
    delta_attn,
    delta_mid,
    hidden_in,
    tables,
    gains,
    late_gains,
    qkv_weight,
    out_weight,
    grad_in,
    gain_grads,
    *refs,
):
    targets = refs[:-4]
    spread, tails, delta_raws, contexts = refs[-4:]
    device = device_ref[0]
    normed_in, key_raw, values, keys, heads, cos_tab, sin_tab = attn_forward(
        hidden_in, qkv_weight, tables, gains
    )
    gain_query = gains[:, D : D + HD]
    gain_key = gains[:, D + HD : D + 2 * HD]
    delta_context = times_transposed(delta_attn[...], out_weight[...]).astype(jnp.bfloat16)
    delta_key = jnp.zeros((CAP, HD), jnp.float32)
    delta_value = jnp.zeros((CAP, HD), jnp.float32)
    query_gain_rows = jnp.zeros((CAP, HD), jnp.float32)
    for head, (query_raw, queries, scores, log_total, context) in enumerate(heads):
        at = slice(head * HD, (head + 1) * HD)
        contexts[:, at] = context
        head_delta = delta_context[:, at]
        row_dot = jnp.sum(
            head_delta.astype(jnp.float32) * context.astype(jnp.float32), axis=-1, keepdims=True
        )
        prob_exact = jnp.exp(scores - log_total)
        delta_prob = times_transposed(head_delta, values)
        delta_score = prob_exact * (delta_prob - row_dot)
        turned = delta_score.T.astype(jnp.bfloat16)
        delta_score = delta_score.astype(jnp.bfloat16)
        delta_query = jnp.dot(delta_score, keys, preferred_element_type=jnp.float32)
        delta_key += jnp.dot(turned, queries, preferred_element_type=jnp.float32)
        delta_value += jnp.dot(
            prob_exact.T.astype(jnp.bfloat16), head_delta, preferred_element_type=jnp.float32
        )
        delta_rot = rotate_pull(delta_query * HD ** (-0.5), cos_tab, sin_tab)
        delta_raw, gain_rows = rms_pull(query_raw, gain_query, delta_rot)
        query_gain_rows += gain_rows
        delta_raws[:, at] = delta_raw.astype(jnp.bfloat16)
    delta_raw, gain_rows = rms_pull(key_raw, gain_key, rotate_pull(delta_key, cos_tab, sin_tab))
    delta_raws[:, HQ : HQ + HD] = delta_raw.astype(jnp.bfloat16)
    delta_raws[:, HQ + HD :] = delta_value.astype(jnp.bfloat16)
    gain_grads[:, D : D + HD] = jnp.sum(query_gain_rows, axis=0, keepdims=True)
    gain_grads[:, D + HD : D + 2 * HD] = jnp.sum(gain_rows, axis=0, keepdims=True)
    delta_in = times_transposed(delta_raws[...], qkv_weight[...])
    delta_part, gain_rows = rms_pull(
        hidden_in[...].astype(jnp.float32), gains[:, :D], delta_in
    )
    grad_in[...] = delta_mid[...] + delta_part
    gain_grads[:, :D] = jnp.sum(gain_rows, axis=0, keepdims=True)
    for late in range(3):
        at = slice((late + 1) * D + 2 * HD, (late + 2) * D + 2 * HD)
        gain_grads[:, at] = late_gains[late : late + 1, :]
    if gain_len:
        tails[...] = jnp.zeros_like(tails)
        lane = lax.broadcasted_iota(jnp.int32, (1, LANES), 1)
        for owner in range(tails.shape[0]):
            row, shift = divmod(owner * gain_len, LANES)
            piece = gain_grads[:, row * LANES : (row + 1) * LANES]
            if shift:
                piece = pltpu.roll(piece, LANES - shift, 1)
            if shift + gain_len > LANES:
                after = gain_grads[:, (row + 1) * LANES : (row + 2) * LANES]
                after = pltpu.roll(after, LANES - shift, 1)
                piece = jnp.where(lane < LANES - shift, piece, after)
            tails[owner, 0:1, :] = jnp.where(lane < gain_len, piece, 0.0)
    turned = normed_in.T
    delta_attn_value = delta_attn[...]
    spread_grads(
        spread,
        (
            (turned, lambda low, high: delta_raws[:, low:high], HQ),
            (turned, lambda low, high: delta_raws[:, HQ + low : HQ + high], HD),
            (turned, lambda low, high: delta_raws[:, HQ + HD + low : HQ + HD + high], HD),
            (contexts[...].T, lambda low, high: delta_attn_value[:, low:high], D),
        ),
    )
    place_blocks(ATTN_PADDED, plan, device, spread, tails, targets)


def back_attn(plan, gain_len, tail_rows, devices, block_shapes, device, *inputs):
    flat_rows = G1LEN // LANES + ATTN_PADDED
    shapes = [
        jax.ShapeDtypeStruct((CAP, D), jnp.float32),
        jax.ShapeDtypeStruct((1, 4 * D + 2 * HD), jnp.float32),
    ] + [jax.ShapeDtypeStruct(shape, jnp.bfloat16) for shape in block_shapes]
    tail_shape = (devices, tail_rows, LANES) if gain_len else (1, ROWS, LANES)
    return pl.pallas_call(
        functools.partial(attn_back_kernel, plan, gain_len),
        out_shape=shapes,
        in_specs=[pl.BlockSpec(memory_space=pltpu.SMEM)] + whole_specs(len(inputs)),
        out_specs=whole_specs(len(shapes)),
        scratch_shapes=[
            pltpu.VMEM((flat_rows, LANES), jnp.float32),
            pltpu.VMEM(tail_shape, jnp.float32),
            pltpu.VMEM((CAP, HQ + 2 * HD), jnp.bfloat16),
            pltpu.VMEM((CAP, HQ), jnp.bfloat16),
        ],
        compiler_params=pltpu.CompilerParams(vmem_limit_bytes=22 << 20),
        cost_estimate=pl.CostEstimate(flops=0, bytes_accessed=0, transcendentals=0),
    )(device, *inputs)


def gathered_blocks(pieces, chunks, orders, each, devices, device):
    arrays, plan, start = [], [], 0
    for piece, blocks, order in zip(pieces, chunks, orders):
        take = min(piece.shape[0], each - start)
        if each % ROWS:
            places = [offset_of(place, list(order) + [0]) for place in range(devices)]
            back = sorted(range(devices), key=places.__getitem__)
            mixed = offset_bits(device[0], list(order) + [0])
            arrays.append(
                jnp.take(jnp.concatenate(blocks), jnp.array(back, jnp.int32) ^ mixed, axis=0)
            )
            continue
        for part, block in enumerate(blocks):
            plan.append((order[:-1], offset_of(part, [order[-1], 0]), take, start, each))
            arrays.append(block)
        start += take
    if each % ROWS == 0:
        return arrays, plan, None
    table = jnp.concatenate(arrays, axis=1)
    flat = table[:, :each].reshape(1, devices * each, LANES)
    return [flat], [([], 0, devices * each, 0, 0)], table[:, each:]


def offset_bits(device, order):
    return sum(((device >> bit) & 1) << k for k, bit in enumerate(order))


def scatter_plan(each, tail_rows, orders, devices):
    parts = cut_rows(each + tail_rows, len(orders))
    half = devices // 2
    if each % ROWS:
        return [(0, [], 0, 0, devices * each, 0, 0)], [(1, devices * each, LANES)], parts
    plan = []
    for with_core in (1, 0):
        for (low, high), order in zip(parts, orders):
            order = order[::-1]
            plan.append((with_core, order, with_core, low, min(high, each) - low, low, each))
            if high > each:
                plan.append((with_core, order, with_core, each, tail_rows, None, each))
    return plan, [(half, each + tail_rows, LANES)] * 2, parts


def blocks_of(found, tails, parts, orders, devices, device):
    if len(found) == 2:
        return found
    table = found[0].reshape(devices, -1, LANES)
    table = table if tails is None else jnp.concatenate([table, tails], axis=1)
    blocks = []
    for with_core in (0, 1):
        chunks = []
        for (low, high), order in zip(parts, orders):
            places = range(devices // 2)
            offsets = [offset_of(place, order[::-1]) ^ with_core for place in places]
            owners = jnp.array(offsets, jnp.int32) ^ device[0]
            chunks.append(jnp.take(table[:, low:high], owners, axis=0))
        blocks.append(jnp.concatenate(chunks, axis=1))
    return blocks


def merge_kernel(parts, *refs):
    pairs = ((refs[0], refs[1]), (refs[2], refs[3]))
    targets = refs[4:]
    half = refs[0].shape[0] // 2
    for number, target in enumerate(targets):
        chunk, second = divmod(number, 2)

        @pl.loop(0, half)
        def _(index, target=target, chunk=chunk, first=second * half):
            at = 0
            for (home, came), (low, high) in zip(pairs, parts[chunk]):
                total = home[first + index, low:high, :].astype(jnp.float32)
                total += came[first + index, low:high, :].astype(jnp.float32)
                target[index, at : at + high - low, :] = total.astype(jnp.bfloat16)
                at += high - low


def cores_merged(parts, *blocks):
    half = blocks[0].shape[0] // 2
    if any((high - low) % ROWS for chunk in parts for low, high in chunk):
        pairs = (blocks[:2], blocks[2:])
        joined = []
        for chunk in parts:
            sums = [
                home[:, low:high].astype(jnp.float32) + came[:, low:high].astype(jnp.float32)
                for (home, came), (low, high) in zip(pairs, chunk)
            ]
            total = jnp.concatenate(sums, axis=1).astype(jnp.bfloat16)
            joined.append((total[:half], total[half:]))
        return joined
    shapes = [
        jax.ShapeDtypeStruct((half, sum(high - low for low, high in chunk), LANES), jnp.bfloat16)
        for chunk in parts
        for _ in range(2)
    ]
    found = pl.pallas_call(
        functools.partial(merge_kernel, parts),
        out_shape=shapes,
        in_specs=whole_specs(4),
        out_specs=whole_specs(len(shapes)),
        compiler_params=pltpu.CompilerParams(vmem_limit_bytes=20 << 20),
        cost_estimate=pl.CostEstimate(flops=0, bytes_accessed=0, transcendentals=0),
    )(*blocks)
    return list(zip(found[::2], found[1::2]))


def adam_update(weight_shard, gradient, moment_one, moment_two):
    moment_one = 0.9 * moment_one + 0.1 * gradient
    moment_two = 0.999 * moment_two + 0.001 * gradient * gradient
    fix_one = 1.0 - 0.9**STEP
    fix_two = 1.0 - 0.999**STEP
    weight_shard = weight_shard - 0.02 * (
        moment_one / fix_one / (jnp.sqrt(moment_two / fix_two) + 1e-08) + 0.1 * weight_shard
    )
    return (weight_shard, moment_one, moment_two)


def per_device(hidden_in, cotangent, params, moment_one, moment_two, seq_lengths, seq_owner):
    devices = lax.axis_size("dp")
    device = lax.axis_index("dp").astype(jnp.int32)
    here = device.reshape(1)
    attn_len = G1LEN // devices
    ffn_len = G2LEN // devices
    gain_len = params.shape[0] - attn_len - ffn_len
    attn_rows = attn_len // LANES
    tail_rows = -(-(attn_rows + 1) // ROWS) * ROWS - attn_rows
    pad = tail_rows * LANES - gain_len
    rounded = params.astype(jnp.bfloat16)
    first_piece = jnp.concatenate(
        [rounded[:attn_len], rounded[attn_len + ffn_len :], jnp.zeros((pad,), jnp.bfloat16)]
    ).reshape(-1, LANES)
    second_piece = rounded[attn_len : attn_len + ffn_len].reshape(-1, LANES)
    ffn_rows = ffn_len // LANES
    second_pieces = [second_piece[low:high] for low, high in cut_rows(ffn_rows, 2)]
    orders = bit_orders(devices, ("abxy", "bxya", "byax"))
    pieces = [first_piece, *second_pieces]
    chunks = gather_chunks(pieces, orders, devices)
    arrays, plan, tails = gathered_blocks(
        pieces[:1], chunks[:1], orders[:1], attn_rows, devices, here
    )
    ffn_arrays, ffn_plan, unused = gathered_blocks(
        pieces[1:], chunks[1:], orders[1:], ffn_rows, devices, here
    )
    aligned = attn_rows % ROWS == 0
    tables = slot_setup(seq_lengths, seq_owner, device)
    given = None
    if not aligned:
        given = tails.reshape(devices, -1)[:, :gain_len].astype(jnp.float32).reshape(1, -1)
    qkv_weight, out_weight, gains, attn_out, mid_stream = forward_attn(
        plan,
        gain_len if aligned else 0,
        tail_rows,
        devices,
        here,
        hidden_in,
        tables,
        given,
        arrays,
    )
    orders = bit_orders(devices, ("yxba", "ayxb", "xayb"))
    out_plan, block_shapes, ffn_parts = scatter_plan(ffn_rows, 0, orders, devices)
    staged = [(0, 0, 0)]
    if len(block_shapes) == 2:
        staged = [
            (part // 2, part % 2 * (devices // 4), low)
            for low, _ in cut_rows(ffn_rows, 2)
            for part in range(4)
        ]
    block_out, delta_mid, delta_attn, late_gains, *found = run_ffn(
        ffn_plan,
        staged,
        out_plan,
        block_shapes,
        here,
        mid_stream,
        attn_out,
        cotangent,
        tables,
        gains,
        ffn_arrays,
    )
    ffn_home, ffn_away = blocks_of(found, None, ffn_parts, orders, devices, here)
    ffn_came = across(ffn_away, 0, devices)
    attn_plan, block_shapes, attn_parts = scatter_plan(attn_rows, tail_rows, orders, devices)
    grad_in, gain_grads, *found = back_attn(
        attn_plan,
        gain_len if aligned else 0,
        tail_rows,
        devices,
        block_shapes,
        here,
        delta_attn,
        delta_mid,
        hidden_in,
        tables,
        gains,
        late_gains,
        qkv_weight,
        out_weight,
    )
    gain_table = None
    if not aligned:
        gain_table = gain_grads.reshape(devices, gain_len).astype(jnp.bfloat16)
        gain_table = jnp.pad(gain_table, ((0, 0), (0, pad))).reshape(devices, tail_rows, LANES)
    attn_home, attn_away = blocks_of(found, gain_table, attn_parts, orders, devices, here)
    attn_came = across(attn_away, 0, devices)
    parts = [
        [cut[chunk] for cut in (ffn_parts, attn_parts) if chunk < len(cut)]
        for chunk in range(len(ffn_parts))
    ]
    chunks = cores_merged(parts, ffn_home, ffn_came, attn_home, attn_came)
    for stage in range(len(orders[0])):
        chunks = merged_blocks(chunks, sent_blocks(chunks, orders, stage, devices))
    rows = [chunk for chunk, _ in chunks]
    ffn_take = [high - low for low, high in ffn_parts]
    ffn_shard = [chunk[:take].reshape(-1) for chunk, take in zip(rows, ffn_take)]
    attn_shard = jnp.concatenate([chunk[take:].reshape(-1) for chunk, take in zip(rows, ffn_take)])
    grad_shard = jnp.concatenate(
        [attn_shard[:attn_len], *ffn_shard, attn_shard[attn_len : attn_len + gain_len]]
    )
    params_new, moment_one_new, moment_two_new = adam_update(
        params, grad_shard, moment_one, moment_two
    )
    return (block_out, grad_in, grad_shard, params_new, moment_one_new, moment_two_new)


def solution(mesh):
    in_specs = (P("dp", None), P("dp", None), P("dp"), P("dp"), P("dp"), P(), P())
    out_specs = (P("dp", None), P("dp", None), P("dp"), P("dp"), P("dp"), P("dp"))
    return jax.shard_map(
        per_device, mesh=mesh, in_specs=in_specs, out_specs=out_specs, check_vma=False
    )
```

```python
import functools
import math

import jax
import jax.numpy as jnp
from jax import lax
from jax.experimental import pallas as pl
from jax.experimental.pallas import tpu as pltpu
from jax.sharding import PartitionSpec as P

D = 640
FF = 2048
HD = 256
HQ = 1024
CAP = 128
WINDOW = 64
STEP = 3
G1LEN = 1638400
G2LEN = 3932160
LANES = 128
ROWS = 16
GELU_SCALE = math.sqrt(2 / math.pi)
ATTN_PADDED, FFN_PADDED = 0, 2 * D


def rms_scale(values, gain_vec):
    return (
        values
        * lax.rsqrt(jnp.mean(values * values, axis=-1, keepdims=True) + 1e-06)
        * (1.0 + gain_vec)
    )


def rotate(values, cos_tab, sin_tab):
    half_dim = values.shape[-1] // 2
    lower_half = values[..., :half_dim]
    upper_half = values[..., half_dim:]
    return jnp.concatenate(
        [lower_half * cos_tab - upper_half * sin_tab, upper_half * cos_tab + lower_half * sin_tab],
        axis=-1,
    )


def gated_gelu(gate_proj, up_proj):
    return jax.nn.gelu(gate_proj, approximate=True) * up_proj


def times_transposed(rows_in, matrix):
    return lax.dot_general(
        rows_in, matrix, (((1,), (1,)), ((), ())), preferred_element_type=jnp.float32
    )


def slot_setup(seq_lengths, seq_owner, device):
    mine_mask = seq_owner == device
    own_lengths = jnp.where(mine_mask, seq_lengths, 0)
    seq_ends = jnp.cumsum(own_lengths, dtype=jnp.int32)
    seq_begins = seq_ends - own_lengths
    slot_index = jnp.arange(CAP, dtype=jnp.int32)
    column = slot_index[:, None]
    inside_mask = (
        mine_mask[None, :] & (seq_begins[None, :] <= column) & (column < seq_ends[None, :])
    )
    live_mask = jnp.any(inside_mask, axis=1)
    seq_label = jnp.sum(
        (mine_mask[None, :] & (seq_ends[None, :] <= column)).astype(jnp.int32),
        axis=1,
        dtype=jnp.int32,
    )
    position = jnp.sum(
        jnp.where(inside_mask, column - seq_begins[None, :], 0), axis=1, dtype=jnp.int32
    )
    row_slot = slot_index[:, None]
    col_slot = slot_index[None, :]
    allowed = live_mask[:, None] & live_mask[None, :] & (
        seq_label[:, None] == seq_label[None, :]
    ) & (col_slot <= row_slot) & (row_slot - col_slot < WINDOW) | (row_slot == col_slot)
    half_dim = HD // 2
    frequency = 10000.0 ** (-2.0 * jnp.arange(half_dim, dtype=jnp.float32) / HD)
    angles = position.astype(jnp.float32)[:, None] * frequency[None, :]
    live_wide = jnp.broadcast_to(live_mask[:, None], (CAP, LANES)).astype(jnp.float32)
    return jnp.concatenate(
        [jnp.cos(angles), jnp.sin(angles), allowed.astype(jnp.float32), live_wide], axis=1
    )


def rms_pull(raw, gain_vec, delta):
    scale = lax.rsqrt(jnp.mean(raw * raw, axis=-1, keepdims=True) + 1e-06)
    weighed = delta * (1.0 + gain_vec)
    shared = jnp.mean(raw * weighed, axis=-1, keepdims=True)
    return scale * weighed - raw * (scale * scale * scale * shared), delta * raw * scale


def rotate_pull(delta, cos_tab, sin_tab):
    half_dim = delta.shape[-1] // 2
    lower_half = delta[:, :half_dim]
    upper_half = delta[:, half_dim:]
    return jnp.concatenate(
        [lower_half * cos_tab + upper_half * sin_tab, upper_half * cos_tab - lower_half * sin_tab],
        axis=-1,
    )


def bit_orders(devices, tuned):
    bits = devices.bit_length() - 1
    if bits == 5:
        return [["cxyab".index(letter) for letter in order] for order in tuned]
    return [[1 + (shift + step) % (bits - 1) for step in range(bits - 1)] for shift in range(3)]


def across(block, bit, devices):
    return lax.ppermute(block, "dp", [(i, i ^ (1 << bit)) for i in range(devices)])


def offset_of(place, order):
    return sum(((place >> k) & 1) << bit for k, bit in enumerate(order))


def gather_chunks(pieces, orders, devices):
    held = [piece[None] for piece in pieces]
    for stage in range(len(orders[0]) - 1):
        came = [across(block, order[stage], devices) for block, order in zip(held, orders)]
        for chunk in range(1, len(came)):
            came[chunk] = lax.optimization_barrier((came[chunk], came[0]))[0]
        held = [jnp.concatenate(pair) for pair in zip(held, came)]
    last = [across(block, order[-1], devices) for block, order in zip(held, orders)]
    chunks = []
    for block, final in zip(held, last):
        if chunks:
            final = lax.optimization_barrier((final, *chunks[0][2:]))[0]
        chunks.append((block, final, across(block, 0, devices), across(final, 0, devices)))
    return chunks


def sent_blocks(chunks, orders, stage, devices):
    return [
        across(away, order[stage], devices)
        for (_, away), order in zip(chunks, orders)
    ]


def merged_blocks(chunks, came):
    merged = []
    for (home, _), arrived in zip(chunks, came):
        half = home.shape[0] // 2

        def added(low, high):
            return home[low:high].astype(jnp.float32) + arrived[low:high].astype(jnp.float32)

        if half:
            merged.append(
                (
                    added(0, half).astype(jnp.bfloat16),
                    added(half, 2 * half).astype(jnp.bfloat16),
                )
            )
        else:
            merged.append((added(0, 1)[0], None))
    return merged


def cut_rows(rows, parts):
    each = -(-rows // (parts * ROWS)) * ROWS
    return [(low, min(low + each, rows)) for low in range(0, rows, each)]


def whole_specs(count):
    return [pl.BlockSpec(memory_space=pltpu.VMEM)] * count


def owner_rows(device, index, order, extra, start, each):
    owner = device ^ extra
    for k, bit in enumerate(order):
        owner = owner ^ (((index >> k) & 1) << bit)
    return owner, owner * each + start


def copy_step(rows):
    return max(step for step in range(ROWS, 513, ROWS) if rows % step == 0)


def each_piece(padded, first, take, visit):
    def visit_plain(shift):
        step = copy_step(take)

        def visit_step(part):
            at = part * step
            visit(at, step, pl.multiple_of(first + shift + at, ROWS))

        if take == step:
            visit_step(0)
        else:
            pl.loop(0, take // step)(visit_step)

    if not padded:
        visit_plain(0)
        return
    units = take // ROWS
    inner = max(count for count in range(1, 41) if units % count == 0)
    number = first // ROWS

    def visit_units(row_of):
        def visit_some(step):
            for part in range(inner):
                at = (step * inner + part) * ROWS
                visit(at, ROWS, row_of(step * inner + part))

        if units == inner:
            visit_some(0)
        else:
            pl.loop(0, units // inner)(visit_some)

    longer = (ROWS + 1) * number
    pl.when(number + units <= padded)(lambda: visit_units(lambda k: longer + (ROWS + 1) * k))
    pl.when(number >= padded)(lambda: visit_plain(padded))
    pl.when((number < padded) & (number + units > padded))(
        lambda: visit_units(lambda k: ROWS * (number + k) + jnp.minimum(number + k, padded))
    )


def spread_blocks(padded, plan, views, device, spread, tails):
    for (order, extra, take, start, each), (block_ref, first_index, count, first_row) in zip(
        plan, views
    ):

        @pl.loop(0, count)
        def _(
            index,
            order=order,
            extra=extra,
            take=take,
            start=start,
            each=each,
            block_ref=block_ref,
            first_index=first_index,
            first_row=first_row,
        ):
            owner, first = owner_rows(device, index, order, extra, start, each)

            def spread_unit(at, unit, row):
                low = first_row + at
                if not isinstance(low, int):
                    low = pl.multiple_of(low, ROWS)
                spread[pl.ds(row, unit), :] = block_ref[
                    first_index + index, pl.ds(low, unit), :
                ].astype(jnp.float32)

            each_piece(padded, first, take, spread_unit)
            if tails is not None:
                tails[owner] = block_ref[index, take : take + tails.shape[1], :]


def pitch_of(columns):
    blocks = columns // LANES
    return blocks + (blocks == ROWS)


def fold_matrices(spread, targets):
    first = 0
    for matrix, offset, rows, columns in targets:
        blocks = columns // LANES
        pitch = pitch_of(columns)

        @pl.loop(0, rows // LANES)
        def _(step, matrix=matrix, offset=offset, blocks=blocks, pitch=pitch, first=first):
            base = first + step * (LANES * pitch)
            at = pl.ds(pl.multiple_of(step * LANES, LANES), LANES)
            for block in range(blocks):
                low = offset + block * LANES
                matrix[at, low : low + LANES] = spread[
                    pl.ds(base + block, LANES, stride=pitch), :
                ].astype(jnp.bfloat16)

        first += rows * pitch


def spread_grads(spread, products):
    first = 0
    for turned, right, columns in products:
        rows = turned.shape[0]
        blocks = columns // LANES
        pitch = pitch_of(columns)
        wide = 2 - blocks % 2
        for block in range(0, blocks, wide):
            product = jnp.dot(
                turned,
                right(block * LANES, (block + wide) * LANES),
                preferred_element_type=jnp.float32,
            )
            for part in range(wide):
                spread[pl.ds(first + block + part, rows, stride=pitch), :] = product[
                    :, part * LANES : (part + 1) * LANES
                ]
        first += rows * pitch


def place_blocks(padded, plan, device, spread, tails, targets):
    for target, order, extra, low, take, start, each in plan:
        target_ref = targets[target]

        @pl.loop(0, target_ref.shape[0])
        def _(
            index,
            target_ref=target_ref,
            order=order,
            extra=extra,
            low=low,
            take=take,
            start=start,
            each=each,
        ):
            owner, first = owner_rows(device, index, order, extra, start or 0, each)
            if start is None:
                target_ref[index, low : low + take, :] = tails[owner].astype(jnp.bfloat16)
                return

            def place_unit(at, unit, row):
                at = low + at
                if not isinstance(at, int):
                    at = pl.multiple_of(at, ROWS)
                target_ref[index, pl.ds(at, unit), :] = spread[pl.ds(row, unit), :].astype(
                    jnp.bfloat16
                )

            each_piece(padded, first, take, place_unit)


def attn_forward(hidden_in, qkv_weight, tables, gains):
    cos_tab = tables[:, :LANES]
    sin_tab = tables[:, LANES : 2 * LANES]
    open_pairs = tables[:, 2 * LANES : 3 * LANES] > 0.0
    gain_query = gains[:, D : D + HD]
    gain_key = gains[:, D + HD : D + 2 * HD]
    normed_in = rms_scale(hidden_in[...].astype(jnp.float32), gains[:, :D]).astype(jnp.bfloat16)
    raw = jnp.dot(normed_in, qkv_weight[...], preferred_element_type=jnp.float32)
    key_raw = raw[:, HQ : HQ + HD]
    values = raw[:, HQ + HD :].astype(jnp.bfloat16)
    keys = rotate(rms_scale(key_raw, gain_key), cos_tab, sin_tab).astype(jnp.bfloat16)
    heads = []
    for head in range(HQ // HD):
        query_raw = raw[:, head * HD : (head + 1) * HD]
        rot_query = rotate(rms_scale(query_raw, gain_query), cos_tab, sin_tab) * HD ** (-0.5)
        rot_query = rot_query.astype(jnp.bfloat16)
        scores = jnp.where(open_pairs, times_transposed(rot_query, keys), -1e30)
        row_max = jnp.max(scores, axis=-1, keepdims=True)
        raised = jnp.exp(scores - row_max)
        summed = jnp.sum(raised, axis=-1, keepdims=True)
        context = jnp.dot(
            (raised / summed).astype(jnp.bfloat16), values, preferred_element_type=jnp.float32
        ).astype(jnp.bfloat16)
        heads.append((query_raw, rot_query, scores, row_max + jnp.log(summed), context))
    return normed_in, key_raw, values, keys, heads, cos_tab, sin_tab


def join_gains(tails, gain_len, gains):
    lane = lax.broadcasted_iota(jnp.int32, (1, LANES), 1)
    tiles = [jnp.zeros((1, LANES), jnp.float32) for _ in range(gains.shape[1] // LANES)]
    for owner in range(tails.shape[0]):
        tile, shift = divmod(owner * gain_len, LANES)
        run = jnp.where(lane < gain_len, tails[owner].astype(jnp.float32)[0:1, :], 0.0)
        if shift:
            run = pltpu.roll(run, shift, 1)
        tiles[tile] += jnp.where(lane >= shift, run, 0.0)
        if shift + gain_len > LANES:
            tiles[tile + 1] += jnp.where(lane < shift, run, 0.0)
    for number, tile in enumerate(tiles):
        gains[:, number * LANES : (number + 1) * LANES] = tile


def layer_kernel(
    attn_plan,
    ffn_plan,
    staged,
    plan_out,
    gain_len,
    device_ref,
    hidden_in,
    cotangent,
    tables,
    *refs,
):
    if not gain_len:
        given, refs = refs[0], refs[1:]
    attn_sources = refs[: len(attn_plan)]
    ffn_sources = refs[len(attn_plan) : len(attn_plan) + len(ffn_plan)]
    refs = refs[len(attn_plan) + len(ffn_plan) :]
    qkv_weight, out_weight, gains = refs[:3]
    block_out, delta_mid_ref, delta_attn_ref, late_gains = refs[3:7]
    targets = refs[7:-16]
    staging, tails, context, attn_out, mid_ref, attn_sems = refs[-16:-10]
    spread, gate_weight, up_weight, down_weight = refs[-10:-6]
    gates, ups, hidden, delta_gate, delta_up, sems = refs[-6:]
    device = device_ref[0]
    ffn_copies, ffn_views = [], []
    for source, (target, first_index, first_row) in zip(ffn_sources, staged):
        count, rows = source.shape[:2]
        held = targets[target]
        ffn_copies.append(
            pltpu.make_async_copy(
                source,
                held.at[pl.ds(first_index, count), pl.ds(first_row, rows), :],
                sems.at[len(ffn_copies)],
            )
        )
        ffn_views.append((held, first_index, count, first_row))
    copies, views = [], []
    for number, source in enumerate(attn_sources):
        count = source.shape[0]
        held = staging.at[pl.ds(number * count, count)]
        copies.append(pltpu.make_async_copy(source, held, attn_sems.at[number]))
        views.append((held, 0, count, 0))
    for copy in copies + ffn_copies:
        copy.start()
    for copy, step, view in zip(copies, attn_plan, views):
        copy.wait()
        spread_blocks(
            ATTN_PADDED,
            [step],
            [view],
            device,
            spread,
            tails if gain_len else None,
        )
    if gain_len:
        join_gains(tails, gain_len, gains)
    else:
        gains[...] = given[...]
    fold_matrices(
        spread,
        (
            (qkv_weight, 0, D, HQ),
            (qkv_weight, HQ, D, HD),
            (qkv_weight, HQ + HD, D, HD),
            (out_weight, 0, HQ, D),
        ),
    )
    heads = attn_forward(hidden_in, qkv_weight, tables, gains)[4]
    for head, parts in enumerate(heads):
        context[:, head * HD : (head + 1) * HD] = parts[-1]
    out = jnp.dot(context[...], out_weight[...], preferred_element_type=jnp.float32)
    attn_out[...] = out
    gain_post = gains[:, D + 2 * HD : 2 * D + 2 * HD]
    mid_ref[...] = hidden_in[...].astype(jnp.float32) + rms_scale(out, gain_post)
    mid_stream = mid_ref[...]
    gain_mid = gains[:, 2 * D + 2 * HD : 3 * D + 2 * HD]
    gain_last = gains[:, 3 * D + 2 * HD :]
    normed_mid = rms_scale(mid_stream, gain_mid).astype(jnp.bfloat16)
    for copy, plan, view in zip(ffn_copies, ffn_plan, ffn_views):
        copy.wait()
        spread_blocks(FFN_PADDED, [plan], [view], device, spread, None)
    fold_matrices(
        spread, ((gate_weight, 0, D, FF), (up_weight, 0, D, FF), (down_weight, 0, FF, D))
    )
    parts = [slice(low, low + 512) for low in range(0, FF, 512)]
    for at in parts:
        gate = jnp.dot(normed_mid, gate_weight[:, at], preferred_element_type=jnp.float32)
        up = jnp.dot(normed_mid, up_weight[:, at], preferred_element_type=jnp.float32)
        gates[:, at] = gate
        ups[:, at] = up
        hidden[:, at] = gated_gelu(gate, up).astype(jnp.bfloat16)
    ffn_out = jnp.dot(hidden[...], down_weight[...], preferred_element_type=jnp.float32)
    block_out[...] = (mid_stream + rms_scale(ffn_out, gain_last)).astype(jnp.bfloat16)
    delta_out = cotangent[...].astype(jnp.float32) * tables[:, 3 * LANES : 3 * LANES + 1]
    delta_ffn, gain_rows = rms_pull(ffn_out, gain_last, delta_out)
    late_gains[2:3, :] = jnp.sum(gain_rows, axis=0, keepdims=True)
    delta_ffn = delta_ffn.astype(jnp.bfloat16)
    delta_normed = jnp.zeros((CAP, D), jnp.float32)
    for at in parts:
        delta_hidden = times_transposed(delta_ffn, down_weight[at, :])
        gate = gates[:, at]
        raised = jnp.tanh(GELU_SCALE * (gate + 0.044715 * (gate * gate * gate)))
        share = 0.5 * (1.0 + raised)
        slope = share + (0.5 * GELU_SCALE) * gate * (1.0 - raised * raised) * (
            1.0 + (3 * 0.044715) * (gate * gate)
        )
        delta_gate[:, at] = (delta_hidden * ups[:, at] * slope).astype(jnp.bfloat16)
        delta_up[:, at] = (delta_hidden * (gate * share)).astype(jnp.bfloat16)
        delta_normed += times_transposed(delta_gate[:, at], gate_weight[:, at])
        delta_normed += times_transposed(delta_up[:, at], up_weight[:, at])
    delta_part, gain_rows = rms_pull(mid_stream, gain_mid, delta_normed)
    late_gains[1:2, :] = jnp.sum(gain_rows, axis=0, keepdims=True)
    delta_mid = delta_out + delta_part
    delta_mid_ref[...] = delta_mid
    delta_attn, gain_rows = rms_pull(attn_out[...], gain_post, delta_mid)
    late_gains[0:1, :] = jnp.sum(gain_rows, axis=0, keepdims=True)
    delta_attn_ref[...] = delta_attn.astype(jnp.bfloat16)
    turned = normed_mid.T
    spread_grads(
        spread,
        (
            (turned, lambda low, high: delta_gate[:, low:high], FF),
            (turned, lambda low, high: delta_up[:, low:high], FF),
            (hidden[...].T, lambda low, high: delta_ffn[:, low:high], D),
        ),
    )
    place_blocks(FFN_PADDED, plan_out, device, spread, None, targets)


def run_layer(
    attn_plan,
    ffn_plan,
    staged,
    plan_out,
    block_shapes,
    gain_len,
    tail_rows,
    devices,
    device,
    hidden_in,
    cotangent,
    tables,
    given,
    attn_arrays,
    ffn_arrays,
):
    shapes = [
        jax.ShapeDtypeStruct((D, HQ + 2 * HD), jnp.bfloat16),
        jax.ShapeDtypeStruct((HQ, D), jnp.bfloat16),
        jax.ShapeDtypeStruct((1, 4 * D + 2 * HD), jnp.float32),
        jax.ShapeDtypeStruct((CAP, D), jnp.bfloat16),
        jax.ShapeDtypeStruct((CAP, D), jnp.float32),
        jax.ShapeDtypeStruct((CAP, D), jnp.bfloat16),
        jax.ShapeDtypeStruct((3, D), jnp.float32),
    ] + [jax.ShapeDtypeStruct(shape, jnp.bfloat16) for shape in block_shapes]
    given = [] if gain_len else [given]
    arrays = [*attn_arrays, *ffn_arrays]
    held = (sum(array.shape[0] for array in attn_arrays),) + attn_arrays[0].shape[1:]
    model = pltpu.VMEM((CAP, D), jnp.float32)
    wide = pltpu.VMEM((CAP, FF), jnp.float32)
    narrow = pltpu.VMEM((CAP, FF), jnp.bfloat16)
    return pl.pallas_call(
        functools.partial(layer_kernel, attn_plan, ffn_plan, staged, plan_out, gain_len),
        out_shape=shapes,
        in_specs=[pl.BlockSpec(memory_space=pltpu.SMEM)]
        + whole_specs(3 + len(given))
        + [pl.BlockSpec(memory_space=pltpu.HBM)] * len(arrays),
        out_specs=whole_specs(len(shapes)),
        scratch_shapes=[
            pltpu.VMEM(held, jnp.bfloat16),
            pltpu.VMEM((devices, tail_rows, LANES) if gain_len else (1, ROWS, LANES), jnp.bfloat16),
            pltpu.VMEM((CAP, HQ), jnp.bfloat16),
            model,
            model,
            pltpu.SemaphoreType.DMA((len(attn_arrays),)),
            pltpu.VMEM((G2LEN // LANES + FFN_PADDED, LANES), jnp.float32),
            pltpu.VMEM((D, FF), jnp.bfloat16),
            pltpu.VMEM((D, FF), jnp.bfloat16),
            pltpu.VMEM((FF, D), jnp.bfloat16),
            wide,
            wide,
            narrow,
            narrow,
            narrow,
            pltpu.SemaphoreType.DMA((len(ffn_arrays),)),
        ],
        compiler_params=pltpu.CompilerParams(vmem_limit_bytes=52 << 20),
        cost_estimate=pl.CostEstimate(flops=0, bytes_accessed=0, transcendentals=0),
    )(device, hidden_in, cotangent, tables, *given, *arrays)


def attn_back_kernel(
    plan,
    gain_len,
    device_ref,
    delta_attn,
    delta_mid,
    hidden_in,
    tables,
    gains,
    late_gains,
    qkv_weight,
    out_weight,
    grad_in,
    gain_grads,
    *refs,
):
    targets = refs[:-4]
    spread, tails, delta_raws, contexts = refs[-4:]
    device = device_ref[0]
    normed_in, key_raw, values, keys, heads, cos_tab, sin_tab = attn_forward(
        hidden_in, qkv_weight, tables, gains
    )
    gain_query = gains[:, D : D + HD]
    gain_key = gains[:, D + HD : D + 2 * HD]
    delta_context = times_transposed(delta_attn[...], out_weight[...]).astype(jnp.bfloat16)
    delta_key = jnp.zeros((CAP, HD), jnp.float32)
    delta_value = jnp.zeros((CAP, HD), jnp.float32)
    query_gain_rows = jnp.zeros((CAP, HD), jnp.float32)
    for head, (query_raw, queries, scores, log_total, context) in enumerate(heads):
        at = slice(head * HD, (head + 1) * HD)
        contexts[:, at] = context
        head_delta = delta_context[:, at]
        row_dot = jnp.sum(
            head_delta.astype(jnp.float32) * context.astype(jnp.float32), axis=-1, keepdims=True
        )
        prob_exact = jnp.exp(scores - log_total)
        delta_prob = times_transposed(head_delta, values)
        delta_score = prob_exact * (delta_prob - row_dot)
        turned = delta_score.T.astype(jnp.bfloat16)
        delta_score = delta_score.astype(jnp.bfloat16)
        delta_query = jnp.dot(delta_score, keys, preferred_element_type=jnp.float32)
        delta_key += jnp.dot(turned, queries, preferred_element_type=jnp.float32)
        delta_value += jnp.dot(
            prob_exact.T.astype(jnp.bfloat16), head_delta, preferred_element_type=jnp.float32
        )
        delta_rot = rotate_pull(delta_query * HD ** (-0.5), cos_tab, sin_tab)
        delta_raw, gain_rows = rms_pull(query_raw, gain_query, delta_rot)
        query_gain_rows += gain_rows
        delta_raws[:, at] = delta_raw.astype(jnp.bfloat16)
    delta_raw, gain_rows = rms_pull(key_raw, gain_key, rotate_pull(delta_key, cos_tab, sin_tab))
    delta_raws[:, HQ : HQ + HD] = delta_raw.astype(jnp.bfloat16)
    delta_raws[:, HQ + HD :] = delta_value.astype(jnp.bfloat16)
    gain_grads[:, D : D + HD] = jnp.sum(query_gain_rows, axis=0, keepdims=True)
    gain_grads[:, D + HD : D + 2 * HD] = jnp.sum(gain_rows, axis=0, keepdims=True)
    delta_in = times_transposed(delta_raws[...], qkv_weight[...])
    delta_part, gain_rows = rms_pull(
        hidden_in[...].astype(jnp.float32), gains[:, :D], delta_in
    )
    grad_in[...] = delta_mid[...] + delta_part
    gain_grads[:, :D] = jnp.sum(gain_rows, axis=0, keepdims=True)
    for late in range(3):
        at = slice((late + 1) * D + 2 * HD, (late + 2) * D + 2 * HD)
        gain_grads[:, at] = late_gains[late : late + 1, :]
    if gain_len:
        tails[...] = jnp.zeros_like(tails)
        lane = lax.broadcasted_iota(jnp.int32, (1, LANES), 1)
        for owner in range(tails.shape[0]):
            row, shift = divmod(owner * gain_len, LANES)
            piece = gain_grads[:, row * LANES : (row + 1) * LANES]
            if shift:
                piece = pltpu.roll(piece, LANES - shift, 1)
            if shift + gain_len > LANES:
                after = gain_grads[:, (row + 1) * LANES : (row + 2) * LANES]
                after = pltpu.roll(after, LANES - shift, 1)
                piece = jnp.where(lane < LANES - shift, piece, after)
            tails[owner, 0:1, :] = jnp.where(lane < gain_len, piece, 0.0)
    turned = normed_in.T
    delta_attn_value = delta_attn[...]
    spread_grads(
        spread,
        (
            (turned, lambda low, high: delta_raws[:, low:high], HQ),
            (turned, lambda low, high: delta_raws[:, HQ + low : HQ + high], HD),
            (turned, lambda low, high: delta_raws[:, HQ + HD + low : HQ + HD + high], HD),
            (contexts[...].T, lambda low, high: delta_attn_value[:, low:high], D),
        ),
    )
    place_blocks(ATTN_PADDED, plan, device, spread, tails, targets)


def back_attn(plan, gain_len, tail_rows, devices, block_shapes, device, *inputs):
    flat_rows = G1LEN // LANES + ATTN_PADDED
    shapes = [
        jax.ShapeDtypeStruct((CAP, D), jnp.float32),
        jax.ShapeDtypeStruct((1, 4 * D + 2 * HD), jnp.float32),
    ] + [jax.ShapeDtypeStruct(shape, jnp.bfloat16) for shape in block_shapes]
    tail_shape = (devices, tail_rows, LANES) if gain_len else (1, ROWS, LANES)
    return pl.pallas_call(
        functools.partial(attn_back_kernel, plan, gain_len),
        out_shape=shapes,
        in_specs=[pl.BlockSpec(memory_space=pltpu.SMEM)] + whole_specs(len(inputs)),
        out_specs=whole_specs(len(shapes)),
        scratch_shapes=[
            pltpu.VMEM((flat_rows, LANES), jnp.float32),
            pltpu.VMEM(tail_shape, jnp.float32),
            pltpu.VMEM((CAP, HQ + 2 * HD), jnp.bfloat16),
            pltpu.VMEM((CAP, HQ), jnp.bfloat16),
        ],
        compiler_params=pltpu.CompilerParams(vmem_limit_bytes=22 << 20),
        cost_estimate=pl.CostEstimate(flops=0, bytes_accessed=0, transcendentals=0),
    )(device, *inputs)


def gathered_blocks(pieces, chunks, orders, each, devices, device):
    arrays, plan, start = [], [], 0
    for piece, blocks, order in zip(pieces, chunks, orders):
        take = min(piece.shape[0], each - start)
        if each % ROWS:
            places = [offset_of(place, list(order) + [0]) for place in range(devices)]
            back = sorted(range(devices), key=places.__getitem__)
            mixed = offset_bits(device[0], list(order) + [0])
            arrays.append(
                jnp.take(jnp.concatenate(blocks), jnp.array(back, jnp.int32) ^ mixed, axis=0)
            )
            continue
        for part, block in enumerate(blocks):
            plan.append((order[:-1], offset_of(part, [order[-1], 0]), take, start, each))
            arrays.append(block)
        start += take
    if each % ROWS == 0:
        return arrays, plan, None
    table = jnp.concatenate(arrays, axis=1)
    flat = table[:, :each].reshape(1, devices * each, LANES)
    return [flat], [([], 0, devices * each, 0, 0)], table[:, each:]


def offset_bits(device, order):
    return sum(((device >> bit) & 1) << k for k, bit in enumerate(order))


def scatter_plan(each, tail_rows, orders, devices):
    parts = cut_rows(each + tail_rows, len(orders))
    half = devices // 2
    if each % ROWS:
        return [(0, [], 0, 0, devices * each, 0, 0)], [(1, devices * each, LANES)], parts
    plan = []
    for with_core in (1, 0):
        for (low, high), order in zip(parts, orders):
            order = order[::-1]
            plan.append((with_core, order, with_core, low, min(high, each) - low, low, each))
            if high > each:
                plan.append((with_core, order, with_core, each, tail_rows, None, each))
    return plan, [(half, each + tail_rows, LANES)] * 2, parts


def blocks_of(found, tails, parts, orders, devices, device):
    if len(found) == 2:
        return found
    table = found[0].reshape(devices, -1, LANES)
    table = table if tails is None else jnp.concatenate([table, tails], axis=1)
    blocks = []
    for with_core in (0, 1):
        chunks = []
        for (low, high), order in zip(parts, orders):
            places = range(devices // 2)
            offsets = [offset_of(place, order[::-1]) ^ with_core for place in places]
            owners = jnp.array(offsets, jnp.int32) ^ device[0]
            chunks.append(jnp.take(table[:, low:high], owners, axis=0))
        blocks.append(jnp.concatenate(chunks, axis=1))
    return blocks


def merge_kernel(parts, *refs):
    pairs = ((refs[0], refs[1]), (refs[2], refs[3]))
    targets = refs[4:]
    half = refs[0].shape[0] // 2
    for number, target in enumerate(targets):
        chunk, second = divmod(number, 2)

        @pl.loop(0, half)
        def _(index, target=target, chunk=chunk, first=second * half):
            at = 0
            for (home, came), (low, high) in zip(pairs, parts[chunk]):
                total = home[first + index, low:high, :].astype(jnp.float32)
                total += came[first + index, low:high, :].astype(jnp.float32)
                target[index, at : at + high - low, :] = total.astype(jnp.bfloat16)
                at += high - low


def cores_merged(parts, *blocks):
    half = blocks[0].shape[0] // 2
    if any((high - low) % ROWS for chunk in parts for low, high in chunk):
        pairs = (blocks[:2], blocks[2:])
        joined = []
        for chunk in parts:
            sums = [
                home[:, low:high].astype(jnp.float32) + came[:, low:high].astype(jnp.float32)
                for (home, came), (low, high) in zip(pairs, chunk)
            ]
            total = jnp.concatenate(sums, axis=1).astype(jnp.bfloat16)
            joined.append((total[:half], total[half:]))
        return joined
    shapes = [
        jax.ShapeDtypeStruct((half, sum(high - low for low, high in chunk), LANES), jnp.bfloat16)
        for chunk in parts
        for _ in range(2)
    ]
    found = pl.pallas_call(
        functools.partial(merge_kernel, parts),
        out_shape=shapes,
        in_specs=whole_specs(4),
        out_specs=whole_specs(len(shapes)),
        compiler_params=pltpu.CompilerParams(vmem_limit_bytes=20 << 20),
        cost_estimate=pl.CostEstimate(flops=0, bytes_accessed=0, transcendentals=0),
    )(*blocks)
    return list(zip(found[::2], found[1::2]))


def adam_update(weight_shard, gradient, moment_one, moment_two):
    moment_one = 0.9 * moment_one + 0.1 * gradient
    moment_two = 0.999 * moment_two + 0.001 * gradient * gradient
    fix_one = 1.0 - 0.9**STEP
    fix_two = 1.0 - 0.999**STEP
    weight_shard = weight_shard - 0.02 * (
        moment_one / fix_one / (jnp.sqrt(moment_two / fix_two) + 1e-08) + 0.1 * weight_shard
    )
    return (weight_shard, moment_one, moment_two)


def per_device(hidden_in, cotangent, params, moment_one, moment_two, seq_lengths, seq_owner):
    devices = lax.axis_size("dp")
    device = lax.axis_index("dp").astype(jnp.int32)
    here = device.reshape(1)
    attn_len = G1LEN // devices
    ffn_len = G2LEN // devices
    gain_len = params.shape[0] - attn_len - ffn_len
    attn_rows = attn_len // LANES
    tail_rows = -(-(attn_rows + 1) // ROWS) * ROWS - attn_rows
    pad = tail_rows * LANES - gain_len
    rounded = params.astype(jnp.bfloat16)
    first_piece = jnp.concatenate(
        [rounded[:attn_len], rounded[attn_len + ffn_len :], jnp.zeros((pad,), jnp.bfloat16)]
    ).reshape(-1, LANES)
    second_piece = rounded[attn_len : attn_len + ffn_len].reshape(-1, LANES)
    ffn_rows = ffn_len // LANES
    second_pieces = [second_piece[low:high] for low, high in cut_rows(ffn_rows, 2)]
    orders = bit_orders(devices, ("abxy", "bxya", "byax"))
    pieces = [first_piece, *second_pieces]
    chunks = gather_chunks(pieces, orders, devices)
    arrays, plan, tails = gathered_blocks(
        pieces[:1], chunks[:1], orders[:1], attn_rows, devices, here
    )
    ffn_arrays, ffn_plan, unused = gathered_blocks(
        pieces[1:], chunks[1:], orders[1:], ffn_rows, devices, here
    )
    aligned = attn_rows % ROWS == 0
    tables = slot_setup(seq_lengths, seq_owner, device)
    given = None
    if not aligned:
        given = tails.reshape(devices, -1)[:, :gain_len].astype(jnp.float32).reshape(1, -1)
    orders = bit_orders(devices, ("yxba", "ayxb", "xayb"))
    out_plan, block_shapes, ffn_parts = scatter_plan(ffn_rows, 0, orders, devices)
    staged = [(0, 0, 0)]
    if len(block_shapes) == 2:
        staged = [
            (part // 2, part % 2 * (devices // 4), low)
            for low, _ in cut_rows(ffn_rows, 2)
            for part in range(4)
        ]
    qkv_weight, out_weight, gains, block_out, delta_mid, delta_attn, late_gains, *found = run_layer(
        plan,
        ffn_plan,
        staged,
        out_plan,
        block_shapes,
        gain_len if aligned else 0,
        tail_rows,
        devices,
        here,
        hidden_in,
        cotangent,
        tables,
        given,
        arrays,
        ffn_arrays,
    )
    ffn_home, ffn_away = blocks_of(found, None, ffn_parts, orders, devices, here)
    ffn_came = across(ffn_away, 0, devices)
    attn_plan, block_shapes, attn_parts = scatter_plan(attn_rows, tail_rows, orders, devices)
    grad_in, gain_grads, *found = back_attn(
        attn_plan,
        gain_len if aligned else 0,
        tail_rows,
        devices,
        block_shapes,
        here,
        delta_attn,
        delta_mid,
        hidden_in,
        tables,
        gains,
        late_gains,
        qkv_weight,
        out_weight,
    )
    gain_table = None
    if not aligned:
        gain_table = gain_grads.reshape(devices, gain_len).astype(jnp.bfloat16)
        gain_table = jnp.pad(gain_table, ((0, 0), (0, pad))).reshape(devices, tail_rows, LANES)
    attn_home, attn_away = blocks_of(found, gain_table, attn_parts, orders, devices, here)
    attn_came = across(attn_away, 0, devices)
    parts = [
        [cut[chunk] for cut in (ffn_parts, attn_parts) if chunk < len(cut)]
        for chunk in range(len(ffn_parts))
    ]
    chunks = cores_merged(parts, ffn_home, ffn_came, attn_home, attn_came)
    for stage in range(len(orders[0])):
        chunks = merged_blocks(chunks, sent_blocks(chunks, orders, stage, devices))
    rows = [chunk for chunk, _ in chunks]
    ffn_take = [high - low for low, high in ffn_parts]
    ffn_shard = [chunk[:take].reshape(-1) for chunk, take in zip(rows, ffn_take)]
    attn_shard = jnp.concatenate([chunk[take:].reshape(-1) for chunk, take in zip(rows, ffn_take)])
    grad_shard = jnp.concatenate(
        [attn_shard[:attn_len], *ffn_shard, attn_shard[attn_len : attn_len + gain_len]]
    )
    params_new, moment_one_new, moment_two_new = adam_update(
        params, grad_shard, moment_one, moment_two
    )
    return (block_out, grad_in, grad_shard, params_new, moment_one_new, moment_two_new)


def solution(mesh):
    in_specs = (P("dp", None), P("dp", None), P("dp"), P("dp"), P("dp"), P(), P())
    out_specs = (P("dp", None), P("dp", None), P("dp"), P("dp"), P("dp"), P("dp"))
    return jax.shard_map(
        per_device, mesh=mesh, in_specs=in_specs, out_specs=out_specs, check_vma=False
    )
```

```python
import functools
import math

import jax
import jax.numpy as jnp
from jax import lax
from jax.experimental import pallas as pl
from jax.experimental.pallas import tpu as pltpu
from jax.sharding import PartitionSpec as P

D = 640
FF = 2048
HD = 256
HQ = 1024
CAP = 128
WINDOW = 64
STEP = 3
G1LEN = 1638400
G2LEN = 3932160
LANES = 128
ROWS = 16
GELU_SCALE = math.sqrt(2 / math.pi)
ATTN_PADDED, FFN_PADDED = 0, 2 * D


def rms_scale(values, gain_vec):
    return (
        values
        * lax.rsqrt(jnp.mean(values * values, axis=-1, keepdims=True) + 1e-06)
        * (1.0 + gain_vec)
    )


def rotate(values, cos_tab, sin_tab):
    half_dim = values.shape[-1] // 2
    lower_half = values[..., :half_dim]
    upper_half = values[..., half_dim:]
    return jnp.concatenate(
        [lower_half * cos_tab - upper_half * sin_tab, upper_half * cos_tab + lower_half * sin_tab],
        axis=-1,
    )


def gated_gelu(gate_proj, up_proj):
    return jax.nn.gelu(gate_proj, approximate=True) * up_proj


def times_transposed(rows_in, matrix):
    return lax.dot_general(
        rows_in, matrix, (((1,), (1,)), ((), ())), preferred_element_type=jnp.float32
    )


def slot_setup(seq_lengths, seq_owner, device):
    mine_mask = seq_owner == device
    own_lengths = jnp.where(mine_mask, seq_lengths, 0)
    seq_ends = jnp.cumsum(own_lengths, dtype=jnp.int32)
    seq_begins = seq_ends - own_lengths
    slot_index = jnp.arange(CAP, dtype=jnp.int32)
    column = slot_index[:, None]
    inside_mask = (
        mine_mask[None, :] & (seq_begins[None, :] <= column) & (column < seq_ends[None, :])
    )
    live_mask = jnp.any(inside_mask, axis=1)
    seq_label = jnp.sum(
        (mine_mask[None, :] & (seq_ends[None, :] <= column)).astype(jnp.int32),
        axis=1,
        dtype=jnp.int32,
    )
    position = jnp.sum(
        jnp.where(inside_mask, column - seq_begins[None, :], 0), axis=1, dtype=jnp.int32
    )
    row_slot = slot_index[:, None]
    col_slot = slot_index[None, :]
    allowed = live_mask[:, None] & live_mask[None, :] & (
        seq_label[:, None] == seq_label[None, :]
    ) & (col_slot <= row_slot) & (row_slot - col_slot < WINDOW) | (row_slot == col_slot)
    half_dim = HD // 2
    frequency = 10000.0 ** (-2.0 * jnp.arange(half_dim, dtype=jnp.float32) / HD)
    angles = position.astype(jnp.float32)[:, None] * frequency[None, :]
    live_wide = jnp.broadcast_to(live_mask[:, None], (CAP, LANES)).astype(jnp.float32)
    return jnp.concatenate(
        [jnp.cos(angles), jnp.sin(angles), allowed.astype(jnp.float32), live_wide], axis=1
    )


def rms_pull(raw, gain_vec, delta):
    scale = lax.rsqrt(jnp.mean(raw * raw, axis=-1, keepdims=True) + 1e-06)
    weighed = delta * (1.0 + gain_vec)
    shared = jnp.mean(raw * weighed, axis=-1, keepdims=True)
    return scale * weighed - raw * (scale * scale * scale * shared), delta * raw * scale


def rotate_pull(delta, cos_tab, sin_tab):
    half_dim = delta.shape[-1] // 2
    lower_half = delta[:, :half_dim]
    upper_half = delta[:, half_dim:]
    return jnp.concatenate(
        [lower_half * cos_tab + upper_half * sin_tab, upper_half * cos_tab - lower_half * sin_tab],
        axis=-1,
    )


def bit_orders(devices, tuned):
    bits = devices.bit_length() - 1
    if bits == 5:
        return [["cxyab".index(letter) for letter in order] for order in tuned]
    return [[1 + (shift + step) % (bits - 1) for step in range(bits - 1)] for shift in range(3)]


def across(block, bit, devices):
    return lax.ppermute(block, "dp", [(i, i ^ (1 << bit)) for i in range(devices)])


def offset_of(place, order):
    return sum(((place >> k) & 1) << bit for k, bit in enumerate(order))


def gather_chunks(pieces, orders, devices):
    held = [piece[None] for piece in pieces]
    for stage in range(len(orders[0]) - 1):
        came = [across(block, order[stage], devices) for block, order in zip(held, orders)]
        for chunk in range(1, len(came)):
            came[chunk] = lax.optimization_barrier((came[chunk], came[0]))[0]
        held = [jnp.concatenate(pair) for pair in zip(held, came)]
    last = [across(block, order[-1], devices) for block, order in zip(held, orders)]
    chunks = []
    for block, final in zip(held, last):
        if chunks:
            final = lax.optimization_barrier((final, *chunks[0][2:]))[0]
        chunks.append((block, final, across(block, 0, devices), across(final, 0, devices)))
    return chunks


def sent_blocks(chunks, orders, stage, devices):
    return [
        across(away, order[stage], devices)
        for (_, away), order in zip(chunks, orders)
    ]


def merged_blocks(chunks, came):
    merged = []
    for (home, _), arrived in zip(chunks, came):
        half = home.shape[0] // 2

        def added(low, high):
            return home[low:high].astype(jnp.float32) + arrived[low:high].astype(jnp.float32)

        if half:
            merged.append(
                (
                    added(0, half).astype(jnp.bfloat16),
                    added(half, 2 * half).astype(jnp.bfloat16),
                )
            )
        else:
            merged.append((added(0, 1)[0], None))
    return merged


def cut_rows(rows, parts):
    each = -(-rows // (parts * ROWS)) * ROWS
    return [(low, min(low + each, rows)) for low in range(0, rows, each)]


def whole_specs(count):
    return [pl.BlockSpec(memory_space=pltpu.VMEM)] * count


def owner_rows(device, index, order, extra, start, each):
    owner = device ^ extra
    for k, bit in enumerate(order):
        owner = owner ^ (((index >> k) & 1) << bit)
    return owner, owner * each + start


def copy_step(rows):
    return max(step for step in range(ROWS, 513, ROWS) if rows % step == 0)


def each_piece(padded, first, take, visit):
    def visit_plain(shift):
        step = copy_step(take)

        def visit_step(part):
            at = part * step
            visit(at, step, pl.multiple_of(first + shift + at, ROWS))

        if take == step:
            visit_step(0)
        else:
            pl.loop(0, take // step)(visit_step)

    if not padded:
        visit_plain(0)
        return
    units = take // ROWS
    inner = max(count for count in range(1, 41) if units % count == 0)
    number = first // ROWS

    def visit_units(row_of):
        def visit_some(step):
            for part in range(inner):
                at = (step * inner + part) * ROWS
                visit(at, ROWS, row_of(step * inner + part))

        if units == inner:
            visit_some(0)
        else:
            pl.loop(0, units // inner)(visit_some)

    longer = (ROWS + 1) * number
    pl.when(number + units <= padded)(lambda: visit_units(lambda k: longer + (ROWS + 1) * k))
    pl.when(number >= padded)(lambda: visit_plain(padded))
    pl.when((number < padded) & (number + units > padded))(
        lambda: visit_units(lambda k: ROWS * (number + k) + jnp.minimum(number + k, padded))
    )


def spread_blocks(padded, plan, views, device, spread, tails):
    for (order, extra, take, start, each), (block_ref, first_index, count, first_row) in zip(
        plan, views
    ):

        @pl.loop(0, count)
        def _(
            index,
            order=order,
            extra=extra,
            take=take,
            start=start,
            each=each,
            block_ref=block_ref,
            first_index=first_index,
            first_row=first_row,
        ):
            owner, first = owner_rows(device, index, order, extra, start, each)

            def spread_unit(at, unit, row):
                low = first_row + at
                if not isinstance(low, int):
                    low = pl.multiple_of(low, ROWS)
                spread[pl.ds(row, unit), :] = block_ref[
                    first_index + index, pl.ds(low, unit), :
                ].astype(jnp.float32)

            each_piece(padded, first, take, spread_unit)
            if tails is not None:
                tails[owner] = block_ref[index, take : take + tails.shape[1], :]


def pitch_of(columns):
    blocks = columns // LANES
    return blocks + (blocks == ROWS)


def fold_matrices(spread, targets):
    first = 0
    for matrix, offset, rows, columns in targets:
        blocks = columns // LANES
        pitch = pitch_of(columns)

        @pl.loop(0, rows // LANES)
        def _(step, matrix=matrix, offset=offset, blocks=blocks, pitch=pitch, first=first):
            base = first + step * (LANES * pitch)
            at = pl.ds(pl.multiple_of(step * LANES, LANES), LANES)
            for block in range(blocks):
                low = offset + block * LANES
                matrix[at, low : low + LANES] = spread[
                    pl.ds(base + block, LANES, stride=pitch), :
                ].astype(jnp.bfloat16)

        first += rows * pitch


def spread_grads(spread, products):
    first = 0
    for turned, right, columns in products:
        rows = turned.shape[0]
        blocks = columns // LANES
        pitch = pitch_of(columns)
        wide = 2 - blocks % 2
        for block in range(0, blocks, wide):
            product = jnp.dot(
                turned,
                right(block * LANES, (block + wide) * LANES),
                preferred_element_type=jnp.float32,
            )
            for part in range(wide):
                spread[pl.ds(first + block + part, rows, stride=pitch), :] = product[
                    :, part * LANES : (part + 1) * LANES
                ]
        first += rows * pitch


def place_blocks(padded, plan, device, spread, tails, targets):
    for target, order, extra, low, take, start, each in plan:
        target_ref = targets[target]

        @pl.loop(0, target_ref.shape[0])
        def _(
            index,
            target_ref=target_ref,
            order=order,
            extra=extra,
            low=low,
            take=take,
            start=start,
            each=each,
        ):
            owner, first = owner_rows(device, index, order, extra, start or 0, each)
            if start is None:
                target_ref[index, low : low + take, :] = tails[owner].astype(jnp.bfloat16)
                return

            def place_unit(at, unit, row):
                at = low + at
                if not isinstance(at, int):
                    at = pl.multiple_of(at, ROWS)
                target_ref[index, pl.ds(at, unit), :] = spread[pl.ds(row, unit), :].astype(
                    jnp.bfloat16
                )

            each_piece(padded, first, take, place_unit)


def attn_forward(hidden_in, qkv_weight, tables, gains):
    cos_tab = tables[:, :LANES]
    sin_tab = tables[:, LANES : 2 * LANES]
    open_pairs = tables[:, 2 * LANES : 3 * LANES] > 0.0
    gain_query = gains[:, D : D + HD]
    gain_key = gains[:, D + HD : D + 2 * HD]
    normed_in = rms_scale(hidden_in[...].astype(jnp.float32), gains[:, :D]).astype(jnp.bfloat16)
    raw = jnp.dot(normed_in, qkv_weight[...], preferred_element_type=jnp.float32)
    key_raw = raw[:, HQ : HQ + HD]
    values = raw[:, HQ + HD :].astype(jnp.bfloat16)
    keys = rotate(rms_scale(key_raw, gain_key), cos_tab, sin_tab).astype(jnp.bfloat16)
    heads = []
    for head in range(HQ // HD):
        query_raw = raw[:, head * HD : (head + 1) * HD]
        rot_query = rotate(rms_scale(query_raw, gain_query), cos_tab, sin_tab) * HD ** (-0.5)
        rot_query = rot_query.astype(jnp.bfloat16)
        scores = jnp.where(open_pairs, times_transposed(rot_query, keys), -1e30)
        row_max = jnp.max(scores, axis=-1, keepdims=True)
        raised = jnp.exp(scores - row_max)
        summed = jnp.sum(raised, axis=-1, keepdims=True)
        context = jnp.dot(
            (raised / summed).astype(jnp.bfloat16), values, preferred_element_type=jnp.float32
        ).astype(jnp.bfloat16)
        heads.append((query_raw, rot_query, scores, row_max + jnp.log(summed), context))
    return normed_in, key_raw, values, keys, heads, cos_tab, sin_tab


def join_gains(tails, gain_len, gains):
    lane = lax.broadcasted_iota(jnp.int32, (1, LANES), 1)
    tiles = [jnp.zeros((1, LANES), jnp.float32) for _ in range(gains.shape[1] // LANES)]
    for owner in range(tails.shape[0]):
        tile, shift = divmod(owner * gain_len, LANES)
        run = jnp.where(lane < gain_len, tails[owner].astype(jnp.float32)[0:1, :], 0.0)
        if shift:
            run = pltpu.roll(run, shift, 1)
        tiles[tile] += jnp.where(lane >= shift, run, 0.0)
        if shift + gain_len > LANES:
            tiles[tile + 1] += jnp.where(lane < shift, run, 0.0)
    for number, tile in enumerate(tiles):
        gains[:, number * LANES : (number + 1) * LANES] = tile


def attn_forward_kernel(plan, gain_len, device_ref, hidden_in, tables, *refs):
    if not gain_len:
        given, refs = refs[0], refs[1:]
    sources = refs[: len(plan)]
    refs = refs[len(plan) :]
    qkv_weight, out_weight, gains, attn_out, mid_stream = refs[:5]
    staging, spread, tails, context, sems = refs[5:]
    copies, views = [], []
    for number, source in enumerate(sources):
        count = source.shape[0]
        held = staging.at[pl.ds(number * count, count)]
        copies.append(pltpu.make_async_copy(source, held, sems.at[number]))
        views.append((held, 0, count, 0))
    for copy in copies:
        copy.start()
    for copy, step, view in zip(copies, plan, views):
        copy.wait()
        spread_blocks(
            ATTN_PADDED,
            [step],
            [view],
            device_ref[0],
            spread,
            tails if gain_len else None,
        )
    if gain_len:
        join_gains(tails, gain_len, gains)
    else:
        gains[...] = given[...]
    fold_matrices(
        spread,
        (
            (qkv_weight, 0, D, HQ),
            (qkv_weight, HQ, D, HD),
            (qkv_weight, HQ + HD, D, HD),
            (out_weight, 0, HQ, D),
        ),
    )
    heads = attn_forward(hidden_in, qkv_weight, tables, gains)[4]
    for head, parts in enumerate(heads):
        context[:, head * HD : (head + 1) * HD] = parts[-1]
    out = jnp.dot(context[...], out_weight[...], preferred_element_type=jnp.float32)
    attn_out[...] = out
    gain_post = gains[:, D + 2 * HD : 2 * D + 2 * HD]
    mid_stream[...] = hidden_in[...].astype(jnp.float32) + rms_scale(out, gain_post)


def forward_attn(plan, gain_len, tail_rows, devices, device, hidden_in, tables, given, arrays):
    shapes = [
        jax.ShapeDtypeStruct((D, HQ + 2 * HD), jnp.bfloat16),
        jax.ShapeDtypeStruct((HQ, D), jnp.bfloat16),
        jax.ShapeDtypeStruct((1, 4 * D + 2 * HD), jnp.float32),
        jax.ShapeDtypeStruct((CAP, D), jnp.float32),
        jax.ShapeDtypeStruct((CAP, D), jnp.float32),
    ]
    given = [] if gain_len else [given]
    held = (sum(array.shape[0] for array in arrays),) + arrays[0].shape[1:]
    return pl.pallas_call(
        functools.partial(attn_forward_kernel, plan, gain_len),
        out_shape=shapes,
        in_specs=[pl.BlockSpec(memory_space=pltpu.SMEM)]
        + whole_specs(2 + len(given))
        + [pl.BlockSpec(memory_space=pltpu.HBM)] * len(arrays),
        out_specs=whole_specs(len(shapes)),
        scratch_shapes=[
            pltpu.VMEM(held, jnp.bfloat16),
            pltpu.VMEM((G1LEN // LANES + ATTN_PADDED, LANES), jnp.float32),
            pltpu.VMEM((devices, tail_rows, LANES) if gain_len else (1, ROWS, LANES), jnp.bfloat16),
            pltpu.VMEM((CAP, HQ), jnp.bfloat16),
            pltpu.SemaphoreType.DMA((len(arrays),)),
        ],
        compiler_params=pltpu.CompilerParams(vmem_limit_bytes=24 << 20),
        cost_estimate=pl.CostEstimate(flops=0, bytes_accessed=64 << 20, transcendentals=0),
    )(device, hidden_in, tables, *given, *arrays)


def ffn_kernel(
    plan_in,
    plan_out,
    device_ref,
    mid_ref,
    attn_out,
    cotangent,
    tables,
    gains,
    *refs,
):
    sources = refs[: len(plan_in)]
    refs = refs[len(plan_in) :]
    block_out, delta_mid_ref, delta_attn_ref, late_gains = refs[:4]
    targets = refs[4:-9]
    spread, gate_weight, up_weight, down_weight = refs[-9:-5]
    gates, ups, hidden, delta_gate, delta_up = refs[-5:]
    device = device_ref[0]
    views = [(source, 0, source.shape[0], 0) for source in sources]
    mid_stream = mid_ref[...]
    gain_post = gains[:, D + 2 * HD : 2 * D + 2 * HD]
    gain_mid = gains[:, 2 * D + 2 * HD : 3 * D + 2 * HD]
    gain_last = gains[:, 3 * D + 2 * HD :]
    normed_mid = rms_scale(mid_stream, gain_mid).astype(jnp.bfloat16)
    spread_blocks(FFN_PADDED, plan_in, views, device, spread, None)
    fold_matrices(
        spread, ((gate_weight, 0, D, FF), (up_weight, 0, D, FF), (down_weight, 0, FF, D))
    )
    parts = [slice(low, low + 512) for low in range(0, FF, 512)]
    for at in parts:
        gate = jnp.dot(normed_mid, gate_weight[:, at], preferred_element_type=jnp.float32)
        up = jnp.dot(normed_mid, up_weight[:, at], preferred_element_type=jnp.float32)
        gates[:, at] = gate
        ups[:, at] = up
        hidden[:, at] = gated_gelu(gate, up).astype(jnp.bfloat16)
    ffn_out = jnp.dot(hidden[...], down_weight[...], preferred_element_type=jnp.float32)
    block_out[...] = (mid_stream + rms_scale(ffn_out, gain_last)).astype(jnp.bfloat16)
    delta_out = cotangent[...].astype(jnp.float32) * tables[:, 3 * LANES : 3 * LANES + 1]
    delta_ffn, gain_rows = rms_pull(ffn_out, gain_last, delta_out)
    late_gains[2:3, :] = jnp.sum(gain_rows, axis=0, keepdims=True)
    delta_ffn = delta_ffn.astype(jnp.bfloat16)
    delta_normed = jnp.zeros((CAP, D), jnp.float32)
    for at in parts:
        delta_hidden = times_transposed(delta_ffn, down_weight[at, :])
        gate = gates[:, at]
        raised = jnp.tanh(GELU_SCALE * (gate + 0.044715 * (gate * gate * gate)))
        share = 0.5 * (1.0 + raised)
        slope = share + (0.5 * GELU_SCALE) * gate * (1.0 - raised * raised) * (
            1.0 + (3 * 0.044715) * (gate * gate)
        )
        delta_gate[:, at] = (delta_hidden * ups[:, at] * slope).astype(jnp.bfloat16)
        delta_up[:, at] = (delta_hidden * (gate * share)).astype(jnp.bfloat16)
        delta_normed += times_transposed(delta_gate[:, at], gate_weight[:, at])
        delta_normed += times_transposed(delta_up[:, at], up_weight[:, at])
    delta_part, gain_rows = rms_pull(mid_stream, gain_mid, delta_normed)
    late_gains[1:2, :] = jnp.sum(gain_rows, axis=0, keepdims=True)
    delta_mid = delta_out + delta_part
    delta_mid_ref[...] = delta_mid
    delta_attn, gain_rows = rms_pull(attn_out[...], gain_post, delta_mid)
    late_gains[0:1, :] = jnp.sum(gain_rows, axis=0, keepdims=True)
    delta_attn_ref[...] = delta_attn.astype(jnp.bfloat16)
    turned = normed_mid.T
    spread_grads(
        spread,
        (
            (turned, lambda low, high: delta_gate[:, low:high], FF),
            (turned, lambda low, high: delta_up[:, low:high], FF),
            (hidden[...].T, lambda low, high: delta_ffn[:, low:high], D),
        ),
    )
    place_blocks(FFN_PADDED, plan_out, device, spread, None, targets)


def run_ffn(
    plan_in, plan_out, block_shapes, device, mid, attn_out, cotangent, tables, gains, arrays
):
    flat_rows = G2LEN // LANES + FFN_PADDED
    shapes = [
        jax.ShapeDtypeStruct((CAP, D), jnp.bfloat16),
        jax.ShapeDtypeStruct((CAP, D), jnp.float32),
        jax.ShapeDtypeStruct((CAP, D), jnp.bfloat16),
        jax.ShapeDtypeStruct((3, D), jnp.float32),
    ] + [jax.ShapeDtypeStruct(shape, jnp.bfloat16) for shape in block_shapes]
    wide = pltpu.VMEM((CAP, FF), jnp.float32)
    narrow = pltpu.VMEM((CAP, FF), jnp.bfloat16)
    return pl.pallas_call(
        functools.partial(ffn_kernel, plan_in, plan_out),
        out_shape=shapes,
        in_specs=[pl.BlockSpec(memory_space=pltpu.SMEM)]
        + whole_specs(5 + len(arrays)),
        out_specs=whole_specs(len(shapes)),
        scratch_shapes=[
            pltpu.VMEM((flat_rows, LANES), jnp.float32),
            pltpu.VMEM((D, FF), jnp.bfloat16),
            pltpu.VMEM((D, FF), jnp.bfloat16),
            pltpu.VMEM((FF, D), jnp.bfloat16),
            wide,
            wide,
            narrow,
            narrow,
            narrow,
        ],
        compiler_params=pltpu.CompilerParams(vmem_limit_bytes=(46 if len(arrays) > 1 else 58) << 20),
        cost_estimate=pl.CostEstimate(flops=0, bytes_accessed=0, transcendentals=0),
    )(device, mid, attn_out, cotangent, tables, gains, *arrays)


def attn_back_kernel(
    plan,
    gain_len,
    device_ref,
    delta_attn,
    delta_mid,
    hidden_in,
    tables,
    gains,
    late_gains,
    qkv_weight,
    out_weight,
    grad_in,
    gain_grads,
    *refs,
):
    targets = refs[:-4]
    spread, tails, delta_raws, contexts = refs[-4:]
    device = device_ref[0]
    normed_in, key_raw, values, keys, heads, cos_tab, sin_tab = attn_forward(
        hidden_in, qkv_weight, tables, gains
    )
    gain_query = gains[:, D : D + HD]
    gain_key = gains[:, D + HD : D + 2 * HD]
    delta_context = times_transposed(delta_attn[...], out_weight[...]).astype(jnp.bfloat16)
    delta_key = jnp.zeros((CAP, HD), jnp.float32)
    delta_value = jnp.zeros((CAP, HD), jnp.float32)
    query_gain_rows = jnp.zeros((CAP, HD), jnp.float32)
    for head, (query_raw, queries, scores, log_total, context) in enumerate(heads):
        at = slice(head * HD, (head + 1) * HD)
        contexts[:, at] = context
        head_delta = delta_context[:, at]
        row_dot = jnp.sum(
            head_delta.astype(jnp.float32) * context.astype(jnp.float32), axis=-1, keepdims=True
        )
        prob_exact = jnp.exp(scores - log_total)
        delta_prob = times_transposed(head_delta, values)
        delta_score = prob_exact * (delta_prob - row_dot)
        turned = delta_score.T.astype(jnp.bfloat16)
        delta_score = delta_score.astype(jnp.bfloat16)
        delta_query = jnp.dot(delta_score, keys, preferred_element_type=jnp.float32)
        delta_key += jnp.dot(turned, queries, preferred_element_type=jnp.float32)
        delta_value += jnp.dot(
            prob_exact.T.astype(jnp.bfloat16), head_delta, preferred_element_type=jnp.float32
        )
        delta_rot = rotate_pull(delta_query * HD ** (-0.5), cos_tab, sin_tab)
        delta_raw, gain_rows = rms_pull(query_raw, gain_query, delta_rot)
        query_gain_rows += gain_rows
        delta_raws[:, at] = delta_raw.astype(jnp.bfloat16)
    delta_raw, gain_rows = rms_pull(key_raw, gain_key, rotate_pull(delta_key, cos_tab, sin_tab))
    delta_raws[:, HQ : HQ + HD] = delta_raw.astype(jnp.bfloat16)
    delta_raws[:, HQ + HD :] = delta_value.astype(jnp.bfloat16)
    gain_grads[:, D : D + HD] = jnp.sum(query_gain_rows, axis=0, keepdims=True)
    gain_grads[:, D + HD : D + 2 * HD] = jnp.sum(gain_rows, axis=0, keepdims=True)
    delta_in = times_transposed(delta_raws[...], qkv_weight[...])
    delta_part, gain_rows = rms_pull(
        hidden_in[...].astype(jnp.float32), gains[:, :D], delta_in
    )
    grad_in[...] = delta_mid[...] + delta_part
    gain_grads[:, :D] = jnp.sum(gain_rows, axis=0, keepdims=True)
    for late in range(3):
        at = slice((late + 1) * D + 2 * HD, (late + 2) * D + 2 * HD)
        gain_grads[:, at] = late_gains[late : late + 1, :]
    if gain_len:
        tails[...] = jnp.zeros_like(tails)
        lane = lax.broadcasted_iota(jnp.int32, (1, LANES), 1)
        for owner in range(tails.shape[0]):
            row, shift = divmod(owner * gain_len, LANES)
            piece = gain_grads[:, row * LANES : (row + 1) * LANES]
            if shift:
                piece = pltpu.roll(piece, LANES - shift, 1)
            if shift + gain_len > LANES:
                after = gain_grads[:, (row + 1) * LANES : (row + 2) * LANES]
                after = pltpu.roll(after, LANES - shift, 1)
                piece = jnp.where(lane < LANES - shift, piece, after)
            tails[owner, 0:1, :] = jnp.where(lane < gain_len, piece, 0.0)
    turned = normed_in.T
    delta_attn_value = delta_attn[...]
    spread_grads(
        spread,
        (
            (turned, lambda low, high: delta_raws[:, low:high], HQ),
            (turned, lambda low, high: delta_raws[:, HQ + low : HQ + high], HD),
            (turned, lambda low, high: delta_raws[:, HQ + HD + low : HQ + HD + high], HD),
            (contexts[...].T, lambda low, high: delta_attn_value[:, low:high], D),
        ),
    )
    place_blocks(ATTN_PADDED, plan, device, spread, tails, targets)


def back_attn(plan, gain_len, tail_rows, devices, block_shapes, device, *inputs):
    flat_rows = G1LEN // LANES + ATTN_PADDED
    shapes = [
        jax.ShapeDtypeStruct((CAP, D), jnp.float32),
        jax.ShapeDtypeStruct((1, 4 * D + 2 * HD), jnp.float32),
    ] + [jax.ShapeDtypeStruct(shape, jnp.bfloat16) for shape in block_shapes]
    tail_shape = (devices, tail_rows, LANES) if gain_len else (1, ROWS, LANES)
    return pl.pallas_call(
        functools.partial(attn_back_kernel, plan, gain_len),
        out_shape=shapes,
        in_specs=[pl.BlockSpec(memory_space=pltpu.SMEM)] + whole_specs(len(inputs)),
        out_specs=whole_specs(len(shapes)),
        scratch_shapes=[
            pltpu.VMEM((flat_rows, LANES), jnp.float32),
            pltpu.VMEM(tail_shape, jnp.float32),
            pltpu.VMEM((CAP, HQ + 2 * HD), jnp.bfloat16),
            pltpu.VMEM((CAP, HQ), jnp.bfloat16),
        ],
        compiler_params=pltpu.CompilerParams(vmem_limit_bytes=22 << 20),
        cost_estimate=pl.CostEstimate(flops=0, bytes_accessed=0, transcendentals=0),
    )(device, *inputs)


def gathered_blocks(pieces, chunks, orders, each, devices, device):
    arrays, plan, start = [], [], 0
    for piece, blocks, order in zip(pieces, chunks, orders):
        take = min(piece.shape[0], each - start)
        if each % ROWS:
            places = [offset_of(place, list(order) + [0]) for place in range(devices)]
            back = sorted(range(devices), key=places.__getitem__)
            mixed = offset_bits(device[0], list(order) + [0])
            arrays.append(
                jnp.take(jnp.concatenate(blocks), jnp.array(back, jnp.int32) ^ mixed, axis=0)
            )
            continue
        for part, block in enumerate(blocks):
            plan.append((order[:-1], offset_of(part, [order[-1], 0]), take, start, each))
            arrays.append(block)
        start += take
    if each % ROWS == 0:
        return arrays, plan, None
    table = jnp.concatenate(arrays, axis=1)
    flat = table[:, :each].reshape(1, devices * each, LANES)
    return [flat], [([], 0, devices * each, 0, 0)], table[:, each:]


def offset_bits(device, order):
    return sum(((device >> bit) & 1) << k for k, bit in enumerate(order))


def scatter_plan(each, tail_rows, orders, devices):
    parts = cut_rows(each + tail_rows, len(orders))
    half = devices // 2
    if each % ROWS:
        return [(0, [], 0, 0, devices * each, 0, 0)], [(1, devices * each, LANES)], parts
    plan = []
    for with_core in (1, 0):
        for (low, high), order in zip(parts, orders):
            order = order[::-1]
            plan.append((with_core, order, with_core, low, min(high, each) - low, low, each))
            if high > each:
                plan.append((with_core, order, with_core, each, tail_rows, None, each))
    return plan, [(half, each + tail_rows, LANES)] * 2, parts


def blocks_of(found, tails, parts, orders, devices, device):
    if len(found) == 2:
        return found
    table = found[0].reshape(devices, -1, LANES)
    table = table if tails is None else jnp.concatenate([table, tails], axis=1)
    blocks = []
    for with_core in (0, 1):
        chunks = []
        for (low, high), order in zip(parts, orders):
            places = range(devices // 2)
            offsets = [offset_of(place, order[::-1]) ^ with_core for place in places]
            owners = jnp.array(offsets, jnp.int32) ^ device[0]
            chunks.append(jnp.take(table[:, low:high], owners, axis=0))
        blocks.append(jnp.concatenate(chunks, axis=1))
    return blocks


def merge_kernel(parts, *refs):
    pairs = ((refs[0], refs[1]), (refs[2], refs[3]))
    targets = refs[4:]
    half = refs[0].shape[0] // 2
    for number, target in enumerate(targets):
        chunk, second = divmod(number, 2)

        @pl.loop(0, half)
        def _(index, target=target, chunk=chunk, first=second * half):
            at = 0
            for (home, came), (low, high) in zip(pairs, parts[chunk]):
                total = home[first + index, low:high, :].astype(jnp.float32)
                total += came[first + index, low:high, :].astype(jnp.float32)
                target[index, at : at + high - low, :] = total.astype(jnp.bfloat16)
                at += high - low


def cores_merged(parts, *blocks):
    half = blocks[0].shape[0] // 2
    if any((high - low) % ROWS for chunk in parts for low, high in chunk):
        pairs = (blocks[:2], blocks[2:])
        joined = []
        for chunk in parts:
            sums = [
                home[:, low:high].astype(jnp.float32) + came[:, low:high].astype(jnp.float32)
                for (home, came), (low, high) in zip(pairs, chunk)
            ]
            total = jnp.concatenate(sums, axis=1).astype(jnp.bfloat16)
            joined.append((total[:half], total[half:]))
        return joined
    shapes = [
        jax.ShapeDtypeStruct((half, sum(high - low for low, high in chunk), LANES), jnp.bfloat16)
        for chunk in parts
        for _ in range(2)
    ]
    found = pl.pallas_call(
        functools.partial(merge_kernel, parts),
        out_shape=shapes,
        in_specs=whole_specs(4),
        out_specs=whole_specs(len(shapes)),
        compiler_params=pltpu.CompilerParams(vmem_limit_bytes=20 << 20),
        cost_estimate=pl.CostEstimate(flops=0, bytes_accessed=0, transcendentals=0),
    )(*blocks)
    return list(zip(found[::2], found[1::2]))


def adam_update(weight_shard, gradient, moment_one, moment_two):
    moment_one = 0.9 * moment_one + 0.1 * gradient
    moment_two = 0.999 * moment_two + 0.001 * gradient * gradient
    fix_one = 1.0 - 0.9**STEP
    fix_two = 1.0 - 0.999**STEP
    weight_shard = weight_shard - 0.02 * (
        moment_one / fix_one / (jnp.sqrt(moment_two / fix_two) + 1e-08) + 0.1 * weight_shard
    )
    return (weight_shard, moment_one, moment_two)


def per_device(hidden_in, cotangent, params, moment_one, moment_two, seq_lengths, seq_owner):
    devices = lax.axis_size("dp")
    device = lax.axis_index("dp").astype(jnp.int32)
    here = device.reshape(1)
    attn_len = G1LEN // devices
    ffn_len = G2LEN // devices
    gain_len = params.shape[0] - attn_len - ffn_len
    attn_rows = attn_len // LANES
    tail_rows = -(-(attn_rows + 1) // ROWS) * ROWS - attn_rows
    pad = tail_rows * LANES - gain_len
    rounded = params.astype(jnp.bfloat16)
    first_piece = jnp.concatenate(
        [rounded[:attn_len], rounded[attn_len + ffn_len :], jnp.zeros((pad,), jnp.bfloat16)]
    ).reshape(-1, LANES)
    second_piece = rounded[attn_len : attn_len + ffn_len].reshape(-1, LANES)
    ffn_rows = ffn_len // LANES
    second_pieces = [second_piece[low:high] for low, high in cut_rows(ffn_rows, 2)]
    orders = bit_orders(devices, ("abxy", "bxya", "byax"))
    pieces = [first_piece, *second_pieces]
    chunks = gather_chunks(pieces, orders, devices)
    arrays, plan, tails = gathered_blocks(
        pieces[:1], chunks[:1], orders[:1], attn_rows, devices, here
    )
    ffn_arrays, ffn_plan, unused = gathered_blocks(
        pieces[1:], chunks[1:], orders[1:], ffn_rows, devices, here
    )
    aligned = attn_rows % ROWS == 0
    tables = slot_setup(seq_lengths, seq_owner, device)
    given = None
    if not aligned:
        given = tails.reshape(devices, -1)[:, :gain_len].astype(jnp.float32).reshape(1, -1)
    qkv_weight, out_weight, gains, attn_out, mid_stream = forward_attn(
        plan,
        gain_len if aligned else 0,
        tail_rows,
        devices,
        here,
        hidden_in,
        tables,
        given,
        arrays,
    )
    orders = bit_orders(devices, ("yxba", "ayxb", "xayb"))
    out_plan, block_shapes, ffn_parts = scatter_plan(ffn_rows, 0, orders, devices)
    block_out, delta_mid, delta_attn, late_gains, *found = run_ffn(
        ffn_plan,
        out_plan,
        block_shapes,
        here,
        mid_stream,
        attn_out,
        cotangent,
        tables,
        gains,
        ffn_arrays,
    )
    ffn_home, ffn_away = blocks_of(found, None, ffn_parts, orders, devices, here)
    ffn_came = across(ffn_away, 0, devices)
    attn_plan, block_shapes, attn_parts = scatter_plan(attn_rows, tail_rows, orders, devices)
    grad_in, gain_grads, *found = back_attn(
        attn_plan,
        gain_len if aligned else 0,
        tail_rows,
        devices,
        block_shapes,
        here,
        delta_attn,
        delta_mid,
        hidden_in,
        tables,
        gains,
        late_gains,
        qkv_weight,
        out_weight,
    )
    gain_table = None
    if not aligned:
        gain_table = gain_grads.reshape(devices, gain_len).astype(jnp.bfloat16)
        gain_table = jnp.pad(gain_table, ((0, 0), (0, pad))).reshape(devices, tail_rows, LANES)
    attn_home, attn_away = blocks_of(found, gain_table, attn_parts, orders, devices, here)
    attn_came = across(attn_away, 0, devices)
    parts = [
        [cut[chunk] for cut in (ffn_parts, attn_parts) if chunk < len(cut)]
        for chunk in range(len(ffn_parts))
    ]
    chunks = cores_merged(parts, ffn_home, ffn_came, attn_home, attn_came)
    for stage in range(len(orders[0])):
        chunks = merged_blocks(chunks, sent_blocks(chunks, orders, stage, devices))
    rows = [chunk for chunk, _ in chunks]
    ffn_take = [high - low for low, high in ffn_parts]
    ffn_shard = [chunk[:take].reshape(-1) for chunk, take in zip(rows, ffn_take)]
    attn_shard = jnp.concatenate([chunk[take:].reshape(-1) for chunk, take in zip(rows, ffn_take)])
    grad_shard = jnp.concatenate(
        [attn_shard[:attn_len], *ffn_shard, attn_shard[attn_len : attn_len + gain_len]]
    )
    params_new, moment_one_new, moment_two_new = adam_update(
        params, grad_shard, moment_one, moment_two
    )
    return (block_out, grad_in, grad_shard, params_new, moment_one_new, moment_two_new)


def solution(mesh):
    in_specs = (P("dp", None), P("dp", None), P("dp"), P("dp"), P("dp"), P(), P())
    out_specs = (P("dp", None), P("dp", None), P("dp"), P("dp"), P("dp"), P("dp"))
    return jax.shard_map(
        per_device, mesh=mesh, in_specs=in_specs, out_specs=out_specs, check_vma=False
    )
```

```python
import functools
import math

import jax
import jax.numpy as jnp
from jax import lax
from jax.experimental import pallas as pl
from jax.experimental.pallas import tpu as pltpu
from jax.sharding import PartitionSpec as P

D = 640
FF = 2048
HD = 256
HQ = 1024
CAP = 128
WINDOW = 64
STEP = 3
G1LEN = 1638400
G2LEN = 3932160
LANES = 128
ROWS = 16
GELU_SCALE = math.sqrt(2 / math.pi)
ATTN_PADDED, FFN_PADDED = 0, 2 * D


def rms_scale(values, gain_vec):
    return (
        values
        * lax.rsqrt(jnp.mean(values * values, axis=-1, keepdims=True) + 1e-06)
        * (1.0 + gain_vec)
    )


def rotate(values, cos_tab, sin_tab):
    half_dim = values.shape[-1] // 2
    lower_half = values[..., :half_dim]
    upper_half = values[..., half_dim:]
    return jnp.concatenate(
        [lower_half * cos_tab - upper_half * sin_tab, upper_half * cos_tab + lower_half * sin_tab],
        axis=-1,
    )


def gated_gelu(gate_proj, up_proj):
    return jax.nn.gelu(gate_proj, approximate=True) * up_proj


def times_transposed(rows_in, matrix):
    return lax.dot_general(
        rows_in, matrix, (((1,), (1,)), ((), ())), preferred_element_type=jnp.float32
    )


def slot_setup(seq_lengths, seq_owner, device):
    mine_mask = seq_owner == device
    own_lengths = jnp.where(mine_mask, seq_lengths, 0)
    seq_ends = jnp.cumsum(own_lengths, dtype=jnp.int32)
    seq_begins = seq_ends - own_lengths
    slot_index = jnp.arange(CAP, dtype=jnp.int32)
    column = slot_index[:, None]
    inside_mask = (
        mine_mask[None, :] & (seq_begins[None, :] <= column) & (column < seq_ends[None, :])
    )
    live_mask = jnp.any(inside_mask, axis=1)
    seq_label = jnp.sum(
        (mine_mask[None, :] & (seq_ends[None, :] <= column)).astype(jnp.int32),
        axis=1,
        dtype=jnp.int32,
    )
    position = jnp.sum(
        jnp.where(inside_mask, column - seq_begins[None, :], 0), axis=1, dtype=jnp.int32
    )
    row_slot = slot_index[:, None]
    col_slot = slot_index[None, :]
    allowed = live_mask[:, None] & live_mask[None, :] & (
        seq_label[:, None] == seq_label[None, :]
    ) & (col_slot <= row_slot) & (row_slot - col_slot < WINDOW) | (row_slot == col_slot)
    half_dim = HD // 2
    frequency = 10000.0 ** (-2.0 * jnp.arange(half_dim, dtype=jnp.float32) / HD)
    angles = position.astype(jnp.float32)[:, None] * frequency[None, :]
    live_wide = jnp.broadcast_to(live_mask[:, None], (CAP, LANES)).astype(jnp.float32)
    return jnp.concatenate(
        [jnp.cos(angles), jnp.sin(angles), allowed.astype(jnp.float32), live_wide], axis=1
    )


def rms_pull(raw, gain_vec, delta):
    scale = lax.rsqrt(jnp.mean(raw * raw, axis=-1, keepdims=True) + 1e-06)
    weighed = delta * (1.0 + gain_vec)
    shared = jnp.mean(raw * weighed, axis=-1, keepdims=True)
    return scale * weighed - raw * (scale * scale * scale * shared), delta * raw * scale


def rotate_pull(delta, cos_tab, sin_tab):
    half_dim = delta.shape[-1] // 2
    lower_half = delta[:, :half_dim]
    upper_half = delta[:, half_dim:]
    return jnp.concatenate(
        [lower_half * cos_tab + upper_half * sin_tab, upper_half * cos_tab - lower_half * sin_tab],
        axis=-1,
    )


def bit_orders(devices, tuned):
    bits = devices.bit_length() - 1
    if bits == 5:
        return [["cxyab".index(letter) for letter in order] for order in tuned]
    return [[1 + (shift + step) % (bits - 1) for step in range(bits - 1)] for shift in range(3)]


def across(block, bit, devices):
    return lax.ppermute(block, "dp", [(i, i ^ (1 << bit)) for i in range(devices)])


def offset_of(place, order):
    return sum(((place >> k) & 1) << bit for k, bit in enumerate(order))


def gather_chunks(pieces, orders, devices):
    held = [piece[None] for piece in pieces]
    for stage in range(len(orders[0]) - 1):
        came = [across(block, order[stage], devices) for block, order in zip(held, orders)]
        for chunk in range(1, len(came)):
            came[chunk] = lax.optimization_barrier((came[chunk], came[0]))[0]
        held = [jnp.concatenate(pair) for pair in zip(held, came)]
    last = [across(block, order[-1], devices) for block, order in zip(held, orders)]
    chunks = []
    for block, final in zip(held, last):
        if chunks:
            final = lax.optimization_barrier((final, *chunks[0][2:]))[0]
        chunks.append((block, final, across(block, 0, devices), across(final, 0, devices)))
    return chunks


def sent_blocks(chunks, orders, stage, devices):
    return [
        across(away, order[stage], devices)
        for (_, away), order in zip(chunks, orders)
    ]


def merged_blocks(chunks, came):
    merged = []
    for (home, _), arrived in zip(chunks, came):
        half = home.shape[0] // 2

        def added(low, high):
            return home[low:high].astype(jnp.float32) + arrived[low:high].astype(jnp.float32)

        if half:
            merged.append(
                (
                    added(0, half).astype(jnp.bfloat16),
                    added(half, 2 * half).astype(jnp.bfloat16),
                )
            )
        else:
            merged.append((added(0, 1)[0], None))
    return merged


def cut_rows(rows, parts):
    each = -(-rows // (parts * ROWS)) * ROWS
    return [(low, min(low + each, rows)) for low in range(0, rows, each)]


def whole_specs(count):
    return [pl.BlockSpec(memory_space=pltpu.VMEM)] * count


def owner_rows(device, index, order, extra, start, each):
    owner = device ^ extra
    for k, bit in enumerate(order):
        owner = owner ^ (((index >> k) & 1) << bit)
    return owner, owner * each + start


def copy_step(rows):
    return max(step for step in range(ROWS, 513, ROWS) if rows % step == 0)


def each_piece(padded, first, take, visit):
    def visit_plain(shift):
        step = copy_step(take)

        def visit_step(part):
            at = part * step
            visit(at, step, pl.multiple_of(first + shift + at, ROWS))

        if take == step:
            visit_step(0)
        else:
            pl.loop(0, take // step)(visit_step)

    if not padded:
        visit_plain(0)
        return
    units = take // ROWS
    inner = max(count for count in range(1, 41) if units % count == 0)
    number = first // ROWS

    def visit_units(row_of):
        def visit_some(step):
            for part in range(inner):
                at = (step * inner + part) * ROWS
                visit(at, ROWS, row_of(step * inner + part))

        if units == inner:
            visit_some(0)
        else:
            pl.loop(0, units // inner)(visit_some)

    longer = (ROWS + 1) * number
    pl.when(number + units <= padded)(lambda: visit_units(lambda k: longer + (ROWS + 1) * k))
    pl.when(number >= padded)(lambda: visit_plain(padded))
    pl.when((number < padded) & (number + units > padded))(
        lambda: visit_units(lambda k: ROWS * (number + k) + jnp.minimum(number + k, padded))
    )


def spread_blocks(padded, plan, views, device, spread, tails):
    for (order, extra, take, start, each), (block_ref, first_index, count, first_row) in zip(
        plan, views
    ):

        @pl.loop(0, count)
        def _(
            index,
            order=order,
            extra=extra,
            take=take,
            start=start,
            each=each,
            block_ref=block_ref,
            first_index=first_index,
            first_row=first_row,
        ):
            owner, first = owner_rows(device, index, order, extra, start, each)

            def spread_unit(at, unit, row):
                low = first_row + at
                if not isinstance(low, int):
                    low = pl.multiple_of(low, ROWS)
                spread[pl.ds(row, unit), :] = block_ref[
                    first_index + index, pl.ds(low, unit), :
                ].astype(jnp.float32)

            each_piece(padded, first, take, spread_unit)
            if tails is not None:
                tails[owner] = block_ref[index, take : take + tails.shape[1], :]


def pitch_of(columns):
    blocks = columns // LANES
    return blocks + (blocks == ROWS)


def fold_matrices(spread, targets):
    first = 0
    for matrix, offset, rows, columns in targets:
        blocks = columns // LANES
        pitch = pitch_of(columns)

        @pl.loop(0, rows // LANES)
        def _(step, matrix=matrix, offset=offset, blocks=blocks, pitch=pitch, first=first):
            base = first + step * (LANES * pitch)
            at = pl.ds(pl.multiple_of(step * LANES, LANES), LANES)
            for block in range(blocks):
                low = offset + block * LANES
                matrix[at, low : low + LANES] = spread[
                    pl.ds(base + block, LANES, stride=pitch), :
                ].astype(jnp.bfloat16)

        first += rows * pitch


def spread_grads(spread, products):
    first = 0
    for turned, right, columns in products:
        rows = turned.shape[0]
        blocks = columns // LANES
        pitch = pitch_of(columns)
        wide = 2 - blocks % 2
        for block in range(0, blocks, wide):
            product = jnp.dot(
                turned,
                right(block * LANES, (block + wide) * LANES),
                preferred_element_type=jnp.float32,
            )
            for part in range(wide):
                spread[pl.ds(first + block + part, rows, stride=pitch), :] = product[
                    :, part * LANES : (part + 1) * LANES
                ]
        first += rows * pitch


def place_blocks(padded, plan, device, spread, tails, targets):
    for target, order, extra, low, take, start, each in plan:
        target_ref = targets[target]

        @pl.loop(0, target_ref.shape[0])
        def _(
            index,
            target_ref=target_ref,
            order=order,
            extra=extra,
            low=low,
            take=take,
            start=start,
            each=each,
        ):
            owner, first = owner_rows(device, index, order, extra, start or 0, each)
            if start is None:
                target_ref[index, low : low + take, :] = tails[owner].astype(jnp.bfloat16)
                return

            def place_unit(at, unit, row):
                at = low + at
                if not isinstance(at, int):
                    at = pl.multiple_of(at, ROWS)
                target_ref[index, pl.ds(at, unit), :] = spread[pl.ds(row, unit), :].astype(
                    jnp.bfloat16
                )

            each_piece(padded, first, take, place_unit)


def attn_forward(hidden_in, qkv_weight, tables, gains):
    cos_tab = tables[:, :LANES]
    sin_tab = tables[:, LANES : 2 * LANES]
    open_pairs = tables[:, 2 * LANES : 3 * LANES] > 0.0
    gain_query = gains[:, D : D + HD]
    gain_key = gains[:, D + HD : D + 2 * HD]
    normed_in = rms_scale(hidden_in[...].astype(jnp.float32), gains[:, :D]).astype(jnp.bfloat16)
    raw = jnp.dot(normed_in, qkv_weight[...], preferred_element_type=jnp.float32)
    key_raw = raw[:, HQ : HQ + HD]
    values = raw[:, HQ + HD :].astype(jnp.bfloat16)
    keys = rotate(rms_scale(key_raw, gain_key), cos_tab, sin_tab).astype(jnp.bfloat16)
    heads = []
    for head in range(HQ // HD):
        query_raw = raw[:, head * HD : (head + 1) * HD]
        rot_query = rotate(rms_scale(query_raw, gain_query), cos_tab, sin_tab) * HD ** (-0.5)
        rot_query = rot_query.astype(jnp.bfloat16)
        scores = jnp.where(open_pairs, times_transposed(rot_query, keys), -1e30)
        row_max = jnp.max(scores, axis=-1, keepdims=True)
        raised = jnp.exp(scores - row_max)
        summed = jnp.sum(raised, axis=-1, keepdims=True)
        context = jnp.dot(
            (raised / summed).astype(jnp.bfloat16), values, preferred_element_type=jnp.float32
        ).astype(jnp.bfloat16)
        heads.append((query_raw, rot_query, scores, row_max + jnp.log(summed), context))
    return normed_in, key_raw, values, keys, heads, cos_tab, sin_tab


def join_gains(tails, gain_len, gains):
    lane = lax.broadcasted_iota(jnp.int32, (1, LANES), 1)
    tiles = [jnp.zeros((1, LANES), jnp.float32) for _ in range(gains.shape[1] // LANES)]
    for owner in range(tails.shape[0]):
        tile, shift = divmod(owner * gain_len, LANES)
        run = jnp.where(lane < gain_len, tails[owner].astype(jnp.float32)[0:1, :], 0.0)
        if shift:
            run = pltpu.roll(run, shift, 1)
        tiles[tile] += jnp.where(lane >= shift, run, 0.0)
        if shift + gain_len > LANES:
            tiles[tile + 1] += jnp.where(lane < shift, run, 0.0)
    for number, tile in enumerate(tiles):
        gains[:, number * LANES : (number + 1) * LANES] = tile


def attn_forward_kernel(plan, gain_len, device_ref, hidden_in, tables, *refs):
    if not gain_len:
        given, refs = refs[0], refs[1:]
    sources = refs[: len(plan)]
    refs = refs[len(plan) :]
    qkv_weight, out_weight, gains, attn_out, mid_stream = refs[:5]
    staging, spread, tails, context, sems = refs[5:]
    copies, views = [], []
    for number, source in enumerate(sources):
        count = source.shape[0]
        held = staging.at[pl.ds(number * count, count)]
        copies.append(pltpu.make_async_copy(source, held, sems.at[number]))
        views.append((held, 0, count, 0))
    for copy in copies:
        copy.start()
    for copy, step, view in zip(copies, plan, views):
        copy.wait()
        spread_blocks(
            ATTN_PADDED,
            [step],
            [view],
            device_ref[0],
            spread,
            tails if gain_len else None,
        )
    if gain_len:
        join_gains(tails, gain_len, gains)
    else:
        gains[...] = given[...]
    fold_matrices(
        spread,
        (
            (qkv_weight, 0, D, HQ),
            (qkv_weight, HQ, D, HD),
            (qkv_weight, HQ + HD, D, HD),
            (out_weight, 0, HQ, D),
        ),
    )
    heads = attn_forward(hidden_in, qkv_weight, tables, gains)[4]
    for head, parts in enumerate(heads):
        context[:, head * HD : (head + 1) * HD] = parts[-1]
    out = jnp.dot(context[...], out_weight[...], preferred_element_type=jnp.float32)
    attn_out[...] = out
    gain_post = gains[:, D + 2 * HD : 2 * D + 2 * HD]
    mid_stream[...] = hidden_in[...].astype(jnp.float32) + rms_scale(out, gain_post)


def forward_attn(plan, gain_len, tail_rows, devices, device, hidden_in, tables, given, arrays):
    shapes = [
        jax.ShapeDtypeStruct((D, HQ + 2 * HD), jnp.bfloat16),
        jax.ShapeDtypeStruct((HQ, D), jnp.bfloat16),
        jax.ShapeDtypeStruct((1, 4 * D + 2 * HD), jnp.float32),
        jax.ShapeDtypeStruct((CAP, D), jnp.float32),
        jax.ShapeDtypeStruct((CAP, D), jnp.float32),
    ]
    given = [] if gain_len else [given]
    held = (sum(array.shape[0] for array in arrays),) + arrays[0].shape[1:]
    return pl.pallas_call(
        functools.partial(attn_forward_kernel, plan, gain_len),
        out_shape=shapes,
        in_specs=[pl.BlockSpec(memory_space=pltpu.SMEM)]
        + whole_specs(2 + len(given))
        + [pl.BlockSpec(memory_space=pltpu.HBM)] * len(arrays),
        out_specs=whole_specs(len(shapes)),
        scratch_shapes=[
            pltpu.VMEM(held, jnp.bfloat16),
            pltpu.VMEM((G1LEN // LANES + ATTN_PADDED, LANES), jnp.float32),
            pltpu.VMEM((devices, tail_rows, LANES) if gain_len else (1, ROWS, LANES), jnp.bfloat16),
            pltpu.VMEM((CAP, HQ), jnp.bfloat16),
            pltpu.SemaphoreType.DMA((len(arrays),)),
        ],
        compiler_params=pltpu.CompilerParams(vmem_limit_bytes=24 << 20),
        cost_estimate=pl.CostEstimate(flops=0, bytes_accessed=64 << 20, transcendentals=0),
    )(device, hidden_in, tables, *given, *arrays)


def ffn_kernel(
    plan_in,
    staged,
    plan_out,
    device_ref,
    mid_ref,
    attn_out,
    cotangent,
    tables,
    gains,
    *refs,
):
    sources = refs[: len(plan_in)]
    refs = refs[len(plan_in) :]
    block_out, delta_mid_ref, delta_attn_ref, late_gains = refs[:4]
    targets = refs[4:-10]
    spread, gate_weight, up_weight, down_weight = refs[-10:-6]
    gates, ups, hidden, delta_gate, delta_up, sems = refs[-6:]
    device = device_ref[0]
    copies, views = [], []
    for source, (target, first_index, first_row) in zip(sources, staged):
        count, rows = source.shape[:2]
        held = targets[target]
        copies.append(
            pltpu.make_async_copy(
                source,
                held.at[pl.ds(first_index, count), pl.ds(first_row, rows), :],
                sems.at[len(copies)],
            )
        )
        views.append((held, first_index, count, first_row))
    for copy in copies:
        copy.start()
    mid_stream = mid_ref[...]
    gain_post = gains[:, D + 2 * HD : 2 * D + 2 * HD]
    gain_mid = gains[:, 2 * D + 2 * HD : 3 * D + 2 * HD]
    gain_last = gains[:, 3 * D + 2 * HD :]
    normed_mid = rms_scale(mid_stream, gain_mid).astype(jnp.bfloat16)
    for copy, plan, view in zip(copies, plan_in, views):
        copy.wait()
        spread_blocks(FFN_PADDED, [plan], [view], device, spread, None)
    fold_matrices(
        spread, ((gate_weight, 0, D, FF), (up_weight, 0, D, FF), (down_weight, 0, FF, D))
    )
    parts = [slice(low, low + 512) for low in range(0, FF, 512)]
    for at in parts:
        gate = jnp.dot(normed_mid, gate_weight[:, at], preferred_element_type=jnp.float32)
        up = jnp.dot(normed_mid, up_weight[:, at], preferred_element_type=jnp.float32)
        gates[:, at] = gate
        ups[:, at] = up
        hidden[:, at] = gated_gelu(gate, up).astype(jnp.bfloat16)
    ffn_out = jnp.dot(hidden[...], down_weight[...], preferred_element_type=jnp.float32)
    block_out[...] = (mid_stream + rms_scale(ffn_out, gain_last)).astype(jnp.bfloat16)
    delta_out = cotangent[...].astype(jnp.float32) * tables[:, 3 * LANES : 3 * LANES + 1]
    delta_ffn, gain_rows = rms_pull(ffn_out, gain_last, delta_out)
    late_gains[2:3, :] = jnp.sum(gain_rows, axis=0, keepdims=True)
    delta_ffn = delta_ffn.astype(jnp.bfloat16)
    delta_normed = jnp.zeros((CAP, D), jnp.float32)
    for at in parts:
        delta_hidden = times_transposed(delta_ffn, down_weight[at, :])
        gate = gates[:, at]
        raised = jnp.tanh(GELU_SCALE * (gate + 0.044715 * (gate * gate * gate)))
        share = 0.5 * (1.0 + raised)
        slope = share + (0.5 * GELU_SCALE) * gate * (1.0 - raised * raised) * (
            1.0 + (3 * 0.044715) * (gate * gate)
        )
        delta_gate[:, at] = (delta_hidden * ups[:, at] * slope).astype(jnp.bfloat16)
        delta_up[:, at] = (delta_hidden * (gate * share)).astype(jnp.bfloat16)
        delta_normed += times_transposed(delta_gate[:, at], gate_weight[:, at])
        delta_normed += times_transposed(delta_up[:, at], up_weight[:, at])
    delta_part, gain_rows = rms_pull(mid_stream, gain_mid, delta_normed)
    late_gains[1:2, :] = jnp.sum(gain_rows, axis=0, keepdims=True)
    delta_mid = delta_out + delta_part
    delta_mid_ref[...] = delta_mid
    delta_attn, gain_rows = rms_pull(attn_out[...], gain_post, delta_mid)
    late_gains[0:1, :] = jnp.sum(gain_rows, axis=0, keepdims=True)
    delta_attn_ref[...] = delta_attn.astype(jnp.bfloat16)
    turned = normed_mid.T
    spread_grads(
        spread,
        (
            (turned, lambda low, high: delta_gate[:, low:high], FF),
            (turned, lambda low, high: delta_up[:, low:high], FF),
            (hidden[...].T, lambda low, high: delta_ffn[:, low:high], D),
        ),
    )
    place_blocks(FFN_PADDED, plan_out, device, spread, None, targets)


def run_ffn(
    plan_in, staged, plan_out, block_shapes, device, mid, attn_out, cotangent, tables, gains, arrays
):
    flat_rows = G2LEN // LANES + FFN_PADDED
    shapes = [
        jax.ShapeDtypeStruct((CAP, D), jnp.bfloat16),
        jax.ShapeDtypeStruct((CAP, D), jnp.float32),
        jax.ShapeDtypeStruct((CAP, D), jnp.bfloat16),
        jax.ShapeDtypeStruct((3, D), jnp.float32),
    ] + [jax.ShapeDtypeStruct(shape, jnp.bfloat16) for shape in block_shapes]
    wide = pltpu.VMEM((CAP, FF), jnp.float32)
    narrow = pltpu.VMEM((CAP, FF), jnp.bfloat16)
    return pl.pallas_call(
        functools.partial(ffn_kernel, plan_in, staged, plan_out),
        out_shape=shapes,
        in_specs=[pl.BlockSpec(memory_space=pltpu.SMEM)]
        + whole_specs(5)
        + [pl.BlockSpec(memory_space=pltpu.HBM)] * len(arrays),
        out_specs=whole_specs(len(shapes)),
        scratch_shapes=[
            pltpu.VMEM((flat_rows, LANES), jnp.float32),
            pltpu.VMEM((D, FF), jnp.bfloat16),
            pltpu.VMEM((D, FF), jnp.bfloat16),
            pltpu.VMEM((FF, D), jnp.bfloat16),
            wide,
            wide,
            narrow,
            narrow,
            narrow,
            pltpu.SemaphoreType.DMA((len(arrays),)),
        ],
        compiler_params=pltpu.CompilerParams(vmem_limit_bytes=44 << 20),
        cost_estimate=pl.CostEstimate(flops=0, bytes_accessed=0, transcendentals=0),
    )(device, mid, attn_out, cotangent, tables, gains, *arrays)


def attn_back_kernel(
    plan,
    gain_len,
    device_ref,
    delta_attn,
    delta_mid,
    hidden_in,
    tables,
    gains,
    late_gains,
    qkv_weight,
    out_weight,
    grad_in,
    gain_grads,
    *refs,
):
    targets = refs[:-4]
    spread, tails, delta_raws, contexts = refs[-4:]
    device = device_ref[0]
    normed_in, key_raw, values, keys, heads, cos_tab, sin_tab = attn_forward(
        hidden_in, qkv_weight, tables, gains
    )
    gain_query = gains[:, D : D + HD]
    gain_key = gains[:, D + HD : D + 2 * HD]
    delta_context = times_transposed(delta_attn[...], out_weight[...]).astype(jnp.bfloat16)
    delta_key = jnp.zeros((CAP, HD), jnp.float32)
    delta_value = jnp.zeros((CAP, HD), jnp.float32)
    query_gain_rows = jnp.zeros((CAP, HD), jnp.float32)
    for head, (query_raw, queries, scores, log_total, context) in enumerate(heads):
        at = slice(head * HD, (head + 1) * HD)
        contexts[:, at] = context
        head_delta = delta_context[:, at]
        row_dot = jnp.sum(
            head_delta.astype(jnp.float32) * context.astype(jnp.float32), axis=-1, keepdims=True
        )
        prob_exact = jnp.exp(scores - log_total)
        delta_prob = times_transposed(head_delta, values)
        delta_score = prob_exact * (delta_prob - row_dot)
        turned = delta_score.T.astype(jnp.bfloat16)
        delta_score = delta_score.astype(jnp.bfloat16)
        delta_query = jnp.dot(delta_score, keys, preferred_element_type=jnp.float32)
        delta_key += jnp.dot(turned, queries, preferred_element_type=jnp.float32)
        delta_value += jnp.dot(
            prob_exact.T.astype(jnp.bfloat16), head_delta, preferred_element_type=jnp.float32
        )
        delta_rot = rotate_pull(delta_query * HD ** (-0.5), cos_tab, sin_tab)
        delta_raw, gain_rows = rms_pull(query_raw, gain_query, delta_rot)
        query_gain_rows += gain_rows
        delta_raws[:, at] = delta_raw.astype(jnp.bfloat16)
    delta_raw, gain_rows = rms_pull(key_raw, gain_key, rotate_pull(delta_key, cos_tab, sin_tab))
    delta_raws[:, HQ : HQ + HD] = delta_raw.astype(jnp.bfloat16)
    delta_raws[:, HQ + HD :] = delta_value.astype(jnp.bfloat16)
    gain_grads[:, D : D + HD] = jnp.sum(query_gain_rows, axis=0, keepdims=True)
    gain_grads[:, D + HD : D + 2 * HD] = jnp.sum(gain_rows, axis=0, keepdims=True)
    delta_in = times_transposed(delta_raws[...], qkv_weight[...])
    delta_part, gain_rows = rms_pull(
        hidden_in[...].astype(jnp.float32), gains[:, :D], delta_in
    )
    grad_in[...] = delta_mid[...] + delta_part
    gain_grads[:, :D] = jnp.sum(gain_rows, axis=0, keepdims=True)
    for late in range(3):
        at = slice((late + 1) * D + 2 * HD, (late + 2) * D + 2 * HD)
        gain_grads[:, at] = late_gains[late : late + 1, :]
    if gain_len:
        tails[...] = jnp.zeros_like(tails)
        lane = lax.broadcasted_iota(jnp.int32, (1, LANES), 1)
        for owner in range(tails.shape[0]):
            row, shift = divmod(owner * gain_len, LANES)
            piece = gain_grads[:, row * LANES : (row + 1) * LANES]
            if shift:
                piece = pltpu.roll(piece, LANES - shift, 1)
            if shift + gain_len > LANES:
                after = gain_grads[:, (row + 1) * LANES : (row + 2) * LANES]
                after = pltpu.roll(after, LANES - shift, 1)
                piece = jnp.where(lane < LANES - shift, piece, after)
            tails[owner, 0:1, :] = jnp.where(lane < gain_len, piece, 0.0)
    turned = normed_in.T
    delta_attn_value = delta_attn[...]
    spread_grads(
        spread,
        (
            (turned, lambda low, high: delta_raws[:, low:high], HQ),
            (turned, lambda low, high: delta_raws[:, HQ + low : HQ + high], HD),
            (turned, lambda low, high: delta_raws[:, HQ + HD + low : HQ + HD + high], HD),
            (contexts[...].T, lambda low, high: delta_attn_value[:, low:high], D),
        ),
    )
    place_blocks(ATTN_PADDED, plan, device, spread, tails, targets)


def back_attn(plan, gain_len, tail_rows, devices, block_shapes, device, *inputs):
    flat_rows = G1LEN // LANES + ATTN_PADDED
    shapes = [
        jax.ShapeDtypeStruct((CAP, D), jnp.float32),
        jax.ShapeDtypeStruct((1, 4 * D + 2 * HD), jnp.float32),
    ] + [jax.ShapeDtypeStruct(shape, jnp.bfloat16) for shape in block_shapes]
    tail_shape = (devices, tail_rows, LANES) if gain_len else (1, ROWS, LANES)
    return pl.pallas_call(
        functools.partial(attn_back_kernel, plan, gain_len),
        out_shape=shapes,
        in_specs=[pl.BlockSpec(memory_space=pltpu.SMEM)] + whole_specs(len(inputs)),
        out_specs=whole_specs(len(shapes)),
        scratch_shapes=[
            pltpu.VMEM((flat_rows, LANES), jnp.float32),
            pltpu.VMEM(tail_shape, jnp.float32),
            pltpu.VMEM((CAP, HQ + 2 * HD), jnp.bfloat16),
            pltpu.VMEM((CAP, HQ), jnp.bfloat16),
        ],
        compiler_params=pltpu.CompilerParams(vmem_limit_bytes=22 << 20),
        cost_estimate=pl.CostEstimate(flops=0, bytes_accessed=0, transcendentals=0),
    )(device, *inputs)


def gathered_blocks(pieces, chunks, orders, each, devices, device):
    arrays, plan, start = [], [], 0
    for piece, blocks, order in zip(pieces, chunks, orders):
        take = min(piece.shape[0], each - start)
        if each % ROWS:
            places = [offset_of(place, list(order) + [0]) for place in range(devices)]
            back = sorted(range(devices), key=places.__getitem__)
            mixed = offset_bits(device[0], list(order) + [0])
            arrays.append(
                jnp.take(jnp.concatenate(blocks), jnp.array(back, jnp.int32) ^ mixed, axis=0)
            )
            continue
        for part, block in enumerate(blocks):
            plan.append((order[:-1], offset_of(part, [order[-1], 0]), take, start, each))
            arrays.append(block)
        start += take
    if each % ROWS == 0:
        return arrays, plan, None
    table = jnp.concatenate(arrays, axis=1)
    flat = table[:, :each].reshape(1, devices * each, LANES)
    return [flat], [([], 0, devices * each, 0, 0)], table[:, each:]


def offset_bits(device, order):
    return sum(((device >> bit) & 1) << k for k, bit in enumerate(order))


def scatter_plan(each, tail_rows, orders, devices):
    parts = cut_rows(each + tail_rows, len(orders))
    if not tail_rows and each % (3 * ROWS) == 0:
        first = each // 3 - 3 * ROWS
        parts = [(0, first), (first, 2 * each // 3 - 2 * ROWS), (2 * each // 3 - 2 * ROWS, each)]
    half = devices // 2
    if each % ROWS:
        return [(0, [], 0, 0, devices * each, 0, 0)], [(1, devices * each, LANES)], parts
    plan = []
    for with_core in (1, 0):
        for (low, high), order in zip(parts, orders):
            order = order[::-1]
            plan.append((with_core, order, with_core, low, min(high, each) - low, low, each))
            if high > each:
                plan.append((with_core, order, with_core, each, tail_rows, None, each))
    return plan, [(half, each + tail_rows, LANES)] * 2, parts


def blocks_of(found, tails, parts, orders, devices, device):
    if len(found) == 2:
        return found
    table = found[0].reshape(devices, -1, LANES)
    table = table if tails is None else jnp.concatenate([table, tails], axis=1)
    blocks = []
    for with_core in (0, 1):
        chunks = []
        for (low, high), order in zip(parts, orders):
            places = range(devices // 2)
            offsets = [offset_of(place, order[::-1]) ^ with_core for place in places]
            owners = jnp.array(offsets, jnp.int32) ^ device[0]
            chunks.append(jnp.take(table[:, low:high], owners, axis=0))
        blocks.append(jnp.concatenate(chunks, axis=1))
    return blocks


def merge_kernel(parts, *refs):
    pairs = ((refs[0], refs[1]), (refs[2], refs[3]))
    targets = refs[4:]
    half = refs[0].shape[0] // 2
    for number, target in enumerate(targets):
        chunk, second = divmod(number, 2)

        @pl.loop(0, half)
        def _(index, target=target, chunk=chunk, first=second * half):
            at = 0
            for (home, came), (low, high) in zip(pairs, parts[chunk]):
                total = home[first + index, low:high, :].astype(jnp.float32)
                total += came[first + index, low:high, :].astype(jnp.float32)
                target[index, at : at + high - low, :] = total.astype(jnp.bfloat16)
                at += high - low


def cores_merged(parts, *blocks):
    half = blocks[0].shape[0] // 2
    if any((high - low) % ROWS for chunk in parts for low, high in chunk):
        pairs = (blocks[:2], blocks[2:])
        joined = []
        for chunk in parts:
            sums = [
                home[:, low:high].astype(jnp.float32) + came[:, low:high].astype(jnp.float32)
                for (home, came), (low, high) in zip(pairs, chunk)
            ]
            total = jnp.concatenate(sums, axis=1).astype(jnp.bfloat16)
            joined.append((total[:half], total[half:]))
        return joined
    shapes = [
        jax.ShapeDtypeStruct((half, sum(high - low for low, high in chunk), LANES), jnp.bfloat16)
        for chunk in parts
        for _ in range(2)
    ]
    found = pl.pallas_call(
        functools.partial(merge_kernel, parts),
        out_shape=shapes,
        in_specs=whole_specs(4),
        out_specs=whole_specs(len(shapes)),
        compiler_params=pltpu.CompilerParams(vmem_limit_bytes=20 << 20),
        cost_estimate=pl.CostEstimate(flops=0, bytes_accessed=0, transcendentals=0),
    )(*blocks)
    return list(zip(found[::2], found[1::2]))


def adam_update(weight_shard, gradient, moment_one, moment_two):
    moment_one = 0.9 * moment_one + 0.1 * gradient
    moment_two = 0.999 * moment_two + 0.001 * gradient * gradient
    fix_one = 1.0 - 0.9**STEP
    fix_two = 1.0 - 0.999**STEP
    weight_shard = weight_shard - 0.02 * (
        moment_one / fix_one / (jnp.sqrt(moment_two / fix_two) + 1e-08) + 0.1 * weight_shard
    )
    return (weight_shard, moment_one, moment_two)


def per_device(hidden_in, cotangent, params, moment_one, moment_two, seq_lengths, seq_owner):
    devices = lax.axis_size("dp")
    device = lax.axis_index("dp").astype(jnp.int32)
    here = device.reshape(1)
    attn_len = G1LEN // devices
    ffn_len = G2LEN // devices
    gain_len = params.shape[0] - attn_len - ffn_len
    attn_rows = attn_len // LANES
    tail_rows = -(-(attn_rows + 1) // ROWS) * ROWS - attn_rows
    pad = tail_rows * LANES - gain_len
    rounded = params.astype(jnp.bfloat16)
    first_piece = jnp.concatenate(
        [rounded[:attn_len], rounded[attn_len + ffn_len :], jnp.zeros((pad,), jnp.bfloat16)]
    ).reshape(-1, LANES)
    second_piece = rounded[attn_len : attn_len + ffn_len].reshape(-1, LANES)
    ffn_rows = ffn_len // LANES
    second_pieces = [second_piece[low:high] for low, high in cut_rows(ffn_rows, 2)]
    orders = bit_orders(devices, ("abxy", "bxya", "byax"))
    pieces = [first_piece, *second_pieces]
    chunks = gather_chunks(pieces, orders, devices)
    arrays, plan, tails = gathered_blocks(
        pieces[:1], chunks[:1], orders[:1], attn_rows, devices, here
    )
    ffn_arrays, ffn_plan, unused = gathered_blocks(
        pieces[1:], chunks[1:], orders[1:], ffn_rows, devices, here
    )
    aligned = attn_rows % ROWS == 0
    tables = slot_setup(seq_lengths, seq_owner, device)
    given = None
    if not aligned:
        given = tails.reshape(devices, -1)[:, :gain_len].astype(jnp.float32).reshape(1, -1)
    qkv_weight, out_weight, gains, attn_out, mid_stream = forward_attn(
        plan,
        gain_len if aligned else 0,
        tail_rows,
        devices,
        here,
        hidden_in,
        tables,
        given,
        arrays,
    )
    orders = bit_orders(devices, ("yxba", "ayxb", "xayb"))
    out_plan, block_shapes, ffn_parts = scatter_plan(ffn_rows, 0, orders, devices)
    staged = [(0, 0, 0)]
    if len(block_shapes) == 2:
        staged = [
            (part // 2, part % 2 * (devices // 4), low)
            for low, _ in cut_rows(ffn_rows, 2)
            for part in range(4)
        ]
    block_out, delta_mid, delta_attn, late_gains, *found = run_ffn(
        ffn_plan,
        staged,
        out_plan,
        block_shapes,
        here,
        mid_stream,
        attn_out,
        cotangent,
        tables,
        gains,
        ffn_arrays,
    )
    ffn_home, ffn_away = blocks_of(found, None, ffn_parts, orders, devices, here)
    ffn_came = across(ffn_away, 0, devices)
    attn_plan, block_shapes, attn_parts = scatter_plan(attn_rows, tail_rows, orders, devices)
    grad_in, gain_grads, *found = back_attn(
        attn_plan,
        gain_len if aligned else 0,
        tail_rows,
        devices,
        block_shapes,
        here,
        delta_attn,
        delta_mid,
        hidden_in,
        tables,
        gains,
        late_gains,
        qkv_weight,
        out_weight,
    )
    gain_table = None
    if not aligned:
        gain_table = gain_grads.reshape(devices, gain_len).astype(jnp.bfloat16)
        gain_table = jnp.pad(gain_table, ((0, 0), (0, pad))).reshape(devices, tail_rows, LANES)
    attn_home, attn_away = blocks_of(found, gain_table, attn_parts, orders, devices, here)
    attn_came = across(attn_away, 0, devices)
    parts = [
        [cut[chunk] for cut in (ffn_parts, attn_parts) if chunk < len(cut)]
        for chunk in range(len(ffn_parts))
    ]
    chunks = cores_merged(parts, ffn_home, ffn_came, attn_home, attn_came)
    for stage in range(len(orders[0])):
        chunks = merged_blocks(chunks, sent_blocks(chunks, orders, stage, devices))
    rows = [chunk for chunk, _ in chunks]
    ffn_take = [high - low for low, high in ffn_parts]
    ffn_shard = [chunk[:take].reshape(-1) for chunk, take in zip(rows, ffn_take)]
    attn_shard = jnp.concatenate([chunk[take:].reshape(-1) for chunk, take in zip(rows, ffn_take)])
    grad_shard = jnp.concatenate(
        [attn_shard[:attn_len], *ffn_shard, attn_shard[attn_len : attn_len + gain_len]]
    )
    params_new, moment_one_new, moment_two_new = adam_update(
        params, grad_shard, moment_one, moment_two
    )
    return (block_out, grad_in, grad_shard, params_new, moment_one_new, moment_two_new)


def solution(mesh):
    in_specs = (P("dp", None), P("dp", None), P("dp"), P("dp"), P("dp"), P(), P())
    out_specs = (P("dp", None), P("dp", None), P("dp"), P("dp"), P("dp"), P("dp"))
    return jax.shard_map(
        per_device, mesh=mesh, in_specs=in_specs, out_specs=out_specs, check_vma=False
    )
```
